32 devices in a mesh: fsdp: 16 (over z, y, core), tp: 2 (over x).
Axes of the slice: x: 2, y: 2, z: 4, core: 2. Of those that a mesh axis runs over, the one named last changes fastest.
Arguments:
- inputs: bfloat16 [32768, 768], P(('fsdp', 'tp')), may hold values from -6 to 6
- w_query: bfloat16 [768, 768], P('fsdp', 'tp'), may hold values from -0.21875 to 0.21875
- w_key: bfloat16 [768, 768], P('fsdp', 'tp'), may hold values from -0.21875 to 0.21875
- w_value: bfloat16 [768, 768], P('fsdp', 'tp'), may hold values from -0.21875 to 0.21875
- b_query: bfloat16 [768], P(('tp', 'fsdp')), may hold values from -4.5 to 3
- b_key: bfloat16 [768], P(('tp', 'fsdp')), may hold values from -4.5 to 3
- b_value: bfloat16 [768], P(('tp', 'fsdp')), may hold values from -0.29882812 to 0.29882812
- w_out: bfloat16 [768, 768], P('tp', 'fsdp'), may hold values from -6 to 6
- b_out: bfloat16 [768], P('fsdp'), may hold values from -3 to 3
- norm_gain: bfloat16 [768], P('fsdp'), may hold values from 0.25 to 1.75
- norm_shift: bfloat16 [768], P('fsdp'), may hold values from -3 to 3
- w_up: bfloat16 [768, 3072], P('fsdp', 'tp'), may hold values from -0.21875 to 0.21875
- b_up: bfloat16 [3072], P(('tp', 'fsdp')), may hold values from -3 to 3
- w_down: bfloat16 [3072, 768], P('tp', 'fsdp'), may hold values from -0.15625 to 0.15625
- b_down: bfloat16 [768], P('fsdp'), may hold values from -3 to 3
- final_gain: bfloat16 [768], P('fsdp'), may hold values from 0.25 to 1.75
- final_shift: bfloat16 [768], P('fsdp'), may hold values from -3 to 3
- piece_starts: int32 [16, 4], P('fsdp'), may hold values from 0 to 1792, as said below
- grad_output: bfloat16 [32768, 768], P(('fsdp', 'tp')), may hold values from -6 to 6
Outputs:
- output: bfloat16 [32768, 768], P(('fsdp', 'tp'))
- grad_inputs: bfloat16 [32768, 768], P(('fsdp', 'tp'))
- grad_w_query: float32 [768, 768], P('fsdp', 'tp')
- grad_w_key: float32 [768, 768], P('fsdp', 'tp')
- grad_w_value: float32 [768, 768], P('fsdp', 'tp')
- grad_b_query: float32 [768], P(('tp', 'fsdp'))
- grad_b_key: float32 [768], P(('tp', 'fsdp'))
- grad_b_value: float32 [768], P(('tp', 'fsdp'))
- grad_w_out: float32 [768, 768], P('tp', 'fsdp')
- grad_b_out: float32 [768], P('fsdp')
- grad_norm_gain: float32 [768], P('fsdp')
- grad_norm_shift: float32 [768], P('fsdp')
- grad_w_up: float32 [768, 3072], P('fsdp', 'tp')
- grad_b_up: float32 [3072], P(('tp', 'fsdp'))
- grad_w_down: float32 [3072, 768], P('tp', 'fsdp')
- grad_b_down: float32 [768], P('fsdp')
- grad_final_gain: float32 [768], P('fsdp')
- grad_final_shift: float32 [768], P('fsdp')
The draws below stay inside these ranges and needn't reach their ends.
Inputs may be any that keep to these rules, and one draw needn't show every extreme that they name: `piece_starts`: each sequence has 4 picture pieces of 256 tokens with distinct starts, each a multiple of 256.
All inputs are finite; a program needn't handle non-finite values.
Results may differ from the reference program's by a relative error of at most 0.019.
Values may be sent and summed in bfloat16 or wider, within the bound.
No kernel may reach another device: no remote copies, remote signals or barrier semaphores. Data moves between devices by JAX's collectives and lax.ppermute only.
A program may use at most 192 MiB of HBM per device.

```python
import math
import jax
import jax.numpy as jnp
from jax import lax

D = 768
HEADS = 12
HEAD_DIM = 64
FF = 3072
SEQ = 2048
PIECE = 256
PIECES = 4
BLOCK = 512
SEQS = 16
TOKENS = 32768


def draw_piece_starts(key, part):
    slot_count = SEQ // PIECE
    row_keys = jax.random.split(key, SEQS)

    def one_row(row_key):
        return jax.random.permutation(row_key, slot_count)[:PIECES]
    return (jax.vmap(one_row)(row_keys) * PIECE).astype(jnp.int32)


def marked_heads(key):
    marked_count = HEADS - max(1, HEADS // 3)
    chosen = jax.random.permutation(jax.random.fold_in(key, 101), HEADS)[:marked_count]
    head_ids = jnp.arange(HEADS, dtype=jnp.int32)
    marked = jnp.any(chosen.astype(jnp.int32)[:, None] == head_ids[None, :], axis=0).astype(jnp.float32)
    return jnp.repeat(marked, HEAD_DIM)


def bias_draw(key, offset_key):
    normal_part = jax.random.normal(jax.random.fold_in(key, offset_key), (D,), jnp.float32)
    return (0.5 * jnp.clip(normal_part, -6.0, 6.0) - 1.5 * marked_heads(key)).astype(jnp.bfloat16)


def draw_b_query(key, part):
    return bias_draw(key, 11)


def draw_b_key(key, part):
    return bias_draw(key, 13)


def strengthened(values, own_key, source, target, blocks, factor):
    def block_of(axis_at):
        return (jnp.arange(values.shape[axis_at]) // (values.shape[axis_at] // blocks)).reshape((-1,) + (1,) * (values.ndim - 1 - axis_at))

    first = jax.random.permutation(own_key, blocks)[block_of(target)]
    second = (block_of(target) + blocks // 2) % blocks
    return jnp.where((block_of(source) == first) | (block_of(source) == second), factor * values, values)


def steps_of(rng, dims, shards, smallest, largest):
    def one(axis_at, parts):
        draws = jax.random.uniform(jax.random.fold_in(jax.random.fold_in(rng, 6), axis_at), (parts,), jnp.float32, smallest / len(shards), largest / len(shards))
        return jnp.repeat(jnp.exp(draws), dims[axis_at] // parts).reshape((-1,) + (1,) * (len(dims) - axis_at - 1))

    level = one(*shards[0])
    for cut in shards[1:]:
        level = level * one(*cut)
    return level


def scatter_about(stream_key, extent, scale, reach, cuts=(), kind=jnp.bfloat16):
    entries = scale * jax.random.normal(stream_key, extent, jnp.float32)
    if cuts:
        entries = entries * steps_of(stream_key, extent, cuts, -0.22, 0.18)
    return jnp.clip(entries, -reach, reach).astype(kind)


def heavy_noise(stream_key, extent, scale, limit, cuts, heavy, held_as=jnp.bfloat16):
    values = scale * jax.random.normal(stream_key, extent, jnp.float32)
    if cuts:
        values = values * steps_of(stream_key, extent, cuts, -0.22, 0.18)
    return jnp.clip(strengthened(values, jax.random.fold_in(stream_key, 3), *heavy), -limit, limit).astype(held_as)


def setup_inputs(seed: int = 0) -> dict:
    splits = jax.random.split(jax.random.key(seed), 20)
    return {
        "inputs": heavy_noise(splits[0], (TOKENS, D), 1.0, 6.0, ((0, 32),), (0, 1, 32, 2.75)),
        "w_query": scatter_about(splits[1], (D, D), D ** -0.5, 0.21875, ((0, 16), (1, 2))),
        "w_key": scatter_about(splits[2], (D, D), D ** -0.5, 0.21875, ((0, 16), (1, 2))),
        "w_value": scatter_about(splits[3], (D, D), D ** -0.5, 0.21875, ((0, 16), (1, 2))),
        "b_query": draw_b_query(jax.random.fold_in(splits[19], 71), 0),
        "b_key": draw_b_key(jax.random.fold_in(splits[19], 71), 0),
        "b_value": scatter_about(splits[6], (D,), 0.05, 0.29882812, ((0, 32),)),
        "w_out": scatter_about(splits[7], (D, D), (max(1, 4 * D // SEQ)) ** -0.5, 6.0, ((0, 2), (1, 16))),
        "b_out": scatter_about(splits[8], (D,), 0.5, 3.0, ((0, 16),)),
        "norm_gain": jnp.clip(1.0 + 0.15 * jax.random.normal(splits[9], (D,), jnp.float32), 0.25, 1.75).astype(jnp.bfloat16),
        "norm_shift": scatter_about(splits[10], (D,), 0.5, 3.0, ((0, 16),)),
        "w_up": scatter_about(splits[11], (D, FF), D ** -0.5, 0.21875, ((0, 16), (1, 2))),
        "b_up": scatter_about(splits[12], (FF,), 0.5, 3.0, ((0, 32),)),
        "w_down": scatter_about(splits[13], (FF, D), (FF // 2) ** -0.5, 0.15625, ((0, 2), (1, 16))),
        "b_down": scatter_about(splits[14], (D,), 0.5, 3.0, ((0, 16),)),
        "final_gain": jnp.clip(1.0 + 0.15 * jax.random.normal(splits[15], (D,), jnp.float32), 0.25, 1.75).astype(jnp.bfloat16),
        "final_shift": scatter_about(splits[16], (D,), 0.5, 3.0, ((0, 16),)),
        "piece_starts": draw_piece_starts(jax.random.fold_in(splits[19], 71), 0),
        "grad_output": heavy_noise(splits[18], (TOKENS, D), 1.0, 6.0, ((0, 32),), (0, 1, 32, 2.75)),
    }


HIGHEST = lax.Precision.HIGHEST
epsilon = 1e-05

@jax.custom_vjp
def low(v):
    return lax.optimization_barrier(v.astype(jnp.bfloat16)).astype(jnp.float32)

@jax.custom_vjp
def low_back(v):
    return v

def low_keep(v):
    return (low(v), None)

def low_pass(kept, grad):
    return (grad,)

def back_keep(v):
    return (v, None)

def back_low(kept, grad):
    return (low(grad),)
low.defvjp(low_keep, low_pass)
low_back.defvjp(back_keep, back_low)

def layer_norm(values, gain, shift):
    average = lax.optimization_barrier(jnp.mean(values, axis=-1, keepdims=True))
    centred = values - average
    variance = lax.optimization_barrier(jnp.mean(centred * centred, axis=-1, keepdims=True))
    return centred * lax.rsqrt(variance + epsilon) * gain + shift

def features(projected, cosines, sines):
    positive = jax.nn.softplus(projected)
    return jnp.concatenate([positive * cosines, positive * sines], axis=-1)

def block_mask(flags, width):
    places = jnp.arange(width, dtype=jnp.int32)
    causal = places[None, :] <= places[:, None]
    same_piece = places[:, None] // PIECE == places[None, :] // PIECE
    return jnp.logical_or(causal, jnp.logical_and(same_piece, flags[..., :, None])).astype(jnp.float32)

def attend(query_features, key_features, values, flags):
    groups, length = flags.shape
    width = BLOCK
    count = length // width

    def split(array):
        return jnp.moveaxis(array.reshape((groups, count, width) + array.shape[2:]), 1, 0)

    def step(carry, block):
        numerator_state, denominator_state = carry
        query_block, key_block, value_block, flag_block = block
        allowed = block_mask(flag_block, width)
        scores = low_back(jnp.einsum('gihf,gjhf->ghij', query_block, key_block, precision=HIGHEST) * allowed[:, None])
        weights = low(scores)
        numerator = low_back(jnp.einsum('ghij,gjhd->gihd', weights, value_block, precision=HIGHEST) + jnp.einsum('gihf,ghfd->gihd', query_block, low(numerator_state), precision=HIGHEST))
        denominator = jnp.moveaxis(lax.optimization_barrier(jnp.sum(scores, axis=-1)), 1, 2) + jnp.einsum('gihf,ghf->gih', query_block, denominator_state, precision=HIGHEST)
        mixed = numerator / jnp.maximum(denominator, 1.0)[..., None]
        numerator_state = numerator_state + low_back(jnp.einsum('gjhf,gjhd->ghfd', key_block, value_block, precision=HIGHEST))
        denominator_state = denominator_state + lax.optimization_barrier(jnp.sum(key_block, axis=1))
        return ((numerator_state, denominator_state), mixed)
    heads = values.shape[2]
    breadth = query_features.shape[3]
    start = (jnp.zeros((groups, heads, breadth, values.shape[3]), jnp.float32), jnp.zeros((groups, heads, breadth), jnp.float32))
    unused, mixed = lax.scan(jax.checkpoint(step), start, (split(query_features), split(key_features), split(values), split(flags)))
    return jnp.moveaxis(mixed, 0, 1).reshape(values.shape)

def layer_forward(inputs, params, flags):
    w_query, w_key, w_value, b_query, b_key, b_value, w_out, b_out, norm_gain, norm_shift, w_up, b_up, w_down, b_down, final_gain, final_shift = params
    groups, length, width = inputs.shape
    heads = width // HEAD_DIM
    flat = inputs.reshape(groups * length, width)
    angle = 0.5 * jnp.pi / length * jnp.arange(length, dtype=jnp.float32)
    cosines = jnp.cos(angle)[None, :, None, None]
    sines = jnp.sin(angle)[None, :, None, None]
    queries = (low_back(jnp.dot(flat, w_query, precision=HIGHEST)) + b_query).reshape(groups, length, heads, HEAD_DIM)
    keys = (low_back(jnp.dot(flat, w_key, precision=HIGHEST)) + b_key).reshape(groups, length, heads, HEAD_DIM)
    values = low(low_back(jnp.dot(flat, w_value, precision=HIGHEST)) + b_value).reshape(groups, length, heads, HEAD_DIM)
    query_features = low(features(queries, cosines, sines))
    key_features = low(features(keys, cosines, sines))
    mixed = low(attend(query_features, key_features, values, flags)).reshape(groups * length, width)
    attended = low_back(jnp.dot(mixed, w_out, precision=HIGHEST)) + b_out
    hidden = layer_norm(flat + attended, norm_gain, norm_shift)
    lifted = low_back(jnp.dot(low(hidden), w_up, precision=HIGHEST)) + b_up
    active = low(jax.nn.gelu(lifted, approximate=False))
    lowered = low_back(jnp.dot(active, w_down, precision=HIGHEST)) + b_down
    return layer_norm(hidden + lowered, final_gain, final_shift).reshape(groups, length, width)

def reference(inputs, w_query, w_key, w_value, b_query, b_key, b_value, w_out, b_out, norm_gain, norm_shift, w_up, b_up, w_down, b_down, final_gain, final_shift, piece_starts, grad_output):
    params = tuple((weight.astype(jnp.float32) for weight in (w_query, w_key, w_value, b_query, b_key, b_value, w_out, b_out, norm_gain, norm_shift, w_up, b_up, w_down, b_down, final_gain, final_shift)))
    places = jnp.arange(SEQ, dtype=jnp.int32)
    flags = jnp.any(piece_starts[:, :, None] == (places // PIECE * PIECE)[None, None, :], axis=1)
    group = math.gcd(SEQS, max(1, 4096 // SEQ))
    batches = SEQS // group
    shaped_inputs = inputs.astype(jnp.float32).reshape(batches, group, SEQ, D)
    shaped_cotangent = grad_output.astype(jnp.float32).reshape(batches, group, SEQ, D)
    shaped_flags = flags.reshape(batches, group, SEQ)

    def one_batch(total, pieces):
        batch_inputs, batch_cotangent, batch_flags = pieces

        def evaluate(layer_input, weights):
            return layer_forward(layer_input, weights, batch_flags)
        result, pullback = jax.vjp(evaluate, batch_inputs, params)
        grad_in, grad_params = pullback(batch_cotangent)
        total = jax.tree.map(jnp.add, total, grad_params)
        return (total, (result, grad_in))
    zeros = jax.tree.map(jnp.zeros_like, params)
    total, (result, grad_in) = lax.scan(one_batch, zeros, (shaped_inputs, shaped_cotangent, shaped_flags))
    grads = tuple((value / SEQS for value in total))
    return (result.reshape(TOKENS, D).astype(jnp.bfloat16), grad_in.reshape(TOKENS, D).astype(jnp.bfloat16), grads[0], grads[1], grads[2], grads[3], grads[4], grads[5], grads[6], grads[7], grads[8], grads[9], grads[10], grads[11], grads[12], grads[13], grads[14], grads[15])
```

```python
import functools
import math

import jax
import jax.numpy as jnp
from jax import lax
from jax.experimental import pallas as pl
from jax.experimental.pallas import tpu as pltpu
from jax.sharding import PartitionSpec as P

HEAD_DIM = 64
PIECE = 256
LANES = 128
EPSILON = 1e-05
F32 = jnp.float32
BF16 = jnp.bfloat16
BOTH = ("fsdp", "tp")


def dot(left, right):
    return lax.dot_general(left, right, (((1,), (0,)), ((), ())), preferred_element_type=F32)


def dot_nt(left, right):
    return lax.dot_general(left, right, (((1,), (1,)), ((), ())), preferred_element_type=F32)


def dot_tn(left, right):
    return lax.dot_general(left, right, (((0,), (0,)), ((), ())), preferred_element_type=F32)


def flat(ref):
    value = ref[...]
    return value.reshape(value.shape[0] * value.shape[1] * value.shape[2], value.shape[3])


def lane_mask(rows, head, dtype=BF16):
    lane = lax.broadcasted_iota(jnp.int32, (rows, LANES), 1)
    return (lane // HEAD_DIM == head).astype(F32).astype(dtype)


def same_head(rows, columns):
    row = lax.broadcasted_iota(jnp.int32, (rows, columns), 0)
    lane = lax.broadcasted_iota(jnp.int32, (rows, columns), 1)
    return (row // HEAD_DIM) % 2 == (lane // HEAD_DIM) % 2


def compact(state):
    left, right = state[:, :LANES], state[:, LANES:]
    row = lax.broadcasted_iota(jnp.int32, left.shape, 0)
    lane = lax.broadcasted_iota(jnp.int32, left.shape, 1)
    first = (row // HEAD_DIM) % 2 == 0
    low = lane < HEAD_DIM
    return jnp.where(
        low,
        jnp.where(first, left, pltpu.roll(left, HEAD_DIM, 1)),
        jnp.where(first, pltpu.roll(right, HEAD_DIM, 1), right),
    )


def expand(packed):
    row = lax.broadcasted_iota(jnp.int32, packed.shape, 0)
    lane = lax.broadcasted_iota(jnp.int32, packed.shape, 1)
    first = (row // HEAD_DIM) % 2 == 0
    low = lane < HEAD_DIM
    turned = pltpu.roll(packed, HEAD_DIM, 1)
    zero = jnp.zeros_like(packed)
    left = jnp.where(first & low, packed, jnp.where(~first & ~low, turned, zero))
    right = jnp.where(first & low, turned, jnp.where(~first & ~low, packed, zero))
    return jnp.concatenate([left, right], axis=1)


def turned_features(values, cosines, sines):
    wide = values.astype(F32)
    return jnp.concatenate([(wide * cosines).astype(BF16), (wide * sines).astype(BF16)], axis=1)


def params(megabytes=56):
    return pltpu.CompilerParams(vmem_limit_bytes=megabytes * 1024 * 1024)


def whole(shape):
    zeros = (0,) * len(shape)
    return pl.BlockSpec(shape, lambda *_: zeros)


def cost(flops, moved, transcendental=0):
    return pl.CostEstimate(
        flops=int(flops), bytes_accessed=int(moved), transcendentals=int(transcendental)
    )


def project_kernel(
    x_ref, w_ref, b_ref, cos_ref, sin_ref,
    sq_ref, sk_ref, v_ref, gq_ref, gk_ref, st_ref, tot_ref,
    *, block, step,
):
    rows = x_ref.shape[0]
    part = sq_ref.shape[1]
    weights = flat(w_ref)

    def body(index, carry):
        here = pl.ds(index * step, step)
        sums = dot(x_ref[here, :], weights)
        for place, (feature_ref, slope_ref) in enumerate(((sq_ref, gq_ref), (sk_ref, gk_ref))):
            value = sums[:, place * part : (place + 1) * part] + b_ref[0, place : place + 1, :]
            positive = jnp.maximum(value, 0.0) + jnp.log1p(jnp.exp(-jnp.abs(value)))
            feature_ref[here, :] = positive.astype(BF16)
            slope_ref[here, :] = jax.nn.sigmoid(value).astype(BF16)
        v_ref[here, :] = (sums[:, 2 * part :] + b_ref[0, 2:3, :]).astype(BF16)
        return carry

    lax.fori_loop(0, rows // step, body, 0)
    keep = same_head(2 * LANES, 2 * LANES)
    ones = jnp.ones((block, LANES), BF16)
    for pair in range(part // LANES):
        lanes = slice(pair * LANES, (pair + 1) * LANES)
        total = jnp.zeros((2 * LANES, 2 * LANES), F32)
        for place in range(rows // block):
            here = slice(place * block, (place + 1) * block)
            features = turned_features(sk_ref[here, lanes], cos_ref[here, :], sin_ref[here, :])
            state = dot_tn(features, jnp.concatenate([v_ref[here, lanes], ones], axis=1))
            state = jnp.where(keep, state, 0.0)
            st_ref[place, pair] = state.astype(BF16)
            total = total + state
        tot_ref[pair] = compact(total).astype(BF16)


def project(x, w, biases, cosines, sines, block):
    rows, width = x.shape
    groups, halves, shard, _ = w.shape
    part = width // halves
    pairs = width // LANES
    half = pairs // halves
    blocks = rows // block
    row_spec = pl.BlockSpec((rows, part), lambda t: (0, t))
    full = jax.ShapeDtypeStruct((rows, width), BF16)
    return pl.pallas_call(
        functools.partial(project_kernel, block=block, step=256),
        grid=(halves,),
        in_specs=[
            whole((rows, width)),
            pl.BlockSpec((groups, 1, shard, 3 * part), lambda t: (0, t, 0, 0)),
            pl.BlockSpec((1, 3, part), lambda t: (t, 0, 0)),
            whole((rows, LANES)),
            whole((rows, LANES)),
        ],
        out_specs=[
            row_spec, row_spec, row_spec, row_spec, row_spec,
            pl.BlockSpec((blocks, half, 2 * LANES, 2 * LANES), lambda t: (0, t, 0, 0)),
            pl.BlockSpec((half, 2 * LANES, LANES), lambda t: (t, 0, 0)),
        ],
        out_shape=[
            full, full, full, full, full,
            jax.ShapeDtypeStruct((blocks, pairs, 2 * LANES, 2 * LANES), BF16),
            jax.ShapeDtypeStruct((pairs, 2 * LANES, LANES), BF16),
        ],
        compiler_params=params(),
        cost_estimate=cost(2 * rows * width * 3 * width, 16e6),
        name="project",
    )(x, w, biases, cosines, sines)


def attend_kernel(sq_ref, sk_ref, v_ref, cm_ref, cos_ref, sin_ref, st_ref, num_ref, den_ref):
    blocks, block, _ = cm_ref.shape
    piece = min(PIECE, block)
    masks = [lane_mask(block, head) for head in range(2)]
    for place in range(blocks):
        start = place * block
        keys = sk_ref[start : start + block, :]
        values = v_ref[start : start + block, :]
        sides = [jnp.concatenate([values * mask, mask], axis=1) for mask in masks]
        for low in range(0, block, piece):
            here = slice(start + low, start + low + piece)
            span = low + piece
            queries = sq_ref[here, :]
            sums = None
            for mask, side in zip(masks, sides):
                scores = dot_nt(queries * mask[:piece], keys[:span])
                weights = (scores * cm_ref[place, low : low + piece, :span]).astype(BF16)
                term = dot(weights, side[:span])
                sums = term if sums is None else sums + term
            for earlier in range(place):
                sums = sums + dot(
                    turned_features(queries, cos_ref[here, :], sin_ref[here, :]), st_ref[earlier, 0]
                )
            num_ref[here, :] = sums[:, :LANES]
            den_ref[here, :] = sums[:, LANES:]


def attend(sq, sk, v, cm, cosines, sines, states):
    rows, width = sq.shape
    pairs = width // LANES
    blocks = cm.shape[0]
    spec = pl.BlockSpec((rows, LANES), lambda p: (0, p))
    full = jax.ShapeDtypeStruct((rows, width), F32)
    return pl.pallas_call(
        attend_kernel,
        grid=(pairs,),
        in_specs=[
            spec, spec, spec,
            whole(cm.shape), whole((rows, LANES)), whole((rows, LANES)),
            pl.BlockSpec((blocks, 1, 2 * LANES, 2 * LANES), lambda p: (0, p, 0, 0)),
        ],
        out_specs=[spec, spec],
        out_shape=[full, full],
        compiler_params=params(),
        cost_estimate=cost(8e9, 14e6),
        name="attend",
    )(sq, sk, v, cm, cosines, sines, states)


def norm_rows(values):
    average = jnp.mean(values, axis=1, keepdims=True)
    centred = values - average
    scale = lax.rsqrt(jnp.mean(centred * centred, axis=1, keepdims=True) + EPSILON)
    return centred * scale, scale


def mix_kernel(
    num_ref, den_ref, sq_ref, in_ref, cos_ref, sin_ref, w_ref, x_ref, vec_ref,
    mixed_ref, rden_ref, normal_ref, scale_ref, low_ref, wide_ref,
):
    pairs = in_ref.shape[0]
    halves = w_ref.shape[1]
    rows, width = x_ref.shape
    part = width // halves

    @pl.when(pl.program_id(0) == 0)
    def _():
        for pair in range(pairs):
            wide_ref[pair] = expand(in_ref[pair].astype(F32)).astype(BF16)

    for pair in range(pairs):
        lanes = slice(pair * LANES, (pair + 1) * LANES)
        sums = dot(turned_features(sq_ref[:, lanes], cos_ref[...], sin_ref[...]), wide_ref[pair])
        inverse = 1.0 / jnp.maximum(den_ref[:, lanes] + sums[:, LANES:], 1.0)
        rden_ref[:, lanes] = inverse
        mixed_ref[:, lanes] = ((num_ref[:, lanes] + sums[:, :LANES]) * inverse).astype(BF16)
    total = x_ref[...].astype(F32) + vec_ref[0:1, :]
    for half in range(halves):
        side = w_ref[:, half]
        side = side.reshape(width, part)
        total = total + dot_nt(mixed_ref[:, half * part : (half + 1) * part], side)
    normal, scale = norm_rows(total)
    normal_ref[...] = normal
    scale_ref[...] = jnp.broadcast_to(scale, scale_ref.shape)
    low_ref[...] = (normal * vec_ref[1:2, :] + vec_ref[2:3, :]).astype(BF16)


def mix(num, den, sq, incoming, cosines, sines, w, x, vectors, step):
    rows, width = x.shape
    groups, halves, shard, _ = w.shape
    part = width // halves
    pairs = incoming.shape[0]
    wide = pl.BlockSpec((step, width), lambda i: (i, 0))
    thin = pl.BlockSpec((step, LANES), lambda i: (i, 0))
    return pl.pallas_call(
        mix_kernel,
        grid=(rows // step,),
        in_specs=[
            wide, wide, wide, whole(incoming.shape), thin, thin,
            pl.BlockSpec((groups, halves, shard, part), lambda i: (0, 0, 0, 3)),
            wide, whole(vectors.shape),
        ],
        out_specs=[wide, wide, wide, thin, wide],
        out_shape=[
            jax.ShapeDtypeStruct((rows, width), BF16),
            jax.ShapeDtypeStruct((rows, width), F32),
            jax.ShapeDtypeStruct((rows, width), F32),
            jax.ShapeDtypeStruct((rows, LANES), F32),
            jax.ShapeDtypeStruct((rows, width), BF16),
        ],
        scratch_shapes=[pltpu.VMEM((pairs, 2 * LANES, 2 * LANES), BF16)],
        compiler_params=params(),
        cost_estimate=cost(2 * rows * width * width * 2, 20e6),
        name="mix",
    )(num, den, sq, incoming, cosines, sines, w, x, vectors)


def norm_back(upstream, normal, scale, gain):
    scaled = upstream * gain
    inner = (
        scaled
        - jnp.mean(scaled, axis=1, keepdims=True)
        - normal * jnp.mean(scaled * normal, axis=1, keepdims=True)
    )
    return inner * scale


def lift_kernel(
    low_ref, up_ref, down_ref, bias_ref, normal_ref, vec_ref, grad_ref,
    act_ref, slope_ref, out_ref, branch_ref, second_ref, sum_ref, total_ref,
    *, step,
):
    rows, width = low_ref.shape
    up, down = flat(up_ref), flat(down_ref)
    index = pl.program_id(0)
    last = pl.num_programs(0) - 1

    def body(place, carry):
        here = pl.ds(place * step, step)
        lifted = dot(low_ref[here, :], up) + bias_ref[0:1, :]
        share = 0.5 + 0.5 * lax.erf(lifted * math.sqrt(0.5))
        bell = jnp.exp(-0.5 * lifted * lifted) * (1.0 / math.sqrt(2.0 * math.pi))
        active = (lifted * share).astype(BF16)
        act_ref[here, :] = active
        slope_ref[here, :] = (share + lifted * bell).astype(BF16)
        term = dot_nt(active, down)

        @pl.when(index == 0)
        def _():
            total_ref[here, :] = term

        @pl.when(index > 0)
        def _():
            total_ref[here, :] = total_ref[here, :] + term

        return carry

    lax.fori_loop(0, rows // step, body, 0)

    @pl.when(index == last)
    def _():
        sum_ref[...] = jnp.zeros_like(sum_ref)

        def finish(place, carry):
            here = pl.ds(place * step, step)
            hidden = normal_ref[here, :] * vec_ref[1:2, :] + vec_ref[2:3, :]
            normal, scale = norm_rows(hidden + total_ref[here, :] + vec_ref[3:4, :])
            gain = vec_ref[4:5, :]
            out_ref[here, :] = (normal * gain + vec_ref[5:6, :]).astype(BF16)
            upstream = grad_ref[here, :].astype(F32)
            second = norm_back(upstream, normal, scale, gain)
            second_ref[here, :] = second
            branch_ref[here, :] = second.astype(BF16)
            sum_ref[0:1, :] += jnp.sum(upstream * normal, axis=0, keepdims=True)
            sum_ref[1:2, :] += jnp.sum(upstream, axis=0, keepdims=True)
            sum_ref[2:3, :] += jnp.sum(second, axis=0, keepdims=True)
            return carry

        lax.fori_loop(0, rows // step, finish, 0)


def lift(low, w, bias, normal, vectors, grad, tile):
    rows, width = low.shape
    groups, halves, shard, columns = w.shape
    units = columns // 2
    tiles = units // tile
    unit_spec = pl.BlockSpec((rows, tile), lambda i: (0, i))
    return pl.pallas_call(
        functools.partial(lift_kernel, step=256),
        grid=(halves * tiles,),
        in_specs=[
            whole((rows, width)),
            pl.BlockSpec((groups, 1, shard, tile), lambda i: (0, i // tiles, 0, i % tiles)),
            pl.BlockSpec((groups, 1, shard, tile), lambda i: (0, i // tiles, 0, tiles + i % tiles)),
            pl.BlockSpec((1, tile), lambda i: (0, i)),
            whole((rows, width)),
            whole(vectors.shape),
            whole((rows, width)),
        ],
        out_specs=[
            unit_spec, unit_spec, whole((rows, width)), whole((rows, width)),
            whole((rows, width)), whole((8, width)),
        ],
        out_shape=[
            jax.ShapeDtypeStruct((rows, halves * units), BF16),
            jax.ShapeDtypeStruct((rows, halves * units), BF16),
            jax.ShapeDtypeStruct((rows, width), BF16),
            jax.ShapeDtypeStruct((rows, width), BF16),
            jax.ShapeDtypeStruct((rows, width), F32),
            jax.ShapeDtypeStruct((8, width), F32),
        ],
        scratch_shapes=[pltpu.VMEM((rows, width), F32)],
        compiler_params=params(),
        cost_estimate=cost(4 * rows * width * halves * units, 40e6),
        name="lift",
    )(low, w, w, bias, normal, vectors, grad)


def lower_kernel(
    branch_ref, low_ref, act_ref, slope_ref, up_ref, down_ref, second_ref, normal_ref, scale_ref,
    vec_ref,
    gdown_ref, gup_ref, gbias_ref, first_ref, firstlow_ref, sum_ref,
    total_ref, turned_branch_ref, turned_low_ref, gl_ref,
    *, step,
):
    rows, width = low_ref.shape
    index = pl.program_id(0)
    last = pl.num_programs(0) - 1
    up, down = flat(up_ref), flat(down_ref)

    @pl.when(index == 0)
    def _():
        turned_branch_ref[...] = branch_ref[...].T
        turned_low_ref[...] = low_ref[...].T

    gdown_ref[...] = dot(turned_branch_ref[...], act_ref[...]).astype(BF16).reshape(gdown_ref.shape)
    gbias_ref[...] = jnp.zeros_like(gbias_ref)

    def body(place, carry):
        here = pl.ds(place * step, step)
        slope = dot(branch_ref[here, :], down) * slope_ref[here, :].astype(F32)
        gbias_ref[0:1, :] += jnp.sum(slope, axis=0, keepdims=True)
        slope = slope.astype(BF16)
        gl_ref[here, :] = slope
        term = dot_nt(slope, up)

        @pl.when(index == 0)
        def _():
            total_ref[here, :] = second_ref[here, :] + term

        @pl.when(index > 0)
        def _():
            total_ref[here, :] = total_ref[here, :] + term

        return carry

    lax.fori_loop(0, rows // step, body, 0)
    gup_ref[...] = dot(turned_low_ref[...], gl_ref[...]).astype(BF16).reshape(gup_ref.shape)

    @pl.when(index == last)
    def _():
        sum_ref[...] = jnp.zeros_like(sum_ref)

        def finish(place, carry):
            here = pl.ds(place * step, step)
            upstream = total_ref[here, :]
            normal = normal_ref[here, :]
            first = norm_back(upstream, normal, scale_ref[here, 0:1], vec_ref[1:2, :])
            first_ref[here, :] = first
            firstlow_ref[here, :] = first.astype(BF16)
            sum_ref[0:1, :] += jnp.sum(upstream * normal, axis=0, keepdims=True)
            sum_ref[1:2, :] += jnp.sum(upstream, axis=0, keepdims=True)
            sum_ref[2:3, :] += jnp.sum(first, axis=0, keepdims=True)
            return carry

        lax.fori_loop(0, rows // step, finish, 0)


def lower(branch, low, act, slope, w, second, normal, scale, vectors, tile):
    rows, width = low.shape
    groups, halves, shard, columns = w.shape
    units = columns // 2
    tiles = units // tile
    unit_spec = pl.BlockSpec((rows, tile), lambda i: (0, i))
    up_spec = pl.BlockSpec((groups, 1, shard, tile), lambda i: (0, i // tiles, 0, i % tiles))
    grad_shape = jax.ShapeDtypeStruct((groups, halves, shard, units), BF16)
    once = functools.partial(pl.BlockSpec, pipeline_mode=pl.Buffered(1))
    row_once = once((rows, width), lambda i: (0, 0))
    return pl.pallas_call(
        functools.partial(lower_kernel, step=256),
        grid=(halves * tiles,),
        in_specs=[
            row_once, row_once, unit_spec, unit_spec, up_spec,
            pl.BlockSpec((groups, 1, shard, tile), lambda i: (0, i // tiles, 0, tiles + i % tiles)),
            row_once, row_once,
            whole((rows, LANES)), whole(vectors.shape),
        ],
        out_specs=[
            up_spec, up_spec, pl.BlockSpec((8, tile), lambda i: (0, i)),
            whole((rows, width)), whole((rows, width)), whole((8, width)),
        ],
        out_shape=[
            grad_shape, grad_shape, jax.ShapeDtypeStruct((8, halves * units), F32),
            jax.ShapeDtypeStruct((rows, width), F32),
            jax.ShapeDtypeStruct((rows, width), BF16),
            jax.ShapeDtypeStruct((8, width), F32),
        ],
        scratch_shapes=[
            pltpu.VMEM((rows, width), F32),
            pltpu.VMEM((width, rows), BF16),
            pltpu.VMEM((width, rows), BF16),
            pltpu.VMEM((rows, tile), BF16),
        ],
        compiler_params=params(),
        cost_estimate=cost(8 * rows * width * halves * units, 50e6),
        name="lower",
    )(branch, low, act, slope, w, w, second, normal, scale, vectors)


def unmix_kernel(
    first_ref, mixed_ref, rden_ref, sq_ref, cos_ref, sin_ref, w_ref,
    gout_ref, gn_ref, gd_ref, st_ref, tot_ref, *, block, step,
):
    rows, width = first_ref.shape
    part = mixed_ref.shape[1]
    side = flat(w_ref)
    group_row = lax.broadcasted_iota(jnp.int32, (LANES, LANES), 0)
    group_lane = lax.broadcasted_iota(jnp.int32, (LANES, LANES), 1)
    group = (group_row // HEAD_DIM == group_lane // HEAD_DIM).astype(F32).astype(BF16)
    lane = lax.broadcasted_iota(jnp.int32, (step, LANES), 1) % HEAD_DIM

    def body(place, carry):
        here = pl.ds(place * step, step)
        grad = dot(first_ref[here, :], side)
        for pair in range(part // LANES):
            lanes = slice(pair * LANES, (pair + 1) * LANES)
            inverse = rden_ref[here, lanes]
            scaled = grad[:, lanes] * inverse
            product = scaled * mixed_ref[here, lanes].astype(F32)
            high = product.astype(BF16)
            rest = (product - high.astype(F32)).astype(BF16)
            inner = dot(high, group) + dot(rest, group)
            slope = jnp.where(inverse < 1.0, -inner, 0.0)
            high = slope.astype(BF16).astype(F32)
            gn_ref[here, lanes] = scaled.astype(BF16)
            gd_ref[here, lanes] = jnp.where(
                lane == 0, high, jnp.where(lane == 1, slope - high, 0.0)
            ).astype(BF16)
        return carry

    lax.fori_loop(0, rows // step, body, 0)
    gout_ref[...] = dot_tn(first_ref[...], mixed_ref[...]).astype(BF16).reshape(gout_ref.shape)
    keep = same_head(2 * LANES, 2 * LANES)
    for pair in range(part // LANES):
        lanes = slice(pair * LANES, (pair + 1) * LANES)
        total = jnp.zeros((2 * LANES, 2 * LANES), F32)
        for place in range(rows // block):
            here = slice(place * block, (place + 1) * block)
            features = turned_features(sq_ref[here, lanes], cos_ref[here, :], sin_ref[here, :])
            state = dot_tn(
                features, jnp.concatenate([gn_ref[here, lanes], gd_ref[here, lanes]], axis=1)
            )
            state = jnp.where(keep, state, 0.0)
            st_ref[place, pair] = state.astype(BF16)
            total = total + state
        tot_ref[pair] = compact(total).astype(BF16)


def unmix(first, mixed, rden, sq, cosines, sines, w, block):
    rows, width = first.shape
    groups, halves, shard, _ = w.shape
    part = width // halves
    pairs = width // LANES
    half = pairs // halves
    blocks = rows // block
    row_spec = pl.BlockSpec((rows, part), lambda t: (0, t))
    full = jax.ShapeDtypeStruct((rows, width), BF16)
    return pl.pallas_call(
        functools.partial(unmix_kernel, block=block, step=256),
        grid=(halves,),
        in_specs=[
            whole((rows, width)), row_spec, row_spec, row_spec,
            whole((rows, LANES)), whole((rows, LANES)),
            pl.BlockSpec((groups, 1, shard, part), lambda t: (0, t, 0, 3)),
        ],
        out_specs=[
            pl.BlockSpec((groups, 1, shard, part), lambda t: (0, t, 0, 0)),
            row_spec, row_spec,
            pl.BlockSpec((blocks, half, 2 * LANES, 2 * LANES), lambda t: (0, t, 0, 0)),
            pl.BlockSpec((half, 2 * LANES, LANES), lambda t: (t, 0, 0)),
        ],
        out_shape=[
            jax.ShapeDtypeStruct((groups, halves, shard, part), BF16),
            full, full,
            jax.ShapeDtypeStruct((blocks, pairs, 2 * LANES, 2 * LANES), BF16),
            jax.ShapeDtypeStruct((pairs, 2 * LANES, LANES), BF16),
        ],
        compiler_params=params(),
        cost_estimate=cost(4 * rows * width * width, 16e6),
        name="unmix",
    )(first, mixed, rden, sq, cosines, sines, w)


def unattend_kernel(
    sq_ref, sk_ref, v_ref, gn_ref, gd_ref, cm_ref, cos_ref, sin_ref, st_ref, in_ref, lt_ref, gq_ref,
    query_ref, dk_ref, dv_ref, sum_ref,
):
    blocks, block, _ = cm_ref.shape
    piece = min(PIECE, block)
    masks = [lane_mask(block, head) for head in range(2)]
    ones = jnp.ones((block, LANES), BF16)
    incoming = expand(in_ref[0].astype(F32))
    sum_ref[...] = jnp.zeros_like(sum_ref)
    for place in range(blocks):
        start = place * block
        all_here = slice(start, start + block)
        keys, values = sk_ref[all_here, :], v_ref[all_here, :]
        sides = jnp.concatenate([values, ones], axis=1)
        key_sides = [keys * mask for mask in masks]
        state = incoming
        for earlier in range(place):
            state = state + st_ref[earlier, 0].astype(F32)
        state = state.astype(BF16)
        grad_keys = [None] * (block // piece)
        grad_values = [None] * (block // piece)
        for low in range(0, block, piece):
            here = slice(start + low, start + low + piece)
            span = low + piece
            queries, grads, slopes = sq_ref[here, :], gn_ref[here, :], gd_ref[here, :]
            grad_queries = None
            for head in range(2):
                mask = masks[head][:piece]
                cm = cm_ref[place, low : low + piece, :span]
                masked_queries, masked_grads = queries * mask, grads * mask
                scores = dot_nt(masked_queries, keys[:span])
                weights = (scores * cm).astype(BF16)
                back = dot_nt(
                    jnp.concatenate([masked_grads, slopes * mask], axis=1), sides[:span]
                )
                back = (back * cm).astype(BF16)
                term = dot(back, key_sides[head][:span])
                grad_queries = term if grad_queries is None else grad_queries + term
                key_term = dot_tn(back, masked_queries)
                value_term = dot_tn(weights, masked_grads)
                for piece_at in range(span // piece):
                    at = slice(piece_at * piece, (piece_at + 1) * piece)
                    old = grad_keys[piece_at]
                    grad_keys[piece_at] = key_term[at] if old is None else old + key_term[at]
                    old = grad_values[piece_at]
                    grad_values[piece_at] = value_term[at] if old is None else old + value_term[at]
            far = dot_nt(jnp.concatenate([grads, slopes], axis=1), state)
            grad_queries = (
                grad_queries
                + far[:, :LANES] * cos_ref[here, :]
                + far[:, LANES:] * sin_ref[here, :]
            ) * gq_ref[here, :].astype(F32)
            query_ref[here, :] = grad_queries.astype(BF16)
            sum_ref[0:1, :] += jnp.sum(grad_queries, axis=0, keepdims=True)
        grad_keys = jnp.concatenate(grad_keys, axis=0)
        grad_values = jnp.concatenate(grad_values, axis=0)
        for later in range(place + 1, blocks):
            far = dot_nt(sides, lt_ref[later, 0])
            grad_keys = (
                grad_keys
                + far[:, :LANES] * cos_ref[all_here, :]
                + far[:, LANES:] * sin_ref[all_here, :]
            )
            features = turned_features(keys, cos_ref[all_here, :], sin_ref[all_here, :])
            grad_values = grad_values + dot(features, lt_ref[later, 0][:, :LANES])
        dk_ref[all_here, :] = grad_keys
        dv_ref[all_here, :] = grad_values


def unattend(sq, sk, v, gn, gd, cm, cosines, sines, states, incoming, later, slope_q):
    rows, width = sq.shape
    pairs = width // LANES
    blocks = cm.shape[0]
    spec = pl.BlockSpec((rows, LANES), lambda p: (0, p))
    state_spec = pl.BlockSpec((blocks, 1, 2 * LANES, 2 * LANES), lambda p: (0, p, 0, 0))
    full = jax.ShapeDtypeStruct((rows, width), F32)
    return pl.pallas_call(
        unattend_kernel,
        grid=(pairs,),
        in_specs=[
            spec, spec, spec, spec, spec,
            whole(cm.shape), whole((rows, LANES)), whole((rows, LANES)),
            state_spec,
            pl.BlockSpec((1, 2 * LANES, LANES), lambda p: (p, 0, 0)),
            state_spec, spec,
        ],
        out_specs=[spec, spec, spec, pl.BlockSpec((8, LANES), lambda p: (0, p))],
        out_shape=[
            jax.ShapeDtypeStruct((rows, width), BF16), full, full,
            jax.ShapeDtypeStruct((8, width), F32),
        ],
        compiler_params=params(),
        cost_estimate=cost(20e9, 20e6),
        name="unattend",
    )(sq, sk, v, gn, gd, cm, cosines, sines, states, incoming, later, slope_q)


def tail_kernel(
    dk_ref, dv_ref, sk_ref, v_ref, gk_ref, cos_ref, sin_ref, in_ref, key_ref, value_ref, sum_ref,
):
    rows = dk_ref.shape[0]
    state = expand(in_ref[0].astype(F32)).astype(BF16)
    ones = jnp.ones((rows, LANES), BF16)
    far = dot_nt(jnp.concatenate([v_ref[...], ones], axis=1), state)
    cosines, sines = cos_ref[...], sin_ref[...]
    keys = (dk_ref[...] + far[:, :LANES] * cosines + far[:, LANES:] * sines) * gk_ref[...].astype(F32)
    values = dv_ref[...] + dot(turned_features(sk_ref[...], cosines, sines), state[:, :LANES])
    key_ref[...] = keys.astype(BF16)
    value_ref[...] = values.astype(BF16)
    sum_ref[...] = jnp.zeros_like(sum_ref)
    sum_ref[0:1, :] = jnp.sum(keys, axis=0, keepdims=True)
    sum_ref[1:2, :] = jnp.sum(values, axis=0, keepdims=True)


def tail(dk, dv, sk, v, slope_k, cosines, sines, incoming):
    rows, width = sk.shape
    pairs = width // LANES
    spec = pl.BlockSpec((rows, LANES), lambda p: (0, p))
    return pl.pallas_call(
        tail_kernel,
        grid=(pairs,),
        in_specs=[
            spec, spec, spec, spec, spec, whole((rows, LANES)), whole((rows, LANES)),
            pl.BlockSpec((1, 2 * LANES, LANES), lambda p: (p, 0, 0)),
        ],
        out_specs=[spec, spec, pl.BlockSpec((8, LANES), lambda p: (0, p))],
        out_shape=[
            jax.ShapeDtypeStruct((rows, width), BF16),
            jax.ShapeDtypeStruct((rows, width), BF16),
            jax.ShapeDtypeStruct((8, width), F32),
        ],
        compiler_params=params(),
        cost_estimate=cost(2e9, 14e6),
        name="tail",
    )(dk, dv, sk, v, slope_k, cosines, sines, incoming)


def weights_kernel(x_ref, q_ref, k_ref, v_ref, g_ref, turned_ref):
    @pl.when(pl.program_id(0) == 0)
    def _():
        turned_ref[...] = x_ref[...].T

    part = q_ref.shape[1]
    for place, ref in enumerate((q_ref, k_ref, v_ref)):
        product = dot(turned_ref[...], ref[...]).astype(BF16)
        g_ref[:, :, :, place * part : (place + 1) * part] = product.reshape(
            g_ref.shape[:3] + (part,)
        )


def weight_gradients(x, q, k, v, groups, halves, shard):
    rows, width = x.shape
    part = width // halves
    spec = pl.BlockSpec((rows, part), lambda t: (0, t))
    return pl.pallas_call(
        weights_kernel,
        grid=(halves,),
        in_specs=[whole((rows, width)), spec, spec, spec],
        out_specs=pl.BlockSpec((groups, 1, shard, 3 * part), lambda t: (0, t, 0, 0)),
        out_shape=jax.ShapeDtypeStruct((groups, halves, shard, 3 * part), BF16),
        scratch_shapes=[pltpu.VMEM((width, rows), BF16)],
        compiler_params=params(),
        cost_estimate=cost(2 * rows * width * 3 * width, 10e6),
        name="weight_gradients",
    )(x, q, k, v)


def inputs_kernel(first_ref, q_ref, k_ref, v_ref, w_ref, out_ref):
    halves = w_ref.shape[1]
    width = first_ref.shape[1]
    part = width // halves
    total = first_ref[...]
    for half in range(halves):
        side = w_ref[:, half].reshape(width, 3 * part)
        at = slice(half * part, (half + 1) * part)
        joined = jnp.concatenate([q_ref[:, at], k_ref[:, at], v_ref[:, at]], axis=1)
        total = total + dot_nt(joined, side)
    out_ref[...] = total.astype(BF16)


def input_gradient(first, q, k, v, w, step):
    rows, width = first.shape
    groups, halves, shard, _ = w.shape
    part = width // halves
    spec = pl.BlockSpec((step, width), lambda i: (i, 0))
    return pl.pallas_call(
        inputs_kernel,
        grid=(rows // step,),
        in_specs=[
            spec, spec, spec, spec,
            pl.BlockSpec((groups, halves, shard, 3 * part), lambda i: (0, 0, 0, 0)),
        ],
        out_specs=spec,
        out_shape=jax.ShapeDtypeStruct((rows, width), BF16),
        compiler_params=params(),
        cost_estimate=cost(2 * rows * width * 3 * width, 14e6),
        name="input_gradient",
    )(first, q, k, v, w)


def local(
    inputs, w_query, w_key, w_value, b_query, b_key, b_value, w_out, b_out, norm_gain, norm_shift,
    w_up, b_up, w_down, b_down, final_gain, final_shift, piece_starts, grad_output,
):
    rows, width = inputs.shape
    halves = lax.axis_size("tp")
    replicas = lax.axis_size("fsdp")
    length = rows * halves
    block = min(512, length)
    blocks = rows // block
    shard = width // replicas
    part = width // halves
    units = w_up.shape[1]
    me = lax.axis_index("tp")
    aligned = shard % 16 == 0
    groups, deep = (replicas, shard) if aligned else (1, width)

    places = me * rows + jnp.arange(rows, dtype=jnp.int32)
    flags = jnp.any(piece_starts[0][:, None] == (places // PIECE * PIECE)[None, :], axis=0)
    angle = 0.5 * jnp.pi / length * places.astype(F32)
    cosines, sines = jnp.cos(angle), jnp.sin(angle)
    at = jnp.arange(block, dtype=jnp.int32)
    allowed = (at[None, None, :] <= at[None, :, None]) | (
        (at[None, None, :] // PIECE == at[None, :, None] // PIECE)
        & flags.reshape(blocks, block)[:, :, None]
    )
    c, s = cosines.reshape(blocks, block), sines.reshape(blocks, block)
    cm = jnp.where(allowed, c[:, :, None] * c[:, None, :] + s[:, :, None] * s[:, None, :], 0.0)
    cosines = jnp.broadcast_to(cosines[:, None], (rows, LANES))
    sines = jnp.broadcast_to(sines[:, None], (rows, LANES))

    thin = jnp.concatenate(
        [b_query, b_key, b_value, b_up, b_out, norm_gain, norm_shift, b_down, final_gain, final_shift]
    )
    slots = thin.shape[0] // shard
    spare = LANES - slots - (1 if thin.shape[0] % shard else 0)
    thin = jnp.pad(thin, (0, (LANES - spare) * shard - thin.shape[0])).reshape(LANES - spare, shard).T
    thin = jnp.pad(thin, ((0, 0), (0, spare)))
    attention_shard = jnp.concatenate([w_query, w_key, w_value, w_out.T, thin], axis=1)
    forward_shard = jnp.concatenate([w_up, w_down.T], axis=1)

    def gather(piece):
        whole_piece = lax.all_gather(piece, BOTH, axis=0, tiled=False)
        whole_piece = whole_piece.reshape(replicas, halves, shard, piece.shape[1])
        if not aligned:
            whole_piece = jnp.moveaxis(whole_piece, 1, 0).reshape(1, halves, width, piece.shape[1])
        return whole_piece

    w_attention = gather(attention_shard)
    w_forward = gather(forward_shard)

    thin = w_attention[..., 4 * part : 4 * part + LANES - spare]
    thin = thin.reshape(replicas, halves, shard, LANES - spare) if aligned else jnp.moveaxis(
        thin.reshape(halves, replicas, shard, LANES - spare), 0, 1
    )
    thin = jnp.moveaxis(thin, 3, 2).reshape(replicas, halves, -1).astype(F32)
    edge = shard // halves
    starts = [0, edge, 2 * edge, 3 * edge]
    biases = jnp.stack(
        [
            jnp.moveaxis(thin[:, :, begin : begin + edge], 0, 1).reshape(halves, part)
            for begin in starts[:3]
        ],
        axis=1,
    )
    begin = 3 * edge
    bias_up = jnp.moveaxis(thin[:, :, begin : begin + units // replicas], 0, 1).reshape(1, halves * units)
    begin += units // replicas
    vectors = jnp.stack(
        [
            thin[:, 0, begin + place * shard : begin + (place + 1) * shard].reshape(width)
            for place in range(6)
        ]
    )
    vectors = jnp.pad(vectors, ((0, 2), (0, 0)))

    sq, sk, v, slope_q, slope_k, states, total = project(
        inputs, w_attention, biases, cosines, sines, block
    )
    incoming = lax.ppermute(total, "tp", [(i, i + 1) for i in range(halves - 1)])
    num, den = attend(sq, sk, v, cm, cosines, sines, states)
    mixed, rden, normal, scale, low = mix(
        num, den, sq, incoming, cosines, sines, w_attention, inputs, vectors, 256
    )
    act, slope, output, branch, second, sums_second = lift(
        low, w_forward, bias_up, normal, vectors, grad_output, 512
    )

    gdown, gup, gbias_up, first, first_low, sums_first = lower(
        branch, low, act, slope, w_forward, second, normal, scale, vectors, 512
    )
    gout, gn, gd, later, later_total = unmix(
        first_low, mixed, rden, sq, cosines, sines, w_attention, block
    )
    later_in = lax.ppermute(later_total, "tp", [(i + 1, i) for i in range(halves - 1)])
    query_low, dk, dv, sum_query = unattend(
        sq, sk, v, gn, gd, cm, cosines, sines, states, incoming, later, slope_q
    )
    key_low, value_low, sum_rest = tail(dk, dv, sk, v, slope_k, cosines, sines, later_in)
    gqkv = weight_gradients(inputs, query_low, key_low, value_low, groups, halves, deep)
    grad_inputs = input_gradient(first, query_low, key_low, value_low, w_attention, 256)

    def split_units(vector):
        return jnp.moveaxis(vector.reshape(halves, replicas, -1), 0, 1)

    def split_width(vector):
        return jnp.broadcast_to(vector.reshape(replicas, 1, shard), (replicas, halves, shard))

    thin = jnp.concatenate(
        [
            split_units(sum_query[0]), split_units(sum_rest[0]), split_units(sum_rest[1]),
            split_units(gbias_up[0]),
            split_width(sums_first[2]), split_width(sums_first[0]), split_width(sums_first[1]),
            split_width(sums_second[2]), split_width(sums_second[0]), split_width(sums_second[1]),
        ],
        axis=2,
    )
    size = thin.shape[2]
    thin = jnp.pad(thin, ((0, 0), (0, 0), (0, (LANES - spare) * shard - size)))
    thin = jnp.moveaxis(thin.reshape(replicas, halves, LANES - spare, shard), 2, 3)
    thin = jnp.pad(thin, ((0, 0), (0, 0), (0, 0), (0, spare))).astype(BF16)

    def spread(grad):
        if not aligned:
            grad = jnp.moveaxis(grad.reshape(halves, replicas, shard, grad.shape[3]), 0, 1)
        return grad

    def scatter(grad):
        grad = grad.reshape(replicas * halves, shard, grad.shape[3])
        return lax.psum_scatter(grad, BOTH, scatter_dimension=0, tiled=False)

    scaling = 1.0 / replicas
    gdown = scatter(spread(gdown)).astype(F32) * scaling
    gup = scatter(spread(gup)).astype(F32) * scaling
    rest = jnp.concatenate([spread(gqkv), spread(gout), thin], axis=3)
    rest = scatter(rest).astype(F32) * scaling
    thin = rest[:, 4 * part : 4 * part + LANES - spare].T.reshape(-1)
    cuts = [0, edge, 2 * edge, 3 * edge, 3 * edge + units // replicas]
    cuts += [cuts[-1] + shard * (place + 1) for place in range(6)]
    pieces = [thin[cuts[place] : cuts[place + 1]] for place in range(10)]
    return (
        output,
        grad_inputs,
        rest[:, :part],
        rest[:, part : 2 * part],
        rest[:, 2 * part : 3 * part],
        pieces[0],
        pieces[1],
        pieces[2],
        rest[:, 3 * part : 4 * part].T,
        pieces[4],
        pieces[5],
        pieces[6],
        gup,
        pieces[3],
        gdown.T,
        pieces[7],
        pieces[8],
        pieces[9],
    )


def solution(mesh):
    row = P(("fsdp", "tp"), None)
    split, turned = P("fsdp", "tp"), P("tp", "fsdp")
    thin, wide = P(("tp", "fsdp")), P("fsdp")
    return jax.shard_map(
        local,
        mesh=mesh,
        in_specs=(
            row, split, split, split, thin, thin, thin, turned, wide, wide, wide,
            split, thin, turned, wide, wide, wide, P("fsdp", None), row,
        ),
        out_specs=(
            row, row, split, split, split, thin, thin, thin, turned, wide, wide, wide,
            split, thin, turned, wide, wide, wide,
        ),
        check_vma=False,
    )
```

```python
import functools
import math

import jax
import jax.numpy as jnp
from jax import lax
from jax.experimental import pallas as pl
from jax.experimental.pallas import tpu as pltpu
from jax.sharding import PartitionSpec as P

HEAD_DIM = 64
PIECE = 256
LANES = 128
EPSILON = 1e-05
F32 = jnp.float32
BF16 = jnp.bfloat16
BOTH = ("fsdp", "tp")


def dot(left, right):
    return lax.dot_general(left, right, (((1,), (0,)), ((), ())), preferred_element_type=F32)


def dot_nt(left, right):
    return lax.dot_general(left, right, (((1,), (1,)), ((), ())), preferred_element_type=F32)


def dot_tn(left, right):
    return lax.dot_general(left, right, (((0,), (0,)), ((), ())), preferred_element_type=F32)


def flat(ref):
    value = ref[...]
    return value.reshape(value.shape[0] * value.shape[1] * value.shape[2], value.shape[3])


def lane_mask(rows, head, dtype=BF16):
    lane = lax.broadcasted_iota(jnp.int32, (rows, LANES), 1)
    return (lane // HEAD_DIM == head).astype(F32).astype(dtype)


def same_head(rows, columns):
    row = lax.broadcasted_iota(jnp.int32, (rows, columns), 0)
    lane = lax.broadcasted_iota(jnp.int32, (rows, columns), 1)
    return (row // HEAD_DIM) % 2 == (lane // HEAD_DIM) % 2


def compact(state):
    left, right = state[:, :LANES], state[:, LANES:]
    row = lax.broadcasted_iota(jnp.int32, left.shape, 0)
    lane = lax.broadcasted_iota(jnp.int32, left.shape, 1)
    first = (row // HEAD_DIM) % 2 == 0
    low = lane < HEAD_DIM
    return jnp.where(
        low,
        jnp.where(first, left, pltpu.roll(left, HEAD_DIM, 1)),
        jnp.where(first, pltpu.roll(right, HEAD_DIM, 1), right),
    )


def expand(packed):
    row = lax.broadcasted_iota(jnp.int32, packed.shape, 0)
    lane = lax.broadcasted_iota(jnp.int32, packed.shape, 1)
    first = (row // HEAD_DIM) % 2 == 0
    low = lane < HEAD_DIM
    turned = pltpu.roll(packed, HEAD_DIM, 1)
    zero = jnp.zeros_like(packed)
    left = jnp.where(first & low, packed, jnp.where(~first & ~low, turned, zero))
    right = jnp.where(first & low, turned, jnp.where(~first & ~low, packed, zero))
    return jnp.concatenate([left, right], axis=1)


def turned_features(values, cosines, sines):
    wide = values.astype(F32)
    return jnp.concatenate([(wide * cosines).astype(BF16), (wide * sines).astype(BF16)], axis=1)


def slot(coords, z, y, c, x):
    across = jnp.where(c == 0, y ^ coords[1], x ^ coords[3])
    beside = jnp.where(c == 0, x ^ coords[1 + 2], y ^ coords[1])
    return across * 8 + beside * 4 + (z ^ coords[0])


def emit(product, half, outs, coords):
    if len(outs) == 1:
        outs[0][half] = product[...]
        return
    core = coords[2]
    shard = outs[0].shape[1]
    for group in range(product.shape[0] // (2 * shard)):
        z, y = group // 2, group % 2
        for out, c in zip(outs, (core, 1 - core)):
            begin = pl.multiple_of((2 * group + c) * shard, 16)
            out[slot(coords, z, y, c, half)] = product[pl.ds(begin, shard), :]


def scalars():
    return pl.BlockSpec(memory_space=pltpu.SMEM)


def params(megabytes=56):
    return pltpu.CompilerParams(vmem_limit_bytes=megabytes * 1024 * 1024)


def whole(shape):
    zeros = (0,) * len(shape)
    return pl.BlockSpec(shape, lambda *_: zeros)


def cost(flops, moved):
    return pl.CostEstimate(flops=int(flops), bytes_accessed=int(moved), transcendentals=0)


def after(value, *others):
    return lax.optimization_barrier((value, others))[0]


def pack_kernel(*refs):
    q_ref, k_ref, v_ref, out_ref, down_ref = refs[:5]
    thins = refs[5:-2]
    first_ref, turned_ref = refs[-2:]
    shard, part = q_ref.shape

    def chosen(columns, start):
        row = lax.broadcasted_iota(jnp.int32, (shard, columns), 0)
        column = lax.broadcasted_iota(jnp.int32, (shard, columns), 1)
        return (row + start == column).astype(F32).astype(BF16)

    for place, ref in enumerate((q_ref, k_ref, v_ref)):
        first_ref[:, place * part : (place + 1) * part] = ref[...]
    first_ref[:, 3 * part : 4 * part] = dot_nt(chosen(shard, 0), out_ref[...]).astype(BF16)
    turned_ref[...] = dot_nt(chosen(shard, 0), down_ref[...]).astype(BF16)
    columns = jnp.zeros((shard, LANES), F32)
    lane = 0
    for ref in thins:
        size = ref.shape[1]
        for start in range(0, size, shard):
            row = lax.broadcasted_iota(jnp.int32, (LANES, size), 0)
            spread = jnp.where(row == lane, ref[...].astype(F32), 0.0).astype(BF16)
            columns = columns + dot_nt(chosen(size, start), spread)
            lane += 1
    first_ref[:, 4 * part :] = columns.astype(BF16)


def pack(q, k, v, out, down, thins):
    shard, part = q.shape
    return pl.pallas_call(
        pack_kernel,
        out_shape=[
            jax.ShapeDtypeStruct((shard, 4 * part + LANES), BF16),
            jax.ShapeDtypeStruct((shard, down.shape[0]), BF16),
        ],
        compiler_params=params(),
        cost_estimate=cost(1e8, 1e6),
        name="pack",
    )(q, k, v, out, down, *[thin.reshape(1, -1) for thin in thins])


def unpack_kernel(thin_ref, bias_ref, up_ref, vec_ref, *, shard, edge, each):
    halves, width = thin_ref.shape[1], thin_ref.shape[2]
    for half in range(halves):
        thin = thin_ref[0, half]
        part = width // halves
        row = lax.broadcasted_iota(jnp.int32, (width, part), 0)
        column = lax.broadcasted_iota(jnp.int32, (width, part), 1)
        chosen = (row % shard < edge) & (row // shard * edge + row % shard == column)
        bias_ref[half] = dot_tn(thin, chosen.astype(F32).astype(BF16))[:8]
        units = each * width
        row = lax.broadcasted_iota(jnp.int32, (width, units), 0)
        column = lax.broadcasted_iota(jnp.int32, (width, units), 1)
        lane = lax.broadcasted_iota(jnp.int32, (LANES, units), 0)
        rows = jnp.zeros((8, units), F32)
        for turn in range(each):
            chosen = row // shard * (each * shard) + turn * shard + row % shard == column
            picked = dot_tn(thin, chosen.astype(F32).astype(BF16))
            picked = jnp.where(lane == 3 + turn, picked, 0.0)
            rows = rows + jnp.sum(picked, axis=0, keepdims=True)
        up_ref[half] = rows
    row = lax.broadcasted_iota(jnp.int32, (width, width), 0)
    column = lax.broadcasted_iota(jnp.int32, (width, width), 1)
    turned = dot_tn(thin_ref[0, 0], (row == column).astype(F32).astype(BF16))
    vec_ref[...] = turned[3 + each : 11 + each]


def unpack(w, shard, each):
    _, halves, width, columns = w.shape
    return pl.pallas_call(
        functools.partial(unpack_kernel, shard=shard, edge=shard // halves, each=each),
        grid=(1,),
        in_specs=[
            pl.BlockSpec((1, halves, width, LANES), lambda i: (0, 0, 0, columns // LANES - 1))
        ],
        out_specs=[
            whole((halves, 8, width // halves)), whole((halves, 8, each * width)), whole((8, width))
        ],
        out_shape=[
            jax.ShapeDtypeStruct((halves, 8, width // halves), F32),
            jax.ShapeDtypeStruct((halves, 8, each * width), F32),
            jax.ShapeDtypeStruct((8, width), F32),
        ],
        compiler_params=params(),
        cost_estimate=cost(1e8, 1e6),
        name="unpack",
    )(w)


def join_kernel(*refs):
    for place, ref in enumerate(refs[:-1]):
        refs[-1][place] = ref[...]


def join(parts):
    return pl.pallas_call(
        join_kernel,
        out_shape=jax.ShapeDtypeStruct((len(parts),) + parts[0].shape, parts[0].dtype),
        compiler_params=params(),
        cost_estimate=cost(0, 1e6),
        name="join",
    )(*parts)


def project_kernel(
    x_ref, w_ref, b_ref, cos_ref, sin_ref,
    sq_ref, sk_ref, v_ref, gq_ref, gk_ref, st_ref, tot_ref,
    *, block, step,
):
    rows = x_ref.shape[0]
    part = sq_ref.shape[1]
    weights = flat(w_ref)

    def body(index, carry):
        here = pl.ds(index * step, step)
        sums = dot(x_ref[here, :], weights)
        for place, (feature_ref, slope_ref) in enumerate(((sq_ref, gq_ref), (sk_ref, gk_ref))):
            value = sums[:, place * part : (place + 1) * part] + b_ref[0, place : place + 1, :]
            positive = jnp.maximum(value, 0.0) + jnp.log1p(jnp.exp(-jnp.abs(value)))
            feature_ref[here, :] = positive.astype(BF16)
            slope_ref[here, :] = jax.nn.sigmoid(value).astype(BF16)
        v_ref[here, :] = (sums[:, 2 * part :] + b_ref[0, 2:3, :]).astype(BF16)
        return carry

    lax.fori_loop(0, rows // step, body, 0)
    keep = same_head(2 * LANES, 2 * LANES)
    ones = jnp.ones((block, LANES), BF16)
    for pair in range(part // LANES):
        lanes = slice(pair * LANES, (pair + 1) * LANES)
        total = jnp.zeros((2 * LANES, 2 * LANES), F32)
        for place in range(rows // block):
            here = slice(place * block, (place + 1) * block)
            features = turned_features(sk_ref[here, lanes], cos_ref[here, :], sin_ref[here, :])
            state = dot_tn(features, jnp.concatenate([v_ref[here, lanes], ones], axis=1))
            state = jnp.where(keep, state, 0.0)
            st_ref[place, pair] = state.astype(BF16)
            total = total + state
        tot_ref[pair] = compact(total).astype(BF16)


def project(x, w, biases, cosines, sines, block):
    rows, width = x.shape
    groups, halves, shard, _ = w.shape
    part = width // halves
    pairs = width // LANES
    half = pairs // halves
    blocks = rows // block
    row_spec = pl.BlockSpec((rows, part), lambda t: (0, t))
    full = jax.ShapeDtypeStruct((rows, width), BF16)
    return pl.pallas_call(
        functools.partial(project_kernel, block=block, step=256),
        grid=(halves,),
        in_specs=[
            whole((rows, width)),
            pl.BlockSpec((groups, 1, shard, 3 * part), lambda t: (0, t, 0, 0)),
            pl.BlockSpec((1, 8, part), lambda t: (t, 0, 0)),
            whole((rows, LANES)),
            whole((rows, LANES)),
        ],
        out_specs=[
            row_spec, row_spec, row_spec, row_spec, row_spec,
            pl.BlockSpec((blocks, half, 2 * LANES, 2 * LANES), lambda t: (0, t, 0, 0)),
            pl.BlockSpec((half, 2 * LANES, LANES), lambda t: (t, 0, 0)),
        ],
        out_shape=[
            full, full, full, full, full,
            jax.ShapeDtypeStruct((blocks, pairs, 2 * LANES, 2 * LANES), BF16),
            jax.ShapeDtypeStruct((pairs, 2 * LANES, LANES), BF16),
        ],
        compiler_params=params(),
        cost_estimate=cost(2 * rows * width * 3 * width, 16e6),
        name="project",
    )(x, w, biases, cosines, sines)


def attend_kernel(sq_ref, sk_ref, v_ref, cm_ref, cos_ref, sin_ref, st_ref, num_ref, den_ref):
    blocks, block, _ = cm_ref.shape
    piece = min(PIECE, block)
    masks = [lane_mask(block, head) for head in range(2)]
    for place in range(blocks):
        start = place * block
        keys = sk_ref[start : start + block, :]
        values = v_ref[start : start + block, :]
        sides = [jnp.concatenate([values * mask, mask], axis=1) for mask in masks]
        for low in range(0, block, piece):
            here = slice(start + low, start + low + piece)
            span = low + piece
            queries = sq_ref[here, :]
            sums = None
            for mask, side in zip(masks, sides):
                scores = dot_nt(queries * mask[:piece], keys[:span])
                weights = (scores * cm_ref[place, low : low + piece, :span]).astype(BF16)
                term = dot(weights, side[:span])
                sums = term if sums is None else sums + term
            for earlier in range(place):
                sums = sums + dot(
                    turned_features(queries, cos_ref[here, :], sin_ref[here, :]), st_ref[earlier, 0]
                )
            num_ref[here, :] = sums[:, :LANES]
            den_ref[here, :] = sums[:, LANES:]


def attend(sq, sk, v, cm, cosines, sines, states):
    rows, width = sq.shape
    pairs = width // LANES
    blocks = cm.shape[0]
    spec = pl.BlockSpec((rows, LANES), lambda p: (0, p))
    full = jax.ShapeDtypeStruct((rows, width), F32)
    return pl.pallas_call(
        attend_kernel,
        grid=(pairs,),
        in_specs=[
            spec, spec, spec,
            whole(cm.shape), whole((rows, LANES)), whole((rows, LANES)),
            pl.BlockSpec((blocks, 1, 2 * LANES, 2 * LANES), lambda p: (0, p, 0, 0)),
        ],
        out_specs=[spec, spec],
        out_shape=[full, full],
        compiler_params=params(),
        cost_estimate=cost(8e9, 14e6),
        name="attend",
    )(sq, sk, v, cm, cosines, sines, states)


def norm_rows(values):
    average = jnp.mean(values, axis=1, keepdims=True)
    centred = values - average
    scale = lax.rsqrt(jnp.mean(centred * centred, axis=1, keepdims=True) + EPSILON)
    return centred * scale, scale


def mix_kernel(
    num_ref, den_ref, sq_ref, in_ref, cos_ref, sin_ref, w_ref, x_ref, vec_ref,
    mixed_ref, rden_ref, normal_ref, scale_ref, low_ref, wide_ref,
):
    pairs = in_ref.shape[0]
    halves = w_ref.shape[1]
    rows, width = x_ref.shape
    part = width // halves

    @pl.when(pl.program_id(0) == 0)
    def _():
        for pair in range(pairs):
            wide_ref[pair] = expand(in_ref[pair].astype(F32)).astype(BF16)

    for pair in range(pairs):
        lanes = slice(pair * LANES, (pair + 1) * LANES)
        sums = dot(turned_features(sq_ref[:, lanes], cos_ref[...], sin_ref[...]), wide_ref[pair])
        inverse = 1.0 / jnp.maximum(den_ref[:, lanes] + sums[:, LANES:], 1.0)
        rden_ref[:, lanes] = inverse
        mixed_ref[:, lanes] = ((num_ref[:, lanes] + sums[:, :LANES]) * inverse).astype(BF16)
    total = x_ref[...].astype(F32) + vec_ref[0:1, :]
    for half in range(halves):
        side = w_ref[:, half]
        side = side.reshape(width, part)
        total = total + dot_nt(mixed_ref[:, half * part : (half + 1) * part], side)
    normal, scale = norm_rows(total)
    normal_ref[...] = normal
    scale_ref[...] = jnp.broadcast_to(scale, scale_ref.shape)
    low_ref[...] = (normal * vec_ref[1:2, :] + vec_ref[2:3, :]).astype(BF16)


def mix(num, den, sq, incoming, cosines, sines, w, x, vectors, step):
    rows, width = x.shape
    groups, halves, shard, _ = w.shape
    part = width // halves
    pairs = incoming.shape[0]
    wide = pl.BlockSpec((step, width), lambda i: (i, 0))
    thin = pl.BlockSpec((step, LANES), lambda i: (i, 0))
    return pl.pallas_call(
        mix_kernel,
        grid=(rows // step,),
        in_specs=[
            wide, wide, wide, whole(incoming.shape), thin, thin,
            pl.BlockSpec((groups, halves, shard, part), lambda i: (0, 0, 0, 3)),
            wide, whole(vectors.shape),
        ],
        out_specs=[wide, wide, wide, thin, wide],
        out_shape=[
            jax.ShapeDtypeStruct((rows, width), BF16),
            jax.ShapeDtypeStruct((rows, width), F32),
            jax.ShapeDtypeStruct((rows, width), F32),
            jax.ShapeDtypeStruct((rows, LANES), F32),
            jax.ShapeDtypeStruct((rows, width), BF16),
        ],
        scratch_shapes=[pltpu.VMEM((pairs, 2 * LANES, 2 * LANES), BF16)],
        compiler_params=params(),
        cost_estimate=cost(2 * rows * width * width * 2, 20e6),
        name="mix",
    )(num, den, sq, incoming, cosines, sines, w, x, vectors)


def norm_back(upstream, normal, scale, gain):
    scaled = upstream * gain
    inner = (
        scaled
        - jnp.mean(scaled, axis=1, keepdims=True)
        - normal * jnp.mean(scaled * normal, axis=1, keepdims=True)
    )
    return inner * scale


def lift_kernel(low_ref, up_ref, bias_ref, act_ref, slope_ref, *, step):
    up = up_ref[0, 0]

    def body(place, carry):
        here = pl.ds(place * step, step)
        lifted = dot(low_ref[here, :], up) + bias_ref[0, 0:1, :]
        share = 0.5 + 0.5 * lax.erf(lifted * math.sqrt(0.5))
        bell = jnp.exp(-0.5 * lifted * lifted) * (1.0 / math.sqrt(2.0 * math.pi))
        act_ref[here, :] = (lifted * share).astype(BF16)
        slope_ref[here, :] = (share + lifted * bell).astype(BF16)
        return carry

    lax.fori_loop(0, low_ref.shape[0] // step, body, 0, unroll=True)


def lift(low, w, bias, half, units, tile):
    rows, width = low.shape
    tiles = units // tile
    unit_spec = pl.BlockSpec((rows, tile), lambda i: (0, i))
    shape = jax.ShapeDtypeStruct((rows, units), BF16)
    return pl.pallas_call(
        functools.partial(lift_kernel, step=256),
        grid=(tiles,),
        in_specs=[
            whole((rows, width)),
            pl.BlockSpec((1, 1, width, tile), lambda i: (0, half, 0, i)),
            pl.BlockSpec((1, 8, tile), lambda i: (half, 0, i)),
        ],
        out_specs=[unit_spec, unit_spec],
        out_shape=[shape, shape],
        compiler_params=params(),
        cost_estimate=cost(2 * rows * width * units, 10e6),
        name="lift",
    )(low, w, bias)


def drop_kernel(*refs):
    acts = refs[:-8]
    down_ref, normal_ref, vec_ref, grad_ref, out_ref, branch_ref, second_ref, sum_ref = refs[-8:]

    @pl.when(pl.program_id(0) == 0)
    def _():
        sum_ref[...] = jnp.zeros_like(sum_ref)

    total = normal_ref[...] * vec_ref[1:2, :] + vec_ref[2:3, :] + vec_ref[3:4, :]
    for half, act_ref in enumerate(acts):
        total = total + dot_nt(act_ref[...], down_ref[0, half])
    normal, scale = norm_rows(total)
    gain = vec_ref[4:5, :]
    out_ref[...] = (normal * gain + vec_ref[5:6, :]).astype(BF16)
    upstream = grad_ref[...].astype(F32)
    second = norm_back(upstream, normal, scale, gain)
    second_ref[...] = second
    branch_ref[...] = second.astype(BF16)
    sum_ref[0:1, :] += jnp.sum(upstream * normal, axis=0, keepdims=True)
    sum_ref[1:2, :] += jnp.sum(upstream, axis=0, keepdims=True)
    sum_ref[2:3, :] += jnp.sum(second, axis=0, keepdims=True)


def drop(act, w, normal, vectors, grad, units, step):
    rows, width = normal.shape
    halves = w.shape[1]
    wide = pl.BlockSpec((step, width), lambda i: (i, 0))
    return pl.pallas_call(
        drop_kernel,
        grid=(rows // step,),
        in_specs=[pl.BlockSpec((step, units), lambda i: (i, 0))] * halves
        + [whole((1, halves, width, units)), wide, whole(vectors.shape), wide],
        out_specs=[wide, wide, wide, whole((8, width))],
        out_shape=[
            jax.ShapeDtypeStruct((rows, width), BF16),
            jax.ShapeDtypeStruct((rows, width), BF16),
            jax.ShapeDtypeStruct((rows, width), F32),
            jax.ShapeDtypeStruct((8, width), F32),
        ],
        compiler_params=params(),
        cost_estimate=cost(2 * rows * width * halves * units, 20e6),
        name="drop",
    )(*act, w, normal, vectors, grad)


def piece_outputs(layout, tile, index_map):
    replicas, halves, shard, columns, pieces = layout[:5]
    if pieces:
        count = replicas * halves // 2
        spec = pl.BlockSpec((count, shard, tile), lambda *at: (0, 0, index_map(*at)))
        shape = jax.ShapeDtypeStruct((count, shard, columns), BF16)
        return [spec, spec], [shape, shape]
    width = replicas * shard
    spec = pl.BlockSpec((halves, width, tile), lambda *at: (0, 0, index_map(*at)))
    return [spec], [jax.ShapeDtypeStruct((halves, width, columns), BF16)]


def wide_gradient_kernel(coords_ref, left_ref, *refs, halves):
    rights, outs = refs[:halves], refs[halves:-2]
    turned_ref, product_ref = refs[-2:]
    coords = [coords_ref[place] for place in range(4)]

    @pl.when(pl.program_id(0) == 0)
    def _():
        turned_ref[...] = left_ref[...].T

    for half, right_ref in enumerate(rights):
        product_ref[...] = dot(turned_ref[...], right_ref[...]).astype(BF16)
        emit(product_ref, half, outs, coords)


def wide_gradient(coords, left, right, layout, units, tile, name):
    rows, width = left.shape
    halves = layout[1]
    tiles = units // tile
    out_specs, out_shapes = piece_outputs(layout, tile, lambda j: j)
    return pl.pallas_call(
        functools.partial(wide_gradient_kernel, halves=halves),
        grid=(tiles,),
        in_specs=[scalars(), whole((rows, width))]
        + [
            pl.BlockSpec((rows, tile), lambda j: (0, j)) for half in range(halves)
        ],
        out_specs=out_specs,
        out_shape=out_shapes,
        scratch_shapes=[pltpu.VMEM((width, rows), BF16), pltpu.VMEM((width, tile), BF16)],
        compiler_params=params(),
        cost_estimate=cost(2 * rows * width * halves * units, 18e6),
        name=name,
    )(coords, left, *right)


def bend_kernel(branch_ref, down_ref, slope_ref, gl_ref, gbias_ref, *, step):
    down = down_ref[0, 0]
    gbias_ref[...] = jnp.zeros_like(gbias_ref)

    def body(place, carry):
        here = pl.ds(place * step, step)
        slope = dot(branch_ref[here, :], down) * slope_ref[here, :].astype(F32)
        gbias_ref[0:1, :] += jnp.sum(slope, axis=0, keepdims=True)
        gl_ref[here, :] = slope.astype(BF16)
        return carry

    lax.fori_loop(0, branch_ref.shape[0] // step, body, 0, unroll=True)


def bend(branch, w, slope, half, units, tile):
    rows, width = branch.shape
    tiles = units // tile
    unit_spec = pl.BlockSpec((rows, tile), lambda i: (0, i))
    return pl.pallas_call(
        functools.partial(bend_kernel, step=256),
        grid=(tiles,),
        in_specs=[
            whole((rows, width)),
            pl.BlockSpec((1, 1, width, tile), lambda i: (0, half, 0, i)),
            unit_spec,
        ],
        out_specs=[unit_spec, pl.BlockSpec((8, tile), lambda i: (0, i))],
        out_shape=[
            jax.ShapeDtypeStruct((rows, units), BF16),
            jax.ShapeDtypeStruct((8, units), F32),
        ],
        compiler_params=params(),
        cost_estimate=cost(2 * rows * width * units, 10e6),
        name="bend",
    )(branch, w, slope)


def lower_kernel(*refs):
    gls = refs[:-8]
    up_ref, second_ref, normal_ref, scale_ref, vec_ref, first_ref, firstlow_ref, sum_ref = refs[-8:]

    @pl.when(pl.program_id(0) == 0)
    def _():
        sum_ref[...] = jnp.zeros_like(sum_ref)

    upstream = second_ref[...]
    for half, gl_ref in enumerate(gls):
        upstream = upstream + dot_nt(gl_ref[...], up_ref[0, half])
    normal = normal_ref[...]
    first = norm_back(upstream, normal, scale_ref[:, 0:1], vec_ref[1:2, :])
    first_ref[...] = first
    firstlow_ref[...] = first.astype(BF16)
    sum_ref[0:1, :] += jnp.sum(upstream * normal, axis=0, keepdims=True)
    sum_ref[1:2, :] += jnp.sum(upstream, axis=0, keepdims=True)
    sum_ref[2:3, :] += jnp.sum(first, axis=0, keepdims=True)


def lower(gl, w, second, normal, scale, vectors, units, step):
    rows, width = second.shape
    halves = w.shape[1]
    wide = pl.BlockSpec((step, width), lambda i: (i, 0))
    return pl.pallas_call(
        lower_kernel,
        grid=(rows // step,),
        in_specs=[pl.BlockSpec((step, units), lambda i: (i, 0))] * halves
        + [
            whole((1, halves, width, units)), wide, wide,
            pl.BlockSpec((step, LANES), lambda i: (i, 0)), whole(vectors.shape),
        ],
        out_specs=[wide, wide, whole((8, width))],
        out_shape=[
            jax.ShapeDtypeStruct((rows, width), F32),
            jax.ShapeDtypeStruct((rows, width), BF16),
            jax.ShapeDtypeStruct((8, width), F32),
        ],
        compiler_params=params(),
        cost_estimate=cost(2 * rows * width * halves * units, 20e6),
        name="lower",
    )(*gl, w, second, normal, scale, vectors)


def unmix_kernel(
    coords_ref, first_ref, mixed_ref, rden_ref, sq_ref, cos_ref, sin_ref, w_ref,
    sum1_ref, sum2_ref, *refs, block, step, shard, halves
):
    biases = [ref[0:1, :] for ref in refs[:halves]]
    refs = refs[halves:]
    refs = refs[(len(refs) - 5) // 2 :]
    bias = biases[0]
    for half in range(1, halves):
        bias = jnp.where(pl.program_id(0) == half, biases[half], bias)
    bias = jnp.broadcast_to(bias, (8, bias.shape[1]))
    outs = refs[:-5]
    gn_ref, gd_ref, st_ref, tot_ref, product_ref = refs[-5:]
    coords = [coords_ref[place] for place in range(4)]
    rows, width = first_ref.shape
    part = mixed_ref.shape[1]
    side = flat(w_ref)
    group_row = lax.broadcasted_iota(jnp.int32, (LANES, LANES), 0)
    group_lane = lax.broadcasted_iota(jnp.int32, (LANES, LANES), 1)
    group = (group_row // HEAD_DIM == group_lane // HEAD_DIM).astype(F32).astype(BF16)
    lane = lax.broadcasted_iota(jnp.int32, (step, LANES), 1) % HEAD_DIM

    def body(place, carry):
        here = pl.ds(place * step, step)
        grad = dot(first_ref[here, :], side)
        for pair in range(part // LANES):
            lanes = slice(pair * LANES, (pair + 1) * LANES)
            inverse = rden_ref[here, lanes]
            scaled = grad[:, lanes] * inverse
            product = scaled * mixed_ref[here, lanes].astype(F32)
            high = product.astype(BF16)
            rest = (product - high.astype(F32)).astype(BF16)
            inner = dot(high, group) + dot(rest, group)
            slope = jnp.where(inverse < 1.0, -inner, 0.0)
            high = slope.astype(BF16).astype(F32)
            gn_ref[here, lanes] = scaled.astype(BF16)
            gd_ref[here, lanes] = jnp.where(
                lane == 0, high, jnp.where(lane == 1, slope - high, 0.0)
            ).astype(BF16)
        return carry

    lax.fori_loop(0, rows // step, body, 0)
    product_ref[:, :part] = dot_tn(first_ref[...], mixed_ref[...]).astype(BF16)
    side_row = lax.broadcasted_iota(jnp.int32, (8, LANES), 0)
    side_lane = lax.broadcasted_iota(jnp.int32, (8, LANES), 1)

    def pick(first_lane, count):
        chosen = (side_row < count) & (side_row + first_lane == side_lane)
        return chosen.astype(F32).astype(BF16)

    columns = dot_tn(sum1_ref[...].astype(BF16), pick(0, 3))
    columns = columns + dot_tn(sum2_ref[...].astype(BF16), pick(3, 3))
    turned = dot_tn(bias.astype(BF16), (side_row == 0).astype(F32).astype(BF16)).astype(BF16)
    each = bias.shape[1] // width
    row = lax.broadcasted_iota(jnp.int32, (width, each * width), 0)
    column = lax.broadcasted_iota(jnp.int32, (width, each * width), 1)
    for turn in range(each):
        source = row // shard * (each * shard) + turn * shard + row % shard
        chosen = (source == column).astype(F32).astype(BF16)
        lane_at = lax.broadcasted_iota(jnp.int32, (width, LANES), 1)
        columns = jnp.where(lane_at == 6 + turn, dot(chosen, turned), columns)
    product_ref[:, part:] = columns.astype(BF16)
    emit(product_ref, pl.program_id(0), outs, coords)
    keep = same_head(2 * LANES, 2 * LANES)
    for pair in range(part // LANES):
        lanes = slice(pair * LANES, (pair + 1) * LANES)
        total = jnp.zeros((2 * LANES, 2 * LANES), F32)
        for place in range(rows // block):
            here = slice(place * block, (place + 1) * block)
            features = turned_features(sq_ref[here, lanes], cos_ref[here, :], sin_ref[here, :])
            state = dot_tn(
                features, jnp.concatenate([gn_ref[here, lanes], gd_ref[here, lanes]], axis=1)
            )
            state = jnp.where(keep, state, 0.0)
            st_ref[place, pair] = state.astype(BF16)
            total = total + state
        tot_ref[pair] = compact(total).astype(BF16)


def unmix(
    coords, first, mixed, rden, sq, cosines, sines, w, sums1, sums2, gbias, partial, layout, block
):
    rows, width = first.shape
    groups, halves, shard, _ = w.shape
    part = width // halves
    pairs = width // LANES
    half = pairs // halves
    blocks = rows // block
    row_spec = pl.BlockSpec((rows, part), lambda t: (0, t))
    tile = part + LANES
    out_specs, out_shapes = piece_outputs(layout, tile, lambda t: layout[3] // tile - 1)
    units = gbias[0].shape[1]
    full = jax.ShapeDtypeStruct((rows, width), BF16)
    return pl.pallas_call(
        functools.partial(
            unmix_kernel, block=block, step=256, shard=layout[2], halves=halves
        ),
        grid=(halves,),
        in_specs=[
            scalars(), whole((rows, width)), row_spec, row_spec, row_spec,
            whole((rows, LANES)), whole((rows, LANES)),
            pl.BlockSpec((groups, 1, shard, part), lambda t: (0, t, 0, 3)),
            whole((8, width)), whole((8, width)),
        ]
        + [whole((8, units))] * halves
        + [pl.BlockSpec(memory_space=pl.ANY)] * len(partial),
        input_output_aliases={10 + halves + at: at for at in range(len(partial))},
        out_specs=out_specs
        + [
            row_spec, row_spec,
            pl.BlockSpec((blocks, half, 2 * LANES, 2 * LANES), lambda t: (0, t, 0, 0)),
            pl.BlockSpec((half, 2 * LANES, LANES), lambda t: (t, 0, 0)),
        ],
        out_shape=out_shapes
        + [
            full, full,
            jax.ShapeDtypeStruct((blocks, pairs, 2 * LANES, 2 * LANES), BF16),
            jax.ShapeDtypeStruct((pairs, 2 * LANES, LANES), BF16),
        ],
        scratch_shapes=[pltpu.VMEM((width, tile), BF16)],
        compiler_params=params(),
        cost_estimate=cost(4 * rows * width * width, 16e6),
        name="unmix",
    )(coords, first, mixed, rden, sq, cosines, sines, w, sums1, sums2, *gbias, *partial)


def unattend_kernel(
    sq_ref, sk_ref, v_ref, gn_ref, gd_ref, cm_ref, cos_ref, sin_ref, st_ref, in_ref, lt_ref, gq_ref,
    *refs,
):
    query_ref, dk_ref, dv_ref = refs[-3:]
    blocks, block, _ = cm_ref.shape
    piece = min(PIECE, block)
    masks = [lane_mask(block, head) for head in range(2)]
    ones = jnp.ones((block, LANES), BF16)
    incoming = expand(in_ref[0].astype(F32))
    for place in range(blocks):
        start = place * block
        all_here = slice(start, start + block)
        keys, values = sk_ref[all_here, :], v_ref[all_here, :]
        sides = jnp.concatenate([values, ones], axis=1)
        key_sides = [keys * mask for mask in masks]
        state = incoming
        for earlier in range(place):
            state = state + st_ref[earlier, 0].astype(F32)
        state = state.astype(BF16)
        grad_keys = [None] * (block // piece)
        grad_values = [None] * (block // piece)
        for low in range(0, block, piece):
            here = slice(start + low, start + low + piece)
            span = low + piece
            queries, grads, slopes = sq_ref[here, :], gn_ref[here, :], gd_ref[here, :]
            grad_queries = None
            for head in range(2):
                mask = masks[head][:piece]
                cm = cm_ref[place, low : low + piece, :span]
                masked_queries, masked_grads = queries * mask, grads * mask
                scores = dot_nt(masked_queries, keys[:span])
                weights = (scores * cm).astype(BF16)
                back = dot_nt(
                    jnp.concatenate([masked_grads, slopes * mask], axis=1), sides[:span]
                )
                back = (back * cm).astype(BF16)
                term = dot(back, key_sides[head][:span])
                grad_queries = term if grad_queries is None else grad_queries + term
                key_term = dot_tn(back, masked_queries)
                value_term = dot_tn(weights, masked_grads)
                for piece_at in range(span // piece):
                    at = slice(piece_at * piece, (piece_at + 1) * piece)
                    old = grad_keys[piece_at]
                    grad_keys[piece_at] = key_term[at] if old is None else old + key_term[at]
                    old = grad_values[piece_at]
                    grad_values[piece_at] = value_term[at] if old is None else old + value_term[at]
            far = dot_nt(jnp.concatenate([grads, slopes], axis=1), state)
            grad_queries = (
                grad_queries
                + far[:, :LANES] * cos_ref[here, :]
                + far[:, LANES:] * sin_ref[here, :]
            ) * gq_ref[here, :].astype(F32)
            query_ref[here, :] = grad_queries.astype(BF16)
        grad_keys = jnp.concatenate(grad_keys, axis=0)
        grad_values = jnp.concatenate(grad_values, axis=0)
        for later in range(place + 1, blocks):
            far = dot_nt(sides, lt_ref[later, 0])
            grad_keys = (
                grad_keys
                + far[:, :LANES] * cos_ref[all_here, :]
                + far[:, LANES:] * sin_ref[all_here, :]
            )
            features = turned_features(keys, cos_ref[all_here, :], sin_ref[all_here, :])
            grad_values = grad_values + dot(features, lt_ref[later, 0][:, :LANES])
        dk_ref[all_here, :] = grad_keys
        dv_ref[all_here, :] = grad_values


def unattend(
    sq, sk, v, gn, gd, cm, cosines, sines, states, incoming, later, slope_q, start, count, partial
):
    rows, width = sq.shape
    blocks = cm.shape[0]
    spec = pl.BlockSpec((rows, LANES), lambda p: (0, start + p))
    state_spec = pl.BlockSpec((blocks, 1, 2 * LANES, 2 * LANES), lambda p: (0, start + p, 0, 0))
    full = jax.ShapeDtypeStruct((rows, width), F32)
    return pl.pallas_call(
        unattend_kernel,
        grid=(count,),
        in_specs=[
            spec, spec, spec, spec, spec,
            whole(cm.shape), whole((rows, LANES)), whole((rows, LANES)),
            state_spec,
            pl.BlockSpec((1, 2 * LANES, LANES), lambda p: (start + p, 0, 0)),
            state_spec, spec,
        ]
        + [pl.BlockSpec(memory_space=pl.ANY)] * len(partial),
        out_specs=[spec, spec, spec],
        out_shape=[jax.ShapeDtypeStruct((rows, width), BF16), full, full],
        input_output_aliases={12 + at: at for at in range(len(partial))},
        compiler_params=params(),
        cost_estimate=cost(20e9, 20e6),
        name="unattend",
    )(sq, sk, v, gn, gd, cm, cosines, sines, states, incoming, later, slope_q, *partial)


def finish_kernel(
    coords_ref, x_ref, q_ref, dk_ref, dv_ref, sk_ref, v_ref, gk_ref, cos_ref, sin_ref, in_ref,
    *refs, shard
):
    outs = refs[:-4]
    key_ref, value_ref, turned_ref, product_ref = refs[-4:]
    coords = [coords_ref[place] for place in range(4)]
    rows, part = q_ref.shape
    width = x_ref.shape[1]

    @pl.when(pl.program_id(0) == 0)
    def _():
        turned_ref[...] = x_ref[...].T

    product_ref[:, :part] = dot(turned_ref[...], q_ref[...]).astype(BF16)
    ones = jnp.ones((rows, LANES), BF16)
    cosines, sines = cos_ref[...], sin_ref[...]
    for pair in range(part // LANES):
        lanes = slice(pair * LANES, (pair + 1) * LANES)
        state = expand(in_ref[pair].astype(F32)).astype(BF16)
        far = dot_nt(jnp.concatenate([v_ref[:, lanes], ones], axis=1), state)
        keys = dk_ref[:, lanes] + far[:, :LANES] * cosines + far[:, LANES:] * sines
        key_ref[:, lanes] = (keys * gk_ref[:, lanes].astype(F32)).astype(BF16)
        features = turned_features(sk_ref[:, lanes], cosines, sines)
        value_ref[:, lanes] = (dv_ref[:, lanes] + dot(features, state[:, :LANES])).astype(BF16)
    product_ref[:, part : 2 * part] = dot(turned_ref[...], key_ref[...]).astype(BF16)
    product_ref[:, 2 * part : 3 * part] = dot(turned_ref[...], value_ref[...]).astype(BF16)
    lane = lax.broadcasted_iota(jnp.int32, (part, LANES), 1)
    sums = jnp.zeros((part, LANES), F32)
    for place, ref in enumerate((q_ref, key_ref, value_ref)):
        sums = jnp.where(lane == place, dot_tn(ref[...], ones), sums)
    edge = shard * part // width
    row = lax.broadcasted_iota(jnp.int32, (width, part), 0)
    column = lax.broadcasted_iota(jnp.int32, (width, part), 1)
    source = row // shard * edge + row % shard
    chosen = (row % shard < edge) & (source == column)
    product_ref[:, 3 * part :] = dot(chosen.astype(F32).astype(BF16), sums.astype(BF16)).astype(BF16)
    emit(product_ref, pl.program_id(0), outs, coords)


def finish(coords, x, q, dk, dv, sk, v, slope_k, cosines, sines, incoming, layout):
    rows, width = x.shape
    halves, shard = layout[1], layout[2]
    part = width // halves
    half = incoming.shape[0] // halves
    spec = pl.BlockSpec((rows, part), lambda t: (0, t))
    full = jax.ShapeDtypeStruct((rows, width), BF16)
    out_specs, out_shapes = piece_outputs(layout, layout[3], lambda t: 0)
    return pl.pallas_call(
        functools.partial(finish_kernel, shard=shard),
        grid=(halves,),
        in_specs=[
            scalars(), whole((rows, width)), spec, spec, spec, spec, spec, spec,
            whole((rows, LANES)), whole((rows, LANES)),
            pl.BlockSpec((half, 2 * LANES, LANES), lambda t: (t, 0, 0)),
        ],
        out_specs=out_specs + [spec, spec],
        out_shape=out_shapes + [full, full],
        scratch_shapes=[pltpu.VMEM((width, rows), BF16), pltpu.VMEM((width, layout[3]), BF16)],
        compiler_params=params(),
        cost_estimate=cost(2 * rows * width * 3 * width, 10e6),
        name="finish",
    )(coords, x, q, dk, dv, sk, v, slope_k, cosines, sines, incoming)


def inputs_kernel(first_ref, q_ref, k_ref, v_ref, w_ref, out_ref):
    halves = w_ref.shape[1]
    width = first_ref.shape[1]
    part = width // halves
    total = first_ref[...]
    for half in range(halves):
        side = w_ref[:, half].reshape(width, 3 * part)
        at = slice(half * part, (half + 1) * part)
        joined = jnp.concatenate([q_ref[:, at], k_ref[:, at], v_ref[:, at]], axis=1)
        total = total + dot_nt(joined, side)
    out_ref[...] = total.astype(BF16)


def input_gradient(first, q, k, v, w, step):
    rows, width = first.shape
    groups, halves, shard, _ = w.shape
    part = width // halves
    spec = pl.BlockSpec((step, width), lambda i: (i, 0))
    return pl.pallas_call(
        inputs_kernel,
        grid=(rows // step,),
        in_specs=[
            spec, spec, spec, spec,
            pl.BlockSpec((groups, halves, shard, 3 * part), lambda i: (0, 0, 0, 0)),
        ],
        out_specs=spec,
        out_shape=jax.ShapeDtypeStruct((rows, width), BF16),
        compiler_params=params(),
        cost_estimate=cost(2 * rows * width * 3 * width, 14e6),
        name="input_gradient",
    )(first, q, k, v, w)


def assemble_kernel(coords_ref, own_ref, other_ref, out_ref, sems):
    coords = [coords_ref[place] for place in range(4)]
    count, shard, _ = own_ref.shape
    copies = []
    for side, ref in enumerate((own_ref, other_ref)):
        c = coords[2] if side == 0 else 1 - coords[2]
        for index in range(count):
            across, beside, z = index // 8, index // 4 % 2, (index % 4) ^ coords[0]
            y = coords[1] ^ jnp.where(c == 0, across, beside)
            x = coords[3] ^ jnp.where(c == 0, beside, across)
            begin = pl.multiple_of((z * 4 + y * 2 + c) * shard, 16)
            copy = pltpu.make_async_copy(
                ref.at[index],
                out_ref.at[0, x, pl.ds(begin, shard), :],
                sems.at[side * count + index],
            )
            copy.start()
            copies.append(copy)
    for copy in copies:
        copy.wait()


def assemble(coords, own, other):
    count, shard, columns = own.shape
    return pl.pallas_call(
        assemble_kernel,
        in_specs=[
            scalars(), pl.BlockSpec(memory_space=pl.ANY), pl.BlockSpec(memory_space=pl.ANY)
        ],
        out_specs=pl.BlockSpec(memory_space=pltpu.VMEM),
        out_shape=jax.ShapeDtypeStruct((1, 2, count * shard, columns), BF16),
        scratch_shapes=[pltpu.SemaphoreType.DMA((2 * count,))],
        compiler_params=params(),
        cost_estimate=cost(0, 4 * count * shard * columns * 2),
        name="assemble",
    )(coords, own, other)


def moves():
    def table(change):
        pairs = []
        for source in range(32):
            z, y, c, x = source // 8, source // 4 % 2, source // 2 % 2, source % 2
            z, y, c, x = change(z, y, c, x)
            pairs.append((source, ((z * 2 + y) * 2 + c) * 2 + x))
        return pairs

    along = [table(lambda z, y, c, x, k=k: (z ^ k, y, c, x)) for k in range(4)]
    beside = table(lambda z, y, c, x: (z, y ^ c, c, x ^ 1 ^ c))
    across = table(lambda z, y, c, x: (z, y ^ 1 ^ c, c, x ^ c))
    core = table(lambda z, y, c, x: (z, y, c ^ 1, x))
    return along, beside, across, core


def add(left, right):
    return (left.astype(F32) + right.astype(F32)).astype(BF16)


def send(value, table, begin, end, axes=BOTH):
    value = after(value, *begin) if begin else value
    value = lax.ppermute(value, axes, table)
    return after(value, *end) if end else value


class Gather:
    def __init__(self, piece):
        self.tables = moves()
        self.held = piece

    def line(self, begin=(), end=()):
        parts = [send(self.held, self.tables[0][k], begin, end) for k in (1, 2, 3)]
        self.held = join([self.held] + parts)

    def beside(self, begin=(), end=()):
        self.held = jnp.concatenate([self.held, send(self.held, self.tables[1], begin, end)], axis=0)

    def across(self, begin=(), end=()):
        self.held = jnp.concatenate([self.held, send(self.held, self.tables[2], begin, end)], axis=0)

    def core(self, coords, begin=(), end=()):
        return assemble(coords, self.held, send(self.held, self.tables[3], begin, end))


class Sum:
    def __init__(self, own, other):
        self.tables = moves()
        self.kept, self.sent = own, other

    def fold(self, table, begin, end):
        arrived = send(self.sent, table, begin, end)
        size = self.kept.shape[0] // 2
        kept = add(self.kept[:size], arrived[:size])
        self.kept, self.sent = kept, add(self.kept[size:], arrived[size:])

    def both(self):
        return [self.kept, self.sent]

    def core(self, begin=(), end=()):
        self.fold(self.tables[3], begin, end)

    def across(self, begin=(), end=()):
        self.fold(self.tables[2], begin, end)

    def beside(self, begin=(), end=()):
        arrived = send(self.sent, self.tables[1], begin, end)
        self.parts = [add(self.kept[k], arrived[k]) for k in range(4)]

    def line(self, begin=(), end=()):
        parts = [send(self.parts[k], self.tables[0][k], begin, end) for k in (1, 2, 3)]
        total = self.parts[0].astype(F32)
        for part in parts:
            total = total + part.astype(F32)
        return total


def local(
    inputs, w_query, w_key, w_value, b_query, b_key, b_value, w_out, b_out, norm_gain, norm_shift,
    w_up, b_up, w_down, b_down, final_gain, final_shift, piece_starts, grad_output,
):
    rows, width = inputs.shape
    halves = lax.axis_size("tp")
    replicas = lax.axis_size("fsdp")
    length = rows * halves
    block = min(512, length)
    blocks = rows // block
    shard = width // replicas
    part = width // halves
    units = w_up.shape[1]
    me = lax.axis_index("tp")
    pieces = replicas == 16 and halves == 2 and shard % 16 == 0
    place = lax.axis_index("fsdp")
    coords = jnp.stack([place // 4, place // 2 % 2, place % 2, me]).astype(jnp.int32)

    def layout(columns):
        return replicas, halves, shard, columns, pieces

    places = me * rows + jnp.arange(rows, dtype=jnp.int32)
    flags = jnp.any(piece_starts[0][:, None] == (places // PIECE * PIECE)[None, :], axis=0)
    angle = 0.5 * jnp.pi / length * places.astype(F32)
    cosines, sines = jnp.cos(angle), jnp.sin(angle)
    at = jnp.arange(block, dtype=jnp.int32)
    allowed = (at[None, None, :] <= at[None, :, None]) | (
        (at[None, None, :] // PIECE == at[None, :, None] // PIECE)
        & flags.reshape(blocks, block)[:, :, None]
    )
    c, s = cosines.reshape(blocks, block), sines.reshape(blocks, block)
    cm = jnp.where(allowed, c[:, :, None] * c[:, None, :] + s[:, :, None] * s[:, None, :], 0.0)
    cosines = jnp.broadcast_to(cosines[:, None], (rows, LANES))
    sines = jnp.broadcast_to(sines[:, None], (rows, LANES))

    each = units // width
    thins = (
        b_query, b_key, b_value, b_up, b_out, norm_gain, norm_shift, b_down, final_gain, final_shift
    )
    if pieces:
        attention_shard, down_shard = pack(w_query, w_key, w_value, w_out, w_down, thins)
    else:
        columns = []
        for thin in thins:
            thin = jnp.pad(thin, (0, -thin.shape[0] % shard))
            columns.append(thin.reshape(-1, shard).T)
        columns = jnp.concatenate(columns, axis=1)
        columns = jnp.pad(columns, ((0, 0), (0, LANES - columns.shape[1])))
        attention_shard = jnp.concatenate([w_query, w_key, w_value, w_out.T, columns], axis=1)
        down_shard = w_down.T

    def gather_all(piece):
        everything = lax.all_gather(piece, BOTH, axis=0, tiled=False)
        everything = everything.reshape(replicas, halves, shard, piece.shape[1])
        return jnp.moveaxis(everything, 1, 0).reshape(1, halves, width, piece.shape[1])

    if pieces:
        first_chunk, up_chunk, down_chunk = Gather(attention_shard), Gather(w_up), Gather(down_shard)
        first_chunk.line()
        four = first_chunk.held
        first_chunk.beside()
        up_chunk.line([four])
        first_chunk.across([cm, cosines, sines])
        sixteen = first_chunk.held
        w_attention = first_chunk.core(coords)
    else:
        w_attention, w_lift, w_drop = [
            gather_all(piece) for piece in (attention_shard, w_up, down_shard)
        ]

    edge = shard // halves
    biases, bias_up, vectors = unpack(w_attention, shard, each)

    sq, sk, v, slope_q, slope_k, states, total = project(
        inputs, w_attention, biases, cosines, sines, block
    )
    queries, there = sq, []
    if pieces:
        four = up_chunk.held
        up_chunk.beside([sixteen], [sq])
        down_chunk.line([sixteen, four], [sq])
        there = [up_chunk.held, down_chunk.held]
        queries = after(sq, *there)
    num, den = attend(queries, sk, v, cm, cosines, sines, states)
    towards = [(i, i + 1) for i in range(halves - 1)]
    incoming = send(total, towards, there, [num], "tp")
    if pieces:
        up_chunk.across(there, [num])
        down_chunk.beside(there, [num])
        there = [up_chunk.held, down_chunk.held, incoming]
        num = after(num, *there)
    mixed, rden, normal, scale, low = mix(
        num, den, sq, incoming, cosines, sines, w_attention, inputs, vectors, 256
    )
    if pieces:
        sixteen = up_chunk.held
        w_lift = up_chunk.core(coords, [], [low])
    act, slope, now = [], [], low
    for half in range(halves):
        act_half, slope_half = lift(now, w_lift, bias_up, half, units, 512)
        act.append(act_half)
        slope.append(slope_half)
        if pieces and half == 0:
            down_chunk.across(there, [act_half])
            now = after(low, down_chunk.held)
    if pieces:
        w_drop = down_chunk.core(coords, [], [act[1]])
    output, branch, second, sums_second = drop(
        act, w_drop, normal, vectors, grad_output, units, 256
    )

    gdown = wide_gradient(coords, branch, act, layout(units), units, 256, "down_gradient")
    there = gdown
    if pieces:
        down_sum = Sum(*gdown)
    gl, gbias_up = [], []
    for half in range(halves):
        now = after(slope[half], *there)
        gl_half, gbias_half = bend(branch, w_drop, now, half, units, 512)
        gl.append(gl_half)
        gbias_up.append(gbias_half)
        if pieces and half == 0:
            down_sum.core([], [gl_half])
            there = down_sum.both()
    wide = units + part + LANES
    gup = wide_gradient(coords, low, gl, layout(wide), units, 256, "up_gradient")
    there = gup
    if pieces:
        down_sum.across([], gup)
        there = [*gup, *down_sum.both()]
    second = after(second, *there)
    first, first_low, sums_first = lower(gl, w_lift, second, normal, scale, vectors, units, 256)
    if pieces:
        down_sum.beside([], [first])
        first_low = after(first_low, *down_sum.parts)
    *gup, gn, gd, later, later_total = unmix(
        coords, first_low, mixed, rden, sq, cosines, sines, w_attention,
        sums_first, sums_second, gbias_up, gup, layout(wide), block,
    )
    there = []
    if pieces:
        gdown = down_sum.line([], [gn])
        there = [gdown]
        gn = after(gn, gdown)
    pairs = width // LANES
    partial = ()
    for half in range(halves):
        per = pairs // halves
        partial = unattend(
            sq, sk, v, gn, gd, cm, cosines, sines, states, incoming, later, slope_q,
            half * per, per, partial,
        )
        if half == 0:
            towards = [(i + 1, i) for i in range(halves - 1)]
            later_in = send(later_total, towards, there, partial, "tp")
        if pieces and half == 0:
            up_sum = Sum(*gup)
            up_sum.core(there, partial)
            partial = after(tuple(partial), later_in, *up_sum.both())
    query_low, dk, dv = partial
    *gqkv, key_low, value_low = finish(
        coords, inputs, query_low, dk, dv, sk, v, slope_k, cosines, sines, later_in,
        layout(3 * part + LANES),
    )
    if pieces:
        up_sum.across([], [key_low])
        rest_sum = Sum(*gqkv)
        rest_sum.core(up_sum.both())
        up_sum.beside()
        gup = up_sum.line()
        rest_sum.across()
        rest_sum.beside()
        rest = rest_sum.line()
    else:

        def scatter(grad):
            grad = jnp.moveaxis(grad.reshape(halves, replicas, shard, grad.shape[2]), 0, 1)
            grad = grad.reshape(replicas * halves, shard, grad.shape[3])
            return lax.psum_scatter(grad, BOTH, scatter_dimension=0, tiled=False).astype(F32)

        gdown, gup, rest = [scatter(grad[0]) for grad in (gdown, gup, gqkv)]
    grad_inputs = input_gradient(first, query_low, key_low, value_low, w_attention, 256)

    scaling = 1.0 / replicas
    gdown, gup, rest = gdown * scaling, gup * scaling, rest * scaling
    sums = gup[:, units + part :].T
    small = rest[:edge, 3 * part :].T
    return (
        output,
        grad_inputs,
        rest[:, :part],
        rest[:, part : 2 * part],
        rest[:, 2 * part : 3 * part],
        small[0],
        small[1],
        small[2],
        gup[:, units : units + part].T,
        sums[2],
        sums[0],
        sums[1],
        gup[:, :units],
        sums[6 : 6 + units // width].reshape(-1),
        gdown.T,
        sums[5],
        sums[3],
        sums[4],
    )


def solution(mesh):
    row = P(("fsdp", "tp"), None)
    split, turned = P("fsdp", "tp"), P("tp", "fsdp")
    thin, wide = P(("tp", "fsdp")), P("fsdp")
    return jax.shard_map(
        local,
        mesh=mesh,
        in_specs=(
            row, split, split, split, thin, thin, thin, turned, wide, wide, wide,
            split, thin, turned, wide, wide, wide, P("fsdp", None), row,
        ),
        out_specs=(
            row, row, split, split, split, thin, thin, thin, turned, wide, wide, wide,
            split, thin, turned, wide, wide, wide,
        ),
        check_vma=False,
    )
```

```python
import functools
import math

import jax
import jax.numpy as jnp
from jax import lax
from jax.experimental import pallas as pl
from jax.experimental.pallas import tpu as pltpu
from jax.sharding import PartitionSpec as P

HEAD_DIM = 64
PIECE = 256
LANES = 128
EPSILON = 1e-05
F32 = jnp.float32
BF16 = jnp.bfloat16
BOTH = ("fsdp", "tp")


def dot(left, right):
    return lax.dot_general(left, right, (((1,), (0,)), ((), ())), preferred_element_type=F32)


def dot_nt(left, right):
    return lax.dot_general(left, right, (((1,), (1,)), ((), ())), preferred_element_type=F32)


def dot_tn(left, right):
    return lax.dot_general(left, right, (((0,), (0,)), ((), ())), preferred_element_type=F32)


def flat(ref):
    value = ref[...]
    return value.reshape(value.shape[0] * value.shape[1] * value.shape[2], value.shape[3])


def lane_mask(rows, head, dtype=BF16):
    lane = lax.broadcasted_iota(jnp.int32, (rows, LANES), 1)
    return (lane // HEAD_DIM == head).astype(F32).astype(dtype)


def same_head(rows, columns):
    row = lax.broadcasted_iota(jnp.int32, (rows, columns), 0)
    lane = lax.broadcasted_iota(jnp.int32, (rows, columns), 1)
    return (row // HEAD_DIM) % 2 == (lane // HEAD_DIM) % 2


def compact(state):
    left, right = state[:, :LANES], state[:, LANES:]
    row = lax.broadcasted_iota(jnp.int32, left.shape, 0)
    lane = lax.broadcasted_iota(jnp.int32, left.shape, 1)
    first = (row // HEAD_DIM) % 2 == 0
    low = lane < HEAD_DIM
    return jnp.where(
        low,
        jnp.where(first, left, pltpu.roll(left, HEAD_DIM, 1)),
        jnp.where(first, pltpu.roll(right, HEAD_DIM, 1), right),
    )


def expand(packed):
    row = lax.broadcasted_iota(jnp.int32, packed.shape, 0)
    lane = lax.broadcasted_iota(jnp.int32, packed.shape, 1)
    first = (row // HEAD_DIM) % 2 == 0
    low = lane < HEAD_DIM
    turned = pltpu.roll(packed, HEAD_DIM, 1)
    zero = jnp.zeros_like(packed)
    left = jnp.where(first & low, packed, jnp.where(~first & ~low, turned, zero))
    right = jnp.where(first & low, turned, jnp.where(~first & ~low, packed, zero))
    return jnp.concatenate([left, right], axis=1)


def turned_features(values, cosines, sines):
    wide = values.astype(F32)
    return jnp.concatenate([(wide * cosines).astype(BF16), (wide * sines).astype(BF16)], axis=1)


def slot(coords, z, y, c, x):
    across = jnp.where(c == 0, y ^ coords[1], x ^ coords[3])
    beside = jnp.where(c == 0, x ^ coords[1 + 2], y ^ coords[1])
    return across * 8 + beside * 4 + (z ^ coords[0])


def emit(product, half, outs, coords):
    if len(outs) == 1:
        outs[0][half] = product[...]
        return
    core = coords[2]
    shard = outs[0].shape[1]
    for group in range(product.shape[0] // (2 * shard)):
        z, y = group // 2, group % 2
        for out, c in zip(outs, (core, 1 - core)):
            begin = pl.multiple_of((2 * group + c) * shard, 16)
            out[slot(coords, z, y, c, half)] = product[pl.ds(begin, shard), :]


class Weights:
    def __init__(self, coords_ref, sources, held, out, sems, out_sems, halves):
        self.coords = [coords_ref[place] for place in range(4)]
        self.sources, self.held, self.out = sources, held, out
        self.sems, self.out_sems, self.halves = sems, out_sems, halves

    def copies(self, place):
        half = self.halves[place]
        if len(self.sources) == 1:
            return [
                pltpu.make_async_copy(
                    self.sources[0].at[0, half], self.held.at[place], self.sems.at[place, 0]
                )
            ]
        copies = []
        shard = self.sources[0].shape[1]
        for side, ref in enumerate(self.sources):
            c = self.coords[2] if side == 0 else 1 - self.coords[2]
            for group in range(8):
                z, y = group // 2, group % 2
                begin = pl.multiple_of((2 * group + c) * shard, 16)
                copies.append(
                    pltpu.make_async_copy(
                        ref.at[slot(self.coords, z, y, c, half)],
                        self.held.at[place, pl.ds(begin, shard), :],
                        self.sems.at[place, side * 8 + group],
                    )
                )
        return copies

    def start(self, place):
        for copy in self.copies(place):
            copy.start()

    def ready(self, place):
        for copy in self.copies(place):
            copy.wait()
        self.leaving(place).start()

    def leaving(self, place):
        return pltpu.make_async_copy(
            self.held.at[place], self.out.at[0, place], self.out_sems.at[place]
        )

    def left(self, place):
        self.leaving(place).wait()

    @staticmethod
    def scratch(halves, width, columns):
        return [
            pltpu.VMEM((halves, width, columns), BF16),
            pltpu.SemaphoreType.DMA((halves, 16)),
            pltpu.SemaphoreType.DMA((halves,)),
        ]


def anywhere(count):
    return [pl.BlockSpec(memory_space=pl.ANY)] * count


def scalars():
    return pl.BlockSpec(memory_space=pltpu.SMEM)


def params(megabytes=56):
    return pltpu.CompilerParams(vmem_limit_bytes=megabytes * 1024 * 1024)


def whole(shape):
    zeros = (0,) * len(shape)
    return pl.BlockSpec(shape, lambda *_: zeros)


def cost(flops, moved):
    return pl.CostEstimate(flops=int(flops), bytes_accessed=int(moved), transcendentals=0)


def after(value, *others):
    return lax.optimization_barrier((value, others))[0]


def pack_kernel(*refs):
    q_ref, k_ref, v_ref, out_ref = refs[:4]
    thins = refs[4:-1]
    first_ref = refs[-1]
    shard, part = q_ref.shape

    def chosen(columns, start):
        row = lax.broadcasted_iota(jnp.int32, (shard, columns), 0)
        column = lax.broadcasted_iota(jnp.int32, (shard, columns), 1)
        return (row + start == column).astype(F32).astype(BF16)

    for place, ref in enumerate((q_ref, k_ref, v_ref, out_ref)):
        first_ref[:, place * part : (place + 1) * part] = ref[...]
    columns = jnp.zeros((shard, LANES), F32)
    lane = 0
    for ref in thins:
        size = ref.shape[1]
        for start in range(0, size, shard):
            row = lax.broadcasted_iota(jnp.int32, (LANES, size), 0)
            spread = jnp.where(row == lane, ref[...].astype(F32), 0.0).astype(BF16)
            columns = columns + dot_nt(chosen(size, start), spread)
            lane += 1
    first_ref[:, 4 * part :] = columns.astype(BF16)


def pack(q, k, v, out, thins):
    shard, part = q.shape
    return pl.pallas_call(
        pack_kernel,
        out_shape=jax.ShapeDtypeStruct((shard, 4 * part + LANES), BF16),
        compiler_params=params(),
        cost_estimate=cost(1e8, 1e6),
        name="pack",
    )(q, k, v, out, *[thin.reshape(1, -1) for thin in thins])


def deal(columns, shard, size, turns):
    count = columns.shape[0] // shard
    runs = []
    for place in range(count):
        piece = columns[place * shard : place * shard + size]
        for turn in range(turns):
            runs.append(pltpu.roll(piece, LANES - turn, 1) if turn else piece)
    return jnp.concatenate(runs, axis=0)


def selectors_kernel(edge_ref, turn_ref, *, shard, edge, each):
    width, part = edge_ref.shape
    row = lax.broadcasted_iota(jnp.int32, (width, part), 0)
    column = lax.broadcasted_iota(jnp.int32, (width, part), 1)
    chosen = (row % shard < edge) & (row // shard * edge + row % shard == column)
    edge_ref[...] = chosen.astype(F32).astype(BF16)
    row = lax.broadcasted_iota(jnp.int32, (width, LANES), 0)
    source = row // shard * (each * shard) + row % shard
    lane = lax.broadcasted_iota(jnp.int32, (width, LANES), 1)
    for turn in range(each):
        for begin in range(0, each * width, LANES):
            chosen = source + (turn * shard - begin) == lane
            turn_ref[turn, :, begin : begin + LANES] = chosen.astype(F32).astype(BF16)


def selectors(width, part, shard, edge, each):
    return pl.pallas_call(
        functools.partial(selectors_kernel, shard=shard, edge=edge, each=each),
        out_shape=[
            jax.ShapeDtypeStruct((width, part), BF16),
            jax.ShapeDtypeStruct((each, width, each * width), BF16),
        ],
        compiler_params=params(),
        cost_estimate=cost(1e8, 1e6),
        name="selectors",
    )()


def unpack_kernel(thin_ref, turn_ref, up_ref, vec_ref, *, shard, each):
    halves = thin_ref.shape[1]
    for half in range(halves):
        thin = thin_ref[0, half]
        if shard % 16 == 0:
            turned = deal(thin.astype(F32), shard, shard, each).T
            up_ref[half] = turned[0:8]
            continue
        rows = jnp.zeros((8, turn_ref.shape[2]), F32)
        for turn in range(each):
            picked = dot_tn(thin, turn_ref[turn])
            rows = rows + picked[3 + turn : 4 + turn]
        up_ref[half] = rows
    turned = thin_ref[0, 0].astype(F32).T
    vec_ref[...] = turned[3 + each : 11 + each]


def unpack(w, turns, shard, each):
    _, halves, width, columns = w.shape
    return pl.pallas_call(
        functools.partial(unpack_kernel, shard=shard, each=each),
        grid=(1,),
        in_specs=[
            pl.BlockSpec((1, halves, width, LANES), lambda i: (0, 0, 0, columns // LANES - 1)),
            whole(turns.shape),
        ],
        out_specs=[whole((halves, 8, each * width)), whole((8, width))],
        out_shape=[
            jax.ShapeDtypeStruct((halves, 8, each * width), F32),
            jax.ShapeDtypeStruct((8, width), F32),
        ],
        compiler_params=params(),
        cost_estimate=cost(1e8, 1e6),
        name="unpack",
    )(w, turns)


def join_kernel(*refs):
    for place, ref in enumerate(refs[:-1]):
        refs[-1][place] = ref[...]


def join(parts):
    return pl.pallas_call(
        join_kernel,
        out_shape=jax.ShapeDtypeStruct((len(parts),) + parts[0].shape, parts[0].dtype),
        compiler_params=params(),
        cost_estimate=cost(0, 1e6),
        name="join",
    )(*parts)


def project_kernel(
    coords_ref, *refs, block, step, shard, halves
):
    sources, refs = refs[: len(refs) - 14], refs[len(refs) - 14 :]
    x_ref, edge_ref, cos_ref, sin_ref, sq_ref, sk_ref, v_ref, gq_ref, gk_ref, st_ref, tot_ref = refs[:11]
    sources, out_ref = sources[:-1], sources[-1]
    held_ref, sems, out_sems = refs[11:]
    rows = x_ref.shape[0]
    part = sq_ref.shape[1]
    now = pl.program_id(0)
    weights = Weights(coords_ref, sources, held_ref, out_ref, sems, out_sems, range(halves))

    @pl.when(now == 0)
    def _():
        for half in range(halves):
            weights.start(half)

    for half in range(halves):

        @pl.when(now == half)
        def _():
            weights.ready(half)

    columns = held_ref.shape[2]
    thin = held_ref[now, :, columns - LANES :]
    if shard % 16 == 0:
        biases = deal(thin.astype(F32), shard, shard * part // x_ref.shape[1], 1).T
    else:
        biases = dot_tn(thin, edge_ref[...])

    def body(index, carry):
        here = pl.ds(index * step, step)
        sums = dot(x_ref[here, :], held_ref[now, :, : 3 * part])
        for place, (feature_ref, slope_ref) in enumerate(((sq_ref, gq_ref), (sk_ref, gk_ref))):
            value = sums[:, place * part : (place + 1) * part] + biases[place : place + 1]
            positive = jnp.maximum(value, 0.0) + jnp.log1p(jnp.exp(-jnp.abs(value)))
            feature_ref[here, :] = positive.astype(BF16)
            slope_ref[here, :] = jax.nn.sigmoid(value).astype(BF16)
        v_ref[here, :] = (sums[:, 2 * part :] + biases[2:3]).astype(BF16)
        return carry

    lax.fori_loop(0, rows // step, body, 0)
    keep = same_head(2 * LANES, 2 * LANES)
    ones = jnp.ones((block, LANES), BF16)
    for pair in range(part // LANES):
        lanes = slice(pair * LANES, (pair + 1) * LANES)
        total = jnp.zeros((2 * LANES, 2 * LANES), F32)
        for place in range(rows // block):
            here = slice(place * block, (place + 1) * block)
            features = turned_features(sk_ref[here, lanes], cos_ref[here, :], sin_ref[here, :])
            state = dot_tn(features, jnp.concatenate([v_ref[here, lanes], ones], axis=1))
            state = jnp.where(keep, state, 0.0)
            st_ref[place, pair] = state.astype(BF16)
            total = total + state
        tot_ref[pair] = compact(total).astype(BF16)

    @pl.when(now == halves - 1)
    def _():
        for half in range(halves):
            weights.left(half)


def project(coords, x, sources, columns, edges, cosines, sines, block, shard, halves):
    rows, width = x.shape
    part = width // halves
    pairs = width // LANES
    half = pairs // halves
    blocks = rows // block
    row_spec = pl.BlockSpec((rows, part), lambda t: (0, t))
    full = jax.ShapeDtypeStruct((rows, width), BF16)

    def kernel(coords_ref, *refs):
        count = len(sources)
        others, outs, scratch = refs[count : count + 4], refs[count + 4 : -3], refs[-3:]
        project_kernel(
            coords_ref, *refs[:count], outs[-1], *others, *outs[:-1], *scratch,
            block=block, step=rows, shard=shard, halves=halves,
        )

    return pl.pallas_call(
        kernel,
        grid=(halves,),
        in_specs=[scalars()]
        + anywhere(len(sources))
        + [
            whole((rows, width)), whole(edges.shape), whole((rows, LANES)), whole((rows, LANES)),
        ],
        out_specs=[
            row_spec, row_spec, row_spec, row_spec, row_spec,
            pl.BlockSpec((blocks, half, 2 * LANES, 2 * LANES), lambda t: (0, t, 0, 0)),
            pl.BlockSpec((half, 2 * LANES, LANES), lambda t: (t, 0, 0)),
        ]
        + anywhere(1),
        out_shape=[
            full, full, full, full, full,
            jax.ShapeDtypeStruct((blocks, pairs, 2 * LANES, 2 * LANES), BF16),
            jax.ShapeDtypeStruct((pairs, 2 * LANES, LANES), BF16),
            jax.ShapeDtypeStruct((1, halves, width, columns), BF16),
        ],
        scratch_shapes=Weights.scratch(halves, width, columns),
        compiler_params=params(),
        cost_estimate=cost(2 * rows * width * 3 * width, 16e6),
        name="project",
    )(coords, *sources, x, edges, cosines, sines)


def attend_kernel(sq_ref, sk_ref, v_ref, cm_ref, cos_ref, sin_ref, st_ref, num_ref, den_ref):
    blocks, block, _ = cm_ref.shape
    piece = min(PIECE, block)
    masks = [lane_mask(block, head) for head in range(2)]
    for place in range(blocks):
        start = place * block
        keys = sk_ref[start : start + block, :]
        values = v_ref[start : start + block, :]
        sides = [jnp.concatenate([values * mask, mask], axis=1) for mask in masks]
        for low in range(0, block, piece):
            here = slice(start + low, start + low + piece)
            span = low + piece
            queries = sq_ref[here, :]
            sums = None
            for mask, side in zip(masks, sides):
                scores = dot_nt(queries * mask[:piece], keys[:span])
                weights = (scores * cm_ref[place, low : low + piece, :span]).astype(BF16)
                term = dot(weights, side[:span])
                sums = term if sums is None else sums + term
            for earlier in range(place):
                sums = sums + dot(
                    turned_features(queries, cos_ref[here, :], sin_ref[here, :]), st_ref[earlier, 0]
                )
            num_ref[here, :] = sums[:, :LANES]
            den_ref[here, :] = sums[:, LANES:]


def attend(sq, sk, v, cm, cosines, sines, states):
    rows, width = sq.shape
    pairs = width // LANES
    blocks = cm.shape[0]
    spec = pl.BlockSpec((rows, LANES), lambda p: (0, p))
    full = jax.ShapeDtypeStruct((rows, width), F32)
    return pl.pallas_call(
        attend_kernel,
        grid=(pairs,),
        in_specs=[
            spec, spec, spec,
            whole(cm.shape), whole((rows, LANES)), whole((rows, LANES)),
            pl.BlockSpec((blocks, 1, 2 * LANES, 2 * LANES), lambda p: (0, p, 0, 0)),
        ],
        out_specs=[spec, spec],
        out_shape=[full, full],
        compiler_params=params(),
        cost_estimate=cost(8e9, 14e6),
        name="attend",
    )(sq, sk, v, cm, cosines, sines, states)


def norm_rows(values):
    average = jnp.mean(values, axis=1, keepdims=True)
    centred = values - average
    scale = lax.rsqrt(jnp.mean(centred * centred, axis=1, keepdims=True) + EPSILON)
    return centred * scale, scale


def mix_kernel(
    num_ref, den_ref, sq_ref, in_ref, cos_ref, sin_ref, w_ref, x_ref, vec_ref,
    mixed_ref, rden_ref, normal_ref, scale_ref, low_ref, wide_ref,
):
    pairs = in_ref.shape[0]
    halves = w_ref.shape[1]
    rows, width = x_ref.shape
    part = width // halves

    @pl.when(pl.program_id(0) == 0)
    def _():
        for pair in range(pairs):
            wide_ref[pair] = expand(in_ref[pair].astype(F32)).astype(BF16)

    for pair in range(pairs):
        lanes = slice(pair * LANES, (pair + 1) * LANES)
        sums = dot(turned_features(sq_ref[:, lanes], cos_ref[...], sin_ref[...]), wide_ref[pair])
        inverse = 1.0 / jnp.maximum(den_ref[:, lanes] + sums[:, LANES:], 1.0)
        rden_ref[:, lanes] = inverse
        mixed_ref[:, lanes] = ((num_ref[:, lanes] + sums[:, :LANES]) * inverse).astype(BF16)
    total = x_ref[...].astype(F32) + vec_ref[0:1, :]
    for half in range(halves):
        side = w_ref[:, half]
        side = side.reshape(width, part)
        total = total + dot_nt(mixed_ref[:, half * part : (half + 1) * part], side)
    normal, scale = norm_rows(total)
    normal_ref[...] = normal
    scale_ref[...] = jnp.broadcast_to(scale, scale_ref.shape)
    low_ref[...] = (normal * vec_ref[1:2, :] + vec_ref[2:3, :]).astype(BF16)


def mix(num, den, sq, incoming, cosines, sines, w, x, vectors, step):
    rows, width = x.shape
    groups, halves, shard, _ = w.shape
    part = width // halves
    pairs = incoming.shape[0]
    wide = pl.BlockSpec((step, width), lambda i: (i, 0))
    thin = pl.BlockSpec((step, LANES), lambda i: (i, 0))
    return pl.pallas_call(
        mix_kernel,
        grid=(rows // step,),
        in_specs=[
            wide, wide, wide, whole(incoming.shape), thin, thin,
            pl.BlockSpec((groups, halves, shard, part), lambda i: (0, 0, 0, 3)),
            wide, whole(vectors.shape),
        ],
        out_specs=[wide, wide, wide, thin, wide],
        out_shape=[
            jax.ShapeDtypeStruct((rows, width), BF16),
            jax.ShapeDtypeStruct((rows, width), F32),
            jax.ShapeDtypeStruct((rows, width), F32),
            jax.ShapeDtypeStruct((rows, LANES), F32),
            jax.ShapeDtypeStruct((rows, width), BF16),
        ],
        scratch_shapes=[pltpu.VMEM((pairs, 2 * LANES, 2 * LANES), BF16)],
        compiler_params=params(),
        cost_estimate=cost(2 * rows * width * width * 2, 20e6),
        name="mix",
    )(num, den, sq, incoming, cosines, sines, w, x, vectors)


def norm_back(upstream, normal, scale, gain):
    scaled = upstream * gain
    inner = (
        scaled
        - jnp.mean(scaled, axis=1, keepdims=True)
        - normal * jnp.mean(scaled * normal, axis=1, keepdims=True)
    )
    return inner * scale


def lift_kernel(coords_ref, *refs, step, row, half):
    sources, refs = refs[:-8], refs[-8:]
    low_ref, bias_ref, act_ref, slope_ref, out_ref, held_ref, sems, out_sems = refs
    tile = act_ref.shape[1]
    now = pl.program_id(0)
    weights = Weights(coords_ref, sources, held_ref, out_ref, sems, out_sems, [half])

    @pl.when(now == 0)
    def _():
        weights.start(0)
        weights.ready(0)

    up = held_ref[0, :, pl.ds(pl.multiple_of(now * tile, tile), tile)]

    def body(place, carry):
        here = pl.ds(place * step, step)
        lifted = dot(low_ref[here, :], up) + bias_ref[0, row : row + 1, :]
        share = 0.5 + 0.5 * lax.erf(lifted * math.sqrt(0.5))
        bell = jnp.exp(-0.5 * lifted * lifted) * (1.0 / math.sqrt(2.0 * math.pi))
        act_ref[here, :] = (lifted * share).astype(BF16)
        slope_ref[here, :] = (share + lifted * bell).astype(BF16)
        return carry

    lax.fori_loop(0, low_ref.shape[0] // step, body, 0, unroll=True)

    @pl.when(now == pl.num_programs(0) - 1)
    def _():
        weights.left(0)


def lift(coords, low, sources, bias, half, units, tile, row):
    rows, width = low.shape
    unit_spec = pl.BlockSpec((rows, tile), lambda i: (0, i))
    shape = jax.ShapeDtypeStruct((rows, units), BF16)
    return pl.pallas_call(
        functools.partial(lift_kernel, step=256, row=row, half=half),
        grid=(units // tile,),
        in_specs=[scalars()]
        + anywhere(len(sources))
        + [whole((rows, width)), pl.BlockSpec((1, 8, tile), lambda i: (half, 0, i))],
        out_specs=[unit_spec, unit_spec] + anywhere(1),
        out_shape=[shape, shape, jax.ShapeDtypeStruct((1, 1, width, units), BF16)],
        scratch_shapes=Weights.scratch(1, width, units),
        compiler_params=params(),
        cost_estimate=cost(2 * rows * width * units, 10e6),
        name="lift",
    )(coords, *sources, low, bias)


def drop_kernel(coords_ref, *refs, halves):
    sources, acts, refs = refs[: -11 - halves], refs[-11 - halves : -11], refs[-11:]
    normal_ref, vec_ref, grad_ref, out_ref, branch_ref, second_ref, sum_ref = refs[:7]
    whole_ref, held_ref, sems, out_sems = refs[7:]
    weights = Weights(coords_ref, sources, held_ref, whole_ref, sems, out_sems, range(halves))

    @pl.when(pl.program_id(0) == 0)
    def _():
        sum_ref[...] = jnp.zeros_like(sum_ref)
        for half in range(halves):
            weights.start(half)
        for half in range(halves):
            weights.ready(half)

    total = normal_ref[...] * vec_ref[1:2, :] + vec_ref[2:3, :] + vec_ref[3:4, :]
    for half, act_ref in enumerate(acts):
        total = total + dot_nt(act_ref[...], held_ref[half])
    normal, scale = norm_rows(total)
    gain = vec_ref[4:5, :]
    out_ref[...] = (normal * gain + vec_ref[5:6, :]).astype(BF16)
    upstream = grad_ref[...].astype(F32)
    second = norm_back(upstream, normal, scale, gain)
    second_ref[...] = second
    branch_ref[...] = second.astype(BF16)
    sum_ref[0:1, :] += jnp.sum(upstream * normal, axis=0, keepdims=True)
    sum_ref[1:2, :] += jnp.sum(upstream, axis=0, keepdims=True)
    sum_ref[2:3, :] += jnp.sum(second, axis=0, keepdims=True)

    @pl.when(pl.program_id(0) == pl.num_programs(0) - 1)
    def _():
        for half in range(halves):
            weights.left(half)


def drop(coords, act, sources, normal, vectors, grad, units, step):
    rows, width = normal.shape
    halves = len(act)
    wide = pl.BlockSpec((step, width), lambda i: (i, 0))
    return pl.pallas_call(
        functools.partial(drop_kernel, halves=halves),
        grid=(rows // step,),
        in_specs=[scalars()]
        + anywhere(len(sources))
        + [pl.BlockSpec((step, units), lambda i: (i, 0))] * halves
        + [wide, whole(vectors.shape), wide],
        out_specs=[wide, wide, wide, whole((8, width))] + anywhere(1),
        out_shape=[
            jax.ShapeDtypeStruct((rows, width), BF16),
            jax.ShapeDtypeStruct((rows, width), BF16),
            jax.ShapeDtypeStruct((rows, width), F32),
            jax.ShapeDtypeStruct((8, width), F32),
            jax.ShapeDtypeStruct((1, halves, width, units), BF16),
        ],
        scratch_shapes=Weights.scratch(halves, width, units),
        compiler_params=params(),
        cost_estimate=cost(2 * rows * width * halves * units, 20e6),
        name="drop",
    )(coords, *sources, *act, normal, vectors, grad)


def piece_outputs(layout, tile, index_map):
    replicas, halves, shard, columns, pieces = layout[:5]
    if pieces:
        count = replicas * halves // 2
        spec = pl.BlockSpec((count, shard, tile), lambda *at: (0, 0, index_map(*at)))
        shape = jax.ShapeDtypeStruct((count, shard, columns), BF16)
        return [spec, spec], [shape, shape]
    width = replicas * shard
    spec = pl.BlockSpec((halves, width, tile), lambda *at: (0, 0, index_map(*at)))
    return [spec], [jax.ShapeDtypeStruct((halves, width, columns), BF16)]


def wide_gradient_kernel(coords_ref, left_ref, *refs, halves):
    rights, outs, product_ref = refs[:halves], refs[halves:-1], refs[-1]
    coords = [coords_ref[place] for place in range(4)]
    for half, right_ref in enumerate(rights):
        product_ref[...] = dot_tn(left_ref[...], right_ref[...]).astype(BF16)
        emit(product_ref, half, outs, coords)


def wide_gradient(coords, left, right, layout, units, tile, name):
    rows, width = left.shape
    halves = layout[1]
    tiles = units // tile
    out_specs, out_shapes = piece_outputs(layout, tile, lambda j: j)
    return pl.pallas_call(
        functools.partial(wide_gradient_kernel, halves=halves),
        grid=(tiles,),
        in_specs=[scalars(), whole((rows, width))]
        + [
            pl.BlockSpec((rows, tile), lambda j: (0, j)) for half in range(halves)
        ],
        out_specs=out_specs,
        out_shape=out_shapes,
        scratch_shapes=[pltpu.VMEM((width, tile), BF16)],
        compiler_params=params(),
        cost_estimate=cost(2 * rows * width * halves * units, 18e6),
        name=name,
    )(coords, left, *right)


def bend_kernel(branch_ref, down_ref, slope_ref, gl_ref, gbias_ref, *, step):
    down = down_ref[0, 0]
    gbias_ref[...] = jnp.zeros_like(gbias_ref)

    def body(place, carry):
        here = pl.ds(place * step, step)
        slope = dot(branch_ref[here, :], down) * slope_ref[here, :].astype(F32)
        gbias_ref[0:1, :] += jnp.sum(slope, axis=0, keepdims=True)
        gl_ref[here, :] = slope.astype(BF16)
        return carry

    lax.fori_loop(0, branch_ref.shape[0] // step, body, 0, unroll=True)


def bend(branch, w, slope, half, units, tile):
    rows, width = branch.shape
    tiles = units // tile
    unit_spec = pl.BlockSpec((rows, tile), lambda i: (0, i))
    return pl.pallas_call(
        functools.partial(bend_kernel, step=256),
        grid=(tiles,),
        in_specs=[
            whole((rows, width)),
            pl.BlockSpec((1, 1, width, tile), lambda i: (0, half, 0, i)),
            unit_spec,
        ],
        out_specs=[unit_spec, pl.BlockSpec((8, tile), lambda i: (0, i))],
        out_shape=[
            jax.ShapeDtypeStruct((rows, units), BF16),
            jax.ShapeDtypeStruct((8, units), F32),
        ],
        compiler_params=params(),
        cost_estimate=cost(2 * rows * width * units, 10e6),
        name="bend",
    )(branch, w, slope)


def lower_kernel(*refs):
    count = (len(refs) - 7) // 2
    gls, ups = refs[:count], refs[count : 2 * count]
    second_ref, normal_ref, scale_ref, vec_ref, first_ref, firstlow_ref, sum_ref = refs[-7:]

    @pl.when(pl.program_id(0) == 0)
    def _():
        sum_ref[...] = jnp.zeros_like(sum_ref)

    upstream = second_ref[...]
    for gl_ref, up_ref in zip(gls, ups):
        upstream = upstream + dot_nt(gl_ref[...], up_ref[0, 0])
    normal = normal_ref[...]
    first = norm_back(upstream, normal, scale_ref[:, 0:1], vec_ref[1:2, :])
    first_ref[...] = first
    firstlow_ref[...] = first.astype(BF16)
    sum_ref[0:1, :] += jnp.sum(upstream * normal, axis=0, keepdims=True)
    sum_ref[1:2, :] += jnp.sum(upstream, axis=0, keepdims=True)
    sum_ref[2:3, :] += jnp.sum(first, axis=0, keepdims=True)


def lower(gl, w, second, normal, scale, vectors, units, step):
    rows, width = second.shape
    halves = len(w)
    wide = pl.BlockSpec((step, width), lambda i: (i, 0))
    return pl.pallas_call(
        lower_kernel,
        grid=(rows // step,),
        in_specs=[pl.BlockSpec((step, units), lambda i: (i, 0))] * halves
        + [
            whole((1, 1, width, units)) for half in range(halves)
        ]
        + [
            wide, wide,
            pl.BlockSpec((step, LANES), lambda i: (i, 0)), whole(vectors.shape),
        ],
        out_specs=[wide, wide, whole((8, width))],
        out_shape=[
            jax.ShapeDtypeStruct((rows, width), F32),
            jax.ShapeDtypeStruct((rows, width), BF16),
            jax.ShapeDtypeStruct((8, width), F32),
        ],
        compiler_params=params(),
        cost_estimate=cost(2 * rows * width * halves * units, 20e6),
        name="lower",
    )(*gl, *w, second, normal, scale, vectors)


def unmix_kernel(
    coords_ref, first_ref, mixed_ref, rden_ref, sq_ref, cos_ref, sin_ref, w_ref,
    sum1_ref, sum2_ref, turn_ref, *refs, block, step, shard, halves
):
    biases = [ref[0:1, :] for ref in refs[:halves]]
    refs = refs[halves:]
    refs = refs[(len(refs) - 5) // 2 :]
    bias = biases[0]
    for half in range(1, halves):
        bias = jnp.where(pl.program_id(0) == half, biases[half], bias)
    bias = jnp.broadcast_to(bias, (8, bias.shape[1]))
    outs = refs[:-5]
    gn_ref, gd_ref, st_ref, tot_ref, product_ref = refs[-5:]
    coords = [coords_ref[place] for place in range(4)]
    rows, width = first_ref.shape
    part = mixed_ref.shape[1]
    side = flat(w_ref)
    group_row = lax.broadcasted_iota(jnp.int32, (LANES, LANES), 0)
    group_lane = lax.broadcasted_iota(jnp.int32, (LANES, LANES), 1)
    group = (group_row // HEAD_DIM == group_lane // HEAD_DIM).astype(F32).astype(BF16)
    group = jnp.concatenate([group, group], axis=0)

    lane = lax.broadcasted_iota(jnp.int32, (step, LANES), 1) % HEAD_DIM

    def body(place, carry):
        here = pl.ds(place * step, step)
        grad = dot(first_ref[here, :], side)
        for pair in range(part // LANES):
            lanes = slice(pair * LANES, (pair + 1) * LANES)
            inverse = rden_ref[here, lanes]
            scaled = grad[:, lanes] * inverse
            product = scaled * mixed_ref[here, lanes].astype(F32)
            high = product.astype(BF16)
            rest = (product - high.astype(F32)).astype(BF16)
            inner = dot(jnp.concatenate([high, rest], axis=1), group)
            slope = jnp.where(inverse < 1.0, -inner, 0.0)
            high = slope.astype(BF16).astype(F32)
            gn_ref[here, lanes] = scaled.astype(BF16)
            gd_ref[here, lanes] = jnp.where(
                lane == 0, high, jnp.where(lane == 1, slope - high, 0.0)
            ).astype(BF16)
        return carry

    lax.fori_loop(0, rows // step, body, 0)
    product_ref[:, :part] = dot_tn(first_ref[...], mixed_ref[...]).astype(BF16)
    row = lax.broadcasted_iota(jnp.int32, (8, width), 0)
    packed = jnp.where(row < 3, sum1_ref[...], pltpu.roll(sum2_ref[...], 3, 0))
    packed = jnp.where(row < 6, packed, 0.0)
    columns = jnp.concatenate([packed, jnp.zeros((LANES - 8, width), F32)], axis=0).T
    units = bias.shape[1]
    each = units // width
    if shard % 16 == 0:
        at = lax.broadcasted_iota(jnp.int32, (8, units), 0)
        both = jnp.where(at >= 6, bias, 0.0)
        turned = jnp.concatenate([both, jnp.zeros((LANES - 8, units), F32)], axis=0).T
        lane_at = lax.broadcasted_iota(jnp.int32, (shard, LANES), 1)
        for place in range(width // shard):
            piece = columns[place * shard : (place + 1) * shard]
            for turn in range(each):
                begin = (place * each + turn) * shard
                piece = jnp.where(lane_at == 6 + turn, turned[begin : begin + shard], piece)
            product_ref[place * shard : (place + 1) * shard, part:] = piece.astype(BF16)
    else:
        side_row = lax.broadcasted_iota(jnp.int32, (8, LANES), 0)
        turned = dot_tn(bias.astype(BF16), (side_row == 0).astype(F32).astype(BF16)).astype(BF16)
        lane_at = lax.broadcasted_iota(jnp.int32, (width, LANES), 1)
        for turn in range(each):
            columns = jnp.where(lane_at == 6 + turn, dot(turn_ref[turn], turned), columns)
        product_ref[:, part:] = columns.astype(BF16)
    emit(product_ref, pl.program_id(0), outs, coords)
    keep = same_head(2 * LANES, 2 * LANES)
    for pair in range(part // LANES):
        lanes = slice(pair * LANES, (pair + 1) * LANES)
        total = jnp.zeros((2 * LANES, 2 * LANES), F32)
        for place in range(rows // block):
            here = slice(place * block, (place + 1) * block)
            features = turned_features(sq_ref[here, lanes], cos_ref[here, :], sin_ref[here, :])
            state = dot_tn(
                features, jnp.concatenate([gn_ref[here, lanes], gd_ref[here, lanes]], axis=1)
            )
            state = jnp.where(keep, state, 0.0)
            st_ref[place, pair] = state.astype(BF16)
            total = total + state
        tot_ref[pair] = compact(total).astype(BF16)


def unmix(
    coords, first, mixed, rden, sq, cosines, sines, w, sums1, sums2, turns, gbias, partial, layout, block
):
    rows, width = first.shape
    groups, halves, shard, _ = w.shape
    part = width // halves
    pairs = width // LANES
    half = pairs // halves
    blocks = rows // block
    row_spec = pl.BlockSpec((rows, part), lambda t: (0, t))
    tile = part + LANES
    out_specs, out_shapes = piece_outputs(layout, tile, lambda t: layout[3] // tile - 1)
    units = gbias[0].shape[1]
    full = jax.ShapeDtypeStruct((rows, width), BF16)
    return pl.pallas_call(
        functools.partial(
            unmix_kernel, block=block, step=512, shard=layout[2], halves=halves
        ),
        grid=(halves,),
        in_specs=[
            scalars(), whole((rows, width)), row_spec, row_spec, row_spec,
            whole((rows, LANES)), whole((rows, LANES)),
            pl.BlockSpec((groups, 1, shard, part), lambda t: (0, t, 0, 3)),
            whole((8, width)), whole((8, width)), whole(turns.shape),
        ]
        + [whole((8, units))] * halves
        + [pl.BlockSpec(memory_space=pl.ANY)] * len(partial),
        input_output_aliases={11 + halves + at: at for at in range(len(partial))},
        out_specs=out_specs
        + [
            row_spec, row_spec,
            pl.BlockSpec((blocks, half, 2 * LANES, 2 * LANES), lambda t: (0, t, 0, 0)),
            pl.BlockSpec((half, 2 * LANES, LANES), lambda t: (t, 0, 0)),
        ],
        out_shape=out_shapes
        + [
            full, full,
            jax.ShapeDtypeStruct((blocks, pairs, 2 * LANES, 2 * LANES), BF16),
            jax.ShapeDtypeStruct((pairs, 2 * LANES, LANES), BF16),
        ],
        scratch_shapes=[pltpu.VMEM((width, tile), BF16)],
        compiler_params=params(),
        cost_estimate=cost(4 * rows * width * width, 16e6),
        name="unmix",
    )(coords, first, mixed, rden, sq, cosines, sines, w, sums1, sums2, turns, *gbias, *partial)


def unattend_kernel(
    sq_ref, sk_ref, v_ref, gn_ref, gd_ref, cm_ref, cos_ref, sin_ref, st_ref, in_ref, lt_ref, gq_ref,
    *refs,
):
    query_ref, dk_ref, dv_ref = refs[-3:]
    blocks, block, _ = cm_ref.shape
    piece = min(PIECE, block)
    masks = [lane_mask(block, head) for head in range(2)]
    ones = jnp.ones((block, LANES), BF16)
    incoming = expand(in_ref[0].astype(F32))
    for place in range(blocks):
        start = place * block
        all_here = slice(start, start + block)
        keys, values = sk_ref[all_here, :], v_ref[all_here, :]
        sides = jnp.concatenate([values, ones], axis=1)
        key_sides = [keys * mask for mask in masks]
        state = incoming
        for earlier in range(place):
            state = state + st_ref[earlier, 0].astype(F32)
        state = state.astype(BF16)
        grad_keys = [None] * (block // piece)
        grad_values = [None] * (block // piece)
        for low in range(0, block, piece):
            here = slice(start + low, start + low + piece)
            span = low + piece
            queries, grads, slopes = sq_ref[here, :], gn_ref[here, :], gd_ref[here, :]
            grad_queries = None
            for head in range(2):
                mask = masks[head][:piece]
                cm = cm_ref[place, low : low + piece, :span]
                masked_queries, masked_grads = queries * mask, grads * mask
                scores = dot_nt(masked_queries, keys[:span])
                weights = (scores * cm).astype(BF16)
                back = dot_nt(
                    jnp.concatenate([masked_grads, slopes * mask], axis=1), sides[:span]
                )
                back = (back * cm).astype(BF16)
                term = dot(back, key_sides[head][:span])
                grad_queries = term if grad_queries is None else grad_queries + term
                key_term = dot_tn(back, masked_queries)
                value_term = dot_tn(weights, masked_grads)
                for piece_at in range(span // piece):
                    at = slice(piece_at * piece, (piece_at + 1) * piece)
                    old = grad_keys[piece_at]
                    grad_keys[piece_at] = key_term[at] if old is None else old + key_term[at]
                    old = grad_values[piece_at]
                    grad_values[piece_at] = value_term[at] if old is None else old + value_term[at]
            far = dot_nt(jnp.concatenate([grads, slopes], axis=1), state)
            grad_queries = (
                grad_queries
                + far[:, :LANES] * cos_ref[here, :]
                + far[:, LANES:] * sin_ref[here, :]
            ) * gq_ref[here, :].astype(F32)
            query_ref[here, :] = grad_queries.astype(BF16)
        grad_keys = jnp.concatenate(grad_keys, axis=0)
        grad_values = jnp.concatenate(grad_values, axis=0)
        for later in range(place + 1, blocks):
            far = dot_nt(sides, lt_ref[later, 0])
            grad_keys = (
                grad_keys
                + far[:, :LANES] * cos_ref[all_here, :]
                + far[:, LANES:] * sin_ref[all_here, :]
            )
            features = turned_features(keys, cos_ref[all_here, :], sin_ref[all_here, :])
            grad_values = grad_values + dot(features, lt_ref[later, 0][:, :LANES])
        dk_ref[all_here, :] = grad_keys
        dv_ref[all_here, :] = grad_values


def unattend(
    sq, sk, v, gn, gd, cm, cosines, sines, states, incoming, later, slope_q, start, count, partial
):
    rows, width = sq.shape
    blocks = cm.shape[0]
    spec = pl.BlockSpec((rows, LANES), lambda p: (0, start + p))
    state_spec = pl.BlockSpec((blocks, 1, 2 * LANES, 2 * LANES), lambda p: (0, start + p, 0, 0))
    full = jax.ShapeDtypeStruct((rows, width), F32)
    return pl.pallas_call(
        unattend_kernel,
        grid=(count,),
        in_specs=[
            spec, spec, spec, spec, spec,
            whole(cm.shape), whole((rows, LANES)), whole((rows, LANES)),
            state_spec,
            pl.BlockSpec((1, 2 * LANES, LANES), lambda p: (start + p, 0, 0)),
            state_spec, spec,
        ]
        + [pl.BlockSpec(memory_space=pl.ANY)] * len(partial),
        out_specs=[spec, spec, spec],
        out_shape=[jax.ShapeDtypeStruct((rows, width), BF16), full, full],
        input_output_aliases={12 + at: at for at in range(len(partial))},
        compiler_params=params(),
        cost_estimate=cost(20e9, 20e6),
        name="unattend",
    )(sq, sk, v, gn, gd, cm, cosines, sines, states, incoming, later, slope_q, *partial)


def tail_kernel(
    dk_ref, dv_ref, sk_ref, v_ref, gk_ref, cos_ref, sin_ref, in_ref, key_ref, value_ref
):
    rows, part = dk_ref.shape
    ones = jnp.ones((rows, LANES), BF16)
    cosines, sines = cos_ref[...], sin_ref[...]
    for pair in range(part // LANES):
        lanes = slice(pair * LANES, (pair + 1) * LANES)
        state = expand(in_ref[pair].astype(F32)).astype(BF16)
        far = dot_nt(jnp.concatenate([v_ref[:, lanes], ones], axis=1), state)
        keys = dk_ref[:, lanes] + far[:, :LANES] * cosines + far[:, LANES:] * sines
        key_ref[:, lanes] = (keys * gk_ref[:, lanes].astype(F32)).astype(BF16)
        features = turned_features(sk_ref[:, lanes], cosines, sines)
        value_ref[:, lanes] = (dv_ref[:, lanes] + dot(features, state[:, :LANES])).astype(BF16)


def tail(dk, dv, sk, v, slope_k, cosines, sines, incoming):
    rows, width = sk.shape
    spec = pl.BlockSpec((rows, LANES), lambda p: (0, p))
    full = jax.ShapeDtypeStruct((rows, width), BF16)
    return pl.pallas_call(
        tail_kernel,
        grid=(width // LANES,),
        in_specs=[
            spec, spec, spec, spec, spec, whole((rows, LANES)), whole((rows, LANES)),
            pl.BlockSpec((1, 2 * LANES, LANES), lambda p: (p, 0, 0)),
        ],
        out_specs=[spec, spec],
        out_shape=[full, full],
        compiler_params=params(),
        cost_estimate=cost(2e9, 14e6),
        name="tail",
    )(dk, dv, sk, v, slope_k, cosines, sines, incoming)


def weights_kernel(coords_ref, x_ref, q_ref, k_ref, v_ref, edge_ref, *refs, shard):
    outs, product_ref = refs[:-1], refs[-1]
    coords = [coords_ref[place] for place in range(4)]
    rows, part = q_ref.shape
    width = x_ref.shape[1]
    ones = jnp.ones((rows, LANES), BF16)
    lane = lax.broadcasted_iota(jnp.int32, (part, LANES), 1)
    sums = jnp.zeros((part, LANES), F32)
    for place, ref in enumerate((q_ref, k_ref, v_ref)):
        at = slice(place * part, (place + 1) * part)
        product_ref[:, at] = dot_tn(x_ref[...], ref[...]).astype(BF16)
        sums = jnp.where(lane == place, dot_tn(ref[...], ones), sums)
    if shard % 16 == 0:
        edge = shard * part // width
        for place in range(width // shard):
            piece = jnp.concatenate(
                [sums[place * edge : (place + 1) * edge], jnp.zeros((shard - edge, LANES), F32)], axis=0
            )
            product_ref[place * shard : (place + 1) * shard, 3 * part :] = piece.astype(BF16)
    else:
        product_ref[:, 3 * part :] = dot(edge_ref[...], sums.astype(BF16)).astype(BF16)
    emit(product_ref, pl.program_id(0), outs, coords)


def weight_gradients(coords, x, q, k, v, edges, layout):
    rows, width = x.shape
    halves = layout[1]
    spec = pl.BlockSpec((rows, width // halves), lambda t: (0, t))
    out_specs, out_shapes = piece_outputs(layout, layout[3], lambda t: 0)
    return pl.pallas_call(
        functools.partial(weights_kernel, shard=layout[2]),
        grid=(halves,),
        in_specs=[scalars(), whole((rows, width)), spec, spec, spec, whole(edges.shape)],
        out_specs=out_specs,
        out_shape=out_shapes,
        scratch_shapes=[pltpu.VMEM((width, layout[3]), BF16)],
        compiler_params=params(),
        cost_estimate=cost(2 * rows * width * 3 * width, 10e6),
        name="weight_gradients",
    )(coords, x, q, k, v, edges)


def inputs_kernel(first_ref, q_ref, k_ref, v_ref, w_ref, out_ref):
    halves = w_ref.shape[1]
    width = first_ref.shape[1]
    part = width // halves
    total = first_ref[...]
    for half in range(halves):
        side = w_ref[:, half].reshape(width, 3 * part)
        at = slice(half * part, (half + 1) * part)
        joined = jnp.concatenate([q_ref[:, at], k_ref[:, at], v_ref[:, at]], axis=1)
        total = total + dot_nt(joined, side)
    out_ref[...] = total.astype(BF16)


def input_gradient(first, q, k, v, w, step):
    rows, width = first.shape
    groups, halves, shard, _ = w.shape
    part = width // halves
    spec = pl.BlockSpec((step, width), lambda i: (i, 0))
    return pl.pallas_call(
        inputs_kernel,
        grid=(rows // step,),
        in_specs=[
            spec, spec, spec, spec,
            pl.BlockSpec((groups, halves, shard, 3 * part), lambda i: (0, 0, 0, 0)),
        ],
        out_specs=spec,
        out_shape=jax.ShapeDtypeStruct((rows, width), BF16),
        compiler_params=params(),
        cost_estimate=cost(2 * rows * width * 3 * width, 14e6),
        name="input_gradient",
    )(first, q, k, v, w)


def moves():
    def table(change):
        pairs = []
        for source in range(32):
            z, y, c, x = source // 8, source // 4 % 2, source // 2 % 2, source % 2
            z, y, c, x = change(z, y, c, x)
            pairs.append((source, ((z * 2 + y) * 2 + c) * 2 + x))
        return pairs

    along = [table(lambda z, y, c, x, k=k: (z ^ k, y, c, x)) for k in range(4)]
    beside = table(lambda z, y, c, x: (z, y ^ c, c, x ^ 1 ^ c))
    across = table(lambda z, y, c, x: (z, y ^ 1 ^ c, c, x ^ c))
    core = table(lambda z, y, c, x: (z, y, c ^ 1, x))
    return along, beside, across, core


def add(left, right):
    return (left.astype(F32) + right.astype(F32)).astype(BF16)


def send(value, table, begin, end, axes=BOTH):
    value = after(value, *begin) if begin else value
    value = lax.ppermute(value, axes, table)
    return after(value, *end) if end else value


class Gather:
    def __init__(self, piece):
        self.tables = moves()
        self.held = piece

    def line(self, begin=(), end=()):
        parts = [send(self.held, self.tables[0][k], begin, end) for k in (1, 2, 3)]
        self.held = join([self.held] + parts)

    def line_parts(self, begin):
        self.held = self.held, [send(self.held, self.tables[0][k], begin, ()) for k in (1, 2, 3)]

    def beside(self, begin=(), end=()):
        self.held = jnp.concatenate([self.held, send(self.held, self.tables[1], begin, end)], axis=0)

    def across(self, begin=(), end=()):
        self.held = jnp.concatenate([self.held, send(self.held, self.tables[2], begin, end)], axis=0)

    def core(self, begin=(), end=()):
        return [self.held, send(self.held, self.tables[3], begin, end)]


class Sum:
    def __init__(self, own, other):
        self.tables = moves()
        self.kept, self.sent = own, other

    def fold(self, table, begin, end):
        arrived = send(self.sent, table, begin, end)
        size = self.kept.shape[0] // 2
        kept = add(self.kept[:size], arrived[:size])
        self.kept, self.sent = kept, add(self.kept[size:], arrived[size:])

    def both(self):
        return [self.kept, self.sent]

    def core(self, begin=(), end=()):
        self.fold(self.tables[3], begin, end)

    def across(self, begin=(), end=()):
        self.fold(self.tables[2], begin, end)

    def beside(self, begin=(), end=()):
        arrived = send(self.sent, self.tables[1], begin, end)
        self.parts = [add(self.kept[k], arrived[k]) for k in range(4)]

    def line(self, begin=(), end=()):
        parts = [send(self.parts[k], self.tables[0][k], begin, end) for k in (1, 2, 3)]
        total = self.parts[0].astype(F32)
        for part in parts:
            total = total + part.astype(F32)
        return total


def local(
    inputs, w_query, w_key, w_value, b_query, b_key, b_value, w_out, b_out, norm_gain, norm_shift,
    w_up, b_up, w_down, b_down, final_gain, final_shift, piece_starts, grad_output,
):
    rows, width = inputs.shape
    halves = lax.axis_size("tp")
    replicas = lax.axis_size("fsdp")
    length = rows * halves
    block = min(512, length)
    blocks = rows // block
    shard = width // replicas
    part = width // halves
    units = w_up.shape[1]
    me = lax.axis_index("tp")
    pieces = replicas == 16 and halves == 2 and shard % 16 == 0
    place = lax.axis_index("fsdp")
    coords = jnp.stack([place // 4, place // 2 % 2, place % 2, me]).astype(jnp.int32)

    def layout(columns):
        return replicas, halves, shard, columns, pieces

    places = me * rows + jnp.arange(rows, dtype=jnp.int32)
    flags = jnp.any(piece_starts[0][:, None] == (places // PIECE * PIECE)[None, :], axis=0)
    angle = 0.5 * jnp.pi / length * places.astype(F32)
    cosines, sines = jnp.cos(angle), jnp.sin(angle)
    at = jnp.arange(block, dtype=jnp.int32)
    allowed = (at[None, None, :] <= at[None, :, None]) | (
        (at[None, None, :] // PIECE == at[None, :, None] // PIECE)
        & flags.reshape(blocks, block)[:, :, None]
    )
    c, s = cosines.reshape(blocks, block), sines.reshape(blocks, block)
    cm = jnp.where(allowed, c[:, :, None] * c[:, None, :] + s[:, :, None] * s[:, None, :], 0.0)
    cosines = jnp.broadcast_to(cosines[:, None], (rows, LANES))
    sines = jnp.broadcast_to(sines[:, None], (rows, LANES))

    each, edge = units // width, shard // halves
    if pieces:
        edges, turns = jnp.zeros((8, LANES), BF16), jnp.zeros((1, 8, LANES), BF16)
    else:
        edges, turns = selectors(width, part, shard, edge, each)
    thins = (
        b_query, b_key, b_value, b_up, b_out, norm_gain, norm_shift, b_down, final_gain, final_shift
    )
    if pieces:
        attention_shard = pack(w_query, w_key, w_value, w_out.T, thins)
    else:
        columns = []
        for thin in thins:
            thin = jnp.pad(thin, (0, -thin.shape[0] % shard))
            columns.append(thin.reshape(-1, shard).T)
        columns = jnp.concatenate(columns, axis=1)
        columns = jnp.pad(columns, ((0, 0), (0, LANES - columns.shape[1])))
        attention_shard = jnp.concatenate([w_query, w_key, w_value, w_out.T, columns], axis=1)
    down_shard = w_down.T

    def gather_all(piece):
        everything = lax.all_gather(piece, BOTH, axis=0, tiled=False)
        everything = everything.reshape(replicas, halves, shard, piece.shape[1])
        return jnp.moveaxis(everything, 1, 0).reshape(1, halves, width, piece.shape[1])

    if pieces:
        first_chunk, up_chunk, down_chunk = Gather(attention_shard), Gather(w_up), Gather(down_shard)
        first_chunk.line()
        four = first_chunk.held
        first_chunk.beside()
        up_chunk.line([four])
        first_chunk.across([cm, cosines, sines, coords])
        sixteen = first_chunk.held
        four = up_chunk.held
        w_attention = first_chunk.core([four])
        up_chunk.beside([sixteen, four], w_attention)
        eight = up_chunk.held
        down_chunk.line_parts([sixteen, four])
        w_attention = [after(w_attention[0], eight), w_attention[1]]
    else:
        w_attention, w_lift, w_drop = [
            [gather_all(piece)] for piece in (attention_shard, w_up, down_shard)
        ]


    columns = 4 * part + LANES
    sq, sk, v, slope_q, slope_k, states, total, w_attention = project(
        coords, inputs, w_attention, columns, edges, cosines, sines, block, shard, halves
    )
    bias_up, vectors = unpack(w_attention, turns, shard, each)
    queries, there = sq, []
    if pieces:
        up_chunk.across([], [sq])
        down_chunk.held = join(
            [down_chunk.held[0]] + [after(part, sq) for part in down_chunk.held[1]]
        )
        there = [up_chunk.held, down_chunk.held]
        queries = after(sq, *there)
    num, den = attend(queries, sk, v, cm, cosines, sines, states)
    towards = [(i, i + 1) for i in range(halves - 1)]
    incoming = send(total, towards, there, [num], "tp")
    if pieces:
        w_lift = up_chunk.core(there, [num])
        down_chunk.beside(there, [num])
        there = [down_chunk.held, incoming, w_lift[1]]
        num = after(num, *there)
    mixed, rden, normal, scale, low = mix(
        num, den, sq, incoming, cosines, sines, w_attention, inputs, vectors, 512
    )
    if pieces:
        down_chunk.across(there, [low])
        there = [down_chunk.held]
        low = after(low, *there)
    act, slope, w_up_halves, now = [], [], [], low
    for half in range(halves):
        act_half, slope_half, w_half = lift(
            coords, now, w_lift, bias_up, half, units, 768, 3 if pieces else 0
        )
        w_up_halves.append(w_half)
        act.append(act_half)
        slope.append(slope_half)
    if pieces:
        w_drop = down_chunk.core(there, [act[1]])
    output, branch, second, sums_second, w_drop = drop(
        coords, act, w_drop, normal, vectors, grad_output, units, 256
    )

    gdown = wide_gradient(coords, branch, act, layout(units), units, 512, "down_gradient")
    there = gdown
    if pieces:
        down_sum = Sum(*gdown)
    gl, gbias_up = [], []
    for half in range(halves):
        now = after(slope[half], *there)
        gl_half, gbias_half = bend(branch, w_drop, now, half, units, 768)
        gl.append(gl_half)
        gbias_up.append(gbias_half)
        if pieces and half == 0:
            down_sum.core([], [gl_half])
            there = down_sum.both()
    wide = units + part + LANES
    gup = wide_gradient(coords, low, gl, layout(wide), units, 512, "up_gradient")
    there = gup
    if pieces:
        down_sum.across([], gup)
        there = [*gup, *down_sum.both()]
    second = after(second, *there)
    first, first_low, sums_first = lower(gl, w_up_halves, second, normal, scale, vectors, units, 256)
    if pieces:
        down_sum.beside([], [first])
        first_low = after(first_low, *down_sum.parts)
    *gup, gn, gd, later, later_total = unmix(
        coords, first_low, mixed, rden, sq, cosines, sines, w_attention,
        sums_first, sums_second, turns, gbias_up, gup, layout(wide), block,
    )
    there = []
    if pieces:
        gdown = down_sum.line([], [gn])
        there = [gdown]
        gn = after(gn, gdown)
    pairs = width // LANES
    partial = ()
    for half in range(halves):
        per = pairs // halves
        partial = unattend(
            sq, sk, v, gn, gd, cm, cosines, sines, states, incoming, later, slope_q,
            half * per, per, partial,
        )
        if half == 0:
            towards = [(i + 1, i) for i in range(halves - 1)]
            later_in = send(later_total, towards, there, partial, "tp")
        if pieces and half == 0:
            up_sum = Sum(*gup)
            up_sum.core(there, partial)
            partial = after(tuple(partial), later_in, *up_sum.both())
    query_low, dk, dv = partial
    key_low, value_low = tail(dk, dv, sk, v, slope_k, cosines, sines, later_in)
    if pieces:
        up_sum.across([], [key_low])
        query_low = after(query_low, *up_sum.both())
    gqkv = weight_gradients(
        coords, inputs, query_low, key_low, value_low, edges, layout(3 * part + LANES)
    )
    if pieces:
        rest_sum = Sum(*gqkv)
        up_sum.beside([], gqkv)
        rest_sum.core(up_sum.parts)
        rest_sum.across()
        gup = up_sum.line([], rest_sum.both())
        rest_sum.beside()
        rest = rest_sum.line()
    else:

        def scatter(grad):
            grad = jnp.moveaxis(grad.reshape(halves, replicas, shard, grad.shape[2]), 0, 1)
            grad = grad.reshape(replicas * halves, shard, grad.shape[3])
            return lax.psum_scatter(grad, BOTH, scatter_dimension=0, tiled=False).astype(F32)

        gdown, gup, rest = [scatter(grad[0]) for grad in (gdown, gup, gqkv)]
    grad_inputs = input_gradient(first, query_low, key_low, value_low, w_attention, 256)

    scaling = 1.0 / replicas
    gdown, gup, rest = gdown * scaling, gup * scaling, rest * scaling
    sums = gup[:, units + part :].T
    small = rest[:edge, 3 * part :].T
    return (
        output,
        grad_inputs,
        rest[:, :part],
        rest[:, part : 2 * part],
        rest[:, 2 * part : 3 * part],
        small[0],
        small[1],
        small[2],
        gup[:, units : units + part].T,
        sums[2],
        sums[0],
        sums[1],
        gup[:, :units],
        sums[6 : 6 + units // width].reshape(-1),
        gdown.T,
        sums[5],
        sums[3],
        sums[4],
    )


def solution(mesh):
    row = P(("fsdp", "tp"), None)
    split, turned = P("fsdp", "tp"), P("tp", "fsdp")
    thin, wide = P(("tp", "fsdp")), P("fsdp")
    return jax.shard_map(
        local,
        mesh=mesh,
        in_specs=(
            row, split, split, split, thin, thin, thin, turned, wide, wide, wide,
            split, thin, turned, wide, wide, wide, P("fsdp", None), row,
        ),
        out_specs=(
            row, row, split, split, split, thin, thin, thin, turned, wide, wide, wide,
            split, thin, turned, wide, wide, wide,
        ),
        check_vma=False,
    )
```

```python
import functools
import math

import jax
import jax.numpy as jnp
from jax import lax
from jax.experimental import pallas as pl
from jax.experimental.pallas import tpu as pltpu
from jax.sharding import PartitionSpec as P

HEAD_DIM = 64
PIECE = 256
LANES = 128
EPSILON = 1e-05
F32 = jnp.float32
BF16 = jnp.bfloat16
BOTH = ("fsdp", "tp")


def dot(left, right):
    return lax.dot_general(left, right, (((1,), (0,)), ((), ())), preferred_element_type=F32)


def dot_nt(left, right):
    return lax.dot_general(left, right, (((1,), (1,)), ((), ())), preferred_element_type=F32)


def dot_tn(left, right):
    return lax.dot_general(left, right, (((0,), (0,)), ((), ())), preferred_element_type=F32)


def flat(ref):
    value = ref[...]
    return value.reshape(value.shape[0] * value.shape[1] * value.shape[2], value.shape[3])


def lane_mask(rows, head, dtype=BF16):
    lane = lax.broadcasted_iota(jnp.int32, (rows, LANES), 1)
    return (lane // HEAD_DIM == head).astype(F32).astype(dtype)


def same_head(rows, columns):
    row = lax.broadcasted_iota(jnp.int32, (rows, columns), 0)
    lane = lax.broadcasted_iota(jnp.int32, (rows, columns), 1)
    return (row // HEAD_DIM) % 2 == (lane // HEAD_DIM) % 2


def compact(state):
    left, right = state[:, :LANES], state[:, LANES:]
    row = lax.broadcasted_iota(jnp.int32, left.shape, 0)
    lane = lax.broadcasted_iota(jnp.int32, left.shape, 1)
    first = (row // HEAD_DIM) % 2 == 0
    low = lane < HEAD_DIM
    return jnp.where(
        low,
        jnp.where(first, left, pltpu.roll(left, HEAD_DIM, 1)),
        jnp.where(first, pltpu.roll(right, HEAD_DIM, 1), right),
    )


def expand(packed):
    row = lax.broadcasted_iota(jnp.int32, packed.shape, 0)
    lane = lax.broadcasted_iota(jnp.int32, packed.shape, 1)
    first = (row // HEAD_DIM) % 2 == 0
    low = lane < HEAD_DIM
    turned = pltpu.roll(packed, HEAD_DIM, 1)
    zero = jnp.zeros_like(packed)
    left = jnp.where(first & low, packed, jnp.where(~first & ~low, turned, zero))
    right = jnp.where(first & low, turned, jnp.where(~first & ~low, packed, zero))
    return jnp.concatenate([left, right], axis=1)


def turned_features(values, cosines, sines):
    wide = values.astype(F32)
    return jnp.concatenate([(wide * cosines).astype(BF16), (wide * sines).astype(BF16)], axis=1)


def slot(coords, z, y, c, x):
    across = jnp.where(c == 0, y ^ coords[1], x ^ coords[3])
    beside = jnp.where(c == 0, x ^ coords[1 + 2], y ^ coords[1])
    return across * 8 + beside * 4 + (z ^ coords[0])


def emit(product, half, outs, coords):
    if len(outs) == 1:
        outs[0][half] = product[...]
        return
    core = coords[2]
    shard = outs[0].shape[1]
    for group in range(product.shape[0] // (2 * shard)):
        z, y = group // 2, group % 2
        for out, c in zip(outs, (core, 1 - core)):
            begin = pl.multiple_of((2 * group + c) * shard, 16)
            out[slot(coords, z, y, c, half)] = product[pl.ds(begin, shard), :]


class Weights:
    def __init__(self, coords_ref, sources, held, out, sems, out_sems, halves):
        self.coords = [coords_ref[place] for place in range(4)]
        self.sources, self.held, self.out = sources, held, out
        self.sems, self.out_sems, self.halves = sems, out_sems, halves

    def copies(self, place):
        half = self.halves[place]
        if len(self.sources) == 1:
            return [
                pltpu.make_async_copy(
                    self.sources[0].at[0, half], self.held.at[place], self.sems.at[place, 0]
                )
            ]
        copies = []
        shard = self.sources[0].shape[1]
        for side, ref in enumerate(self.sources):
            c = self.coords[2] if side == 0 else 1 - self.coords[2]
            for group in range(8):
                z, y = group // 2, group % 2
                begin = pl.multiple_of((2 * group + c) * shard, 16)
                copies.append(
                    pltpu.make_async_copy(
                        ref.at[slot(self.coords, z, y, c, half)],
                        self.held.at[place, pl.ds(begin, shard), :],
                        self.sems.at[place, side * 8 + group],
                    )
                )
        return copies

    def start(self, place):
        for copy in self.copies(place):
            copy.start()

    def ready(self, place):
        for copy in self.copies(place):
            copy.wait()
        self.leaving(place).start()

    def leaving(self, place):
        return pltpu.make_async_copy(
            self.held.at[place], self.out.at[0, place], self.out_sems.at[place]
        )

    def left(self, place):
        self.leaving(place).wait()

    @staticmethod
    def scratch(halves, width, columns):
        return [
            pltpu.VMEM((halves, width, columns), BF16),
            pltpu.SemaphoreType.DMA((halves, 16)),
            pltpu.SemaphoreType.DMA((halves,)),
        ]


def anywhere(count):
    return [pl.BlockSpec(memory_space=pl.ANY)] * count


def scalars():
    return pl.BlockSpec(memory_space=pltpu.SMEM)


def params(megabytes=32):
    return pltpu.CompilerParams(vmem_limit_bytes=megabytes * 1024 * 1024)


def call(kernel, *, out_shape, near_in=(), near_out=(), least=65536, **options):
    shapes = list(out_shape) if isinstance(out_shape, (list, tuple)) else [out_shape]

    def large(value):
        return math.prod(value.shape) * value.dtype.itemsize > least

    placed = [
        pltpu.HBM(shape.shape, shape.dtype) if large(shape) and at not in near_out else shape
        for at, shape in enumerate(shapes)
    ]
    function = pl.pallas_call(
        kernel, out_shape=placed if isinstance(out_shape, (list, tuple)) else placed[0], **options
    )

    def run(*operands):
        count = len(operands)
        near = {at % count for at in near_in}
        return function(
            *[
                pltpu.with_memory_space_constraint(value, pltpu.HBM)
                if large(value) and at not in near
                else value
                for at, value in enumerate(operands)
            ]
        )

    return run


def whole(shape):
    zeros = (0,) * len(shape)
    return pl.BlockSpec(shape, lambda *_: zeros)


def cost(flops, moved):
    return pl.CostEstimate(flops=int(flops), bytes_accessed=int(moved), transcendentals=0)


def after(value, *others):
    return lax.optimization_barrier((value, others))[0]


def pack_kernel(*refs):
    q_ref, k_ref, v_ref, out_ref = refs[:4]
    thins = refs[4:-1]
    first_ref = refs[-1]
    shard, part = q_ref.shape

    def chosen(columns, start):
        row = lax.broadcasted_iota(jnp.int32, (shard, columns), 0)
        column = lax.broadcasted_iota(jnp.int32, (shard, columns), 1)
        return (row + start == column).astype(F32).astype(BF16)

    for place, ref in enumerate((q_ref, k_ref, v_ref, out_ref)):
        first_ref[:, place * part : (place + 1) * part] = ref[...]
    columns = jnp.zeros((shard, LANES), F32)
    lane = 0
    for ref in thins:
        size = ref.shape[1]
        for start in range(0, size, shard):
            row = lax.broadcasted_iota(jnp.int32, (LANES, size), 0)
            spread = jnp.where(row == lane, ref[...].astype(F32), 0.0).astype(BF16)
            columns = columns + dot_nt(chosen(size, start), spread)
            lane += 1
    first_ref[:, 4 * part :] = columns.astype(BF16)


def pack(q, k, v, out, thins):
    shard, part = q.shape
    return call(
        pack_kernel,
        out_shape=jax.ShapeDtypeStruct((shard, 4 * part + LANES), BF16),
        compiler_params=params(),
        cost_estimate=cost(1e8, 1e6),
        name="pack",
        least=0,
    )(q, k, v, out, *[thin.reshape(1, -1) for thin in thins])


def deal(columns, shard, size, turns):
    count = columns.shape[0] // shard
    runs = []
    for place in range(count):
        piece = columns[place * shard : place * shard + size]
        for turn in range(turns):
            runs.append(pltpu.roll(piece, LANES - turn, 1) if turn else piece)
    return jnp.concatenate(runs, axis=0)


def selectors_kernel(edge_ref, turn_ref, *, shard, edge, each):
    width, part = edge_ref.shape
    row = lax.broadcasted_iota(jnp.int32, (width, part), 0)
    column = lax.broadcasted_iota(jnp.int32, (width, part), 1)
    chosen = (row % shard < edge) & (row // shard * edge + row % shard == column)
    edge_ref[...] = chosen.astype(F32).astype(BF16)
    row = lax.broadcasted_iota(jnp.int32, (width, LANES), 0)
    source = row // shard * (each * shard) + row % shard
    lane = lax.broadcasted_iota(jnp.int32, (width, LANES), 1)
    for turn in range(each):
        for begin in range(0, each * width, LANES):
            chosen = source + (turn * shard - begin) == lane
            turn_ref[turn, :, begin : begin + LANES] = chosen.astype(F32).astype(BF16)


def selectors(width, part, shard, edge, each):
    return call(
        functools.partial(selectors_kernel, shard=shard, edge=edge, each=each),
        out_shape=[
            jax.ShapeDtypeStruct((width, part), BF16),
            jax.ShapeDtypeStruct((each, width, each * width), BF16),
        ],
        compiler_params=params(),
        cost_estimate=cost(1e8, 1e6),
        name="selectors",
    )()


def unpack_kernel(thin_ref, turn_ref, up_ref, vec_ref, *, shard, each):
    halves = thin_ref.shape[1]
    for half in range(halves):
        thin = thin_ref[0, half]
        if shard % 16 == 0:
            turned = deal(thin.astype(F32), shard, shard, each).T
            up_ref[half] = turned[0:8]
            continue
        rows = jnp.zeros((8, turn_ref.shape[2]), F32)
        for turn in range(each):
            picked = dot_tn(thin, turn_ref[turn])
            rows = rows + picked[3 + turn : 4 + turn]
        up_ref[half] = rows
    turned = thin_ref[0, 0].astype(F32).T
    vec_ref[...] = turned[3 + each : 11 + each]


def unpack(w, turns, shard, each):
    _, halves, width, columns = w.shape
    return call(
        functools.partial(unpack_kernel, shard=shard, each=each),
        grid=(1,),
        in_specs=[
            pl.BlockSpec((1, halves, width, LANES), lambda i: (0, 0, 0, columns // LANES - 1)),
            whole(turns.shape),
        ],
        out_specs=[whole((halves, 8, each * width)), whole((8, width))],
        out_shape=[
            jax.ShapeDtypeStruct((halves, 8, each * width), F32),
            jax.ShapeDtypeStruct((8, width), F32),
        ],
        compiler_params=params(),
        cost_estimate=cost(1e8, 1e6),
        name="unpack",
    )(w, turns)


def join_kernel(*refs):
    for place, ref in enumerate(refs[:-1]):
        refs[-1][place] = ref[...]


def join(parts):
    return call(
        join_kernel,
        out_shape=jax.ShapeDtypeStruct((len(parts),) + parts[0].shape, parts[0].dtype),
        compiler_params=params(),
        cost_estimate=cost(0, 1e6),
        name="join",
        least=0,
    )(*parts)


def project_kernel(
    coords_ref, *refs, block, step, shard, halves
):
    sources, refs = refs[: len(refs) - 14], refs[len(refs) - 14 :]
    x_ref, edge_ref, cos_ref, sin_ref, sq_ref, sk_ref, v_ref, gq_ref, gk_ref, st_ref, tot_ref = refs[:11]
    sources, out_ref = sources[:-1], sources[-1]
    held_ref, sems, out_sems = refs[11:]
    rows = x_ref.shape[0]
    part = sq_ref.shape[1]
    now = pl.program_id(0)
    weights = Weights(coords_ref, sources, held_ref, out_ref, sems, out_sems, range(halves))

    @pl.when(now == 0)
    def _():
        for half in range(halves):
            weights.start(half)

    for half in range(halves):

        @pl.when(now == half)
        def _():
            weights.ready(half)

    columns = held_ref.shape[2]
    thin = held_ref[now, :, columns - LANES :]
    if shard % 16 == 0:
        biases = deal(thin.astype(F32), shard, shard * part // x_ref.shape[1], 1).T
    else:
        biases = dot_tn(thin, edge_ref[...])

    def body(index, carry):
        here = pl.ds(index * step, step)
        sums = dot(x_ref[here, :], held_ref[now, :, : 3 * part])
        for place, (feature_ref, slope_ref) in enumerate(((sq_ref, gq_ref), (sk_ref, gk_ref))):
            value = sums[:, place * part : (place + 1) * part] + biases[place : place + 1]
            positive = jnp.maximum(value, 0.0) + jnp.log1p(jnp.exp(-jnp.abs(value)))
            feature_ref[here, :] = positive.astype(BF16)
            slope_ref[here, :] = jax.nn.sigmoid(value).astype(BF16)
        v_ref[here, :] = (sums[:, 2 * part :] + biases[2:3]).astype(BF16)
        return carry

    lax.fori_loop(0, rows // step, body, 0)
    keep = same_head(2 * LANES, 2 * LANES)
    ones = jnp.ones((block, LANES), BF16)
    for pair in range(part // LANES):
        lanes = slice(pair * LANES, (pair + 1) * LANES)
        total = jnp.zeros((2 * LANES, 2 * LANES), F32)
        for place in range(rows // block):
            here = slice(place * block, (place + 1) * block)
            features = turned_features(sk_ref[here, lanes], cos_ref[here, :], sin_ref[here, :])
            state = dot_tn(features, jnp.concatenate([v_ref[here, lanes], ones], axis=1))
            state = jnp.where(keep, state, 0.0)
            st_ref[place, pair] = state.astype(BF16)
            total = total + state
        tot_ref[pair] = compact(total).astype(BF16)

    @pl.when(now == halves - 1)
    def _():
        for half in range(halves):
            weights.left(half)


def project(coords, x, sources, columns, edges, cosines, sines, block, shard, halves):
    rows, width = x.shape
    part = width // halves
    pairs = width // LANES
    half = pairs // halves
    blocks = rows // block
    row_spec = pl.BlockSpec((rows, part), lambda t: (0, t))
    full = jax.ShapeDtypeStruct((rows, width), BF16)

    def kernel(coords_ref, *refs):
        count = len(sources)
        others, outs, scratch = refs[count : count + 4], refs[count + 4 : -3], refs[-3:]
        project_kernel(
            coords_ref, *refs[:count], outs[-1], *others, *outs[:-1], *scratch,
            block=block, step=rows, shard=shard, halves=halves,
        )

    return call(
        kernel,
        grid=(halves,),
        in_specs=[scalars()]
        + anywhere(len(sources))
        + [
            whole((rows, width)), whole(edges.shape), whole((rows, LANES)), whole((rows, LANES)),
        ],
        out_specs=[
            row_spec, row_spec, row_spec, row_spec, row_spec,
            pl.BlockSpec((blocks, half, 2 * LANES, 2 * LANES), lambda t: (0, t, 0, 0)),
            pl.BlockSpec((half, 2 * LANES, LANES), lambda t: (t, 0, 0)),
        ]
        + anywhere(1),
        out_shape=[
            full, full, full, full, full,
            jax.ShapeDtypeStruct((blocks, pairs, 2 * LANES, 2 * LANES), BF16),
            jax.ShapeDtypeStruct((pairs, 2 * LANES, LANES), BF16),
            jax.ShapeDtypeStruct((1, halves, width, columns), BF16),
        ],
        scratch_shapes=Weights.scratch(halves, width, columns),
        compiler_params=params(),
        cost_estimate=cost(2 * rows * width * 3 * width, 16e6),
        name="project",
    )(coords, *sources, x, edges, cosines, sines)


def attend_kernel(sq_ref, sk_ref, v_ref, cm_ref, cos_ref, sin_ref, st_ref, num_ref, den_ref):
    blocks, block, _ = cm_ref.shape
    piece = min(PIECE, block)
    masks = [lane_mask(block, head) for head in range(2)]
    for place in range(blocks):
        start = place * block
        keys = sk_ref[start : start + block, :]
        values = v_ref[start : start + block, :]
        sides = [jnp.concatenate([values * mask, mask], axis=1) for mask in masks]
        for low in range(0, block, piece):
            here = slice(start + low, start + low + piece)
            span = low + piece
            queries = sq_ref[here, :]
            sums = None
            for mask, side in zip(masks, sides):
                scores = dot_nt(queries * mask[:piece], keys[:span])
                weights = (scores * cm_ref[place, low : low + piece, :span]).astype(BF16)
                term = dot(weights, side[:span])
                sums = term if sums is None else sums + term
            for earlier in range(place):
                sums = sums + dot(
                    turned_features(queries, cos_ref[here, :], sin_ref[here, :]), st_ref[earlier, 0]
                )
            num_ref[here, :] = sums[:, :LANES]
            den_ref[here, :] = sums[:, LANES:]


def attend(sq, sk, v, cm, cosines, sines, states):
    rows, width = sq.shape
    pairs = width // LANES
    blocks = cm.shape[0]
    spec = pl.BlockSpec((rows, LANES), lambda p: (0, p))
    full = jax.ShapeDtypeStruct((rows, width), F32)
    return call(
        attend_kernel,
        grid=(pairs,),
        in_specs=[
            spec, spec, spec,
            whole(cm.shape), whole((rows, LANES)), whole((rows, LANES)),
            pl.BlockSpec((blocks, 1, 2 * LANES, 2 * LANES), lambda p: (0, p, 0, 0)),
        ],
        out_specs=[spec, spec],
        out_shape=[full, full],
        compiler_params=params(),
        cost_estimate=cost(8e9, 14e6),
        name="attend",
        near_out=(0, 1),
    )(sq, sk, v, cm, cosines, sines, states)


def norm_rows(values):
    average = jnp.mean(values, axis=1, keepdims=True)
    centred = values - average
    scale = lax.rsqrt(jnp.mean(centred * centred, axis=1, keepdims=True) + EPSILON)
    return centred * scale, scale


def mix_kernel(
    num_ref, den_ref, sq_ref, in_ref, cos_ref, sin_ref, w_ref, x_ref, vec_ref,
    mixed_ref, rden_ref, normal_ref, scale_ref, low_ref, wide_ref,
):
    pairs = in_ref.shape[0]
    halves = w_ref.shape[1]
    rows, width = x_ref.shape
    part = width // halves

    @pl.when(pl.program_id(0) == 0)
    def _():
        for pair in range(pairs):
            wide_ref[pair] = expand(in_ref[pair].astype(F32)).astype(BF16)

    for pair in range(pairs):
        lanes = slice(pair * LANES, (pair + 1) * LANES)
        sums = dot(turned_features(sq_ref[:, lanes], cos_ref[...], sin_ref[...]), wide_ref[pair])
        inverse = 1.0 / jnp.maximum(den_ref[:, lanes] + sums[:, LANES:], 1.0)
        rden_ref[:, lanes] = inverse
        mixed_ref[:, lanes] = ((num_ref[:, lanes] + sums[:, :LANES]) * inverse).astype(BF16)
    total = x_ref[...].astype(F32) + vec_ref[0:1, :]
    for half in range(halves):
        side = w_ref[:, half]
        side = side.reshape(width, part)
        total = total + dot_nt(mixed_ref[:, half * part : (half + 1) * part], side)
    normal, scale = norm_rows(total)
    normal_ref[...] = normal
    scale_ref[...] = jnp.broadcast_to(scale, scale_ref.shape)
    low_ref[...] = (normal * vec_ref[1:2, :] + vec_ref[2:3, :]).astype(BF16)


def mix(num, den, sq, incoming, cosines, sines, w, x, vectors, step):
    rows, width = x.shape
    groups, halves, shard, _ = w.shape
    part = width // halves
    pairs = incoming.shape[0]
    wide = pl.BlockSpec((step, width), lambda i: (i, 0))
    thin = pl.BlockSpec((step, LANES), lambda i: (i, 0))
    return call(
        mix_kernel,
        grid=(rows // step,),
        in_specs=[
            wide, wide, wide, whole(incoming.shape), thin, thin,
            pl.BlockSpec((groups, halves, shard, part), lambda i: (0, 0, 0, 3)),
            wide, whole(vectors.shape),
        ],
        out_specs=[wide, wide, wide, thin, wide],
        out_shape=[
            jax.ShapeDtypeStruct((rows, width), BF16),
            jax.ShapeDtypeStruct((rows, width), F32),
            jax.ShapeDtypeStruct((rows, width), F32),
            jax.ShapeDtypeStruct((rows, LANES), F32),
            jax.ShapeDtypeStruct((rows, width), BF16),
        ],
        scratch_shapes=[pltpu.VMEM((pairs, 2 * LANES, 2 * LANES), BF16)],
        compiler_params=params(),
        cost_estimate=cost(2 * rows * width * width * 2, 20e6),
        name="mix",
        near_in=(0, 1),
        near_out=(2, 4),
    )(num, den, sq, incoming, cosines, sines, w, x, vectors)


def norm_back(upstream, normal, scale, gain):
    scaled = upstream * gain
    inner = (
        scaled
        - jnp.mean(scaled, axis=1, keepdims=True)
        - normal * jnp.mean(scaled * normal, axis=1, keepdims=True)
    )
    return inner * scale


def lift_kernel(coords_ref, *refs, step, row, halves):
    sources, refs = refs[:-8], refs[-8:]
    low_ref, bias_ref, act_ref, slope_ref, out_ref, held_ref, sems, out_sems = refs
    tile = act_ref.shape[1]
    now = pl.program_id(0)
    tiles = pl.num_programs(0) // halves
    weights = Weights(coords_ref, sources, held_ref, out_ref, sems, out_sems, range(halves))

    @pl.when(now == 0)
    def _():
        for half in range(halves):
            weights.start(half)

    for half in range(halves):

        @pl.when(now == half * tiles)
        def _():
            weights.ready(half)

    begin = pl.multiple_of(now % tiles * tile, tile)
    up = held_ref[now // tiles, :, pl.ds(begin, tile)]

    def body(place, carry):
        here = pl.ds(place * step, step)
        lifted = dot(low_ref[here, :], up) + bias_ref[0, row : row + 1, :]
        share = 0.5 + 0.5 * lax.erf(lifted * math.sqrt(0.5))
        bell = jnp.exp(-0.5 * lifted * lifted) * (1.0 / math.sqrt(2.0 * math.pi))
        act_ref[here, :] = (lifted * share).astype(BF16)
        slope_ref[here, :] = (share + lifted * bell).astype(BF16)
        return carry

    lax.fori_loop(0, low_ref.shape[0] // step, body, 0, unroll=True)

    @pl.when(now == pl.num_programs(0) - 1)
    def _():
        for half in range(halves):
            weights.left(half)


def lift(coords, low, sources, bias, units, tile, row):
    rows, width = low.shape
    halves = bias.shape[0]
    tiles = units // tile
    unit_spec = pl.BlockSpec((rows, tile), lambda i: (0, i))
    shape = jax.ShapeDtypeStruct((rows, halves * units), BF16)
    return call(
        functools.partial(lift_kernel, step=256, row=row, halves=halves),
        grid=(halves * tiles,),
        in_specs=[scalars()]
        + anywhere(len(sources))
        + [whole((rows, width)), pl.BlockSpec((1, 8, tile), lambda i: (i // tiles, 0, i % tiles))],
        out_specs=[unit_spec, unit_spec] + anywhere(1),
        out_shape=[shape, shape, jax.ShapeDtypeStruct((1, halves, width, units), BF16)],
        scratch_shapes=Weights.scratch(halves, width, units),
        compiler_params=params(),
        cost_estimate=cost(2 * rows * width * halves * units, 20e6),
        name="lift",
        near_in=(-2,),
        near_out=(0, 1),
    )(coords, *sources, low, bias)


def in_turn(product, finish, total_ref):
    now = pl.program_id(0)
    last = pl.num_programs(0) - 1

    @pl.when(now == 0)
    def _():
        total_ref[0] = product()

    @pl.when((now > 0) & (now < last))
    def _():
        finish(total_ref[(now - 1) % 2])
        total_ref[now % 2] = product()

    @pl.when(now == last)
    def _():
        finish(total_ref[(now - 1) % 2])


def drop_kernel(coords_ref, *refs, halves):
    sources, act_ref, refs = refs[:-13], refs[-13], refs[-12:]
    normal_ref, vec_ref, grad_ref, out_ref, branch_ref, second_ref, sum_ref = refs[:7]
    whole_ref, held_ref, sems, out_sems, total_ref = refs[7:]
    weights = Weights(coords_ref, sources, held_ref, whole_ref, sems, out_sems, range(halves))
    units = held_ref.shape[2]

    @pl.when(pl.program_id(0) == 0)
    def _():
        sum_ref[...] = jnp.zeros_like(sum_ref)
        for half in range(halves):
            weights.start(half)
        for half in range(halves):
            weights.ready(half)

    def product():
        total = None
        for half in range(halves):
            term = dot_nt(act_ref[:, half * units : (half + 1) * units], held_ref[half])
            total = term if total is None else total + term
        return total

    def finish(total):
        total = total + normal_ref[...] * vec_ref[1:2, :] + vec_ref[2:3, :] + vec_ref[3:4, :]
        normal, scale = norm_rows(total)
        gain = vec_ref[4:5, :]
        out_ref[...] = (normal * gain + vec_ref[5:6, :]).astype(BF16)
        upstream = grad_ref[...].astype(F32)
        second = norm_back(upstream, normal, scale, gain)
        second_ref[...] = second
        branch_ref[...] = second.astype(BF16)
        sum_ref[0:1, :] += jnp.sum(upstream * normal, axis=0, keepdims=True)
        sum_ref[1:2, :] += jnp.sum(upstream, axis=0, keepdims=True)
        sum_ref[2:3, :] += jnp.sum(second, axis=0, keepdims=True)

    in_turn(product, finish, total_ref)

    @pl.when(pl.program_id(0) == pl.num_programs(0) - 1)
    def _():
        for half in range(halves):
            weights.left(half)


def drop(coords, act, sources, normal, vectors, grad, units, step):
    rows, width = normal.shape
    halves = act.shape[1] // units
    steps = rows // step
    wide = pl.BlockSpec((step, width), lambda i: (jnp.maximum(i - 1, 0), 0))
    return call(
        functools.partial(drop_kernel, halves=halves),
        grid=(steps + 1,),
        in_specs=[scalars()]
        + anywhere(len(sources))
        + [
            pl.BlockSpec((step, halves * units), lambda i: (jnp.minimum(i, steps - 1), 0)),
            wide, whole(vectors.shape), wide,
        ],
        out_specs=[wide, wide, wide, whole((8, width))] + anywhere(1),
        out_shape=[
            jax.ShapeDtypeStruct((rows, width), BF16),
            jax.ShapeDtypeStruct((rows, width), BF16),
            jax.ShapeDtypeStruct((rows, width), F32),
            jax.ShapeDtypeStruct((8, width), F32),
            jax.ShapeDtypeStruct((1, halves, width, units), BF16),
        ],
        scratch_shapes=Weights.scratch(halves, width, units) + [pltpu.VMEM((2, step, width), F32)],
        compiler_params=params(),
        cost_estimate=cost(2 * rows * width * halves * units, 20e6),
        name="drop",
        near_in=(-4, -3),
        near_out=(1, 2),
    )(coords, *sources, act, normal, vectors, grad)


def piece_outputs(layout, tile, index_map):
    replicas, halves, shard, columns, pieces = layout[:5]
    if pieces:
        count = replicas * halves // 2
        spec = pl.BlockSpec((count, shard, tile), lambda *at: (0, 0, index_map(*at)))
        shape = jax.ShapeDtypeStruct((count, shard, columns), BF16)
        return [spec, spec], [shape, shape]
    width = replicas * shard
    spec = pl.BlockSpec((halves, width, tile), lambda *at: (0, 0, index_map(*at)))
    return [spec], [jax.ShapeDtypeStruct((halves, width, columns), BF16)]


def wide_gradient_kernel(coords_ref, left_ref, *refs, halves, partial):
    rights, product_ref = refs[:halves], refs[-1]
    outs = refs[(len(refs) - 1 + halves) // 2 : -1] if partial else refs[halves:-1]
    coords = [coords_ref[place] for place in range(4)]
    for half, right_ref in enumerate(rights):
        product_ref[...] = dot_tn(left_ref[...], right_ref[...]).astype(BF16)
        emit(product_ref, half, outs, coords)


def wide_gradient(coords, left, right, layout, units, tile, name, partial=()):
    rows, width = left.shape
    halves = layout[1]
    tiles = units // tile
    out_specs, out_shapes = piece_outputs(layout, tile, lambda j: j)
    return call(
        functools.partial(wide_gradient_kernel, halves=halves, partial=bool(partial)),
        grid=(tiles,),
        in_specs=[scalars(), whole((rows, width))]
        + [
            pl.BlockSpec((rows, tile), lambda j, half=half: (0, half * tiles + j))
            for half in range(halves)
        ]
        + anywhere(len(partial)),
        out_specs=out_specs,
        out_shape=out_shapes,
        input_output_aliases={2 + halves + at: at for at in range(len(partial))},
        scratch_shapes=[pltpu.VMEM((width, tile), BF16)],
        compiler_params=params(),
        cost_estimate=cost(2 * rows * width * halves * units, 18e6),
        name=name,
        near_in=(1, 2, 3),
    )(coords, left, *([right] * halves), *partial)


def bend_kernel(branch_ref, down_ref, slope_ref, gl_ref, gbias_ref, *, step):
    down = down_ref[0, 0]
    gbias_ref[...] = jnp.zeros_like(gbias_ref)

    def body(place, carry):
        here = pl.ds(place * step, step)
        slope = dot(branch_ref[here, :], down) * slope_ref[here, :].astype(F32)
        gbias_ref[0:1, :] += jnp.sum(slope, axis=0, keepdims=True)
        gl_ref[here, :] = slope.astype(BF16)
        return carry

    lax.fori_loop(0, branch_ref.shape[0] // step, body, 0, unroll=True)


def bend(branch, w, slope, units, tile):
    rows, width = branch.shape
    halves = w.shape[1]
    tiles = units // tile
    unit_spec = pl.BlockSpec((rows, tile), lambda i: (0, i))
    return call(
        functools.partial(bend_kernel, step=256),
        grid=(halves * tiles,),
        in_specs=[
            whole((rows, width)),
            pl.BlockSpec((1, 1, width, tile), lambda i: (0, i // tiles, 0, i % tiles)),
            unit_spec,
        ],
        out_specs=[unit_spec, pl.BlockSpec((8, tile), lambda i: (0, i))],
        out_shape=[
            jax.ShapeDtypeStruct(slope.shape, BF16),
            jax.ShapeDtypeStruct((8, halves * units), F32),
        ],
        compiler_params=params(),
        cost_estimate=cost(2 * rows * width * halves * units, 20e6),
        name="bend",
        near_in=(0, 2),
        near_out=(0,),
    )(branch, w, slope)


def lower_kernel(
    gl_ref, up_ref, second_ref, normal_ref, scale_ref, vec_ref, first_ref, firstlow_ref, sum_ref,
    total_ref,
):
    halves, units = up_ref.shape[1], up_ref.shape[3]

    @pl.when(pl.program_id(0) == 0)
    def _():
        sum_ref[...] = jnp.zeros_like(sum_ref)

    def product():
        total = None
        for half in range(halves):
            term = dot_nt(gl_ref[:, half * units : (half + 1) * units], up_ref[0, half])
            total = term if total is None else total + term
        return total

    def finish(total):
        upstream = second_ref[...] + total
        normal = normal_ref[...]
        first = norm_back(upstream, normal, scale_ref[:, 0:1], vec_ref[1:2, :])
        first_ref[...] = first
        firstlow_ref[...] = first.astype(BF16)
        sum_ref[0:1, :] += jnp.sum(upstream * normal, axis=0, keepdims=True)
        sum_ref[1:2, :] += jnp.sum(upstream, axis=0, keepdims=True)
        sum_ref[2:3, :] += jnp.sum(first, axis=0, keepdims=True)

    in_turn(product, finish, total_ref)


def lower(gl, w, second, normal, scale, vectors, units, step):
    rows, width = second.shape
    steps = rows // step
    wide = pl.BlockSpec((step, width), lambda i: (jnp.maximum(i - 1, 0), 0))
    return call(
        lower_kernel,
        grid=(steps + 1,),
        in_specs=[
            pl.BlockSpec((step, gl.shape[1]), lambda i: (jnp.minimum(i, steps - 1), 0)),
            whole(w.shape), wide, wide,
            pl.BlockSpec((step, LANES), lambda i: (jnp.maximum(i - 1, 0), 0)),
            whole(vectors.shape),
        ],
        out_specs=[wide, wide, whole((8, width))],
        out_shape=[
            jax.ShapeDtypeStruct((rows, width), F32),
            jax.ShapeDtypeStruct((rows, width), BF16),
            jax.ShapeDtypeStruct((8, width), F32),
        ],
        scratch_shapes=[pltpu.VMEM((2, step, width), F32)],
        compiler_params=params(),
        cost_estimate=cost(2 * rows * width * gl.shape[1], 20e6),
        name="lower",
        near_in=(0, 2, 3),
        near_out=(1,),
    )(gl, w, second, normal, scale, vectors)


def unmix_kernel(
    coords_ref, first_ref, mixed_ref, rden_ref, sq_ref, cos_ref, sin_ref, w_ref,
    sum1_ref, sum2_ref, turn_ref, *refs, block, step, shard
):
    bias = jnp.broadcast_to(refs[0][0:1, :], refs[0].shape)
    refs = refs[1:]
    outs = refs[:-5]
    gn_ref, gd_ref, st_ref, tot_ref, product_ref = refs[-5:]
    coords = [coords_ref[place] for place in range(4)]
    rows, width = first_ref.shape
    part = mixed_ref.shape[1]
    side = flat(w_ref)
    group_row = lax.broadcasted_iota(jnp.int32, (LANES, LANES), 0)
    group_lane = lax.broadcasted_iota(jnp.int32, (LANES, LANES), 1)
    group = (group_row // HEAD_DIM == group_lane // HEAD_DIM).astype(F32).astype(BF16)
    group = jnp.concatenate([group, group], axis=0)

    lane = lax.broadcasted_iota(jnp.int32, (step, LANES), 1) % HEAD_DIM

    def body(place, carry):
        here = pl.ds(place * step, step)
        grad = dot(first_ref[here, :], side)
        for pair in range(part // LANES):
            lanes = slice(pair * LANES, (pair + 1) * LANES)
            inverse = rden_ref[here, lanes]
            scaled = grad[:, lanes] * inverse
            product = scaled * mixed_ref[here, lanes].astype(F32)
            high = product.astype(BF16)
            rest = (product - high.astype(F32)).astype(BF16)
            inner = dot(jnp.concatenate([high, rest], axis=1), group)
            slope = jnp.where(inverse < 1.0, -inner, 0.0)
            high = slope.astype(BF16).astype(F32)
            gn_ref[here, lanes] = scaled.astype(BF16)
            gd_ref[here, lanes] = jnp.where(
                lane == 0, high, jnp.where(lane == 1, slope - high, 0.0)
            ).astype(BF16)
        return carry

    lax.fori_loop(0, rows // step, body, 0)
    product_ref[:, :part] = dot_tn(first_ref[...], mixed_ref[...]).astype(BF16)
    row = lax.broadcasted_iota(jnp.int32, (8, width), 0)
    packed = jnp.where(row < 3, sum1_ref[...], pltpu.roll(sum2_ref[...], 3, 0))
    packed = jnp.where(row < 6, packed, 0.0)
    columns = jnp.concatenate([packed, jnp.zeros((LANES - 8, width), F32)], axis=0).T
    units = bias.shape[1]
    each = units // width
    if shard % 16 == 0:
        at = lax.broadcasted_iota(jnp.int32, (8, units), 0)
        both = jnp.where(at >= 6, bias, 0.0)
        turned = jnp.concatenate([both, jnp.zeros((LANES - 8, units), F32)], axis=0).T
        lane_at = lax.broadcasted_iota(jnp.int32, (shard, LANES), 1)
        for place in range(width // shard):
            piece = columns[place * shard : (place + 1) * shard]
            for turn in range(each):
                begin = (place * each + turn) * shard
                piece = jnp.where(lane_at == 6 + turn, turned[begin : begin + shard], piece)
            product_ref[place * shard : (place + 1) * shard, part:] = piece.astype(BF16)
    else:
        side_row = lax.broadcasted_iota(jnp.int32, (8, LANES), 0)
        turned = dot_tn(bias.astype(BF16), (side_row == 0).astype(F32).astype(BF16)).astype(BF16)
        lane_at = lax.broadcasted_iota(jnp.int32, (width, LANES), 1)
        for turn in range(each):
            columns = jnp.where(lane_at == 6 + turn, dot(turn_ref[turn], turned), columns)
        product_ref[:, part:] = columns.astype(BF16)
    emit(product_ref, pl.program_id(0), outs, coords)
    keep = same_head(2 * LANES, 2 * LANES)
    for pair in range(part // LANES):
        lanes = slice(pair * LANES, (pair + 1) * LANES)
        total = jnp.zeros((2 * LANES, 2 * LANES), F32)
        for place in range(rows // block):
            here = slice(place * block, (place + 1) * block)
            features = turned_features(sq_ref[here, lanes], cos_ref[here, :], sin_ref[here, :])
            state = dot_tn(
                features, jnp.concatenate([gn_ref[here, lanes], gd_ref[here, lanes]], axis=1)
            )
            state = jnp.where(keep, state, 0.0)
            st_ref[place, pair] = state.astype(BF16)
            total = total + state
        tot_ref[pair] = compact(total).astype(BF16)


def unmix(
    coords, first, mixed, rden, sq, cosines, sines, w, sums1, sums2, turns, gbias, layout, block
):
    rows, width = first.shape
    groups, halves, shard, _ = w.shape
    part = width // halves
    pairs = width // LANES
    half = pairs // halves
    blocks = rows // block
    row_spec = pl.BlockSpec((rows, part), lambda t: (0, t))
    tile = part + LANES
    out_specs, out_shapes = piece_outputs(layout, tile, lambda t: layout[3] // tile - 1)
    units = gbias.shape[1] // halves
    full = jax.ShapeDtypeStruct((rows, width), BF16)
    return call(
        functools.partial(
            unmix_kernel, block=block, step=512, shard=layout[2]
        ),
        grid=(halves,),
        in_specs=[
            scalars(), whole((rows, width)), row_spec, row_spec, row_spec,
            whole((rows, LANES)), whole((rows, LANES)),
            pl.BlockSpec((groups, 1, shard, part), lambda t: (0, t, 0, 3)),
            whole((8, width)), whole((8, width)), whole(turns.shape),
        ]
        + [pl.BlockSpec((8, units), lambda t: (0, t))],
        out_specs=out_specs
        + [
            row_spec, row_spec,
            pl.BlockSpec((blocks, half, 2 * LANES, 2 * LANES), lambda t: (0, t, 0, 0)),
            pl.BlockSpec((half, 2 * LANES, LANES), lambda t: (t, 0, 0)),
        ],
        out_shape=out_shapes
        + [
            full, full,
            jax.ShapeDtypeStruct((blocks, pairs, 2 * LANES, 2 * LANES), BF16),
            jax.ShapeDtypeStruct((pairs, 2 * LANES, LANES), BF16),
        ],
        scratch_shapes=[pltpu.VMEM((width, tile), BF16)],
        compiler_params=params(),
        cost_estimate=cost(4 * rows * width * width, 16e6),
        name="unmix",
        near_in=(1,),
        near_out=(len(out_shapes), len(out_shapes) + 1),
    )(coords, first, mixed, rden, sq, cosines, sines, w, sums1, sums2, turns, gbias)


def unattend_kernel(
    sq_ref, sk_ref, v_ref, gn_ref, gd_ref, cm_ref, cos_ref, sin_ref, st_ref, in_ref, lt_ref, gq_ref,
    gk_ref, later_ref, *refs,
):
    query_ref, dk_ref, dv_ref = refs[-3:]
    blocks, block, _ = cm_ref.shape
    piece = min(PIECE, block)
    masks = [lane_mask(block, head) for head in range(2)]
    ones = jnp.ones((block, LANES), BF16)
    incoming = expand(in_ref[0].astype(F32))
    outgoing = expand(later_ref[0].astype(F32))
    for place in range(blocks):
        start = place * block
        all_here = slice(start, start + block)
        keys, values = sk_ref[all_here, :], v_ref[all_here, :]
        sides = jnp.concatenate([values, ones], axis=1)
        key_sides = [keys * mask for mask in masks]
        state = incoming
        for earlier in range(place):
            state = state + st_ref[earlier, 0].astype(F32)
        state = state.astype(BF16)
        grad_keys = [None] * (block // piece)
        grad_values = [None] * (block // piece)
        for low in range(0, block, piece):
            here = slice(start + low, start + low + piece)
            span = low + piece
            queries, grads, slopes = sq_ref[here, :], gn_ref[here, :], gd_ref[here, :]
            grad_queries = None
            for head in range(2):
                mask = masks[head][:piece]
                cm = cm_ref[place, low : low + piece, :span]
                masked_queries, masked_grads = queries * mask, grads * mask
                scores = dot_nt(masked_queries, keys[:span])
                weights = (scores * cm).astype(BF16)
                back = dot_nt(
                    jnp.concatenate([masked_grads, slopes * mask], axis=1), sides[:span]
                )
                back = (back * cm).astype(BF16)
                term = dot(back, key_sides[head][:span])
                grad_queries = term if grad_queries is None else grad_queries + term
                key_term = dot_tn(back, masked_queries)
                value_term = dot_tn(weights, masked_grads)
                for piece_at in range(span // piece):
                    at = slice(piece_at * piece, (piece_at + 1) * piece)
                    old = grad_keys[piece_at]
                    grad_keys[piece_at] = key_term[at] if old is None else old + key_term[at]
                    old = grad_values[piece_at]
                    grad_values[piece_at] = value_term[at] if old is None else old + value_term[at]
            far = dot_nt(jnp.concatenate([grads, slopes], axis=1), state)
            grad_queries = (
                grad_queries
                + far[:, :LANES] * cos_ref[here, :]
                + far[:, LANES:] * sin_ref[here, :]
            ) * gq_ref[here, :].astype(F32)
            query_ref[here, :] = grad_queries.astype(BF16)
        grad_keys = jnp.concatenate(grad_keys, axis=0)
        grad_values = jnp.concatenate(grad_values, axis=0)
        state = outgoing
        for later in range(place + 1, blocks):
            state = state + lt_ref[later, 0].astype(F32)
        state = state.astype(BF16)
        far = dot_nt(sides, state)
        grad_keys = (
            grad_keys
            + far[:, :LANES] * cos_ref[all_here, :]
            + far[:, LANES:] * sin_ref[all_here, :]
        ) * gk_ref[all_here, :].astype(F32)
        features = turned_features(keys, cos_ref[all_here, :], sin_ref[all_here, :])
        grad_values = grad_values + dot(features, state[:, :LANES])
        dk_ref[all_here, :] = grad_keys.astype(BF16)
        dv_ref[all_here, :] = grad_values.astype(BF16)


def unattend(
    sq, sk, v, gn, gd, cm, cosines, sines, states, incoming, later, slope_q, slope_k,
    later_in, start, count, partial
):
    rows, width = sq.shape
    blocks = cm.shape[0]
    spec = pl.BlockSpec((rows, LANES), lambda p: (0, start + p))
    state_spec = pl.BlockSpec((blocks, 1, 2 * LANES, 2 * LANES), lambda p: (0, start + p, 0, 0))
    full = jax.ShapeDtypeStruct((rows, width), BF16)
    return call(
        unattend_kernel,
        grid=(count,),
        in_specs=[
            spec, spec, spec, spec, spec,
            whole(cm.shape), whole((rows, LANES)), whole((rows, LANES)),
            state_spec,
            pl.BlockSpec((1, 2 * LANES, LANES), lambda p: (start + p, 0, 0)),
            state_spec, spec, spec,
            pl.BlockSpec((1, 2 * LANES, LANES), lambda p: (start + p, 0, 0)),
        ]
        + [pl.BlockSpec(memory_space=pl.ANY)] * len(partial),
        out_specs=[spec, spec, spec],
        out_shape=[jax.ShapeDtypeStruct((rows, width), BF16), full, full],
        input_output_aliases={14 + at: at for at in range(len(partial))},
        compiler_params=params(),
        cost_estimate=cost(20e9, 20e6),
        name="unattend",
        near_in=(3, 4, 14, 15, 16),
        near_out=(0, 1, 2),
    )(sq, sk, v, gn, gd, cm, cosines, sines, states, incoming, later, slope_q, slope_k, later_in, *partial)


def weights_kernel(coords_ref, x_ref, q_ref, k_ref, v_ref, edge_ref, *refs, shard):
    outs, product_ref = refs[:-1], refs[-1]
    coords = [coords_ref[place] for place in range(4)]
    rows, part = q_ref.shape
    width = x_ref.shape[1]
    ones = jnp.ones((rows, LANES), BF16)
    lane = lax.broadcasted_iota(jnp.int32, (part, LANES), 1)
    sums = jnp.zeros((part, LANES), F32)
    for place, ref in enumerate((q_ref, k_ref, v_ref)):
        at = slice(place * part, (place + 1) * part)
        product_ref[:, at] = dot_tn(x_ref[...], ref[...]).astype(BF16)
        sums = jnp.where(lane == place, dot_tn(ref[...], ones), sums)
    if shard % 16 == 0:
        edge = shard * part // width
        for place in range(width // shard):
            piece = jnp.concatenate(
                [sums[place * edge : (place + 1) * edge], jnp.zeros((shard - edge, LANES), F32)], axis=0
            )
            product_ref[place * shard : (place + 1) * shard, 3 * part :] = piece.astype(BF16)
    else:
        product_ref[:, 3 * part :] = dot(edge_ref[...], sums.astype(BF16)).astype(BF16)
    emit(product_ref, pl.program_id(0), outs, coords)


def weight_gradients(coords, x, q, k, v, edges, layout):
    rows, width = x.shape
    halves = layout[1]
    spec = pl.BlockSpec((rows, width // halves), lambda t: (0, t))
    out_specs, out_shapes = piece_outputs(layout, layout[3], lambda t: 0)
    return call(
        functools.partial(weights_kernel, shard=layout[2]),
        grid=(halves,),
        in_specs=[scalars(), whole((rows, width)), spec, spec, spec, whole(edges.shape)],
        out_specs=out_specs,
        out_shape=out_shapes,
        scratch_shapes=[pltpu.VMEM((width, layout[3]), BF16)],
        compiler_params=params(),
        cost_estimate=cost(2 * rows * width * 3 * width, 10e6),
        name="weight_gradients",
        near_in=(2, 3, 4),
    )(coords, x, q, k, v, edges)


def inputs_kernel(first_ref, q_ref, k_ref, v_ref, w_ref, out_ref):
    halves = w_ref.shape[1]
    width = first_ref.shape[1]
    part = width // halves
    total = first_ref[...]
    for half in range(halves):
        side = w_ref[:, half].reshape(width, 3 * part)
        at = slice(half * part, (half + 1) * part)
        joined = jnp.concatenate([q_ref[:, at], k_ref[:, at], v_ref[:, at]], axis=1)
        total = total + dot_nt(joined, side)
    out_ref[...] = total.astype(BF16)


def input_gradient(first, q, k, v, w, step):
    rows, width = first.shape
    groups, halves, shard, _ = w.shape
    part = width // halves
    spec = pl.BlockSpec((step, width), lambda i: (i, 0))
    return call(
        inputs_kernel,
        grid=(rows // step,),
        in_specs=[
            spec, spec, spec, spec,
            pl.BlockSpec((groups, halves, shard, 3 * part), lambda i: (0, 0, 0, 0)),
        ],
        out_specs=spec,
        out_shape=jax.ShapeDtypeStruct((rows, width), BF16),
        compiler_params=params(),
        cost_estimate=cost(2 * rows * width * 3 * width, 14e6),
        name="input_gradient",
        near_in=(1, 2, 3),
    )(first, q, k, v, w)


def moves():
    def table(change):
        pairs = []
        for source in range(32):
            z, y, c, x = source // 8, source // 4 % 2, source // 2 % 2, source % 2
            z, y, c, x = change(z, y, c, x)
            pairs.append((source, ((z * 2 + y) * 2 + c) * 2 + x))
        return pairs

    along = [table(lambda z, y, c, x, k=k: (z ^ k, y, c, x)) for k in range(4)]
    beside = table(lambda z, y, c, x: (z, y ^ c, c, x ^ 1 ^ c))
    across = table(lambda z, y, c, x: (z, y ^ 1 ^ c, c, x ^ c))
    core = table(lambda z, y, c, x: (z, y, c ^ 1, x))
    return along, beside, across, core


def add(left, right):
    return (left.astype(F32) + right.astype(F32)).astype(BF16)


def send(value, table, begin, end, axes=BOTH):
    value = after(value, *begin) if begin else value
    value = lax.ppermute(value, axes, table)
    return after(value, *end) if end else value


class Gather:
    def __init__(self, piece):
        self.tables = moves()
        self.held = piece

    def line(self, begin=(), end=()):
        parts = [send(self.held, self.tables[0][k], begin, end) for k in (1, 2, 3)]
        self.held = join([self.held] + parts)

    def line_parts(self, begin):
        self.held = self.held, [send(self.held, self.tables[0][k], begin, ()) for k in (1, 2, 3)]

    def beside(self, begin=(), end=()):
        self.held = jnp.concatenate([self.held, send(self.held, self.tables[1], begin, end)], axis=0)

    def across(self, begin=(), end=()):
        self.held = jnp.concatenate([self.held, send(self.held, self.tables[2], begin, end)], axis=0)

    def core(self, begin=(), end=()):
        return [self.held, send(self.held, self.tables[3], begin, end)]


class Sum:
    def __init__(self, own, other):
        self.tables = moves()
        self.kept, self.sent = own, other

    def fold(self, table, begin, end):
        arrived = send(self.sent, table, begin, end)
        size = self.kept.shape[0] // 2
        kept = add(self.kept[:size], arrived[:size])
        self.kept, self.sent = kept, add(self.kept[size:], arrived[size:])

    def both(self):
        return [self.kept, self.sent]

    def core(self, begin=(), end=()):
        self.fold(self.tables[3], begin, end)

    def across(self, begin=(), end=()):
        self.fold(self.tables[2], begin, end)

    def beside(self, begin=(), end=()):
        arrived = send(self.sent, self.tables[1], begin, end)
        self.parts = [add(self.kept[k], arrived[k]) for k in range(4)]

    def line(self, begin=(), end=()):
        parts = [send(self.parts[k], self.tables[0][k], begin, end) for k in (1, 2, 3)]
        total = self.parts[0].astype(F32)
        for part in parts:
            total = total + part.astype(F32)
        return total


def local(
    inputs, w_query, w_key, w_value, b_query, b_key, b_value, w_out, b_out, norm_gain, norm_shift,
    w_up, b_up, w_down, b_down, final_gain, final_shift, piece_starts, grad_output,
):
    rows, width = inputs.shape
    halves = lax.axis_size("tp")
    replicas = lax.axis_size("fsdp")
    length = rows * halves
    block = min(512, length)
    blocks = rows // block
    shard = width // replicas
    part = width // halves
    units = w_up.shape[1]
    me = lax.axis_index("tp")
    pieces = replicas == 16 and halves == 2 and shard % 16 == 0
    place = lax.axis_index("fsdp")
    coords = jnp.stack([place // 4, place // 2 % 2, place % 2, me]).astype(jnp.int32)

    def layout(columns):
        return replicas, halves, shard, columns, pieces

    places = me * rows + jnp.arange(rows, dtype=jnp.int32)
    flags = jnp.any(piece_starts[0][:, None] == (places // PIECE * PIECE)[None, :], axis=0)
    angle = 0.5 * jnp.pi / length * places.astype(F32)
    cosines, sines = jnp.cos(angle), jnp.sin(angle)
    at = jnp.arange(block, dtype=jnp.int32)
    allowed = (at[None, None, :] <= at[None, :, None]) | (
        (at[None, None, :] // PIECE == at[None, :, None] // PIECE)
        & flags.reshape(blocks, block)[:, :, None]
    )
    c, s = cosines.reshape(blocks, block), sines.reshape(blocks, block)
    cm = jnp.where(allowed, c[:, :, None] * c[:, None, :] + s[:, :, None] * s[:, None, :], 0.0)
    cosines = jnp.broadcast_to(cosines[:, None], (rows, LANES))
    sines = jnp.broadcast_to(sines[:, None], (rows, LANES))

    each, edge = units // width, shard // halves
    if pieces:
        edges, turns = jnp.zeros((8, LANES), BF16), jnp.zeros((1, 8, LANES), BF16)
    else:
        edges, turns = selectors(width, part, shard, edge, each)
    thins = (
        b_query, b_key, b_value, b_up, b_out, norm_gain, norm_shift, b_down, final_gain, final_shift
    )
    if pieces:
        attention_shard = pack(w_query, w_key, w_value, w_out.T, thins)
    else:
        columns = []
        for thin in thins:
            thin = jnp.pad(thin, (0, -thin.shape[0] % shard))
            columns.append(thin.reshape(-1, shard).T)
        columns = jnp.concatenate(columns, axis=1)
        columns = jnp.pad(columns, ((0, 0), (0, LANES - columns.shape[1])))
        attention_shard = jnp.concatenate([w_query, w_key, w_value, w_out.T, columns], axis=1)
    down_shard = w_down.T

    def gather_all(piece):
        everything = lax.all_gather(piece, BOTH, axis=0, tiled=False)
        everything = everything.reshape(replicas, halves, shard, piece.shape[1])
        return jnp.moveaxis(everything, 1, 0).reshape(1, halves, width, piece.shape[1])

    if pieces:
        first_chunk, up_chunk, down_chunk = Gather(attention_shard), Gather(w_up), Gather(down_shard)
        first_chunk.line()
        four = first_chunk.held
        first_chunk.beside()
        up_chunk.line([four])
        first_chunk.across([cm, cosines, sines, coords])
        sixteen = first_chunk.held
        four = up_chunk.held
        w_attention = first_chunk.core([four])
        up_chunk.beside([sixteen, four], w_attention)
        eight = up_chunk.held
        down_chunk.line_parts([sixteen, four])
        w_attention = [after(w_attention[0], eight), w_attention[1]]
    else:
        w_attention, w_lift, w_drop = [
            [gather_all(piece)] for piece in (attention_shard, w_up, down_shard)
        ]


    columns = 4 * part + LANES
    sq, sk, v, slope_q, slope_k, states, total, w_attention = project(
        coords, inputs, w_attention, columns, edges, cosines, sines, block, shard, halves
    )
    bias_up, vectors = unpack(w_attention, turns, shard, each)
    queries, there = sq, []
    if pieces:
        up_chunk.across([], [sq])
        down_chunk.held = join(
            [down_chunk.held[0]] + [after(part, sq) for part in down_chunk.held[1]]
        )
        there = [up_chunk.held, down_chunk.held]
        queries = after(sq, *there)
    num, den = attend(queries, sk, v, cm, cosines, sines, states)
    towards = [(i, i + 1) for i in range(halves - 1)]
    incoming = send(total, towards, there, [num], "tp")
    if pieces:
        w_lift = up_chunk.core(there, [num])
        down_chunk.beside(there, [num])
        there = [down_chunk.held, incoming, w_lift[1]]
        num = after(num, *there)
    mixed, rden, normal, scale, low = mix(
        num, den, sq, incoming, cosines, sines, w_attention, inputs, vectors, 512
    )
    if pieces:
        down_chunk.across(there, [low])
        there = [down_chunk.held]
        low = after(low, *there)
    act, slope, w_lift = lift(
        coords, low, w_lift, bias_up, units, 768, 3 if pieces else 0
    )
    if pieces:
        w_drop = down_chunk.core(there, [act])
    output, branch, second, sums_second, w_drop = drop(
        coords, act, w_drop, normal, vectors, grad_output, units, 256
    )

    gdown = wide_gradient(coords, branch, act, layout(units), units, 512, "down_gradient")
    gl, gbias_up = bend(branch, w_drop, after(slope, *gdown), units, 768)
    if pieces:
        down_sum = Sum(*gdown)
        down_sum.core([], [gl])
        second = after(second, *down_sum.both())
    first, first_low, sums_first = lower(gl, w_lift, second, normal, scale, vectors, units, 256)
    wide = units + part + LANES
    *gup, gn, gd, later, later_total = unmix(
        coords, first_low, mixed, rden, sq, cosines, sines, w_attention,
        sums_first, sums_second, turns, gbias_up, layout(wide), block,
    )
    there = []
    if pieces:
        down_sum.across([], [gn])
        there = down_sum.both()
    gup = wide_gradient(
        coords, after(low, *there, *gup), gl, layout(wide), units, 512, "up_gradient", gup
    )
    towards = [(i + 1, i) for i in range(halves - 1)]
    later_in = send(later_total, towards, there, gup, "tp")
    there = [later_in, *gup]
    if pieces:
        down_sum.beside([], gup)
        there += down_sum.parts
        up_sum = Sum(*gup)
    gn = after(gn, *there)
    pairs = width // LANES
    partial = ()
    for half in range(halves):
        per = pairs // halves
        partial = unattend(
            sq, sk, v, gn, gd, cm, cosines, sines, states, incoming, later, slope_q, slope_k,
            later_in, half * per, per, partial,
        )
        if pieces and half == 0:
            up_sum.core(there, partial)
            partial = after(tuple(partial), *up_sum.both())
    query_low, key_low, value_low = partial
    if pieces:
        gdown = down_sum.line(there, [key_low])
        query_low = after(query_low, gdown)
    gqkv = weight_gradients(
        coords, inputs, query_low, key_low, value_low, edges, layout(3 * part + LANES)
    )
    if pieces:
        up_sum.across([], gqkv)
        rest_sum = Sum(*gqkv)
        rest_sum.core(up_sum.both())
        up_sum.beside([])
        rest_sum.across()
        gup = up_sum.line([], rest_sum.both())
        rest_sum.beside()
        rest = rest_sum.line()
    else:

        def scatter(grad):
            grad = jnp.moveaxis(grad.reshape(halves, replicas, shard, grad.shape[2]), 0, 1)
            grad = grad.reshape(replicas * halves, shard, grad.shape[3])
            return lax.psum_scatter(grad, BOTH, scatter_dimension=0, tiled=False).astype(F32)

        gdown, gup, rest = [scatter(grad[0]) for grad in (gdown, gup, gqkv)]
    grad_inputs = input_gradient(first, query_low, key_low, value_low, w_attention, 256)

    scaling = 1.0 / replicas
    gdown, gup, rest = gdown * scaling, gup * scaling, rest * scaling
    sums = gup[:, units + part :].T
    small = rest[:edge, 3 * part :].T
    return (
        output,
        grad_inputs,
        rest[:, :part],
        rest[:, part : 2 * part],
        rest[:, 2 * part : 3 * part],
        small[0],
        small[1],
        small[2],
        gup[:, units : units + part].T,
        sums[2],
        sums[0],
        sums[1],
        gup[:, :units],
        sums[6 : 6 + units // width].reshape(-1),
        gdown.T,
        sums[5],
        sums[3],
        sums[4],
    )


def solution(mesh):
    row = P(("fsdp", "tp"), None)
    split, turned = P("fsdp", "tp"), P("tp", "fsdp")
    thin, wide = P(("tp", "fsdp")), P("fsdp")
    return jax.shard_map(
        local,
        mesh=mesh,
        in_specs=(
            row, split, split, split, thin, thin, thin, turned, wide, wide, wide,
            split, thin, turned, wide, wide, wide, P("fsdp", None), row,
        ),
        out_specs=(
            row, row, split, split, split, thin, thin, thin, turned, wide, wide, wide,
            split, thin, turned, wide, wide, wide,
        ),
        check_vma=False,
    )
```

```python
import functools
import math

import jax
import jax.numpy as jnp
from jax import lax
from jax.experimental import pallas as pl
from jax.experimental.pallas import tpu as pltpu
from jax.sharding import PartitionSpec as P

HEAD_DIM = 64
PIECE = 256
LANES = 128
EPSILON = 1e-05
F32 = jnp.float32
BF16 = jnp.bfloat16
BOTH = ("fsdp", "tp")


def dot(left, right):
    return lax.dot_general(left, right, (((1,), (0,)), ((), ())), preferred_element_type=F32)


def dot_nt(left, right):
    return lax.dot_general(left, right, (((1,), (1,)), ((), ())), preferred_element_type=F32)


def dot_tn(left, right):
    return lax.dot_general(left, right, (((0,), (0,)), ((), ())), preferred_element_type=F32)


def flat(ref):
    value = ref[...]
    return value.reshape(value.shape[0] * value.shape[1] * value.shape[2], value.shape[3])


def lane_mask(rows, head, dtype=BF16):
    lane = lax.broadcasted_iota(jnp.int32, (rows, LANES), 1)
    return (lane // HEAD_DIM == head).astype(F32).astype(dtype)


def same_head(rows, columns):
    row = lax.broadcasted_iota(jnp.int32, (rows, columns), 0)
    lane = lax.broadcasted_iota(jnp.int32, (rows, columns), 1)
    return (row // HEAD_DIM) % 2 == (lane // HEAD_DIM) % 2


def same_rows(shape):
    row = lax.broadcasted_iota(jnp.int32, shape, 0)
    lane = lax.broadcasted_iota(jnp.int32, shape, 1)
    return (row // HEAD_DIM) % 2 == 0, lane


def compact(state, packet_ref, place, half, spread):
    left, right = state[:, :LANES], state[:, LANES:]
    first, lane = same_rows(left.shape)
    low = lane < HEAD_DIM
    narrow = jnp.where(first, left, pltpu.roll(left, HEAD_DIM, 1))
    narrow = jnp.where(half == 0, narrow, pltpu.roll(narrow, HEAD_DIM, 1))
    narrow = jnp.where(low == (half == 0), narrow, 0.0)
    column = jnp.where(first, right, pltpu.roll(right, HEAD_DIM, 1))
    column = jnp.where(low, column, 0.0)
    if not spread:
        column = jnp.broadcast_to(jnp.sum(column, axis=1, keepdims=True), column.shape)
    count = packet_ref.shape[0] - 1
    column = jnp.where(lane == half * count + place, column, 0.0)
    fresh = half == 0
    old = packet_ref[place].astype(F32)
    packet_ref[place] = jnp.where(fresh, narrow, old + narrow).astype(BF16)
    old = packet_ref[count].astype(F32)
    begun = jnp.logical_and(fresh, place == 0)
    packet_ref[count] = jnp.where(begun, column, old + column).astype(BF16)


def expand(packet_ref, place, half, spread):
    narrow = packet_ref[place].astype(F32)
    first, lane = same_rows(narrow.shape)
    low = lane < HEAD_DIM
    turned = pltpu.roll(narrow, HEAD_DIM, 1)
    here, there = (narrow, turned) if half == 0 else (turned, narrow)
    own = first == low
    left = jnp.where(own, jnp.where(first, here, there), 0.0)
    count = packet_ref.shape[0] - 1
    column = packet_ref[count].astype(F32)
    column = jnp.sum(jnp.where(lane == half * count + place, column, 0.0), axis=1, keepdims=True)
    if not spread:
        own = jnp.logical_and(own, lane % HEAD_DIM == 0)
    right = jnp.where(own, jnp.broadcast_to(column, own.shape), 0.0)
    return jnp.concatenate([left, right], axis=1)


def turned_features(values, cosines, sines):
    wide = values.astype(F32)
    return jnp.concatenate([(wide * cosines).astype(BF16), (wide * sines).astype(BF16)], axis=1)


def slot(coords, z, y, c, x):
    across = jnp.where(c == 0, y ^ coords[1], x ^ coords[3])
    beside = jnp.where(c == 0, x ^ coords[1 + 2], y ^ coords[1])
    return across * 8 + beside * 4 + (z ^ coords[0])


def emit(product, half, outs, coords):
    if len(outs) == 1:
        outs[0][half] = product[...]
        return
    core = coords[2]
    shard = outs[0].shape[1]
    for group in range(product.shape[0] // (2 * shard)):
        z, y = group // 2, group % 2
        for out, c in zip(outs, (core, 1 - core)):
            begin = pl.multiple_of((2 * group + c) * shard, 16)
            out[slot(coords, z, y, c, half)] = product[pl.ds(begin, shard), :]


class Weights:
    def __init__(self, coords_ref, sources, held, out, sems, out_sems, halves):
        self.coords = [coords_ref[place] for place in range(4)]
        self.sources, self.held, self.out = sources, held, out
        self.sems, self.out_sems, self.halves = sems, out_sems, halves

    def copies(self, place):
        half = self.halves[place]
        if len(self.sources) == 1:
            return [
                pltpu.make_async_copy(
                    self.sources[0].at[0, half], self.held.at[place], self.sems.at[place, 0]
                )
            ]
        copies = []
        shard = self.sources[0].shape[1]
        for side, ref in enumerate(self.sources):
            c = self.coords[2] if side == 0 else 1 - self.coords[2]
            for group in range(8):
                z, y = group // 2, group % 2
                begin = pl.multiple_of((2 * group + c) * shard, 16)
                copies.append(
                    pltpu.make_async_copy(
                        ref.at[slot(self.coords, z, y, c, half)],
                        self.held.at[place, pl.ds(begin, shard), :],
                        self.sems.at[place, side * 8 + group],
                    )
                )
        return copies

    def start(self, place):
        for copy in self.copies(place):
            copy.start()

    def ready(self, place):
        for copy in self.copies(place):
            copy.wait()
        self.leaving(place).start()

    def leaving(self, place):
        return pltpu.make_async_copy(
            self.held.at[place], self.out.at[0, place], self.out_sems.at[place]
        )

    def left(self, place):
        self.leaving(place).wait()

    @staticmethod
    def scratch(halves, width, columns):
        return [
            pltpu.VMEM((halves, width, columns), BF16),
            pltpu.SemaphoreType.DMA((halves, 16)),
            pltpu.SemaphoreType.DMA((halves,)),
        ]


def anywhere(count):
    return [pl.BlockSpec(memory_space=pl.ANY)] * count


def scalars():
    return pl.BlockSpec(memory_space=pltpu.SMEM)


def params(megabytes=32):
    return pltpu.CompilerParams(vmem_limit_bytes=megabytes * 1024 * 1024)


def call(kernel, *, out_shape, near_in=(), near_out=(), least=65536, **options):
    shapes = list(out_shape) if isinstance(out_shape, (list, tuple)) else [out_shape]

    def large(value):
        return math.prod(value.shape) * value.dtype.itemsize > least

    placed = [
        pltpu.HBM(shape.shape, shape.dtype) if large(shape) and at not in near_out else shape
        for at, shape in enumerate(shapes)
    ]
    function = pl.pallas_call(
        kernel, out_shape=placed if isinstance(out_shape, (list, tuple)) else placed[0], **options
    )

    def run(*operands):
        count = len(operands)
        near = {at % count for at in near_in}
        return function(
            *[
                pltpu.with_memory_space_constraint(value, pltpu.HBM)
                if large(value) and at not in near
                else value
                for at, value in enumerate(operands)
            ]
        )

    return run


def whole(shape):
    zeros = (0,) * len(shape)
    return pl.BlockSpec(shape, lambda *_: zeros)


def cost(flops, moved):
    return pl.CostEstimate(flops=int(flops), bytes_accessed=int(moved), transcendentals=0)


def after(value, *others):
    return lax.optimization_barrier((value, others))[0]


def pack_kernel(*refs):
    q_ref, k_ref, v_ref, out_ref = refs[:4]
    thins = refs[4:-1]
    first_ref = refs[-1]
    shard, part = q_ref.shape

    def chosen(columns, start):
        row = lax.broadcasted_iota(jnp.int32, (shard, columns), 0)
        column = lax.broadcasted_iota(jnp.int32, (shard, columns), 1)
        return (row + start == column).astype(F32).astype(BF16)

    for place, ref in enumerate((q_ref, k_ref, v_ref, out_ref)):
        first_ref[:, place * part : (place + 1) * part] = ref[...]
    columns = jnp.zeros((shard, LANES), F32)
    lane = 0
    for ref in thins:
        size = ref.shape[1]
        for start in range(0, size, shard):
            row = lax.broadcasted_iota(jnp.int32, (LANES, size), 0)
            spread = jnp.where(row == lane, ref[...].astype(F32), 0.0).astype(BF16)
            columns = columns + dot_nt(chosen(size, start), spread)
            lane += 1
    first_ref[:, 4 * part :] = columns.astype(BF16)


def pack(q, k, v, out, thins):
    shard, part = q.shape
    return call(
        pack_kernel,
        out_shape=jax.ShapeDtypeStruct((shard, 4 * part + LANES), BF16),
        compiler_params=params(),
        cost_estimate=cost(1e8, 1e6),
        name="pack",
        least=0,
    )(q, k, v, out, *[thin.reshape(1, -1) for thin in thins])


def deal(columns, shard, size, turns):
    count = columns.shape[0] // shard
    runs = []
    for place in range(count):
        piece = columns[place * shard : place * shard + size]
        for turn in range(turns):
            runs.append(pltpu.roll(piece, LANES - turn, 1) if turn else piece)
    return jnp.concatenate(runs, axis=0)


def selectors_kernel(edge_ref, turn_ref, *, shard, edge, each):
    width, part = edge_ref.shape
    row = lax.broadcasted_iota(jnp.int32, (width, part), 0)
    column = lax.broadcasted_iota(jnp.int32, (width, part), 1)
    chosen = (row % shard < edge) & (row // shard * edge + row % shard == column)
    edge_ref[...] = chosen.astype(F32).astype(BF16)
    row = lax.broadcasted_iota(jnp.int32, (width, LANES), 0)
    source = row // shard * (each * shard) + row % shard
    lane = lax.broadcasted_iota(jnp.int32, (width, LANES), 1)
    for turn in range(each):
        for begin in range(0, each * width, LANES):
            chosen = source + (turn * shard - begin) == lane
            turn_ref[turn, :, begin : begin + LANES] = chosen.astype(F32).astype(BF16)


def selectors(width, part, shard, edge, each):
    return call(
        functools.partial(selectors_kernel, shard=shard, edge=edge, each=each),
        out_shape=[
            jax.ShapeDtypeStruct((width, part), BF16),
            jax.ShapeDtypeStruct((each, width, each * width), BF16),
        ],
        compiler_params=params(),
        cost_estimate=cost(1e8, 1e6),
        name="selectors",
    )()


def unpack_kernel(thin_ref, turn_ref, up_ref, vec_ref, *, shard, each):
    halves = thin_ref.shape[1]
    for half in range(halves):
        thin = thin_ref[0, half]
        if shard % 16 == 0:
            turned = deal(thin.astype(F32), shard, shard, each).T
            up_ref[half] = turned[0:8]
            continue
        rows = jnp.zeros((8, turn_ref.shape[2]), F32)
        for turn in range(each):
            picked = dot_tn(thin, turn_ref[turn])
            rows = rows + picked[3 + turn : 4 + turn]
        up_ref[half] = rows
    turned = thin_ref[0, 0].astype(F32).T
    vec_ref[...] = turned[3 + each : 11 + each]


def unpack(w, turns, shard, each):
    _, halves, width, columns = w.shape
    return call(
        functools.partial(unpack_kernel, shard=shard, each=each),
        grid=(1,),
        in_specs=[
            pl.BlockSpec((1, halves, width, LANES), lambda i: (0, 0, 0, columns // LANES - 1)),
            whole(turns.shape),
        ],
        out_specs=[whole((halves, 8, each * width)), whole((8, width))],
        out_shape=[
            jax.ShapeDtypeStruct((halves, 8, each * width), F32),
            jax.ShapeDtypeStruct((8, width), F32),
        ],
        compiler_params=params(),
        cost_estimate=cost(1e8, 1e6),
        name="unpack",
    )(w, turns)


def join_kernel(*refs):
    for place, ref in enumerate(refs[:-1]):
        refs[-1][place] = ref[...]


def join(parts):
    return call(
        join_kernel,
        out_shape=jax.ShapeDtypeStruct((len(parts),) + parts[0].shape, parts[0].dtype),
        compiler_params=params(),
        cost_estimate=cost(0, 1e6),
        name="join",
        least=0,
    )(*parts)


def project_kernel(
    coords_ref, *refs, block, step, shard, halves
):
    sources, refs = refs[: len(refs) - 14], refs[len(refs) - 14 :]
    x_ref, edge_ref, cos_ref, sin_ref, sq_ref, sk_ref, v_ref, gq_ref, gk_ref, st_ref, tot_ref = refs[:11]
    sources, out_ref = sources[:-1], sources[-1]
    held_ref, sems, out_sems = refs[11:]
    rows = x_ref.shape[0]
    part = sq_ref.shape[1]
    now = pl.program_id(0)
    weights = Weights(coords_ref, sources, held_ref, out_ref, sems, out_sems, range(halves))

    @pl.when(now == 0)
    def _():
        for half in range(halves):
            weights.start(half)

    for half in range(halves):

        @pl.when(now == half)
        def _():
            weights.ready(half)

    columns = held_ref.shape[2]
    thin = held_ref[now, :, columns - LANES :]
    if shard % 16 == 0:
        biases = deal(thin.astype(F32), shard, shard * part // x_ref.shape[1], 1).T
    else:
        biases = dot_tn(thin, edge_ref[...])

    def body(index, carry):
        here = pl.ds(index * step, step)
        sums = dot(x_ref[here, :], held_ref[now, :, : 3 * part])
        for place, (feature_ref, slope_ref) in enumerate(((sq_ref, gq_ref), (sk_ref, gk_ref))):
            value = sums[:, place * part : (place + 1) * part] + biases[place : place + 1]
            positive = jnp.maximum(value, 0.0) + jnp.log1p(jnp.exp(-jnp.abs(value)))
            feature_ref[here, :] = positive.astype(BF16)
            slope_ref[here, :] = jax.nn.sigmoid(value).astype(BF16)
        v_ref[here, :] = (sums[:, 2 * part :] + biases[2:3]).astype(BF16)
        return carry

    lax.fori_loop(0, rows // step, body, 0)
    keep = same_head(2 * LANES, 2 * LANES)
    ones = jnp.ones((block, LANES), BF16)
    for pair in range(part // LANES):
        lanes = slice(pair * LANES, (pair + 1) * LANES)
        total = jnp.zeros((2 * LANES, 2 * LANES), F32)
        for place in range(rows // block):
            here = slice(place * block, (place + 1) * block)
            features = turned_features(sk_ref[here, lanes], cos_ref[here, :], sin_ref[here, :])
            state = dot_tn(features, jnp.concatenate([v_ref[here, lanes], ones], axis=1))
            state = jnp.where(keep, state, 0.0)
            st_ref[place, pair] = state.astype(BF16)
            total = total + state
        compact(total, tot_ref, pair, pl.program_id(0), True)

    @pl.when(now == halves - 1)
    def _():
        for half in range(halves):
            weights.left(half)


def project(coords, x, sources, columns, edges, cosines, sines, block, shard, halves):
    rows, width = x.shape
    part = width // halves
    pairs = width // LANES
    half = pairs // halves
    blocks = rows // block
    row_spec = pl.BlockSpec((rows, part), lambda t: (0, t))
    full = jax.ShapeDtypeStruct((rows, width), BF16)

    def kernel(coords_ref, *refs):
        count = len(sources)
        others, outs, scratch = refs[count : count + 4], refs[count + 4 : -3], refs[-3:]
        project_kernel(
            coords_ref, *refs[:count], outs[-1], *others, *outs[:-1], *scratch,
            block=block, step=rows, shard=shard, halves=halves,
        )

    return call(
        kernel,
        grid=(halves,),
        in_specs=[scalars()]
        + anywhere(len(sources))
        + [
            whole((rows, width)), whole(edges.shape), whole((rows, LANES)), whole((rows, LANES)),
        ],
        out_specs=[
            row_spec, row_spec, row_spec, row_spec, row_spec,
            pl.BlockSpec((blocks, half, 2 * LANES, 2 * LANES), lambda t: (0, t, 0, 0)),
            whole((half + 1, 2 * LANES, LANES)),
        ]
        + anywhere(1),
        out_shape=[
            full, full, full, full, full,
            jax.ShapeDtypeStruct((blocks, pairs, 2 * LANES, 2 * LANES), BF16),
            jax.ShapeDtypeStruct((half + 1, 2 * LANES, LANES), BF16),
            jax.ShapeDtypeStruct((1, halves, width, columns), BF16),
        ],
        scratch_shapes=Weights.scratch(halves, width, columns),
        compiler_params=params(),
        cost_estimate=cost(2 * rows * width * 3 * width, 16e6),
        name="project",
    )(coords, *sources, x, edges, cosines, sines)


def attend_kernel(sq_ref, sk_ref, v_ref, cm_ref, cos_ref, sin_ref, st_ref, num_ref, den_ref):
    blocks, block, _ = cm_ref.shape
    piece = min(PIECE, block)
    masks = [lane_mask(block, head) for head in range(2)]
    for place in range(blocks):
        start = place * block
        keys = sk_ref[start : start + block, :]
        values = v_ref[start : start + block, :]
        sides = [jnp.concatenate([values * mask, mask], axis=1) for mask in masks]
        for low in range(0, block, piece):
            here = slice(start + low, start + low + piece)
            span = low + piece
            queries = sq_ref[here, :]
            sums = None
            for mask, side in zip(masks, sides):
                scores = dot_nt(queries * mask[:piece], keys[:span])
                weights = (scores * cm_ref[place, low : low + piece, :span]).astype(BF16)
                term = dot(weights, side[:span])
                sums = term if sums is None else sums + term
            for earlier in range(place):
                sums = sums + dot(
                    turned_features(queries, cos_ref[here, :], sin_ref[here, :]), st_ref[earlier, 0]
                )
            num_ref[here, :] = sums[:, :LANES]
            den_ref[here, :] = sums[:, LANES:]


def attend(sq, sk, v, cm, cosines, sines, states):
    rows, width = sq.shape
    pairs = width // LANES
    blocks = cm.shape[0]
    spec = pl.BlockSpec((rows, LANES), lambda p: (0, p))
    full = jax.ShapeDtypeStruct((rows, width), F32)
    return call(
        attend_kernel,
        grid=(pairs,),
        in_specs=[
            spec, spec, spec,
            whole(cm.shape), whole((rows, LANES)), whole((rows, LANES)),
            pl.BlockSpec((blocks, 1, 2 * LANES, 2 * LANES), lambda p: (0, p, 0, 0)),
        ],
        out_specs=[spec, spec],
        out_shape=[full, full],
        compiler_params=params(),
        cost_estimate=cost(8e9, 14e6),
        name="attend",
        near_out=(0, 1),
    )(sq, sk, v, cm, cosines, sines, states)


def norm_rows(values):
    average = jnp.mean(values, axis=1, keepdims=True)
    centred = values - average
    scale = lax.rsqrt(jnp.mean(centred * centred, axis=1, keepdims=True) + EPSILON)
    return centred * scale, scale


def mix_kernel(
    num_ref, den_ref, sq_ref, in_ref, cos_ref, sin_ref, w_ref, x_ref, vec_ref,
    mixed_ref, rden_ref, normal_ref, scale_ref, low_ref, wide_ref,
):
    pairs = wide_ref.shape[0]
    halves = w_ref.shape[1]
    rows, width = x_ref.shape
    part = width // halves

    @pl.when(pl.program_id(0) == 0)
    def _():
        for pair in range(pairs):
            place, half = pair % (pairs // halves), pair // (pairs // halves)
            wide_ref[pair] = expand(in_ref, place, half, True).astype(BF16)

    for pair in range(pairs):
        lanes = slice(pair * LANES, (pair + 1) * LANES)
        sums = dot(turned_features(sq_ref[:, lanes], cos_ref[...], sin_ref[...]), wide_ref[pair])
        inverse = 1.0 / jnp.maximum(den_ref[:, lanes] + sums[:, LANES:], 1.0)
        rden_ref[:, lanes] = inverse
        mixed_ref[:, lanes] = ((num_ref[:, lanes] + sums[:, :LANES]) * inverse).astype(BF16)
    total = x_ref[...].astype(F32) + vec_ref[0:1, :]
    for half in range(halves):
        side = w_ref[:, half]
        side = side.reshape(width, part)
        total = total + dot_nt(mixed_ref[:, half * part : (half + 1) * part], side)
    normal, scale = norm_rows(total)
    normal_ref[...] = normal
    scale_ref[...] = jnp.broadcast_to(scale, scale_ref.shape)
    low_ref[...] = (normal * vec_ref[1:2, :] + vec_ref[2:3, :]).astype(BF16)


def mix(num, den, sq, incoming, cosines, sines, w, x, vectors, step):
    rows, width = x.shape
    groups, halves, shard, _ = w.shape
    part = width // halves
    pairs = width // LANES
    wide = pl.BlockSpec((step, width), lambda i: (i, 0))
    thin = pl.BlockSpec((step, LANES), lambda i: (i, 0))
    return call(
        mix_kernel,
        grid=(rows // step,),
        in_specs=[
            wide, wide, wide, whole(incoming.shape), thin, thin,
            pl.BlockSpec((groups, halves, shard, part), lambda i: (0, 0, 0, 3)),
            wide, whole(vectors.shape),
        ],
        out_specs=[wide, wide, wide, thin, wide],
        out_shape=[
            jax.ShapeDtypeStruct((rows, width), BF16),
            jax.ShapeDtypeStruct((rows, width), F32),
            jax.ShapeDtypeStruct((rows, width), F32),
            jax.ShapeDtypeStruct((rows, LANES), F32),
            jax.ShapeDtypeStruct((rows, width), BF16),
        ],
        scratch_shapes=[pltpu.VMEM((pairs, 2 * LANES, 2 * LANES), BF16)],
        compiler_params=params(),
        cost_estimate=cost(2 * rows * width * width * 2, 20e6),
        name="mix",
        near_in=(0, 1),
        near_out=(2, 4),
    )(num, den, sq, incoming, cosines, sines, w, x, vectors)


def norm_back(upstream, normal, scale, gain):
    scaled = upstream * gain
    inner = (
        scaled
        - jnp.mean(scaled, axis=1, keepdims=True)
        - normal * jnp.mean(scaled * normal, axis=1, keepdims=True)
    )
    return inner * scale


def lift_kernel(coords_ref, *refs, step, row, halves):
    sources, refs = refs[:-8], refs[-8:]
    low_ref, bias_ref, act_ref, slope_ref, out_ref, held_ref, sems, out_sems = refs
    tile = act_ref.shape[1]
    now = pl.program_id(0)
    tiles = pl.num_programs(0) // halves
    weights = Weights(coords_ref, sources, held_ref, out_ref, sems, out_sems, range(halves))

    @pl.when(now == 0)
    def _():
        for half in range(halves):
            weights.start(half)

    for half in range(halves):

        @pl.when(now == half * tiles)
        def _():
            weights.ready(half)

    begin = pl.multiple_of(now % tiles * tile, tile)
    up = held_ref[now // tiles, :, pl.ds(begin, tile)]

    def body(place, carry):
        here = pl.ds(place * step, step)
        lifted = dot(low_ref[here, :], up) + bias_ref[0, row : row + 1, :]
        share = 0.5 + 0.5 * lax.erf(lifted * math.sqrt(0.5))
        bell = jnp.exp(-0.5 * lifted * lifted) * (1.0 / math.sqrt(2.0 * math.pi))
        act_ref[here, :] = (lifted * share).astype(BF16)
        slope_ref[here, :] = (share + lifted * bell).astype(BF16)
        return carry

    lax.fori_loop(0, low_ref.shape[0] // step, body, 0, unroll=True)

    @pl.when(now == pl.num_programs(0) - 1)
    def _():
        for half in range(halves):
            weights.left(half)


def lift(coords, low, sources, bias, units, tile, row):
    rows, width = low.shape
    halves = bias.shape[0]
    tiles = units // tile
    unit_spec = pl.BlockSpec((rows, tile), lambda i: (0, i))
    shape = jax.ShapeDtypeStruct((rows, halves * units), BF16)
    return call(
        functools.partial(lift_kernel, step=256, row=row, halves=halves),
        grid=(halves * tiles,),
        in_specs=[scalars()]
        + anywhere(len(sources))
        + [whole((rows, width)), pl.BlockSpec((1, 8, tile), lambda i: (i // tiles, 0, i % tiles))],
        out_specs=[unit_spec, unit_spec] + anywhere(1),
        out_shape=[shape, shape, jax.ShapeDtypeStruct((1, halves, width, units), BF16)],
        scratch_shapes=Weights.scratch(halves, width, units),
        compiler_params=params(),
        cost_estimate=cost(2 * rows * width * halves * units, 20e6),
        name="lift",
        near_in=(-2,),
        near_out=(0, 1),
    )(coords, *sources, low, bias)


def in_turn(product, finish, total_ref):
    now = pl.program_id(0)
    last = pl.num_programs(0) - 1

    @pl.when(now == 0)
    def _():
        total_ref[0] = product(True)

    @pl.when((now > 0) & (now < last))
    def _():
        finish(total_ref[(now - 1) % 2])
        total_ref[now % 2] = product()

    @pl.when(now == last)
    def _():
        finish(total_ref[(now - 1) % 2])


def drop_kernel(coords_ref, *refs, halves):
    sources, act_ref, refs = refs[:-13], refs[-13], refs[-12:]
    normal_ref, vec_ref, grad_ref, out_ref, branch_ref, second_ref, sum_ref = refs[:7]
    whole_ref, held_ref, sems, out_sems, total_ref = refs[7:]
    weights = Weights(coords_ref, sources, held_ref, whole_ref, sems, out_sems, range(halves))
    units = held_ref.shape[2]

    @pl.when(pl.program_id(0) == 0)
    def _():
        sum_ref[...] = jnp.zeros_like(sum_ref)
        for half in range(halves):
            weights.start(half)

    def product(fresh=False):
        total = None
        for half in range(halves):
            if fresh:
                weights.ready(half)
            term = dot_nt(act_ref[:, half * units : (half + 1) * units], held_ref[half])
            total = term if total is None else total + term
        return total

    def finish(total):
        total = total + normal_ref[...] * vec_ref[1:2, :] + vec_ref[2:3, :] + vec_ref[3:4, :]
        normal, scale = norm_rows(total)
        gain = vec_ref[4:5, :]
        out_ref[...] = (normal * gain + vec_ref[5:6, :]).astype(BF16)
        upstream = grad_ref[...].astype(F32)
        second = norm_back(upstream, normal, scale, gain)
        second_ref[...] = second
        branch_ref[...] = second.astype(BF16)
        sum_ref[0:1, :] += jnp.sum(upstream * normal, axis=0, keepdims=True)
        sum_ref[1:2, :] += jnp.sum(upstream, axis=0, keepdims=True)
        sum_ref[2:3, :] += jnp.sum(second, axis=0, keepdims=True)

    in_turn(product, finish, total_ref)

    @pl.when(pl.program_id(0) == pl.num_programs(0) - 1)
    def _():
        for half in range(halves):
            weights.left(half)


def drop(coords, act, sources, normal, vectors, grad, units, step):
    rows, width = normal.shape
    halves = act.shape[1] // units
    steps = rows // step
    wide = pl.BlockSpec((step, width), lambda i: (jnp.maximum(i - 1, 0), 0))
    return call(
        functools.partial(drop_kernel, halves=halves),
        grid=(steps + 1,),
        in_specs=[scalars()]
        + anywhere(len(sources))
        + [
            pl.BlockSpec((step, halves * units), lambda i: (jnp.minimum(i, steps - 1), 0)),
            wide, whole(vectors.shape), wide,
        ],
        out_specs=[wide, wide, wide, whole((8, width))] + anywhere(1),
        out_shape=[
            jax.ShapeDtypeStruct((rows, width), BF16),
            jax.ShapeDtypeStruct((rows, width), BF16),
            jax.ShapeDtypeStruct((rows, width), F32),
            jax.ShapeDtypeStruct((8, width), F32),
            jax.ShapeDtypeStruct((1, halves, width, units), BF16),
        ],
        scratch_shapes=Weights.scratch(halves, width, units) + [pltpu.VMEM((2, step, width), F32)],
        compiler_params=params(),
        cost_estimate=cost(2 * rows * width * halves * units, 20e6),
        name="drop",
        near_in=(-4, -3),
        near_out=(1, 2),
    )(coords, *sources, act, normal, vectors, grad)


def piece_outputs(layout, tile, index_map):
    replicas, halves, shard, columns, pieces = layout[:5]
    if pieces:
        count = replicas * halves // 2
        spec = pl.BlockSpec((count, shard, tile), lambda *at: (0, 0, index_map(*at)))
        shape = jax.ShapeDtypeStruct((count, shard, columns), BF16)
        return [spec, spec], [shape, shape]
    width = replicas * shard
    spec = pl.BlockSpec((halves, width, tile), lambda *at: (0, 0, index_map(*at)))
    return [spec], [jax.ShapeDtypeStruct((halves, width, columns), BF16)]


def wide_gradient_kernel(coords_ref, left_ref, *refs, halves, partial):
    rights, product_ref = refs[:halves], refs[-1]
    outs = refs[(len(refs) - 1 + halves) // 2 : -1] if partial else refs[halves:-1]
    coords = [coords_ref[place] for place in range(4)]
    for half, right_ref in enumerate(rights):
        product_ref[...] = dot_tn(left_ref[...], right_ref[...]).astype(BF16)
        emit(product_ref, half, outs, coords)


def wide_gradient(coords, left, right, layout, units, tile, name, partial=()):
    rows, width = left.shape
    halves = layout[1]
    tiles = units // tile
    out_specs, out_shapes = piece_outputs(layout, tile, lambda j: j)
    return call(
        functools.partial(wide_gradient_kernel, halves=halves, partial=bool(partial)),
        grid=(tiles,),
        in_specs=[scalars(), whole((rows, width))]
        + [
            pl.BlockSpec((rows, tile), lambda j, half=half: (0, half * tiles + j))
            for half in range(halves)
        ]
        + anywhere(len(partial)),
        out_specs=out_specs,
        out_shape=out_shapes,
        input_output_aliases={2 + halves + at: at for at in range(len(partial))},
        scratch_shapes=[pltpu.VMEM((width, tile), BF16)],
        compiler_params=params(),
        cost_estimate=cost(2 * rows * width * halves * units, 18e6),
        name=name,
        near_in=(1, 2, 3),
    )(coords, left, *([right] * halves), *partial)


def bend_kernel(branch_ref, down_ref, slope_ref, gl_ref, gbias_ref, *, step):
    down = down_ref[0, 0]
    gbias_ref[...] = jnp.zeros_like(gbias_ref)

    def body(place, carry):
        here = pl.ds(place * step, step)
        slope = dot(branch_ref[here, :], down) * slope_ref[here, :].astype(F32)
        gbias_ref[0:1, :] += jnp.sum(slope, axis=0, keepdims=True)
        gl_ref[here, :] = slope.astype(BF16)
        return carry

    lax.fori_loop(0, branch_ref.shape[0] // step, body, 0, unroll=True)


def bend(branch, w, slope, units, tile):
    rows, width = branch.shape
    halves = w.shape[1]
    tiles = units // tile
    unit_spec = pl.BlockSpec((rows, tile), lambda i: (0, i))
    return call(
        functools.partial(bend_kernel, step=256),
        grid=(halves * tiles,),
        in_specs=[
            whole((rows, width)),
            pl.BlockSpec((1, 1, width, tile), lambda i: (0, i // tiles, 0, i % tiles)),
            unit_spec,
        ],
        out_specs=[unit_spec, pl.BlockSpec((8, tile), lambda i: (0, i))],
        out_shape=[
            jax.ShapeDtypeStruct(slope.shape, BF16),
            jax.ShapeDtypeStruct((8, halves * units), F32),
        ],
        compiler_params=params(),
        cost_estimate=cost(2 * rows * width * halves * units, 20e6),
        name="bend",
        near_in=(0, 2),
        near_out=(0,),
    )(branch, w, slope)


def lower_kernel(
    gl_ref, up_ref, second_ref, normal_ref, scale_ref, vec_ref, first_ref, firstlow_ref, sum_ref,
    total_ref,
):
    halves, units = up_ref.shape[1], up_ref.shape[3]

    @pl.when(pl.program_id(0) == 0)
    def _():
        sum_ref[...] = jnp.zeros_like(sum_ref)

    def product(fresh=False):
        total = None
        for half in range(halves):
            term = dot_nt(gl_ref[:, half * units : (half + 1) * units], up_ref[0, half])
            total = term if total is None else total + term
        return total

    def finish(total):
        upstream = second_ref[...] + total
        normal = normal_ref[...]
        first = norm_back(upstream, normal, scale_ref[:, 0:1], vec_ref[1:2, :])
        first_ref[...] = first
        firstlow_ref[...] = first.astype(BF16)
        sum_ref[0:1, :] += jnp.sum(upstream * normal, axis=0, keepdims=True)
        sum_ref[1:2, :] += jnp.sum(upstream, axis=0, keepdims=True)
        sum_ref[2:3, :] += jnp.sum(first, axis=0, keepdims=True)

    in_turn(product, finish, total_ref)


def lower(gl, w, second, normal, scale, vectors, units, step):
    rows, width = second.shape
    steps = rows // step
    wide = pl.BlockSpec((step, width), lambda i: (jnp.maximum(i - 1, 0), 0))
    return call(
        lower_kernel,
        grid=(steps + 1,),
        in_specs=[
            pl.BlockSpec((step, gl.shape[1]), lambda i: (jnp.minimum(i, steps - 1), 0)),
            whole(w.shape), wide, wide,
            pl.BlockSpec((step, LANES), lambda i: (jnp.maximum(i - 1, 0), 0)),
            whole(vectors.shape),
        ],
        out_specs=[wide, wide, whole((8, width))],
        out_shape=[
            jax.ShapeDtypeStruct((rows, width), F32),
            jax.ShapeDtypeStruct((rows, width), BF16),
            jax.ShapeDtypeStruct((8, width), F32),
        ],
        scratch_shapes=[pltpu.VMEM((2, step, width), F32)],
        compiler_params=params(),
        cost_estimate=cost(2 * rows * width * gl.shape[1], 20e6),
        name="lower",
        near_in=(0, 2, 3),
        near_out=(1,),
    )(gl, w, second, normal, scale, vectors)


def unmix_kernel(
    coords_ref, first_ref, mixed_ref, rden_ref, sq_ref, cos_ref, sin_ref, w_ref,
    sum1_ref, sum2_ref, turn_ref, *refs, block, step, shard
):
    bias = jnp.broadcast_to(refs[0][0:1, :], refs[0].shape)
    refs = refs[1:]
    outs = refs[:-5]
    gn_ref, gd_ref, st_ref, tot_ref, product_ref = refs[-5:]
    coords = [coords_ref[place] for place in range(4)]
    rows, width = first_ref.shape
    part = mixed_ref.shape[1]
    side = flat(w_ref)
    group_row = lax.broadcasted_iota(jnp.int32, (LANES, LANES), 0)
    group_lane = lax.broadcasted_iota(jnp.int32, (LANES, LANES), 1)
    group = (group_row // HEAD_DIM == group_lane // HEAD_DIM).astype(F32).astype(BF16)
    group = jnp.concatenate([group, group], axis=0)

    lane = lax.broadcasted_iota(jnp.int32, (step, LANES), 1) % HEAD_DIM

    def body(place, carry):
        here = pl.ds(place * step, step)
        grad = dot(first_ref[here, :], side)
        for pair in range(part // LANES):
            lanes = slice(pair * LANES, (pair + 1) * LANES)
            inverse = rden_ref[here, lanes]
            scaled = grad[:, lanes] * inverse
            product = scaled * mixed_ref[here, lanes].astype(F32)
            high = product.astype(BF16)
            rest = (product - high.astype(F32)).astype(BF16)
            inner = dot(jnp.concatenate([high, rest], axis=1), group)
            slope = jnp.where(inverse < 1.0, -inner, 0.0)
            high = slope.astype(BF16).astype(F32)
            gn_ref[here, lanes] = scaled.astype(BF16)
            gd_ref[here, lanes] = jnp.where(
                lane == 0, high, jnp.where(lane == 1, slope - high, 0.0)
            ).astype(BF16)
        return carry

    lax.fori_loop(0, rows // step, body, 0)
    product_ref[:, :part] = dot_tn(first_ref[...], mixed_ref[...]).astype(BF16)
    row = lax.broadcasted_iota(jnp.int32, (8, width), 0)
    packed = jnp.where(row < 3, sum1_ref[...], pltpu.roll(sum2_ref[...], 3, 0))
    packed = jnp.where(row < 6, packed, 0.0)
    columns = jnp.concatenate([packed, jnp.zeros((LANES - 8, width), F32)], axis=0).T
    units = bias.shape[1]
    each = units // width
    if shard % 16 == 0:
        at = lax.broadcasted_iota(jnp.int32, (8, units), 0)
        both = jnp.where(at >= 6, bias, 0.0)
        turned = jnp.concatenate([both, jnp.zeros((LANES - 8, units), F32)], axis=0).T
        lane_at = lax.broadcasted_iota(jnp.int32, (shard, LANES), 1)
        for place in range(width // shard):
            piece = columns[place * shard : (place + 1) * shard]
            for turn in range(each):
                begin = (place * each + turn) * shard
                piece = jnp.where(lane_at == 6 + turn, turned[begin : begin + shard], piece)
            product_ref[place * shard : (place + 1) * shard, part:] = piece.astype(BF16)
    else:
        side_row = lax.broadcasted_iota(jnp.int32, (8, LANES), 0)
        turned = dot_tn(bias.astype(BF16), (side_row == 0).astype(F32).astype(BF16)).astype(BF16)
        lane_at = lax.broadcasted_iota(jnp.int32, (width, LANES), 1)
        for turn in range(each):
            columns = jnp.where(lane_at == 6 + turn, dot(turn_ref[turn], turned), columns)
        product_ref[:, part:] = columns.astype(BF16)
    emit(product_ref, pl.program_id(0), outs, coords)
    keep = same_head(2 * LANES, 2 * LANES)
    for pair in range(part // LANES):
        lanes = slice(pair * LANES, (pair + 1) * LANES)
        total = jnp.zeros((2 * LANES, 2 * LANES), F32)
        for place in range(rows // block):
            here = slice(place * block, (place + 1) * block)
            features = turned_features(sq_ref[here, lanes], cos_ref[here, :], sin_ref[here, :])
            state = dot_tn(
                features, jnp.concatenate([gn_ref[here, lanes], gd_ref[here, lanes]], axis=1)
            )
            state = jnp.where(keep, state, 0.0)
            st_ref[place, pair] = state.astype(BF16)
            total = total + state
        compact(total, tot_ref, pair, pl.program_id(0), False)


def unmix(
    coords, first, mixed, rden, sq, cosines, sines, w, sums1, sums2, turns, gbias, layout, block
):
    rows, width = first.shape
    groups, halves, shard, _ = w.shape
    part = width // halves
    pairs = width // LANES
    half = pairs // halves
    blocks = rows // block
    row_spec = pl.BlockSpec((rows, part), lambda t: (0, t))
    tile = part + LANES
    out_specs, out_shapes = piece_outputs(layout, tile, lambda t: layout[3] // tile - 1)
    units = gbias.shape[1] // halves
    full = jax.ShapeDtypeStruct((rows, width), BF16)
    return call(
        functools.partial(
            unmix_kernel, block=block, step=512, shard=layout[2]
        ),
        grid=(halves,),
        in_specs=[
            scalars(), whole((rows, width)), row_spec, row_spec, row_spec,
            whole((rows, LANES)), whole((rows, LANES)),
            pl.BlockSpec((groups, 1, shard, part), lambda t: (0, t, 0, 3)),
            whole((8, width)), whole((8, width)), whole(turns.shape),
        ]
        + [pl.BlockSpec((8, units), lambda t: (0, t))],
        out_specs=out_specs
        + [
            row_spec, row_spec,
            pl.BlockSpec((blocks, half, 2 * LANES, 2 * LANES), lambda t: (0, t, 0, 0)),
            whole((half + 1, 2 * LANES, LANES)),
        ],
        out_shape=out_shapes
        + [
            full, full,
            jax.ShapeDtypeStruct((blocks, pairs, 2 * LANES, 2 * LANES), BF16),
            jax.ShapeDtypeStruct((half + 1, 2 * LANES, LANES), BF16),
        ],
        scratch_shapes=[pltpu.VMEM((width, tile), BF16)],
        compiler_params=params(),
        cost_estimate=cost(4 * rows * width * width, 16e6),
        name="unmix",
        near_in=(1,),
        near_out=(len(out_shapes), len(out_shapes) + 1),
    )(coords, first, mixed, rden, sq, cosines, sines, w, sums1, sums2, turns, gbias)


def unattend_kernel(
    sq_ref, sk_ref, v_ref, gn_ref, gd_ref, cm_ref, cos_ref, sin_ref, st_ref, in_ref, lt_ref, gq_ref,
    gk_ref, later_ref, *refs, half
):
    query_ref, dk_ref, dv_ref = refs[-3:]
    blocks, block, _ = cm_ref.shape
    piece = min(PIECE, block)
    masks = [lane_mask(block, head) for head in range(2)]
    ones = jnp.ones((block, LANES), BF16)
    incoming = expand(in_ref, pl.program_id(0), half, True)
    outgoing = expand(later_ref, pl.program_id(0), half, False)
    for place in range(blocks):
        start = place * block
        all_here = slice(start, start + block)
        keys, values = sk_ref[all_here, :], v_ref[all_here, :]
        sides = jnp.concatenate([values, ones], axis=1)
        key_sides = [keys * mask for mask in masks]
        state = incoming
        for earlier in range(place):
            state = state + st_ref[earlier, 0].astype(F32)
        state = state.astype(BF16)
        grad_keys = [None] * (block // piece)
        grad_values = [None] * (block // piece)
        for low in range(0, block, piece):
            here = slice(start + low, start + low + piece)
            span = low + piece
            queries, grads, slopes = sq_ref[here, :], gn_ref[here, :], gd_ref[here, :]
            grad_queries = None
            for head in range(2):
                mask = masks[head][:piece]
                cm = cm_ref[place, low : low + piece, :span]
                masked_queries, masked_grads = queries * mask, grads * mask
                scores = dot_nt(masked_queries, keys[:span])
                weights = (scores * cm).astype(BF16)
                back = dot_nt(
                    jnp.concatenate([masked_grads, slopes * mask], axis=1), sides[:span]
                )
                back = (back * cm).astype(BF16)
                term = dot(back, key_sides[head][:span])
                grad_queries = term if grad_queries is None else grad_queries + term
                key_term = dot_tn(back, masked_queries)
                value_term = dot_tn(weights, masked_grads)
                for piece_at in range(span // piece):
                    at = slice(piece_at * piece, (piece_at + 1) * piece)
                    old = grad_keys[piece_at]
                    grad_keys[piece_at] = key_term[at] if old is None else old + key_term[at]
                    old = grad_values[piece_at]
                    grad_values[piece_at] = value_term[at] if old is None else old + value_term[at]
            far = dot_nt(jnp.concatenate([grads, slopes], axis=1), state)
            grad_queries = (
                grad_queries
                + far[:, :LANES] * cos_ref[here, :]
                + far[:, LANES:] * sin_ref[here, :]
            ) * gq_ref[here, :].astype(F32)
            query_ref[here, :] = grad_queries.astype(BF16)
        grad_keys = jnp.concatenate(grad_keys, axis=0)
        grad_values = jnp.concatenate(grad_values, axis=0)
        state = outgoing
        for later in range(place + 1, blocks):
            state = state + lt_ref[later, 0].astype(F32)
        state = state.astype(BF16)
        far = dot_nt(sides, state)
        grad_keys = (
            grad_keys
            + far[:, :LANES] * cos_ref[all_here, :]
            + far[:, LANES:] * sin_ref[all_here, :]
        ) * gk_ref[all_here, :].astype(F32)
        features = turned_features(keys, cos_ref[all_here, :], sin_ref[all_here, :])
        grad_values = grad_values + dot(features, state[:, :LANES])
        dk_ref[all_here, :] = grad_keys.astype(BF16)
        dv_ref[all_here, :] = grad_values.astype(BF16)


def unattend(
    sq, sk, v, gn, gd, cm, cosines, sines, states, incoming, later, slope_q, slope_k,
    later_in, start, count, partial
):
    rows, width = sq.shape
    blocks = cm.shape[0]
    spec = pl.BlockSpec((rows, LANES), lambda p: (0, start + p))
    state_spec = pl.BlockSpec((blocks, 1, 2 * LANES, 2 * LANES), lambda p: (0, start + p, 0, 0))
    full = jax.ShapeDtypeStruct((rows, width), BF16)
    return call(
        functools.partial(unattend_kernel, half=start // count),
        grid=(count,),
        in_specs=[
            spec, spec, spec, spec, spec,
            whole(cm.shape), whole((rows, LANES)), whole((rows, LANES)),
            state_spec,
            whole(incoming.shape),
            state_spec, spec, spec, whole(later_in.shape),
        ]
        + [pl.BlockSpec(memory_space=pl.ANY)] * len(partial),
        out_specs=[spec, spec, spec],
        out_shape=[jax.ShapeDtypeStruct((rows, width), BF16), full, full],
        input_output_aliases={14 + at: at for at in range(len(partial))},
        compiler_params=params(),
        cost_estimate=cost(20e9, 20e6),
        name="unattend",
        near_in=(3, 4, 14, 15, 16),
        near_out=(0, 1, 2),
    )(sq, sk, v, gn, gd, cm, cosines, sines, states, incoming, later, slope_q, slope_k, later_in, *partial)


def weights_kernel(coords_ref, x_ref, q_ref, k_ref, v_ref, edge_ref, *refs, shard):
    outs, product_ref = refs[:-1], refs[-1]
    coords = [coords_ref[place] for place in range(4)]
    rows, part = q_ref.shape
    width = x_ref.shape[1]
    ones = jnp.ones((rows, LANES), BF16)
    lane = lax.broadcasted_iota(jnp.int32, (part, LANES), 1)
    sums = jnp.zeros((part, LANES), F32)
    for place, ref in enumerate((q_ref, k_ref, v_ref)):
        at = slice(place * part, (place + 1) * part)
        product_ref[:, at] = dot_tn(x_ref[...], ref[...]).astype(BF16)
        sums = jnp.where(lane == place, dot_tn(ref[...], ones), sums)
    if shard % 16 == 0:
        edge = shard * part // width
        for place in range(width // shard):
            piece = jnp.concatenate(
                [sums[place * edge : (place + 1) * edge], jnp.zeros((shard - edge, LANES), F32)], axis=0
            )
            product_ref[place * shard : (place + 1) * shard, 3 * part :] = piece.astype(BF16)
    else:
        product_ref[:, 3 * part :] = dot(edge_ref[...], sums.astype(BF16)).astype(BF16)
    emit(product_ref, pl.program_id(0), outs, coords)


def weight_gradients(coords, x, q, k, v, edges, layout):
    rows, width = x.shape
    halves = layout[1]
    spec = pl.BlockSpec((rows, width // halves), lambda t: (0, t))
    out_specs, out_shapes = piece_outputs(layout, layout[3], lambda t: 0)
    return call(
        functools.partial(weights_kernel, shard=layout[2]),
        grid=(halves,),
        in_specs=[scalars(), whole((rows, width)), spec, spec, spec, whole(edges.shape)],
        out_specs=out_specs,
        out_shape=out_shapes,
        scratch_shapes=[pltpu.VMEM((width, layout[3]), BF16)],
        compiler_params=params(),
        cost_estimate=cost(2 * rows * width * 3 * width, 10e6),
        name="weight_gradients",
        near_in=(2, 3, 4),
    )(coords, x, q, k, v, edges)


def inputs_kernel(first_ref, q_ref, k_ref, v_ref, w_ref, out_ref):
    halves = w_ref.shape[1]
    width = first_ref.shape[1]
    part = width // halves
    total = first_ref[...]
    for half in range(halves):
        side = w_ref[:, half].reshape(width, 3 * part)
        at = slice(half * part, (half + 1) * part)
        joined = jnp.concatenate([q_ref[:, at], k_ref[:, at], v_ref[:, at]], axis=1)
        total = total + dot_nt(joined, side)
    out_ref[...] = total.astype(BF16)


def input_gradient(first, q, k, v, w, step):
    rows, width = first.shape
    groups, halves, shard, _ = w.shape
    part = width // halves
    spec = pl.BlockSpec((step, width), lambda i: (i, 0))
    return call(
        inputs_kernel,
        grid=(rows // step,),
        in_specs=[
            spec, spec, spec, spec,
            pl.BlockSpec((groups, halves, shard, 3 * part), lambda i: (0, 0, 0, 0)),
        ],
        out_specs=spec,
        out_shape=jax.ShapeDtypeStruct((rows, width), BF16),
        compiler_params=params(),
        cost_estimate=cost(2 * rows * width * 3 * width, 14e6),
        name="input_gradient",
        near_in=(1, 2, 3),
    )(first, q, k, v, w)


def moves():
    def table(change):
        pairs = []
        for source in range(32):
            z, y, c, x = source // 8, source // 4 % 2, source // 2 % 2, source % 2
            z, y, c, x = change(z, y, c, x)
            pairs.append((source, ((z * 2 + y) * 2 + c) * 2 + x))
        return pairs

    along = [table(lambda z, y, c, x, k=k: (z ^ k, y, c, x)) for k in range(4)]
    beside = table(lambda z, y, c, x: (z, y ^ c, c, x ^ 1 ^ c))
    across = table(lambda z, y, c, x: (z, y ^ 1 ^ c, c, x ^ c))
    core = table(lambda z, y, c, x: (z, y, c ^ 1, x))
    return along, beside, across, core


def add(left, right):
    return (left.astype(F32) + right.astype(F32)).astype(BF16)


def send(value, table, begin, end, axes=BOTH):
    value = after(value, *begin) if begin else value
    value = lax.ppermute(value, axes, table)
    return after(value, *end) if end else value


class Gather:
    def __init__(self, piece):
        self.tables = moves()
        self.held = piece

    def line(self, begin=(), end=()):
        parts = [send(self.held, self.tables[0][k], begin, end) for k in (1, 2, 3)]
        self.held = join([self.held] + parts)

    def line_parts(self, begin):
        self.held = self.held, [send(self.held, self.tables[0][k], begin, ()) for k in (1, 2, 3)]

    def beside(self, begin=(), end=()):
        self.held = jnp.concatenate([self.held, send(self.held, self.tables[1], begin, end)], axis=0)

    def across(self, begin=(), end=()):
        self.held = jnp.concatenate([self.held, send(self.held, self.tables[2], begin, end)], axis=0)

    def core(self, begin=(), end=()):
        return [self.held, send(self.held, self.tables[3], begin, end)]


class Sum:
    def __init__(self, own, other):
        self.tables = moves()
        self.kept, self.sent = own, other

    def fold(self, table, begin, end):
        arrived = send(self.sent, table, begin, end)
        size = self.kept.shape[0] // 2
        kept = add(self.kept[:size], arrived[:size])
        self.kept, self.sent = kept, add(self.kept[size:], arrived[size:])

    def both(self):
        return [self.kept, self.sent]

    def core(self, begin=(), end=()):
        self.fold(self.tables[3], begin, end)

    def across(self, begin=(), end=()):
        self.fold(self.tables[2], begin, end)

    def beside(self, begin=(), end=()):
        arrived = send(self.sent, self.tables[1], begin, end)
        self.parts = [add(self.kept[k], arrived[k]) for k in range(4)]

    def line(self, begin=(), end=()):
        parts = [send(self.parts[k], self.tables[0][k], begin, end) for k in (1, 2, 3)]
        total = self.parts[0].astype(F32)
        for part in parts:
            total = total + part.astype(F32)
        return total


def local(
    inputs, w_query, w_key, w_value, b_query, b_key, b_value, w_out, b_out, norm_gain, norm_shift,
    w_up, b_up, w_down, b_down, final_gain, final_shift, piece_starts, grad_output,
):
    rows, width = inputs.shape
    halves = lax.axis_size("tp")
    replicas = lax.axis_size("fsdp")
    length = rows * halves
    block = min(512, length)
    blocks = rows // block
    shard = width // replicas
    part = width // halves
    units = w_up.shape[1]
    me = lax.axis_index("tp")
    pieces = replicas == 16 and halves == 2 and shard % 16 == 0
    place = lax.axis_index("fsdp")
    coords = jnp.stack([place // 4, place // 2 % 2, place % 2, me]).astype(jnp.int32)

    def layout(columns):
        return replicas, halves, shard, columns, pieces

    places = me * rows + jnp.arange(rows, dtype=jnp.int32)
    flags = jnp.any(piece_starts[0][:, None] == (places // PIECE * PIECE)[None, :], axis=0)
    angle = 0.5 * jnp.pi / length * places.astype(F32)
    cosines, sines = jnp.cos(angle), jnp.sin(angle)
    at = jnp.arange(block, dtype=jnp.int32)
    allowed = (at[None, None, :] <= at[None, :, None]) | (
        (at[None, None, :] // PIECE == at[None, :, None] // PIECE)
        & flags.reshape(blocks, block)[:, :, None]
    )
    c, s = cosines.reshape(blocks, block), sines.reshape(blocks, block)
    cm = jnp.where(allowed, c[:, :, None] * c[:, None, :] + s[:, :, None] * s[:, None, :], 0.0)
    cosines = jnp.broadcast_to(cosines[:, None], (rows, LANES))
    sines = jnp.broadcast_to(sines[:, None], (rows, LANES))

    each, edge = units // width, shard // halves
    if pieces:
        edges, turns = jnp.zeros((8, LANES), BF16), jnp.zeros((1, 8, LANES), BF16)
    else:
        edges, turns = selectors(width, part, shard, edge, each)
    thins = (
        b_query, b_key, b_value, b_up, b_out, norm_gain, norm_shift, b_down, final_gain, final_shift
    )
    if pieces:
        attention_shard = pack(w_query, w_key, w_value, w_out.T, thins)
    else:
        columns = []
        for thin in thins:
            thin = jnp.pad(thin, (0, -thin.shape[0] % shard))
            columns.append(thin.reshape(-1, shard).T)
        columns = jnp.concatenate(columns, axis=1)
        columns = jnp.pad(columns, ((0, 0), (0, LANES - columns.shape[1])))
        attention_shard = jnp.concatenate([w_query, w_key, w_value, w_out.T, columns], axis=1)
    down_shard = w_down.T

    def gather_all(piece):
        everything = lax.all_gather(piece, BOTH, axis=0, tiled=False)
        everything = everything.reshape(replicas, halves, shard, piece.shape[1])
        return jnp.moveaxis(everything, 1, 0).reshape(1, halves, width, piece.shape[1])

    if pieces:
        first_chunk, up_chunk, down_chunk = Gather(attention_shard), Gather(w_up), Gather(down_shard)
        first_chunk.line([], [cm, cosines, sines, coords])
        four = first_chunk.held
        first_chunk.beside()
        up_chunk.line([four])
        first_chunk.across()
        sixteen = first_chunk.held
        four = up_chunk.held
        w_attention = first_chunk.core([four])
        up_chunk.beside([sixteen, four], w_attention)
        eight = up_chunk.held
        down_chunk.line_parts([sixteen, four])
        w_attention = [after(w_attention[0], eight), w_attention[1]]
    else:
        w_attention, w_lift, w_drop = [
            [gather_all(piece)] for piece in (attention_shard, w_up, down_shard)
        ]


    columns = 4 * part + LANES
    sq, sk, v, slope_q, slope_k, states, total, w_attention = project(
        coords, inputs, w_attention, columns, edges, cosines, sines, block, shard, halves
    )
    queries, there = sq, []
    if pieces:
        up_chunk.across([], [sq])
        down_chunk.held = join(
            [down_chunk.held[0]] + [after(part, sq) for part in down_chunk.held[1]]
        )
        there = [up_chunk.held, down_chunk.held]
        queries = after(sq, *there)
    num, den = attend(queries, sk, v, cm, cosines, sines, states)
    bias_up, vectors = unpack(after(w_attention, num), turns, shard, each)
    towards = [(i, i + 1) for i in range(halves - 1)]
    incoming = send(total, towards, there, [num, vectors], "tp")
    if pieces:
        w_lift = up_chunk.core(there, [num, vectors])
        down_chunk.beside(there, [num, vectors])
        there = [down_chunk.held, incoming, w_lift[1]]
        num = after(num, *there)
    mixed, rden, normal, scale, low = mix(
        num, den, sq, incoming, cosines, sines, w_attention, inputs, vectors, 512
    )
    if pieces:
        down_chunk.across(there, [low])
        there = [down_chunk.held]
        low = after(low, *there)
    act, slope, w_lift = lift(
        coords, low, w_lift, bias_up, units, 768, 3 if pieces else 0
    )
    if pieces:
        w_drop = down_chunk.core(there, [act])
    output, branch, second, sums_second, w_drop = drop(
        coords, act, w_drop, normal, vectors, grad_output, units, 256
    )

    gdown = wide_gradient(coords, branch, act, layout(units), units, 512, "down_gradient")
    gl, gbias_up = bend(branch, w_drop, after(slope, *gdown), units, 768)
    if pieces:
        down_sum = Sum(*gdown)
        down_sum.core([], [gl])
        second = after(second, *down_sum.both())
    first, first_low, sums_first = lower(gl, w_lift, second, normal, scale, vectors, units, 256)
    wide = units + part + LANES
    *gup, gn, gd, later, later_total = unmix(
        coords, first_low, mixed, rden, sq, cosines, sines, w_attention,
        sums_first, sums_second, turns, gbias_up, layout(wide), block,
    )
    there = []
    if pieces:
        down_sum.across([], [gn])
        there = down_sum.both()
    gup = wide_gradient(
        coords, after(low, *there, *gup), gl, layout(wide), units, 512, "up_gradient", gup
    )
    towards = [(i + 1, i) for i in range(halves - 1)]
    later_in = send(later_total, towards, there, gup, "tp")
    there = [later_in, *gup]
    gn = after(gn, *there)
    pairs = width // LANES
    partial = ()
    for half in range(halves):
        per = pairs // halves
        partial = unattend(
            sq, sk, v, gn, gd, cm, cosines, sines, states, incoming, later, slope_q, slope_k,
            later_in, half * per, per, partial,
        )
        if pieces and half == 0:
            up_sum = Sum(*gup)
            up_sum.core(there, partial)
            down_sum.beside(there, partial)
            there = [*up_sum.both(), *down_sum.parts]
            partial = after(tuple(partial), *there)
    query_low, key_low, value_low = partial
    gqkv = weight_gradients(
        coords, inputs, query_low, key_low, value_low, edges, layout(3 * part + LANES)
    )
    if pieces:
        up_sum.across(there, gqkv)
        gdown = down_sum.line(there, gqkv)
        rest_sum = Sum(*gqkv)
        rest_sum.core([*up_sum.both(), gdown])
        up_sum.beside([])
        rest_sum.across()
        gup = up_sum.line([], rest_sum.both())
        rest_sum.beside()
        rest = rest_sum.line()
    else:

        def scatter(grad):
            grad = jnp.moveaxis(grad.reshape(halves, replicas, shard, grad.shape[2]), 0, 1)
            grad = grad.reshape(replicas * halves, shard, grad.shape[3])
            return lax.psum_scatter(grad, BOTH, scatter_dimension=0, tiled=False).astype(F32)

        gdown, gup, rest = [scatter(grad[0]) for grad in (gdown, gup, gqkv)]
    grad_inputs = input_gradient(first, query_low, key_low, value_low, w_attention, 256)

    scaling = 1.0 / replicas
    gdown, gup, rest = gdown * scaling, gup * scaling, rest * scaling
    sums = gup[:, units + part :].T
    small = rest[:edge, 3 * part :].T
    return (
        output,
        grad_inputs,
        rest[:, :part],
        rest[:, part : 2 * part],
        rest[:, 2 * part : 3 * part],
        small[0],
        small[1],
        small[2],
        gup[:, units : units + part].T,
        sums[2],
        sums[0],
        sums[1],
        gup[:, :units],
        sums[6 : 6 + units // width].reshape(-1),
        gdown.T,
        sums[5],
        sums[3],
        sums[4],
    )


def solution(mesh):
    row = P(("fsdp", "tp"), None)
    split, turned = P("fsdp", "tp"), P("tp", "fsdp")
    thin, wide = P(("tp", "fsdp")), P("fsdp")
    return jax.shard_map(
        local,
        mesh=mesh,
        in_specs=(
            row, split, split, split, thin, thin, thin, turned, wide, wide, wide,
            split, thin, turned, wide, wide, wide, P("fsdp", None), row,
        ),
        out_specs=(
            row, row, split, split, split, thin, thin, thin, turned, wide, wide, wide,
            split, thin, turned, wide, wide, wide,
        ),
        check_vma=False,
    )
```

```python
import functools
import math

import jax
import jax.numpy as jnp
from jax import lax
from jax.experimental import pallas as pl
from jax.experimental.pallas import tpu as pltpu
from jax.sharding import PartitionSpec as P

HEAD_DIM = 64
PIECE = 256
LANES = 128
EPSILON = 1e-05
F32 = jnp.float32
BF16 = jnp.bfloat16
BOTH = ("fsdp", "tp")


def dot(left, right):
    return lax.dot_general(left, right, (((1,), (0,)), ((), ())), preferred_element_type=F32)


def dot_nt(left, right):
    return lax.dot_general(left, right, (((1,), (1,)), ((), ())), preferred_element_type=F32)


def dot_tn(left, right):
    return lax.dot_general(left, right, (((0,), (0,)), ((), ())), preferred_element_type=F32)


def flat(ref):
    value = ref[...]
    return value.reshape(value.shape[0] * value.shape[1] * value.shape[2], value.shape[3])


def lane_mask(rows, head, dtype=BF16):
    lane = lax.broadcasted_iota(jnp.int32, (rows, LANES), 1)
    return (lane // HEAD_DIM == head).astype(F32).astype(dtype)


def same_head(rows, columns):
    row = lax.broadcasted_iota(jnp.int32, (rows, columns), 0)
    lane = lax.broadcasted_iota(jnp.int32, (rows, columns), 1)
    return (row // HEAD_DIM) % 2 == (lane // HEAD_DIM) % 2


def same_rows(shape):
    row = lax.broadcasted_iota(jnp.int32, shape, 0)
    lane = lax.broadcasted_iota(jnp.int32, shape, 1)
    return (row // HEAD_DIM) % 2 == 0, lane


def compact(state, held_ref, packet_ref, place, half, spread):
    left, right = state[:, :LANES], state[:, LANES:]
    first, lane = same_rows(left.shape)
    low = lane < HEAD_DIM
    narrow = jnp.where(first, left, pltpu.roll(left, HEAD_DIM, 1))
    column = jnp.where(first, right, pltpu.roll(right, HEAD_DIM, 1))
    if not spread:
        column = column + pltpu.roll(column, LANES - 1, 1)
        column = jnp.where(lane == 0, column, 0.0)
        column = jnp.broadcast_to(jnp.sum(column, axis=1, keepdims=True), column.shape)
    count = packet_ref.shape[0] - 1
    column = jnp.where(lane == half * count + place, column, 0.0)

    @pl.when(half == 0)
    def _():
        held_ref[place] = narrow
        held_ref[count] = column if place == 0 else held_ref[count] + column

    @pl.when(half == 1)
    def _():
        turned = pltpu.roll(narrow, HEAD_DIM, 1)
        packet_ref[place] = jnp.where(low, held_ref[place], turned).astype(BF16)
        held_ref[count] = held_ref[count] + column
        if place == count - 1:
            packet_ref[count] = held_ref[count].astype(BF16)


def expand(packet_ref, place, half, spread):
    narrow = packet_ref[place].astype(F32)
    first, lane = same_rows(narrow.shape)
    low = lane < HEAD_DIM
    turned = pltpu.roll(narrow, HEAD_DIM, 1)
    here = jnp.where(half == 0, narrow, turned)
    there = jnp.where(half == 0, turned, narrow)
    own = first == low
    left = jnp.where(own, jnp.where(first, here, there), 0.0)
    count = packet_ref.shape[0] - 1
    column = packet_ref[count].astype(F32)
    column = jnp.sum(jnp.where(lane == half * count + place, column, 0.0), axis=1, keepdims=True)
    if not spread:
        own = jnp.logical_and(own, lane % HEAD_DIM == 0)
    right = jnp.where(own, jnp.broadcast_to(column, own.shape), 0.0)
    return jnp.concatenate([left, right], axis=1)


def turned_features(values, cosines, sines):
    wide = values.astype(F32)
    return jnp.concatenate([(wide * cosines).astype(BF16), (wide * sines).astype(BF16)], axis=1)


def slot(coords, z, y, c, x):
    across = jnp.where(c == 0, y ^ coords[1], x ^ coords[3])
    beside = jnp.where(c == 0, x ^ coords[1 + 2], y ^ coords[1])
    return across * 8 + beside * 4 + (z ^ coords[0])


def emit(product, half, outs, coords):
    if len(outs) == 1:
        outs[0][half] = product[...]
        return
    core = coords[2]
    shard = outs[0].shape[1]
    for group in range(product.shape[0] // (2 * shard)):
        z, y = group // 2, group % 2
        for out, c in zip(outs, (core, 1 - core)):
            begin = pl.multiple_of((2 * group + c) * shard, 16)
            out[slot(coords, z, y, c, half)] = product[pl.ds(begin, shard), :]


class Weights:
    def __init__(self, coords_ref, sources, held, out, sems, out_sems, halves):
        self.coords = [coords_ref[place] for place in range(4)]
        self.sources, self.held, self.out = sources, held, out
        self.sems, self.out_sems, self.halves = sems, out_sems, halves

    def copies(self, place):
        half = self.halves[place]
        if len(self.sources) == 1:
            return [
                pltpu.make_async_copy(
                    self.sources[0].at[0, half], self.held.at[place], self.sems.at[place, 0]
                )
            ]
        copies = []
        shard = self.sources[0].shape[1]
        for side, ref in enumerate(self.sources):
            c = self.coords[2] if side == 0 else 1 - self.coords[2]
            for group in range(8):
                z, y = group // 2, group % 2
                begin = pl.multiple_of((2 * group + c) * shard, 16)
                copies.append(
                    pltpu.make_async_copy(
                        ref.at[slot(self.coords, z, y, c, half)],
                        self.held.at[place, pl.ds(begin, shard), :],
                        self.sems.at[place, side * 8 + group],
                    )
                )
        return copies

    def start(self, place):
        for copy in self.copies(place):
            copy.start()

    def ready(self, place):
        for copy in self.copies(place):
            copy.wait()
        self.leaving(place).start()

    def leaving(self, place):
        return pltpu.make_async_copy(
            self.held.at[place], self.out.at[0, place], self.out_sems.at[place]
        )

    def left(self, place):
        self.leaving(place).wait()

    @staticmethod
    def scratch(halves, width, columns):
        return [
            pltpu.VMEM((halves, width, columns), BF16),
            pltpu.SemaphoreType.DMA((halves, 16)),
            pltpu.SemaphoreType.DMA((halves,)),
        ]


def anywhere(count):
    return [pl.BlockSpec(memory_space=pl.ANY)] * count


def scalars():
    return pl.BlockSpec(memory_space=pltpu.SMEM)


def params(megabytes=32):
    return pltpu.CompilerParams(vmem_limit_bytes=megabytes * 1024 * 1024)


def call(kernel, *, out_shape, near_in=(), near_out=(), least=65536, **options):
    shapes = list(out_shape) if isinstance(out_shape, (list, tuple)) else [out_shape]

    def large(value):
        return math.prod(value.shape) * value.dtype.itemsize > least

    placed = [
        pltpu.HBM(shape.shape, shape.dtype) if large(shape) and at not in near_out else shape
        for at, shape in enumerate(shapes)
    ]
    function = pl.pallas_call(
        kernel, out_shape=placed if isinstance(out_shape, (list, tuple)) else placed[0], **options
    )

    def run(*operands):
        count = len(operands)
        near = {at % count for at in near_in}
        return function(
            *[
                pltpu.with_memory_space_constraint(value, pltpu.HBM)
                if large(value) and at not in near
                else value
                for at, value in enumerate(operands)
            ]
        )

    return run


def whole(shape):
    zeros = (0,) * len(shape)
    return pl.BlockSpec(shape, lambda *_: zeros)


def cost(flops, moved):
    return pl.CostEstimate(flops=int(flops), bytes_accessed=int(moved), transcendentals=0)


def after(value, *others):
    return lax.optimization_barrier((value, others))[0]


def pack_kernel(*refs):
    q_ref, k_ref, v_ref, out_ref = refs[:4]
    thins = refs[4:-1]
    first_ref = refs[-1]
    shard, part = q_ref.shape

    def chosen(columns, start):
        row = lax.broadcasted_iota(jnp.int32, (shard, columns), 0)
        column = lax.broadcasted_iota(jnp.int32, (shard, columns), 1)
        return (row + start == column).astype(F32).astype(BF16)

    for place, ref in enumerate((q_ref, k_ref, v_ref, out_ref)):
        first_ref[:, place * part : (place + 1) * part] = ref[...]
    columns = jnp.zeros((shard, LANES), F32)
    lane = 0
    for ref in thins:
        size = ref.shape[1]
        for start in range(0, size, shard):
            row = lax.broadcasted_iota(jnp.int32, (LANES, size), 0)
            spread = jnp.where(row == lane, ref[...].astype(F32), 0.0).astype(BF16)
            columns = columns + dot_nt(chosen(size, start), spread)
            lane += 1
    first_ref[:, 4 * part :] = columns.astype(BF16)


def pack(q, k, v, out, thins):
    shard, part = q.shape
    return call(
        pack_kernel,
        out_shape=jax.ShapeDtypeStruct((shard, 4 * part + LANES), BF16),
        compiler_params=params(),
        cost_estimate=cost(1e8, 1e6),
        name="pack",
        least=0,
    )(q, k, v, out, *[thin.reshape(1, -1) for thin in thins])


def deal(columns, shard, size, turns):
    count = columns.shape[0] // shard
    runs = []
    for place in range(count):
        piece = columns[place * shard : place * shard + size]
        for turn in range(turns):
            runs.append(pltpu.roll(piece, LANES - turn, 1) if turn else piece)
    return jnp.concatenate(runs, axis=0)


def selectors_kernel(edge_ref, turn_ref, *, shard, edge, each):
    width, part = edge_ref.shape
    row = lax.broadcasted_iota(jnp.int32, (width, part), 0)
    column = lax.broadcasted_iota(jnp.int32, (width, part), 1)
    chosen = (row % shard < edge) & (row // shard * edge + row % shard == column)
    edge_ref[...] = chosen.astype(F32).astype(BF16)
    row = lax.broadcasted_iota(jnp.int32, (width, LANES), 0)
    source = row // shard * (each * shard) + row % shard
    lane = lax.broadcasted_iota(jnp.int32, (width, LANES), 1)
    for turn in range(each):
        for begin in range(0, each * width, LANES):
            chosen = source + (turn * shard - begin) == lane
            turn_ref[turn, :, begin : begin + LANES] = chosen.astype(F32).astype(BF16)


def selectors(width, part, shard, edge, each):
    return call(
        functools.partial(selectors_kernel, shard=shard, edge=edge, each=each),
        out_shape=[
            jax.ShapeDtypeStruct((width, part), BF16),
            jax.ShapeDtypeStruct((each, width, each * width), BF16),
        ],
        compiler_params=params(),
        cost_estimate=cost(1e8, 1e6),
        name="selectors",
    )()


def unpack_kernel(thin_ref, turn_ref, up_ref, vec_ref, *, shard, each):
    halves = thin_ref.shape[1]
    for half in range(halves):
        thin = thin_ref[0, half]
        if shard % 16 == 0:
            turned = deal(thin.astype(F32), shard, shard, each).T
            up_ref[half] = turned[0:8]
            continue
        rows = jnp.zeros((8, turn_ref.shape[2]), F32)
        for turn in range(each):
            picked = dot_tn(thin, turn_ref[turn])
            rows = rows + picked[3 + turn : 4 + turn]
        up_ref[half] = rows
    turned = thin_ref[0, 0].astype(F32).T
    vec_ref[...] = turned[3 + each : 11 + each]


def unpack(w, turns, shard, each):
    _, halves, width, columns = w.shape
    return call(
        functools.partial(unpack_kernel, shard=shard, each=each),
        grid=(1,),
        in_specs=[
            pl.BlockSpec((1, halves, width, LANES), lambda i: (0, 0, 0, columns // LANES - 1)),
            whole(turns.shape),
        ],
        out_specs=[whole((halves, 8, each * width)), whole((8, width))],
        out_shape=[
            jax.ShapeDtypeStruct((halves, 8, each * width), F32),
            jax.ShapeDtypeStruct((8, width), F32),
        ],
        compiler_params=params(),
        cost_estimate=cost(1e8, 1e6),
        name="unpack",
    )(w, turns)


def join_kernel(*refs):
    for place, ref in enumerate(refs[:-1]):
        refs[-1][place] = ref[...]


def join(parts):
    return call(
        join_kernel,
        out_shape=jax.ShapeDtypeStruct((len(parts),) + parts[0].shape, parts[0].dtype),
        compiler_params=params(),
        cost_estimate=cost(0, 1e6),
        name="join",
        least=0,
    )(*parts)


def project_kernel(
    coords_ref, *refs, block, step, shard, halves
):
    sources, refs = refs[: len(refs) - 15], refs[len(refs) - 15 :]
    x_ref, edge_ref, cos_ref, sin_ref, sq_ref, sk_ref, v_ref, gq_ref, gk_ref, st_ref, tot_ref = refs[:11]
    sources, out_ref = sources[:-1], sources[-1]
    packed_ref, held_ref, sems, out_sems = refs[11:]
    rows = x_ref.shape[0]
    part = sq_ref.shape[1]
    now = pl.program_id(0)
    weights = Weights(coords_ref, sources, held_ref, out_ref, sems, out_sems, range(halves))

    @pl.when(now == 0)
    def _():
        for half in range(halves):
            weights.start(half)

    for half in range(halves):

        @pl.when(now == half)
        def _():
            weights.ready(half)

    columns = held_ref.shape[2]
    thin = held_ref[now, :, columns - LANES :]
    if shard % 16 == 0:
        biases = deal(thin.astype(F32), shard, shard * part // x_ref.shape[1], 1).T
    else:
        biases = dot_tn(thin, edge_ref[...])

    def body(index, carry):
        here = pl.ds(index * step, step)
        sums = dot(x_ref[here, :], held_ref[now, :, : 3 * part])
        for place, (feature_ref, slope_ref) in enumerate(((sq_ref, gq_ref), (sk_ref, gk_ref))):
            value = sums[:, place * part : (place + 1) * part] + biases[place : place + 1]
            positive = jnp.maximum(value, 0.0) + jnp.log1p(jnp.exp(-jnp.abs(value)))
            feature_ref[here, :] = positive.astype(BF16)
            slope_ref[here, :] = jax.nn.sigmoid(value).astype(BF16)
        v_ref[here, :] = (sums[:, 2 * part :] + biases[2:3]).astype(BF16)
        return carry

    lax.fori_loop(0, rows // step, body, 0)
    keep = same_head(2 * LANES, 2 * LANES)
    ones = jnp.ones((block, LANES), BF16)
    for pair in range(part // LANES):
        lanes = slice(pair * LANES, (pair + 1) * LANES)
        total = jnp.zeros((2 * LANES, 2 * LANES), F32)
        for place in range(rows // block):
            here = slice(place * block, (place + 1) * block)
            features = turned_features(sk_ref[here, lanes], cos_ref[here, :], sin_ref[here, :])
            state = dot_tn(features, jnp.concatenate([v_ref[here, lanes], ones], axis=1))
            state = jnp.where(keep, state, 0.0)
            st_ref[place, pair] = state.astype(BF16)
            total = total + state
        compact(total, packed_ref, tot_ref, pair, pl.program_id(0), True)

    @pl.when(now == halves - 1)
    def _():
        for half in range(halves):
            weights.left(half)


def project(coords, x, sources, columns, edges, cosines, sines, block, shard, halves):
    rows, width = x.shape
    part = width // halves
    pairs = width // LANES
    half = pairs // halves
    blocks = rows // block
    row_spec = pl.BlockSpec((rows, part), lambda t: (0, t))
    full = jax.ShapeDtypeStruct((rows, width), BF16)

    def kernel(coords_ref, *refs):
        count = len(sources)
        others, outs, scratch = refs[count : count + 4], refs[count + 4 : -4], refs[-4:]
        project_kernel(
            coords_ref, *refs[:count], outs[-1], *others, *outs[:-1], *scratch,
            block=block, step=rows, shard=shard, halves=halves,
        )

    return call(
        kernel,
        grid=(halves,),
        in_specs=[scalars()]
        + anywhere(len(sources))
        + [
            whole((rows, width)), whole(edges.shape), whole((rows, LANES)), whole((rows, LANES)),
        ],
        out_specs=[
            row_spec, row_spec, row_spec, row_spec, row_spec,
            pl.BlockSpec((blocks, half, 2 * LANES, 2 * LANES), lambda t: (0, t, 0, 0)),
            whole((half + 1, 2 * LANES, LANES)),
        ]
        + anywhere(1),
        out_shape=[
            full, full, full, full, full,
            jax.ShapeDtypeStruct((blocks, pairs, 2 * LANES, 2 * LANES), BF16),
            jax.ShapeDtypeStruct((half + 1, 2 * LANES, LANES), BF16),
            jax.ShapeDtypeStruct((1, halves, width, columns), BF16),
        ],
        scratch_shapes=[pltpu.VMEM((half + 1, 2 * LANES, LANES), F32)]
        + Weights.scratch(halves, width, columns),
        compiler_params=params(),
        cost_estimate=cost(2 * rows * width * 3 * width, 16e6),
        name="project",
        near_out=(0, 1, 2),
    )(coords, *sources, x, edges, cosines, sines)


def attend_kernel(sq_ref, sk_ref, v_ref, cm_ref, cos_ref, sin_ref, st_ref, num_ref, den_ref):
    blocks, block, _ = cm_ref.shape
    piece = min(PIECE, block)
    masks = [lane_mask(block, head) for head in range(2)]
    for place in range(blocks):
        start = place * block
        keys = sk_ref[start : start + block, :]
        values = v_ref[start : start + block, :]
        sides = [jnp.concatenate([values * mask, mask], axis=1) for mask in masks]
        for low in range(0, block, piece):
            here = slice(start + low, start + low + piece)
            span = low + piece
            queries = sq_ref[here, :]
            sums = None
            for mask, side in zip(masks, sides):
                scores = dot_nt(queries * mask[:piece], keys[:span])
                weights = (scores * cm_ref[place, low : low + piece, :span]).astype(BF16)
                term = dot(weights, side[:span])
                sums = term if sums is None else sums + term
            for earlier in range(place):
                sums = sums + dot(
                    turned_features(queries, cos_ref[here, :], sin_ref[here, :]), st_ref[earlier, 0]
                )
            num_ref[here, :] = sums[:, :LANES]
            den_ref[here, :] = sums[:, LANES:]


def attend(sq, sk, v, cm, cosines, sines, states):
    rows, width = sq.shape
    pairs = width // LANES
    blocks = cm.shape[0]
    spec = pl.BlockSpec((rows, LANES), lambda p: (0, p))
    full = jax.ShapeDtypeStruct((rows, width), F32)
    return call(
        attend_kernel,
        grid=(pairs,),
        in_specs=[
            spec, spec, spec,
            whole(cm.shape), whole((rows, LANES)), whole((rows, LANES)),
            pl.BlockSpec((blocks, 1, 2 * LANES, 2 * LANES), lambda p: (0, p, 0, 0)),
        ],
        out_specs=[spec, spec],
        out_shape=[full, full],
        compiler_params=params(),
        cost_estimate=cost(8e9, 14e6),
        name="attend",
        near_in=(0, 1, 2),
        near_out=(0, 1),
    )(sq, sk, v, cm, cosines, sines, states)


def norm_rows(values):
    average = jnp.mean(values, axis=1, keepdims=True)
    centred = values - average
    scale = lax.rsqrt(jnp.mean(centred * centred, axis=1, keepdims=True) + EPSILON)
    return centred * scale, scale


def mix_kernel(
    num_ref, den_ref, sq_ref, in_ref, cos_ref, sin_ref, w_ref, x_ref, vec_ref,
    mixed_ref, rden_ref, normal_ref, scale_ref, low_ref, wide_ref,
):
    pairs = wide_ref.shape[0]
    halves = w_ref.shape[1]
    rows, width = x_ref.shape
    part = width // halves

    @pl.when(pl.program_id(0) == 0)
    def _():
        for pair in range(pairs):
            place, half = pair % (pairs // halves), pair // (pairs // halves)
            wide_ref[pair] = expand(in_ref, place, half, True).astype(BF16)

    for pair in range(pairs):
        lanes = slice(pair * LANES, (pair + 1) * LANES)
        sums = dot(turned_features(sq_ref[:, lanes], cos_ref[...], sin_ref[...]), wide_ref[pair])
        inverse = 1.0 / jnp.maximum(den_ref[:, lanes] + sums[:, LANES:], 1.0)
        rden_ref[:, lanes] = inverse
        mixed_ref[:, lanes] = ((num_ref[:, lanes] + sums[:, :LANES]) * inverse).astype(BF16)
    total = x_ref[...].astype(F32) + vec_ref[0:1, :]
    for half in range(halves):
        side = w_ref[:, half]
        side = side.reshape(width, part)
        total = total + dot_nt(mixed_ref[:, half * part : (half + 1) * part], side)
    normal, scale = norm_rows(total)
    normal_ref[...] = normal
    scale_ref[...] = jnp.broadcast_to(scale, scale_ref.shape)
    low_ref[...] = (normal * vec_ref[1:2, :] + vec_ref[2:3, :]).astype(BF16)


def mix(num, den, sq, incoming, cosines, sines, w, x, vectors, step):
    rows, width = x.shape
    groups, halves, shard, _ = w.shape
    part = width // halves
    pairs = width // LANES
    wide = pl.BlockSpec((step, width), lambda i: (i, 0))
    thin = pl.BlockSpec((step, LANES), lambda i: (i, 0))
    return call(
        mix_kernel,
        grid=(rows // step,),
        in_specs=[
            wide, wide, wide, whole(incoming.shape), thin, thin,
            pl.BlockSpec((groups, halves, shard, part), lambda i: (0, 0, 0, 3)),
            wide, whole(vectors.shape),
        ],
        out_specs=[wide, wide, wide, thin, wide],
        out_shape=[
            jax.ShapeDtypeStruct((rows, width), BF16),
            jax.ShapeDtypeStruct((rows, width), F32),
            jax.ShapeDtypeStruct((rows, width), F32),
            jax.ShapeDtypeStruct((rows, LANES), F32),
            jax.ShapeDtypeStruct((rows, width), BF16),
        ],
        scratch_shapes=[pltpu.VMEM((pairs, 2 * LANES, 2 * LANES), BF16)],
        compiler_params=params(),
        cost_estimate=cost(2 * rows * width * width * 2, 20e6),
        name="mix",
        near_in=(0, 1, 2),
        near_out=(2, 4),
    )(num, den, sq, incoming, cosines, sines, w, x, vectors)


def norm_back(upstream, normal, scale, gain):
    scaled = upstream * gain
    inner = (
        scaled
        - jnp.mean(scaled, axis=1, keepdims=True)
        - normal * jnp.mean(scaled * normal, axis=1, keepdims=True)
    )
    return inner * scale


def lift_kernel(coords_ref, *refs, step, row, halves):
    sources, refs = refs[:-8], refs[-8:]
    low_ref, bias_ref, act_ref, slope_ref, out_ref, held_ref, sems, out_sems = refs
    tile = act_ref.shape[1]
    now = pl.program_id(0)
    tiles = pl.num_programs(0) // halves
    weights = Weights(coords_ref, sources, held_ref, out_ref, sems, out_sems, range(halves))

    @pl.when(now == 0)
    def _():
        for half in range(halves):
            weights.start(half)

    for half in range(halves):

        @pl.when(now == half * tiles)
        def _():
            weights.ready(half)

    begin = pl.multiple_of(now % tiles * tile, tile)
    up = held_ref[now // tiles, :, pl.ds(begin, tile)]

    def body(place, carry):
        here = pl.ds(place * step, step)
        lifted = dot(low_ref[here, :], up) + bias_ref[0, row : row + 1, :]
        share = 0.5 + 0.5 * lax.erf(lifted * math.sqrt(0.5))
        bell = jnp.exp(-0.5 * lifted * lifted) * (1.0 / math.sqrt(2.0 * math.pi))
        act_ref[here, :] = (lifted * share).astype(BF16)
        slope_ref[here, :] = (share + lifted * bell).astype(BF16)
        return carry

    lax.fori_loop(0, low_ref.shape[0] // step, body, 0, unroll=True)

    @pl.when(now == pl.num_programs(0) - 1)
    def _():
        for half in range(halves):
            weights.left(half)


def lift(coords, low, sources, bias, units, tile, row):
    rows, width = low.shape
    halves = bias.shape[0]
    tiles = units // tile
    unit_spec = pl.BlockSpec((rows, tile), lambda i: (0, i))
    shape = jax.ShapeDtypeStruct((rows, halves * units), BF16)
    return call(
        functools.partial(lift_kernel, step=256, row=row, halves=halves),
        grid=(halves * tiles,),
        in_specs=[scalars()]
        + anywhere(len(sources))
        + [whole((rows, width)), pl.BlockSpec((1, 8, tile), lambda i: (i // tiles, 0, i % tiles))],
        out_specs=[unit_spec, unit_spec] + anywhere(1),
        out_shape=[shape, shape, jax.ShapeDtypeStruct((1, halves, width, units), BF16)],
        scratch_shapes=Weights.scratch(halves, width, units),
        compiler_params=params(),
        cost_estimate=cost(2 * rows * width * halves * units, 20e6),
        name="lift",
        near_in=(-2,),
        near_out=(0, 1),
    )(coords, *sources, low, bias)


def in_turn(product, finish, total_ref):
    now = pl.program_id(0)
    last = pl.num_programs(0) - 1

    @pl.when(now == 0)
    def _():
        total_ref[0] = product(True)

    @pl.when((now > 0) & (now < last))
    def _():
        finish(total_ref[(now - 1) % 2])
        total_ref[now % 2] = product()

    @pl.when(now == last)
    def _():
        finish(total_ref[(now - 1) % 2])


def drop_kernel(coords_ref, *refs, halves):
    sources, act_ref, refs = refs[:-13], refs[-13], refs[-12:]
    normal_ref, vec_ref, grad_ref, out_ref, branch_ref, second_ref, sum_ref = refs[:7]
    whole_ref, held_ref, sems, out_sems, total_ref = refs[7:]
    weights = Weights(coords_ref, sources, held_ref, whole_ref, sems, out_sems, range(halves))
    units = held_ref.shape[2]

    @pl.when(pl.program_id(0) == 0)
    def _():
        sum_ref[...] = jnp.zeros_like(sum_ref)
        for half in range(halves):
            weights.start(half)

    def product(fresh=False):
        total = None
        for half in range(halves):
            if fresh:
                weights.ready(half)
            term = dot_nt(act_ref[:, half * units : (half + 1) * units], held_ref[half])
            total = term if total is None else total + term
        return total

    def finish(total):
        total = total + normal_ref[...] * vec_ref[1:2, :] + vec_ref[2:3, :] + vec_ref[3:4, :]
        normal, scale = norm_rows(total)
        gain = vec_ref[4:5, :]
        out_ref[...] = (normal * gain + vec_ref[5:6, :]).astype(BF16)
        upstream = grad_ref[...].astype(F32)
        second = norm_back(upstream, normal, scale, gain)
        second_ref[...] = second
        branch_ref[...] = second.astype(BF16)
        sum_ref[0:1, :] += jnp.sum(upstream * normal, axis=0, keepdims=True)
        sum_ref[1:2, :] += jnp.sum(upstream, axis=0, keepdims=True)
        sum_ref[2:3, :] += jnp.sum(second, axis=0, keepdims=True)

    in_turn(product, finish, total_ref)

    @pl.when(pl.program_id(0) == pl.num_programs(0) - 1)
    def _():
        for half in range(halves):
            weights.left(half)


def drop(coords, act, sources, normal, vectors, grad, units, step):
    rows, width = normal.shape
    halves = act.shape[1] // units
    steps = rows // step
    wide = pl.BlockSpec((step, width), lambda i: (jnp.maximum(i - 1, 0), 0))
    return call(
        functools.partial(drop_kernel, halves=halves),
        grid=(steps + 1,),
        in_specs=[scalars()]
        + anywhere(len(sources))
        + [
            pl.BlockSpec((step, halves * units), lambda i: (jnp.minimum(i, steps - 1), 0)),
            wide, whole(vectors.shape), wide,
        ],
        out_specs=[wide, wide, wide, whole((8, width))] + anywhere(1),
        out_shape=[
            jax.ShapeDtypeStruct((rows, width), BF16),
            jax.ShapeDtypeStruct((rows, width), BF16),
            jax.ShapeDtypeStruct((rows, width), F32),
            jax.ShapeDtypeStruct((8, width), F32),
            jax.ShapeDtypeStruct((1, halves, width, units), BF16),
        ],
        scratch_shapes=Weights.scratch(halves, width, units) + [pltpu.VMEM((2, step, width), F32)],
        compiler_params=params(),
        cost_estimate=cost(2 * rows * width * halves * units, 20e6),
        name="drop",
        near_in=(-4, -3),
        near_out=(1, 2),
    )(coords, *sources, act, normal, vectors, grad)


def piece_outputs(layout, tile, index_map):
    replicas, halves, shard, columns, pieces = layout[:5]
    if pieces:
        count = replicas * halves // 2
        spec = pl.BlockSpec((count, shard, tile), lambda *at: (0, 0, index_map(*at)))
        shape = jax.ShapeDtypeStruct((count, shard, columns), BF16)
        return [spec, spec], [shape, shape]
    width = replicas * shard
    spec = pl.BlockSpec((halves, width, tile), lambda *at: (0, 0, index_map(*at)))
    return [spec], [jax.ShapeDtypeStruct((halves, width, columns), BF16)]


def wide_gradient_kernel(coords_ref, left_ref, *refs, halves, partial):
    rights, product_ref = refs[:halves], refs[-1]
    outs = refs[(len(refs) - 1 + halves) // 2 : -1] if partial else refs[halves:-1]
    coords = [coords_ref[place] for place in range(4)]
    for half, right_ref in enumerate(rights):
        product_ref[...] = dot_tn(left_ref[...], right_ref[...]).astype(BF16)
        emit(product_ref, half, outs, coords)


def wide_gradient(coords, left, right, layout, units, tile, name, partial=()):
    rows, width = left.shape
    halves = layout[1]
    tiles = units // tile
    out_specs, out_shapes = piece_outputs(layout, tile, lambda j: j)
    return call(
        functools.partial(wide_gradient_kernel, halves=halves, partial=bool(partial)),
        grid=(tiles,),
        in_specs=[scalars(), whole((rows, width))]
        + [
            pl.BlockSpec((rows, tile), lambda j, half=half: (0, half * tiles + j))
            for half in range(halves)
        ]
        + anywhere(len(partial)),
        out_specs=out_specs,
        out_shape=out_shapes,
        input_output_aliases={2 + halves + at: at for at in range(len(partial))},
        scratch_shapes=[pltpu.VMEM((width, tile), BF16)],
        compiler_params=params(),
        cost_estimate=cost(2 * rows * width * halves * units, 18e6),
        name=name,
        near_in=(1, 2, 3),
    )(coords, left, *([right] * halves), *partial)


def bend_kernel(branch_ref, down_ref, slope_ref, gl_ref, gbias_ref, *, step):
    down = down_ref[0, 0]
    gbias_ref[...] = jnp.zeros_like(gbias_ref)

    def body(place, carry):
        here = pl.ds(place * step, step)
        slope = dot(branch_ref[here, :], down) * slope_ref[here, :].astype(F32)
        gbias_ref[0:1, :] += jnp.sum(slope, axis=0, keepdims=True)
        gl_ref[here, :] = slope.astype(BF16)
        return carry

    lax.fori_loop(0, branch_ref.shape[0] // step, body, 0, unroll=True)


def bend(branch, w, slope, units, tile):
    rows, width = branch.shape
    halves = w.shape[1]
    tiles = units // tile
    unit_spec = pl.BlockSpec((rows, tile), lambda i: (0, i))
    return call(
        functools.partial(bend_kernel, step=256),
        grid=(halves * tiles,),
        in_specs=[
            whole((rows, width)),
            pl.BlockSpec((1, 1, width, tile), lambda i: (0, i // tiles, 0, i % tiles)),
            unit_spec,
        ],
        out_specs=[unit_spec, pl.BlockSpec((8, tile), lambda i: (0, i))],
        out_shape=[
            jax.ShapeDtypeStruct(slope.shape, BF16),
            jax.ShapeDtypeStruct((8, halves * units), F32),
        ],
        compiler_params=params(),
        cost_estimate=cost(2 * rows * width * halves * units, 20e6),
        name="bend",
        near_in=(0, 2),
        near_out=(0,),
    )(branch, w, slope)


def lower_kernel(
    gl_ref, up_ref, second_ref, normal_ref, scale_ref, vec_ref, first_ref, firstlow_ref, sum_ref,
    total_ref,
):
    halves, units = up_ref.shape[1], up_ref.shape[3]

    @pl.when(pl.program_id(0) == 0)
    def _():
        sum_ref[...] = jnp.zeros_like(sum_ref)

    def product(fresh=False):
        total = None
        for half in range(halves):
            term = dot_nt(gl_ref[:, half * units : (half + 1) * units], up_ref[0, half])
            total = term if total is None else total + term
        return total

    def finish(total):
        upstream = second_ref[...] + total
        normal = normal_ref[...]
        first = norm_back(upstream, normal, scale_ref[:, 0:1], vec_ref[1:2, :])
        first_ref[...] = first
        firstlow_ref[...] = first.astype(BF16)
        sum_ref[0:1, :] += jnp.sum(upstream * normal, axis=0, keepdims=True)
        sum_ref[1:2, :] += jnp.sum(upstream, axis=0, keepdims=True)
        sum_ref[2:3, :] += jnp.sum(first, axis=0, keepdims=True)

    in_turn(product, finish, total_ref)


def lower(gl, w, second, normal, scale, vectors, units, step):
    rows, width = second.shape
    steps = rows // step
    wide = pl.BlockSpec((step, width), lambda i: (jnp.maximum(i - 1, 0), 0))
    return call(
        lower_kernel,
        grid=(steps + 1,),
        in_specs=[
            pl.BlockSpec((step, gl.shape[1]), lambda i: (jnp.minimum(i, steps - 1), 0)),
            whole(w.shape), wide, wide,
            pl.BlockSpec((step, LANES), lambda i: (jnp.maximum(i - 1, 0), 0)),
            whole(vectors.shape),
        ],
        out_specs=[wide, wide, whole((8, width))],
        out_shape=[
            jax.ShapeDtypeStruct((rows, width), F32),
            jax.ShapeDtypeStruct((rows, width), BF16),
            jax.ShapeDtypeStruct((8, width), F32),
        ],
        scratch_shapes=[pltpu.VMEM((2, step, width), F32)],
        compiler_params=params(),
        cost_estimate=cost(2 * rows * width * gl.shape[1], 20e6),
        name="lower",
        near_in=(0, 2, 3),
        near_out=(1,),
    )(gl, w, second, normal, scale, vectors)


def unmix_kernel(
    coords_ref, first_ref, mixed_ref, rden_ref, sq_ref, cos_ref, sin_ref, w_ref,
    sum1_ref, sum2_ref, turn_ref, *refs, block, step, shard
):
    bias = jnp.broadcast_to(refs[0][0:1, :], refs[0].shape)
    refs = refs[1:]
    outs = refs[:-6]
    gn_ref, gd_ref, st_ref, tot_ref, product_ref, packed_ref = refs[-6:]
    coords = [coords_ref[place] for place in range(4)]
    rows, width = first_ref.shape
    part = mixed_ref.shape[1]
    side = flat(w_ref)
    group_row = lax.broadcasted_iota(jnp.int32, (LANES, LANES), 0)
    group_lane = lax.broadcasted_iota(jnp.int32, (LANES, LANES), 1)
    group = (group_row // HEAD_DIM == group_lane // HEAD_DIM).astype(F32).astype(BF16)
    group = jnp.concatenate([group, group], axis=0)

    lane = lax.broadcasted_iota(jnp.int32, (step, LANES), 1) % HEAD_DIM

    def body(place, carry):
        here = pl.ds(place * step, step)
        grad = dot(first_ref[here, :], side)
        for pair in range(part // LANES):
            lanes = slice(pair * LANES, (pair + 1) * LANES)
            inverse = rden_ref[here, lanes]
            scaled = grad[:, lanes] * inverse
            product = scaled * mixed_ref[here, lanes].astype(F32)
            high = product.astype(BF16)
            rest = (product - high.astype(F32)).astype(BF16)
            inner = dot(jnp.concatenate([high, rest], axis=1), group)
            slope = jnp.where(inverse < 1.0, -inner, 0.0)
            high = slope.astype(BF16).astype(F32)
            gn_ref[here, lanes] = scaled.astype(BF16)
            gd_ref[here, lanes] = jnp.where(
                lane == 0, high, jnp.where(lane == 1, slope - high, 0.0)
            ).astype(BF16)
        return carry

    lax.fori_loop(0, rows // step, body, 0)
    product_ref[:, :part] = dot_tn(first_ref[...], mixed_ref[...]).astype(BF16)
    row = lax.broadcasted_iota(jnp.int32, (8, width), 0)
    packed = jnp.where(row < 3, sum1_ref[...], pltpu.roll(sum2_ref[...], 3, 0))
    packed = jnp.where(row < 6, packed, 0.0)
    columns = jnp.concatenate([packed, jnp.zeros((LANES - 8, width), F32)], axis=0).T
    units = bias.shape[1]
    each = units // width
    if shard % 16 == 0:
        at = lax.broadcasted_iota(jnp.int32, (8, units), 0)
        both = jnp.where(at >= 6, bias, 0.0)
        turned = jnp.concatenate([both, jnp.zeros((LANES - 8, units), F32)], axis=0).T
        lane_at = lax.broadcasted_iota(jnp.int32, (shard, LANES), 1)
        for place in range(width // shard):
            piece = columns[place * shard : (place + 1) * shard]
            for turn in range(each):
                begin = (place * each + turn) * shard
                piece = jnp.where(lane_at == 6 + turn, turned[begin : begin + shard], piece)
            product_ref[place * shard : (place + 1) * shard, part:] = piece.astype(BF16)
    else:
        side_row = lax.broadcasted_iota(jnp.int32, (8, LANES), 0)
        turned = dot_tn(bias.astype(BF16), (side_row == 0).astype(F32).astype(BF16)).astype(BF16)
        lane_at = lax.broadcasted_iota(jnp.int32, (width, LANES), 1)
        for turn in range(each):
            columns = jnp.where(lane_at == 6 + turn, dot(turn_ref[turn], turned), columns)
        product_ref[:, part:] = columns.astype(BF16)
    emit(product_ref, pl.program_id(0), outs, coords)
    keep = same_head(2 * LANES, 2 * LANES)
    for pair in range(part // LANES):
        lanes = slice(pair * LANES, (pair + 1) * LANES)
        total = jnp.zeros((2 * LANES, 2 * LANES), F32)
        for place in range(rows // block):
            here = slice(place * block, (place + 1) * block)
            features = turned_features(sq_ref[here, lanes], cos_ref[here, :], sin_ref[here, :])
            state = dot_tn(
                features, jnp.concatenate([gn_ref[here, lanes], gd_ref[here, lanes]], axis=1)
            )
            state = jnp.where(keep, state, 0.0)
            st_ref[place, pair] = state.astype(BF16)
            total = total + state
        compact(total, packed_ref, tot_ref, pair, pl.program_id(0), False)


def unmix(
    coords, first, mixed, rden, sq, cosines, sines, w, sums1, sums2, turns, gbias, layout, block
):
    rows, width = first.shape
    groups, halves, shard, _ = w.shape
    part = width // halves
    pairs = width // LANES
    half = pairs // halves
    blocks = rows // block
    row_spec = pl.BlockSpec((rows, part), lambda t: (0, t))
    tile = part + LANES
    out_specs, out_shapes = piece_outputs(layout, tile, lambda t: layout[3] // tile - 1)
    units = gbias.shape[1] // halves
    full = jax.ShapeDtypeStruct((rows, width), BF16)
    return call(
        functools.partial(
            unmix_kernel, block=block, step=512, shard=layout[2]
        ),
        grid=(halves,),
        in_specs=[
            scalars(), whole((rows, width)), row_spec, row_spec, row_spec,
            whole((rows, LANES)), whole((rows, LANES)),
            pl.BlockSpec((groups, 1, shard, part), lambda t: (0, t, 0, 3)),
            whole((8, width)), whole((8, width)), whole(turns.shape),
        ]
        + [pl.BlockSpec((8, units), lambda t: (0, t))],
        out_specs=out_specs
        + [
            row_spec, row_spec,
            pl.BlockSpec((blocks, half, 2 * LANES, 2 * LANES), lambda t: (0, t, 0, 0)),
            whole((half + 1, 2 * LANES, LANES)),
        ],
        out_shape=out_shapes
        + [
            full, full,
            jax.ShapeDtypeStruct((blocks, pairs, 2 * LANES, 2 * LANES), BF16),
            jax.ShapeDtypeStruct((half + 1, 2 * LANES, LANES), BF16),
        ],
        scratch_shapes=[
            pltpu.VMEM((width, tile), BF16), pltpu.VMEM((half + 1, 2 * LANES, LANES), F32)
        ],
        compiler_params=params(),
        cost_estimate=cost(4 * rows * width * width, 16e6),
        name="unmix",
        near_in=(1, 4),
        near_out=(len(out_shapes), len(out_shapes) + 1),
    )(coords, first, mixed, rden, sq, cosines, sines, w, sums1, sums2, turns, gbias)


def unattend_kernel(
    sq_ref, sk_ref, v_ref, gn_ref, gd_ref, cm_ref, cos_ref, sin_ref, st_ref, in_ref, lt_ref, gq_ref,
    gk_ref, later_ref, *refs, start_pair
):
    query_ref, dk_ref, dv_ref = refs[-3:]
    blocks, block, _ = cm_ref.shape
    piece = min(PIECE, block)
    masks = [lane_mask(block, head) for head in range(2)]
    ones = jnp.ones((block, LANES), BF16)
    pair = start_pair + pl.program_id(0)
    each = in_ref.shape[0] - 1
    incoming = expand(in_ref, pair % each, pair // each, True)
    outgoing = expand(later_ref, pair % each, pair // each, False)
    for place in range(blocks):
        start = place * block
        all_here = slice(start, start + block)
        keys, values = sk_ref[all_here, :], v_ref[all_here, :]
        sides = jnp.concatenate([values, ones], axis=1)
        key_sides = [keys * mask for mask in masks]
        state = incoming
        for earlier in range(place):
            state = state + st_ref[earlier, 0].astype(F32)
        state = state.astype(BF16)
        grad_keys = [None] * (block // piece)
        grad_values = [None] * (block // piece)
        for low in range(0, block, piece):
            here = slice(start + low, start + low + piece)
            span = low + piece
            queries, grads, slopes = sq_ref[here, :], gn_ref[here, :], gd_ref[here, :]
            grad_queries = None
            for head in range(2):
                mask = masks[head][:piece]
                cm = cm_ref[place, low : low + piece, :span]
                masked_queries, masked_grads = queries * mask, grads * mask
                scores = dot_nt(masked_queries, keys[:span])
                weights = (scores * cm).astype(BF16)
                back = dot_nt(
                    jnp.concatenate([masked_grads, slopes * mask], axis=1), sides[:span]
                )
                back = (back * cm).astype(BF16)
                term = dot(back, key_sides[head][:span])
                grad_queries = term if grad_queries is None else grad_queries + term
                key_term = dot_tn(back, masked_queries)
                value_term = dot_tn(weights, masked_grads)
                for piece_at in range(span // piece):
                    at = slice(piece_at * piece, (piece_at + 1) * piece)
                    old = grad_keys[piece_at]
                    grad_keys[piece_at] = key_term[at] if old is None else old + key_term[at]
                    old = grad_values[piece_at]
                    grad_values[piece_at] = value_term[at] if old is None else old + value_term[at]
            far = dot_nt(jnp.concatenate([grads, slopes], axis=1), state)
            grad_queries = (
                grad_queries
                + far[:, :LANES] * cos_ref[here, :]
                + far[:, LANES:] * sin_ref[here, :]
            ) * gq_ref[here, :].astype(F32)
            query_ref[here, :] = grad_queries.astype(BF16)
        grad_keys = jnp.concatenate(grad_keys, axis=0)
        grad_values = jnp.concatenate(grad_values, axis=0)
        state = outgoing
        for later in range(place + 1, blocks):
            state = state + lt_ref[later, 0].astype(F32)
        state = state.astype(BF16)
        far = dot_nt(sides, state)
        grad_keys = (
            grad_keys
            + far[:, :LANES] * cos_ref[all_here, :]
            + far[:, LANES:] * sin_ref[all_here, :]
        ) * gk_ref[all_here, :].astype(F32)
        features = turned_features(keys, cos_ref[all_here, :], sin_ref[all_here, :])
        grad_values = grad_values + dot(features, state[:, :LANES])
        dk_ref[all_here, :] = grad_keys.astype(BF16)
        dv_ref[all_here, :] = grad_values.astype(BF16)


def unattend(
    sq, sk, v, gn, gd, cm, cosines, sines, states, incoming, later, slope_q, slope_k,
    later_in, start, count, partial
):
    rows, width = sq.shape
    blocks = cm.shape[0]
    spec = pl.BlockSpec((rows, LANES), lambda p: (0, start + p))
    state_spec = pl.BlockSpec((blocks, 1, 2 * LANES, 2 * LANES), lambda p: (0, start + p, 0, 0))
    full = jax.ShapeDtypeStruct((rows, width), BF16)
    return call(
        functools.partial(unattend_kernel, start_pair=start),
        grid=(count,),
        in_specs=[
            spec, spec, spec, spec, spec,
            whole(cm.shape), whole((rows, LANES)), whole((rows, LANES)),
            state_spec,
            whole(incoming.shape),
            state_spec, spec, spec, whole(later_in.shape),
        ]
        + [pl.BlockSpec(memory_space=pl.ANY)] * len(partial),
        out_specs=[spec, spec, spec],
        out_shape=[jax.ShapeDtypeStruct((rows, width), BF16), full, full],
        input_output_aliases={14 + at: at for at in range(len(partial))},
        compiler_params=params(),
        cost_estimate=cost(20e9, 20e6),
        name="unattend",
        near_in=(0, 1, 2, 3, 4, 14, 15, 16),
        near_out=(0, 1, 2),
    )(sq, sk, v, gn, gd, cm, cosines, sines, states, incoming, later, slope_q, slope_k, later_in, *partial)


def weights_kernel(coords_ref, x_ref, q_ref, k_ref, v_ref, edge_ref, *refs, shard):
    outs, product_ref = refs[:-1], refs[-1]
    coords = [coords_ref[place] for place in range(4)]
    rows, part = q_ref.shape
    width = x_ref.shape[1]
    ones = jnp.ones((rows, LANES), BF16)
    lane = lax.broadcasted_iota(jnp.int32, (part, LANES), 1)
    sums = jnp.zeros((part, LANES), F32)
    for place, ref in enumerate((q_ref, k_ref, v_ref)):
        at = slice(place * part, (place + 1) * part)
        product_ref[:, at] = dot_tn(x_ref[...], ref[...]).astype(BF16)
        sums = jnp.where(lane == place, dot_tn(ref[...], ones), sums)
    if shard % 16 == 0:
        edge = shard * part // width
        for place in range(width // shard):
            piece = jnp.concatenate(
                [sums[place * edge : (place + 1) * edge], jnp.zeros((shard - edge, LANES), F32)], axis=0
            )
            product_ref[place * shard : (place + 1) * shard, 3 * part :] = piece.astype(BF16)
    else:
        product_ref[:, 3 * part :] = dot(edge_ref[...], sums.astype(BF16)).astype(BF16)
    emit(product_ref, pl.program_id(0), outs, coords)


def weight_gradients(coords, x, q, k, v, edges, layout):
    rows, width = x.shape
    halves = layout[1]
    spec = pl.BlockSpec((rows, width // halves), lambda t: (0, t))
    out_specs, out_shapes = piece_outputs(layout, layout[3], lambda t: 0)
    return call(
        functools.partial(weights_kernel, shard=layout[2]),
        grid=(halves,),
        in_specs=[scalars(), whole((rows, width)), spec, spec, spec, whole(edges.shape)],
        out_specs=out_specs,
        out_shape=out_shapes,
        scratch_shapes=[pltpu.VMEM((width, layout[3]), BF16)],
        compiler_params=params(),
        cost_estimate=cost(2 * rows * width * 3 * width, 10e6),
        name="weight_gradients",
        near_in=(2, 3, 4),
    )(coords, x, q, k, v, edges)


def inputs_kernel(first_ref, q_ref, k_ref, v_ref, w_ref, out_ref):
    halves = w_ref.shape[1]
    width = first_ref.shape[1]
    part = width // halves
    total = first_ref[...]
    for half in range(halves):
        side = w_ref[:, half].reshape(width, 3 * part)
        at = slice(half * part, (half + 1) * part)
        joined = jnp.concatenate([q_ref[:, at], k_ref[:, at], v_ref[:, at]], axis=1)
        total = total + dot_nt(joined, side)
    out_ref[...] = total.astype(BF16)


def input_gradient(first, q, k, v, w, step):
    rows, width = first.shape
    groups, halves, shard, _ = w.shape
    part = width // halves
    spec = pl.BlockSpec((step, width), lambda i: (i, 0))
    return call(
        inputs_kernel,
        grid=(rows // step,),
        in_specs=[
            spec, spec, spec, spec,
            pl.BlockSpec((groups, halves, shard, 3 * part), lambda i: (0, 0, 0, 0)),
        ],
        out_specs=spec,
        out_shape=jax.ShapeDtypeStruct((rows, width), BF16),
        compiler_params=params(),
        cost_estimate=cost(2 * rows * width * 3 * width, 14e6),
        name="input_gradient",
        near_in=(1, 2, 3),
    )(first, q, k, v, w)


def moves():
    def table(change):
        pairs = []
        for source in range(32):
            z, y, c, x = source // 8, source // 4 % 2, source // 2 % 2, source % 2
            z, y, c, x = change(z, y, c, x)
            pairs.append((source, ((z * 2 + y) * 2 + c) * 2 + x))
        return pairs

    along = [table(lambda z, y, c, x, k=k: (z ^ k, y, c, x)) for k in range(4)]
    beside = table(lambda z, y, c, x: (z, y ^ c, c, x ^ 1 ^ c))
    across = table(lambda z, y, c, x: (z, y ^ 1 ^ c, c, x ^ c))
    core = table(lambda z, y, c, x: (z, y, c ^ 1, x))
    return along, beside, across, core


def add(left, right):
    return (left.astype(F32) + right.astype(F32)).astype(BF16)


def send(value, table, begin, end, axes=BOTH):
    value = after(value, *begin) if begin else value
    value = lax.ppermute(value, axes, table)
    return after(value, *end) if end else value


class Gather:
    def __init__(self, piece):
        self.tables = moves()
        self.held = piece

    def line(self, begin=(), end=()):
        parts = [send(self.held, self.tables[0][k], begin, end) for k in (1, 2, 3)]
        self.held = join([self.held] + parts)

    def line_parts(self, begin):
        self.held = self.held, [send(self.held, self.tables[0][k], begin, ()) for k in (1, 2, 3)]

    def beside(self, begin=(), end=()):
        self.held = jnp.concatenate([self.held, send(self.held, self.tables[1], begin, end)], axis=0)

    def across(self, begin=(), end=()):
        self.held = jnp.concatenate([self.held, send(self.held, self.tables[2], begin, end)], axis=0)

    def core(self, begin=(), end=()):
        return [self.held, send(self.held, self.tables[3], begin, end)]


class Sum:
    def __init__(self, own, other):
        self.tables = moves()
        self.kept, self.sent = own, other

    def fold(self, table, begin, end):
        arrived = send(self.sent, table, begin, end)
        size = self.kept.shape[0] // 2
        kept = add(self.kept[:size], arrived[:size])
        self.kept, self.sent = kept, add(self.kept[size:], arrived[size:])

    def both(self):
        return [self.kept, self.sent]

    def core(self, begin=(), end=()):
        self.fold(self.tables[3], begin, end)

    def across(self, begin=(), end=()):
        self.fold(self.tables[2], begin, end)

    def beside(self, begin=(), end=()):
        arrived = send(self.sent, self.tables[1], begin, end)
        self.parts = [add(self.kept[k], arrived[k]) for k in range(4)]

    def line(self, begin=(), end=()):
        parts = [send(self.parts[k], self.tables[0][k], begin, end) for k in (1, 2, 3)]
        total = self.parts[0].astype(F32)
        for part in parts:
            total = total + part.astype(F32)
        return total


def local(
    inputs, w_query, w_key, w_value, b_query, b_key, b_value, w_out, b_out, norm_gain, norm_shift,
    w_up, b_up, w_down, b_down, final_gain, final_shift, piece_starts, grad_output,
):
    rows, width = inputs.shape
    halves = lax.axis_size("tp")
    replicas = lax.axis_size("fsdp")
    length = rows * halves
    block = min(512, length)
    blocks = rows // block
    shard = width // replicas
    part = width // halves
    units = w_up.shape[1]
    me = lax.axis_index("tp")
    pieces = replicas == 16 and halves == 2 and shard % 16 == 0
    place = lax.axis_index("fsdp")
    coords = jnp.stack([place // 4, place // 2 % 2, place % 2, me]).astype(jnp.int32)

    def layout(columns):
        return replicas, halves, shard, columns, pieces

    places = me * rows + jnp.arange(rows, dtype=jnp.int32)
    flags = jnp.any(piece_starts[0][:, None] == (places // PIECE * PIECE)[None, :], axis=0)
    angle = 0.5 * jnp.pi / length * places.astype(F32)
    cosines, sines = jnp.cos(angle), jnp.sin(angle)
    at = jnp.arange(block, dtype=jnp.int32)
    allowed = (at[None, None, :] <= at[None, :, None]) | (
        (at[None, None, :] // PIECE == at[None, :, None] // PIECE)
        & flags.reshape(blocks, block)[:, :, None]
    )
    c, s = cosines.reshape(blocks, block), sines.reshape(blocks, block)
    cm = jnp.where(allowed, c[:, :, None] * c[:, None, :] + s[:, :, None] * s[:, None, :], 0.0)
    cosines = jnp.broadcast_to(cosines[:, None], (rows, LANES))
    sines = jnp.broadcast_to(sines[:, None], (rows, LANES))

    each, edge = units // width, shard // halves
    if pieces:
        edges, turns = jnp.zeros((8, LANES), BF16), jnp.zeros((1, 8, LANES), BF16)
    else:
        edges, turns = selectors(width, part, shard, edge, each)
    thins = (
        b_query, b_key, b_value, b_up, b_out, norm_gain, norm_shift, b_down, final_gain, final_shift
    )
    if pieces:
        attention_shard = pack(w_query, w_key, w_value, w_out.T, thins)
    else:
        columns = []
        for thin in thins:
            thin = jnp.pad(thin, (0, -thin.shape[0] % shard))
            columns.append(thin.reshape(-1, shard).T)
        columns = jnp.concatenate(columns, axis=1)
        columns = jnp.pad(columns, ((0, 0), (0, LANES - columns.shape[1])))
        attention_shard = jnp.concatenate([w_query, w_key, w_value, w_out.T, columns], axis=1)
    down_shard = w_down.T

    def gather_all(piece):
        everything = lax.all_gather(piece, BOTH, axis=0, tiled=False)
        everything = everything.reshape(replicas, halves, shard, piece.shape[1])
        return jnp.moveaxis(everything, 1, 0).reshape(1, halves, width, piece.shape[1])

    if pieces:
        first_chunk, up_chunk, down_chunk = Gather(attention_shard), Gather(w_up), Gather(down_shard)
        first_chunk.line([], [cm, cosines, sines, coords])
        four = first_chunk.held
        first_chunk.beside()
        up_chunk.line([four])
        first_chunk.across()
        sixteen = first_chunk.held
        four = up_chunk.held
        w_attention = first_chunk.core([four])
        up_chunk.beside([sixteen, four], w_attention)
        eight = up_chunk.held
        down_chunk.line_parts([sixteen, four])
        w_attention = [after(w_attention[0], eight), w_attention[1]]
    else:
        w_attention, w_lift, w_drop = [
            [gather_all(piece)] for piece in (attention_shard, w_up, down_shard)
        ]


    columns = 4 * part + LANES
    sq, sk, v, slope_q, slope_k, states, total, w_attention = project(
        coords, inputs, w_attention, columns, edges, cosines, sines, block, shard, halves
    )
    queries, there = sq, []
    if pieces:
        up_chunk.across([], [sq])
        down_chunk.held = join(
            [down_chunk.held[0]] + [after(part, sq) for part in down_chunk.held[1]]
        )
        there = [up_chunk.held, down_chunk.held]
        queries = after(sq, *there)
    num, den = attend(queries, sk, v, cm, cosines, sines, states)
    bias_up, vectors = unpack(after(w_attention, num), turns, shard, each)
    towards = [(i, i + 1) for i in range(halves - 1)]
    incoming = send(total, towards, there, [num, vectors], "tp")
    if pieces:
        w_lift = up_chunk.core(there, [num, vectors])
        down_chunk.beside(there, [num, vectors])
        there = [down_chunk.held, incoming, w_lift[1]]
        num = after(num, *there)
    mixed, rden, normal, scale, low = mix(
        num, den, sq, incoming, cosines, sines, w_attention, inputs, vectors, 512
    )
    if pieces:
        down_chunk.across(there, [low])
        there = [down_chunk.held]
        low = after(low, *there)
    act, slope, w_lift = lift(
        coords, low, w_lift, bias_up, units, 768, 3 if pieces else 0
    )
    if pieces:
        w_drop = down_chunk.core(there, [act])
    output, branch, second, sums_second, w_drop = drop(
        coords, act, w_drop, normal, vectors, grad_output, units, 256
    )

    gdown = wide_gradient(coords, branch, act, layout(units), units, 512, "down_gradient")
    gl, gbias_up = bend(branch, w_drop, after(slope, *gdown), units, 768)
    if pieces:
        down_sum = Sum(*gdown)
        down_sum.core([], [gl])
        second = after(second, *down_sum.both())
    first, first_low, sums_first = lower(gl, w_lift, second, normal, scale, vectors, units, 256)
    wide = units + part + LANES
    *gup, gn, gd, later, later_total = unmix(
        coords, first_low, mixed, rden, sq, cosines, sines, w_attention,
        sums_first, sums_second, turns, gbias_up, layout(wide), block,
    )
    there = []
    if pieces:
        down_sum.across([], [gn])
        there = down_sum.both()
    gup = wide_gradient(
        coords, after(low, *there, *gup), gl, layout(wide), units, 512, "up_gradient", gup
    )
    towards = [(i + 1, i) for i in range(halves - 1)]
    later_in = send(later_total, towards, there, gup, "tp")
    there = [later_in, *gup]
    gn = after(gn, *there)
    pairs = width // LANES
    partial = ()
    for turn, (begin, count) in enumerate(((0, pairs // 3), (pairs // 3, pairs - pairs // 3))):
        partial = unattend(
            sq, sk, v, gn, gd, cm, cosines, sines, states, incoming, later, slope_q, slope_k,
            later_in, begin, count, partial,
        )
        if pieces and turn == 0:
            up_sum = Sum(*gup)
            up_sum.core(there, partial)
            down_sum.beside(there, partial)
            there = [*up_sum.both(), *down_sum.parts]
            partial = after(tuple(partial), *there)
    query_low, key_low, value_low = partial
    if pieces:
        up_sum.across(there, [key_low])
        gdown = down_sum.line(there, [key_low])
        query_low = after(query_low, *up_sum.both(), gdown)
    gqkv = weight_gradients(
        coords, inputs, query_low, key_low, value_low, edges, layout(3 * part + LANES)
    )
    if pieces:
        up_sum.beside([], gqkv)
        rest_sum = Sum(*gqkv)
        rest_sum.core(up_sum.parts)
        rest_sum.across()
        first = after(first, *rest_sum.both())
        grad_inputs = input_gradient(first, query_low, key_low, value_low, w_attention, 256)
        gup = up_sum.line([], [*rest_sum.both(), grad_inputs])
        rest_sum.beside()
        rest = rest_sum.line()
    else:

        def scatter(grad):
            grad = jnp.moveaxis(grad.reshape(halves, replicas, shard, grad.shape[2]), 0, 1)
            grad = grad.reshape(replicas * halves, shard, grad.shape[3])
            return lax.psum_scatter(grad, BOTH, scatter_dimension=0, tiled=False).astype(F32)

        gdown, gup, rest = [scatter(grad[0]) for grad in (gdown, gup, gqkv)]
        grad_inputs = input_gradient(first, query_low, key_low, value_low, w_attention, 256)

    scaling = 1.0 / replicas
    gdown, gup, rest = gdown * scaling, gup * scaling, rest * scaling
    sums = gup[:, units + part :].T
    small = rest[:edge, 3 * part :].T
    return (
        output,
        grad_inputs,
        rest[:, :part],
        rest[:, part : 2 * part],
        rest[:, 2 * part : 3 * part],
        small[0],
        small[1],
        small[2],
        gup[:, units : units + part].T,
        sums[2],
        sums[0],
        sums[1],
        gup[:, :units],
        sums[6 : 6 + units // width].reshape(-1),
        gdown.T,
        sums[5],
        sums[3],
        sums[4],
    )


def solution(mesh):
    row = P(("fsdp", "tp"), None)
    split, turned = P("fsdp", "tp"), P("tp", "fsdp")
    thin, wide = P(("tp", "fsdp")), P("fsdp")
    return jax.shard_map(
        local,
        mesh=mesh,
        in_specs=(
            row, split, split, split, thin, thin, thin, turned, wide, wide, wide,
            split, thin, turned, wide, wide, wide, P("fsdp", None), row,
        ),
        out_specs=(
            row, row, split, split, split, thin, thin, thin, turned, wide, wide, wide,
            split, thin, turned, wide, wide, wide,
        ),
        check_vma=False,
    )
```

```python
import functools
import math

import jax
import jax.numpy as jnp
from jax import lax
from jax.experimental import pallas as pl
from jax.experimental.pallas import tpu as pltpu
from jax.sharding import PartitionSpec as P

HEAD_DIM = 64
PIECE = 256
LANES = 128
EPSILON = 1e-05
F32 = jnp.float32
BF16 = jnp.bfloat16
BOTH = ("fsdp", "tp")


def dot(left, right):
    return lax.dot_general(left, right, (((1,), (0,)), ((), ())), preferred_element_type=F32)


def dot_nt(left, right):
    return lax.dot_general(left, right, (((1,), (1,)), ((), ())), preferred_element_type=F32)


def dot_tn(left, right):
    return lax.dot_general(left, right, (((0,), (0,)), ((), ())), preferred_element_type=F32)


def flat(ref):
    value = ref[...]
    return value.reshape(value.shape[0] * value.shape[1] * value.shape[2], value.shape[3])


def lane_mask(rows, head, dtype=BF16):
    lane = lax.broadcasted_iota(jnp.int32, (rows, LANES), 1)
    return (lane // HEAD_DIM == head).astype(F32).astype(dtype)


def same_head(rows, columns):
    row = lax.broadcasted_iota(jnp.int32, (rows, columns), 0)
    lane = lax.broadcasted_iota(jnp.int32, (rows, columns), 1)
    return (row // HEAD_DIM) % 2 == (lane // HEAD_DIM) % 2


def same_rows(shape):
    row = lax.broadcasted_iota(jnp.int32, shape, 0)
    lane = lax.broadcasted_iota(jnp.int32, shape, 1)
    return (row // HEAD_DIM) % 2 == 0, lane


def compact(state, held_ref, packet_ref, place, half, spread):
    left, right = state[:, :LANES], state[:, LANES:]
    first, lane = same_rows(left.shape)
    low = lane < HEAD_DIM
    narrow = jnp.where(first, left, pltpu.roll(left, HEAD_DIM, 1))
    column = jnp.where(first, right, pltpu.roll(right, HEAD_DIM, 1))
    if not spread:
        column = column + pltpu.roll(column, LANES - 1, 1)
        column = jnp.where(lane == 0, column, 0.0)
        column = jnp.broadcast_to(jnp.sum(column, axis=1, keepdims=True), column.shape)
    count = packet_ref.shape[0] - 1
    column = jnp.where(lane == half * count + place, column, 0.0)

    @pl.when(half == 0)
    def _():
        held_ref[place] = narrow
        held_ref[count] = column if place == 0 else held_ref[count] + column

    @pl.when(half == 1)
    def _():
        turned = pltpu.roll(narrow, HEAD_DIM, 1)
        packet_ref[place] = jnp.where(low, held_ref[place], turned).astype(BF16)
        held_ref[count] = held_ref[count] + column
        if place == count - 1:
            packet_ref[count] = held_ref[count].astype(BF16)


def expand(packet_ref, place, half, spread):
    narrow = packet_ref[place].astype(F32)
    first, lane = same_rows(narrow.shape)
    low = lane < HEAD_DIM
    turned = pltpu.roll(narrow, HEAD_DIM, 1)
    here = jnp.where(half == 0, narrow, turned)
    there = jnp.where(half == 0, turned, narrow)
    own = first == low
    left = jnp.where(own, jnp.where(first, here, there), 0.0)
    count = packet_ref.shape[0] - 1
    column = packet_ref[count].astype(F32)
    column = jnp.sum(jnp.where(lane == half * count + place, column, 0.0), axis=1, keepdims=True)
    if not spread:
        own = jnp.logical_and(own, lane % HEAD_DIM == 0)
    right = jnp.where(own, jnp.broadcast_to(column, own.shape), 0.0)
    return jnp.concatenate([left, right], axis=1)


def turned_features(values, cosines, sines):
    wide = values.astype(F32)
    return jnp.concatenate([(wide * cosines).astype(BF16), (wide * sines).astype(BF16)], axis=1)


def slot(coords, z, y, c, x):
    across = jnp.where(c == 0, y ^ coords[1], x ^ coords[3])
    beside = jnp.where(c == 0, x ^ coords[1 + 2], y ^ coords[1])
    return across * 8 + beside * 4 + (z ^ coords[0])


def emit(product, half, outs, coords):
    if len(outs) == 1:
        outs[0][half] = product[...]
        return
    core = coords[2]
    shard = outs[0].shape[1]
    for group in range(product.shape[0] // (2 * shard)):
        z, y = group // 2, group % 2
        for out, c in zip(outs, (core, 1 - core)):
            begin = pl.multiple_of((2 * group + c) * shard, 16)
            out[slot(coords, z, y, c, half)] = product[pl.ds(begin, shard), :]


class Weights:
    def __init__(self, coords_ref, sources, held, out, sems, out_sems, halves):
        self.coords = [coords_ref[place] for place in range(4)]
        self.sources, self.held, self.out = sources, held, out
        self.sems, self.out_sems, self.halves = sems, out_sems, halves

    def copies(self, place):
        half = self.halves[place]
        if len(self.sources) == 1:
            return [
                pltpu.make_async_copy(
                    self.sources[0].at[0, half], self.held.at[place], self.sems.at[place, 0]
                )
            ]
        copies = []
        shard = self.sources[0].shape[1]
        for side, ref in enumerate(self.sources):
            c = self.coords[2] if side == 0 else 1 - self.coords[2]
            for group in range(8):
                z, y = group // 2, group % 2
                begin = pl.multiple_of((2 * group + c) * shard, 16)
                copies.append(
                    pltpu.make_async_copy(
                        ref.at[slot(self.coords, z, y, c, half)],
                        self.held.at[place, pl.ds(begin, shard), :],
                        self.sems.at[place, side * 8 + group],
                    )
                )
        return copies

    def start(self, place):
        for copy in self.copies(place):
            copy.start()

    def ready(self, place):
        for copy in self.copies(place):
            copy.wait()
        self.leaving(place).start()

    def leaving(self, place):
        return pltpu.make_async_copy(
            self.held.at[place], self.out.at[0, place], self.out_sems.at[place]
        )

    def left(self, place):
        self.leaving(place).wait()

    @staticmethod
    def scratch(halves, width, columns):
        return [
            pltpu.VMEM((halves, width, columns), BF16),
            pltpu.SemaphoreType.DMA((halves, 16)),
            pltpu.SemaphoreType.DMA((halves,)),
        ]


def anywhere(count):
    return [pl.BlockSpec(memory_space=pl.ANY)] * count


def scalars():
    return pl.BlockSpec(memory_space=pltpu.SMEM)


def params(megabytes=32):
    return pltpu.CompilerParams(vmem_limit_bytes=megabytes * 1024 * 1024)


def call(kernel, *, out_shape, near_in=(), near_out=(), least=65536, **options):
    shapes = list(out_shape) if isinstance(out_shape, (list, tuple)) else [out_shape]

    def large(value):
        return math.prod(value.shape) * value.dtype.itemsize > least

    placed = [
        pltpu.HBM(shape.shape, shape.dtype) if large(shape) and at not in near_out else shape
        for at, shape in enumerate(shapes)
    ]
    function = pl.pallas_call(
        kernel, out_shape=placed if isinstance(out_shape, (list, tuple)) else placed[0], **options
    )

    def run(*operands):
        count = len(operands)
        near = {at % count for at in near_in}
        return function(
            *[
                pltpu.with_memory_space_constraint(value, pltpu.HBM)
                if large(value) and at not in near
                else value
                for at, value in enumerate(operands)
            ]
        )

    return run


def whole(shape):
    zeros = (0,) * len(shape)
    return pl.BlockSpec(shape, lambda *_: zeros)


def cost(flops, moved):
    return pl.CostEstimate(flops=int(flops), bytes_accessed=int(moved), transcendentals=0)


def after(value, *others):
    return lax.optimization_barrier((value, others))[0]


def pack_kernel(*refs):
    q_ref, k_ref, v_ref, out_ref = refs[:4]
    thins = refs[4:-1]
    first_ref = refs[-1]
    shard, part = q_ref.shape

    def chosen(columns, start):
        row = lax.broadcasted_iota(jnp.int32, (shard, columns), 0)
        column = lax.broadcasted_iota(jnp.int32, (shard, columns), 1)
        return (row + start == column).astype(F32).astype(BF16)

    for place, ref in enumerate((q_ref, k_ref, v_ref, out_ref)):
        first_ref[:, place * part : (place + 1) * part] = ref[...]
    columns = jnp.zeros((shard, LANES), F32)
    lane = 0
    for ref in thins:
        size = ref.shape[1]
        for start in range(0, size, shard):
            row = lax.broadcasted_iota(jnp.int32, (LANES, size), 0)
            spread = jnp.where(row == lane, ref[...].astype(F32), 0.0).astype(BF16)
            columns = columns + dot_nt(chosen(size, start), spread)
            lane += 1
    first_ref[:, 4 * part :] = columns.astype(BF16)


def pack(q, k, v, out, thins):
    shard, part = q.shape
    return call(
        pack_kernel,
        out_shape=jax.ShapeDtypeStruct((shard, 4 * part + LANES), BF16),
        compiler_params=params(),
        cost_estimate=cost(1e8, 1e6),
        name="pack",
        least=0,
    )(q, k, v, out, *[thin.reshape(1, -1) for thin in thins])


def deal(columns, shard, size, turns):
    count = columns.shape[0] // shard
    runs = []
    for place in range(count):
        piece = columns[place * shard : place * shard + size]
        for turn in range(turns):
            runs.append(pltpu.roll(piece, LANES - turn, 1) if turn else piece)
    return jnp.concatenate(runs, axis=0)


def selectors_kernel(edge_ref, turn_ref, *, shard, edge, each):
    width, part = edge_ref.shape
    row = lax.broadcasted_iota(jnp.int32, (width, part), 0)
    column = lax.broadcasted_iota(jnp.int32, (width, part), 1)
    chosen = (row % shard < edge) & (row // shard * edge + row % shard == column)
    edge_ref[...] = chosen.astype(F32).astype(BF16)
    row = lax.broadcasted_iota(jnp.int32, (width, LANES), 0)
    source = row // shard * (each * shard) + row % shard
    lane = lax.broadcasted_iota(jnp.int32, (width, LANES), 1)
    for turn in range(each):
        for begin in range(0, each * width, LANES):
            chosen = source + (turn * shard - begin) == lane
            turn_ref[turn, :, begin : begin + LANES] = chosen.astype(F32).astype(BF16)


def selectors(width, part, shard, edge, each):
    return call(
        functools.partial(selectors_kernel, shard=shard, edge=edge, each=each),
        out_shape=[
            jax.ShapeDtypeStruct((width, part), BF16),
            jax.ShapeDtypeStruct((each, width, each * width), BF16),
        ],
        compiler_params=params(),
        cost_estimate=cost(1e8, 1e6),
        name="selectors",
    )()


def unpack_kernel(thin_ref, turn_ref, up_ref, vec_ref, *, shard, each):
    halves = thin_ref.shape[1]
    for half in range(halves):
        thin = thin_ref[0, half]
        if shard % 16 == 0:
            turned = deal(thin.astype(F32), shard, shard, each).T
            up_ref[half] = turned[0:8]
            continue
        rows = jnp.zeros((8, turn_ref.shape[2]), F32)
        for turn in range(each):
            picked = dot_tn(thin, turn_ref[turn])
            rows = rows + picked[3 + turn : 4 + turn]
        up_ref[half] = rows
    turned = thin_ref[0, 0].astype(F32).T
    vec_ref[...] = turned[3 + each : 11 + each]


def unpack(w, turns, shard, each):
    _, halves, width, columns = w.shape
    return call(
        functools.partial(unpack_kernel, shard=shard, each=each),
        grid=(1,),
        in_specs=[
            pl.BlockSpec((1, halves, width, LANES), lambda i: (0, 0, 0, columns // LANES - 1)),
            whole(turns.shape),
        ],
        out_specs=[whole((halves, 8, each * width)), whole((8, width))],
        out_shape=[
            jax.ShapeDtypeStruct((halves, 8, each * width), F32),
            jax.ShapeDtypeStruct((8, width), F32),
        ],
        compiler_params=params(),
        cost_estimate=cost(1e8, 1e6),
        name="unpack",
    )(w, turns)


def join_kernel(*refs):
    for place, ref in enumerate(refs[:-1]):
        refs[-1][place] = ref[...]


def join(parts):
    return call(
        join_kernel,
        out_shape=jax.ShapeDtypeStruct((len(parts),) + parts[0].shape, parts[0].dtype),
        compiler_params=params(),
        cost_estimate=cost(0, 1e6),
        name="join",
        least=0,
    )(*parts)


def project_kernel(
    coords_ref, *refs, block, step, shard, halves
):
    sources, refs = refs[: len(refs) - 15], refs[len(refs) - 15 :]
    x_ref, edge_ref, cos_ref, sin_ref, sq_ref, sk_ref, v_ref, gq_ref, gk_ref, st_ref, tot_ref = refs[:11]
    sources, out_ref = sources[:-1], sources[-1]
    packed_ref, held_ref, sems, out_sems = refs[11:]
    rows = x_ref.shape[0]
    part = sq_ref.shape[1]
    now = pl.program_id(0)
    weights = Weights(coords_ref, sources, held_ref, out_ref, sems, out_sems, range(halves))

    @pl.when(now == 0)
    def _():
        for half in range(halves):
            weights.start(half)

    for half in range(halves):

        @pl.when(now == half)
        def _():
            weights.ready(half)

    columns = held_ref.shape[2]
    thin = held_ref[now, :, columns - LANES :]
    if shard % 16 == 0:
        biases = deal(thin.astype(F32), shard, shard * part // x_ref.shape[1], 1).T
    else:
        biases = dot_tn(thin, edge_ref[...])

    def body(index, carry):
        here = pl.ds(index * step, step)
        sums = dot(x_ref[here, :], held_ref[now, :, : 3 * part])
        for place, (feature_ref, slope_ref) in enumerate(((sq_ref, gq_ref), (sk_ref, gk_ref))):
            value = sums[:, place * part : (place + 1) * part] + biases[place : place + 1]
            positive = jnp.maximum(value, 0.0) + jnp.log1p(jnp.exp(-jnp.abs(value)))
            feature_ref[here, :] = positive.astype(BF16)
            slope_ref[here, :] = jax.nn.sigmoid(value).astype(BF16)
        v_ref[here, :] = (sums[:, 2 * part :] + biases[2:3]).astype(BF16)
        return carry

    lax.fori_loop(0, rows // step, body, 0)
    keep = same_head(2 * LANES, 2 * LANES)
    ones = jnp.ones((block, LANES), BF16)
    for pair in range(part // LANES):
        lanes = slice(pair * LANES, (pair + 1) * LANES)
        total = jnp.zeros((2 * LANES, 2 * LANES), F32)
        for place in range(rows // block):
            here = slice(place * block, (place + 1) * block)
            features = turned_features(sk_ref[here, lanes], cos_ref[here, :], sin_ref[here, :])
            state = dot_tn(features, jnp.concatenate([v_ref[here, lanes], ones], axis=1))
            state = jnp.where(keep, state, 0.0)
            st_ref[place, pair] = state.astype(BF16)
            total = total + state
        compact(total, packed_ref, tot_ref, pair, pl.program_id(0), True)

    @pl.when(now == halves - 1)
    def _():
        for half in range(halves):
            weights.left(half)


def project(coords, x, sources, columns, edges, cosines, sines, block, shard, halves):
    rows, width = x.shape
    part = width // halves
    pairs = width // LANES
    half = pairs // halves
    blocks = rows // block
    row_spec = pl.BlockSpec((rows, part), lambda t: (0, t))
    full = jax.ShapeDtypeStruct((rows, width), BF16)

    def kernel(coords_ref, *refs):
        count = len(sources)
        others, outs, scratch = refs[count : count + 4], refs[count + 4 : -4], refs[-4:]
        project_kernel(
            coords_ref, *refs[:count], outs[-1], *others, *outs[:-1], *scratch,
            block=block, step=rows, shard=shard, halves=halves,
        )

    return call(
        kernel,
        grid=(halves,),
        in_specs=[scalars()]
        + anywhere(len(sources))
        + [
            whole((rows, width)), whole(edges.shape), whole((rows, LANES)), whole((rows, LANES)),
        ],
        out_specs=[
            row_spec, row_spec, row_spec, row_spec, row_spec,
            pl.BlockSpec((blocks, half, 2 * LANES, 2 * LANES), lambda t: (0, t, 0, 0)),
            whole((half + 1, 2 * LANES, LANES)),
        ]
        + anywhere(1),
        out_shape=[
            full, full, full, full, full,
            jax.ShapeDtypeStruct((blocks, pairs, 2 * LANES, 2 * LANES), BF16),
            jax.ShapeDtypeStruct((half + 1, 2 * LANES, LANES), BF16),
            jax.ShapeDtypeStruct((1, halves, width, columns), BF16),
        ],
        scratch_shapes=[pltpu.VMEM((half + 1, 2 * LANES, LANES), F32)]
        + Weights.scratch(halves, width, columns),
        compiler_params=params(),
        cost_estimate=cost(2 * rows * width * 3 * width, 16e6),
        name="project",
        near_out=(0, 1, 2),
    )(coords, *sources, x, edges, cosines, sines)


def attend_kernel(sq_ref, sk_ref, v_ref, cm_ref, cos_ref, sin_ref, st_ref, num_ref, den_ref):
    blocks, block, _ = cm_ref.shape
    piece = min(PIECE, block)
    masks = [lane_mask(block, head) for head in range(2)]
    for place in range(blocks):
        start = place * block
        keys = sk_ref[start : start + block, :]
        values = v_ref[start : start + block, :]
        sides = [jnp.concatenate([values * mask, mask], axis=1) for mask in masks]
        for low in range(0, block, piece):
            here = slice(start + low, start + low + piece)
            span = low + piece
            queries = sq_ref[here, :]
            sums = None
            for mask, side in zip(masks, sides):
                scores = dot_nt(queries * mask[:piece], keys[:span])
                weights = (scores * cm_ref[place, low : low + piece, :span]).astype(BF16)
                term = dot(weights, side[:span])
                sums = term if sums is None else sums + term
            for earlier in range(place):
                sums = sums + dot(
                    turned_features(queries, cos_ref[here, :], sin_ref[here, :]), st_ref[earlier, 0]
                )
            num_ref[here, :] = sums[:, :LANES]
            den_ref[here, :] = sums[:, LANES:]


def attend(sq, sk, v, cm, cosines, sines, states):
    rows, width = sq.shape
    pairs = width // LANES
    blocks = cm.shape[0]
    spec = pl.BlockSpec((rows, LANES), lambda p: (0, p))
    full = jax.ShapeDtypeStruct((rows, width), F32)
    return call(
        attend_kernel,
        grid=(pairs,),
        in_specs=[
            spec, spec, spec,
            whole(cm.shape), whole((rows, LANES)), whole((rows, LANES)),
            pl.BlockSpec((blocks, 1, 2 * LANES, 2 * LANES), lambda p: (0, p, 0, 0)),
        ],
        out_specs=[spec, spec],
        out_shape=[full, full],
        compiler_params=params(),
        cost_estimate=cost(8e9, 14e6),
        name="attend",
        near_in=(0, 1, 2),
        near_out=(0, 1),
    )(sq, sk, v, cm, cosines, sines, states)


def norm_rows(values):
    average = jnp.mean(values, axis=1, keepdims=True)
    centred = values - average
    scale = lax.rsqrt(jnp.mean(centred * centred, axis=1, keepdims=True) + EPSILON)
    return centred * scale, scale


def mix_kernel(
    num_ref, den_ref, sq_ref, in_ref, cos_ref, sin_ref, w_ref, x_ref, vec_ref,
    mixed_ref, rden_ref, normal_ref, scale_ref, low_ref, wide_ref,
):
    pairs = wide_ref.shape[0]
    halves = w_ref.shape[1]
    rows, width = x_ref.shape
    part = width // halves

    @pl.when(pl.program_id(0) == 0)
    def _():
        for pair in range(pairs):
            place, half = pair % (pairs // halves), pair // (pairs // halves)
            wide_ref[pair] = expand(in_ref, place, half, True).astype(BF16)

    for pair in range(pairs):
        lanes = slice(pair * LANES, (pair + 1) * LANES)
        sums = dot(turned_features(sq_ref[:, lanes], cos_ref[...], sin_ref[...]), wide_ref[pair])
        denominator = den_ref[:, lanes] + sums[:, LANES:]
        inverse = 1.0 / jnp.maximum(denominator, 1.0)
        rden_ref[:, lanes] = jnp.where(denominator > 1.0, inverse, -1.0).astype(BF16)
        mixed_ref[:, lanes] = ((num_ref[:, lanes] + sums[:, :LANES]) * inverse).astype(BF16)
    total = x_ref[...].astype(F32) + vec_ref[0:1, :]
    for half in range(halves):
        side = w_ref[:, half]
        side = side.reshape(width, part)
        total = total + dot_nt(mixed_ref[:, half * part : (half + 1) * part], side)
    normal, scale = norm_rows(total)
    normal_ref[...] = normal
    scale_ref[...] = jnp.broadcast_to(scale, scale_ref.shape)
    low_ref[...] = (normal * vec_ref[1:2, :] + vec_ref[2:3, :]).astype(BF16)


def mix(num, den, sq, incoming, cosines, sines, w, x, vectors, step):
    rows, width = x.shape
    groups, halves, shard, _ = w.shape
    part = width // halves
    pairs = width // LANES
    wide = pl.BlockSpec((step, width), lambda i: (i, 0))
    thin = pl.BlockSpec((step, LANES), lambda i: (i, 0))
    return call(
        mix_kernel,
        grid=(rows // step,),
        in_specs=[
            wide, wide, wide, whole(incoming.shape), thin, thin,
            pl.BlockSpec((groups, halves, shard, part), lambda i: (0, 0, 0, 3)),
            wide, whole(vectors.shape),
        ],
        out_specs=[wide, wide, wide, thin, wide],
        out_shape=[
            jax.ShapeDtypeStruct((rows, width), BF16),
            jax.ShapeDtypeStruct((rows, width), BF16),
            jax.ShapeDtypeStruct((rows, width), F32),
            jax.ShapeDtypeStruct((rows, LANES), F32),
            jax.ShapeDtypeStruct((rows, width), BF16),
        ],
        scratch_shapes=[pltpu.VMEM((pairs, 2 * LANES, 2 * LANES), BF16)],
        compiler_params=params(),
        cost_estimate=cost(2 * rows * width * width * 2, 20e6),
        name="mix",
        near_in=(0, 1, 2),
        near_out=(2, 4),
    )(num, den, sq, incoming, cosines, sines, w, x, vectors)


def norm_back(upstream, normal, scale, gain):
    scaled = upstream * gain
    inner = (
        scaled
        - jnp.mean(scaled, axis=1, keepdims=True)
        - normal * jnp.mean(scaled * normal, axis=1, keepdims=True)
    )
    return inner * scale


def lift_kernel(coords_ref, *refs, step, row, halves):
    sources, refs = refs[:-8], refs[-8:]
    low_ref, bias_ref, act_ref, slope_ref, out_ref, held_ref, sems, out_sems = refs
    tile = act_ref.shape[1]
    now = pl.program_id(0)
    tiles = pl.num_programs(0) // halves
    weights = Weights(coords_ref, sources, held_ref, out_ref, sems, out_sems, range(halves))

    @pl.when(now == 0)
    def _():
        for half in range(halves):
            weights.start(half)

    for half in range(halves):

        @pl.when(now == half * tiles)
        def _():
            weights.ready(half)

    begin = pl.multiple_of(now % tiles * tile, tile)
    up = held_ref[now // tiles, :, pl.ds(begin, tile)]

    def body(place, carry):
        here = pl.ds(place * step, step)
        lifted = dot(low_ref[here, :], up) + bias_ref[0, row : row + 1, :]
        share = 0.5 + 0.5 * lax.erf(lifted * math.sqrt(0.5))
        bell = jnp.exp(-0.5 * lifted * lifted) * (1.0 / math.sqrt(2.0 * math.pi))
        act_ref[here, :] = (lifted * share).astype(BF16)
        slope_ref[here, :] = (share + lifted * bell).astype(BF16)
        return carry

    lax.fori_loop(0, low_ref.shape[0] // step, body, 0, unroll=True)

    @pl.when(now == pl.num_programs(0) - 1)
    def _():
        for half in range(halves):
            weights.left(half)


def lift(coords, low, sources, bias, units, tile, row):
    rows, width = low.shape
    halves = bias.shape[0]
    tiles = units // tile
    unit_spec = pl.BlockSpec((rows, tile), lambda i: (0, i))
    shape = jax.ShapeDtypeStruct((rows, halves * units), BF16)
    return call(
        functools.partial(lift_kernel, step=256, row=row, halves=halves),
        grid=(halves * tiles,),
        in_specs=[scalars()]
        + anywhere(len(sources))
        + [whole((rows, width)), pl.BlockSpec((1, 8, tile), lambda i: (i // tiles, 0, i % tiles))],
        out_specs=[unit_spec, unit_spec] + anywhere(1),
        out_shape=[shape, shape, jax.ShapeDtypeStruct((1, halves, width, units), BF16)],
        scratch_shapes=Weights.scratch(halves, width, units),
        compiler_params=params(),
        cost_estimate=cost(2 * rows * width * halves * units, 20e6),
        name="lift",
        near_in=(-2,),
        near_out=(0, 1),
    )(coords, *sources, low, bias)


def in_turn(product, finish, total_ref):
    now = pl.program_id(0)
    last = pl.num_programs(0) - 1

    @pl.when(now == 0)
    def _():
        total_ref[0] = product(True)

    @pl.when((now > 0) & (now < last))
    def _():
        finish(total_ref[(now - 1) % 2])
        total_ref[now % 2] = product()

    @pl.when(now == last)
    def _():
        finish(total_ref[(now - 1) % 2])


def drop_kernel(coords_ref, *refs, halves):
    sources, act_ref, refs = refs[:-12], refs[-12], refs[-11:]
    normal_ref, vec_ref, grad_ref, out_ref, branch_ref, sum_ref = refs[:6]
    whole_ref, held_ref, sems, out_sems, total_ref = refs[6:]
    weights = Weights(coords_ref, sources, held_ref, whole_ref, sems, out_sems, range(halves))
    units = held_ref.shape[2]

    @pl.when(pl.program_id(0) == 0)
    def _():
        sum_ref[...] = jnp.zeros_like(sum_ref)
        for half in range(halves):
            weights.start(half)

    def product(fresh=False):
        total = None
        for half in range(halves):
            if fresh:
                weights.ready(half)
            term = dot_nt(act_ref[:, half * units : (half + 1) * units], held_ref[half])
            total = term if total is None else total + term
        return total

    def finish(total):
        total = total + normal_ref[...] * vec_ref[1:2, :] + vec_ref[2:3, :] + vec_ref[3:4, :]
        normal, scale = norm_rows(total)
        gain = vec_ref[4:5, :]
        out_ref[...] = (normal * gain + vec_ref[5:6, :]).astype(BF16)
        upstream = grad_ref[...].astype(F32)
        second = norm_back(upstream, normal, scale, gain)
        branch_ref[...] = second.astype(BF16)
        sum_ref[0:1, :] += jnp.sum(upstream * normal, axis=0, keepdims=True)
        sum_ref[1:2, :] += jnp.sum(upstream, axis=0, keepdims=True)
        sum_ref[2:3, :] += jnp.sum(second, axis=0, keepdims=True)

    in_turn(product, finish, total_ref)

    @pl.when(pl.program_id(0) == pl.num_programs(0) - 1)
    def _():
        for half in range(halves):
            weights.left(half)


def drop(coords, act, sources, normal, vectors, grad, units, step):
    rows, width = normal.shape
    halves = act.shape[1] // units
    steps = rows // step
    wide = pl.BlockSpec((step, width), lambda i: (jnp.maximum(i - 1, 0), 0))
    return call(
        functools.partial(drop_kernel, halves=halves),
        grid=(steps + 1,),
        in_specs=[scalars()]
        + anywhere(len(sources))
        + [
            pl.BlockSpec((step, halves * units), lambda i: (jnp.minimum(i, steps - 1), 0)),
            wide, whole(vectors.shape), wide,
        ],
        out_specs=[wide, wide, whole((8, width))] + anywhere(1),
        out_shape=[
            jax.ShapeDtypeStruct((rows, width), BF16),
            jax.ShapeDtypeStruct((rows, width), BF16),
            jax.ShapeDtypeStruct((8, width), F32),
            jax.ShapeDtypeStruct((1, halves, width, units), BF16),
        ],
        scratch_shapes=Weights.scratch(halves, width, units) + [pltpu.VMEM((2, step, width), F32)],
        compiler_params=params(),
        cost_estimate=cost(2 * rows * width * halves * units, 20e6),
        name="drop",
        near_in=(-4, -3),
        near_out=(1,),
    )(coords, *sources, act, normal, vectors, grad)


def piece_outputs(layout, tile, index_map):
    replicas, halves, shard, columns, pieces = layout[:5]
    if pieces:
        count = replicas * halves // 2
        spec = pl.BlockSpec((count, shard, tile), lambda *at: (0, 0, index_map(*at)))
        shape = jax.ShapeDtypeStruct((count, shard, columns), BF16)
        return [spec, spec], [shape, shape]
    width = replicas * shard
    spec = pl.BlockSpec((halves, width, tile), lambda *at: (0, 0, index_map(*at)))
    return [spec], [jax.ShapeDtypeStruct((halves, width, columns), BF16)]


def wide_gradient_kernel(coords_ref, left_ref, *refs, halves, partial):
    rights, product_ref = refs[:halves], refs[-1]
    outs = refs[(len(refs) - 1 + halves) // 2 : -1] if partial else refs[halves:-1]
    coords = [coords_ref[place] for place in range(4)]
    for half, right_ref in enumerate(rights):
        product_ref[...] = dot_tn(left_ref[...], right_ref[...]).astype(BF16)
        emit(product_ref, half, outs, coords)


def wide_gradient(coords, left, right, layout, units, tile, name, partial=()):
    rows, width = left.shape
    halves = layout[1]
    tiles = units // tile
    out_specs, out_shapes = piece_outputs(layout, tile, lambda j: j)
    return call(
        functools.partial(wide_gradient_kernel, halves=halves, partial=bool(partial)),
        grid=(tiles,),
        in_specs=[scalars(), whole((rows, width))]
        + [
            pl.BlockSpec((rows, tile), lambda j, half=half: (0, half * tiles + j))
            for half in range(halves)
        ]
        + anywhere(len(partial)),
        out_specs=out_specs,
        out_shape=out_shapes,
        input_output_aliases={2 + halves + at: at for at in range(len(partial))},
        scratch_shapes=[pltpu.VMEM((width, tile), BF16)],
        compiler_params=params(),
        cost_estimate=cost(2 * rows * width * halves * units, 18e6),
        name=name,
        near_in=(1, 2, 3),
    )(coords, left, *([right] * halves), *partial)


def bend_kernel(branch_ref, down_ref, slope_ref, gl_ref, gbias_ref, *, step):
    down = down_ref[0, 0]
    gbias_ref[...] = jnp.zeros_like(gbias_ref)

    def body(place, carry):
        here = pl.ds(place * step, step)
        slope = dot(branch_ref[here, :], down) * slope_ref[here, :].astype(F32)
        gbias_ref[0:1, :] += jnp.sum(slope, axis=0, keepdims=True)
        gl_ref[here, :] = slope.astype(BF16)
        return carry

    lax.fori_loop(0, branch_ref.shape[0] // step, body, 0, unroll=True)


def bend(branch, w, slope, units, tile):
    rows, width = branch.shape
    halves = w.shape[1]
    tiles = units // tile
    unit_spec = pl.BlockSpec((rows, tile), lambda i: (0, i))
    return call(
        functools.partial(bend_kernel, step=256),
        grid=(halves * tiles,),
        in_specs=[
            whole((rows, width)),
            pl.BlockSpec((1, 1, width, tile), lambda i: (0, i // tiles, 0, i % tiles)),
            unit_spec,
        ],
        out_specs=[unit_spec, pl.BlockSpec((8, tile), lambda i: (0, i))],
        out_shape=[
            jax.ShapeDtypeStruct(slope.shape, BF16),
            jax.ShapeDtypeStruct((8, halves * units), F32),
        ],
        compiler_params=params(),
        cost_estimate=cost(2 * rows * width * halves * units, 20e6),
        name="bend",
        near_in=(0, 2),
        near_out=(0,),
    )(branch, w, slope)


def lower_kernel(
    gl_ref, up_ref, branch_ref, normal_ref, scale_ref, vec_ref, firstlow_ref, sum_ref,
    total_ref,
):
    halves, units = up_ref.shape[1], up_ref.shape[3]

    @pl.when(pl.program_id(0) == 0)
    def _():
        sum_ref[...] = jnp.zeros_like(sum_ref)

    def product(fresh=False):
        total = None
        for half in range(halves):
            term = dot_nt(gl_ref[:, half * units : (half + 1) * units], up_ref[0, half])
            total = term if total is None else total + term
        return total

    def finish(total):
        upstream = branch_ref[...].astype(F32) + total
        normal = normal_ref[...]
        first = norm_back(upstream, normal, scale_ref[:, 0:1], vec_ref[1:2, :])
        firstlow_ref[...] = first.astype(BF16)
        sum_ref[0:1, :] += jnp.sum(upstream * normal, axis=0, keepdims=True)
        sum_ref[1:2, :] += jnp.sum(upstream, axis=0, keepdims=True)
        sum_ref[2:3, :] += jnp.sum(first, axis=0, keepdims=True)

    in_turn(product, finish, total_ref)


def lower(gl, w, branch, normal, scale, vectors, units, step):
    rows, width = branch.shape
    steps = rows // step
    wide = pl.BlockSpec((step, width), lambda i: (jnp.maximum(i - 1, 0), 0))
    return call(
        lower_kernel,
        grid=(steps + 1,),
        in_specs=[
            pl.BlockSpec((step, gl.shape[1]), lambda i: (jnp.minimum(i, steps - 1), 0)),
            whole(w.shape), wide, wide,
            pl.BlockSpec((step, LANES), lambda i: (jnp.maximum(i - 1, 0), 0)),
            whole(vectors.shape),
        ],
        out_specs=[wide, whole((8, width))],
        out_shape=[
            jax.ShapeDtypeStruct((rows, width), BF16),
            jax.ShapeDtypeStruct((8, width), F32),
        ],
        scratch_shapes=[pltpu.VMEM((2, step, width), F32)],
        compiler_params=params(),
        cost_estimate=cost(2 * rows * width * gl.shape[1], 20e6),
        name="lower",
        near_in=(0, 2, 3),
        near_out=(0,),
    )(gl, w, branch, normal, scale, vectors)


def unmix_kernel(
    coords_ref, first_ref, mixed_ref, rden_ref, sq_ref, cos_ref, sin_ref, w_ref,
    sum1_ref, sum2_ref, turn_ref, *refs, block, step, shard
):
    bias = jnp.broadcast_to(refs[0][0:1, :], refs[0].shape)
    refs = refs[1:]
    outs = refs[:-6]
    gn_ref, gd_ref, st_ref, tot_ref, product_ref, packed_ref = refs[-6:]
    coords = [coords_ref[place] for place in range(4)]
    rows, width = first_ref.shape
    part = mixed_ref.shape[1]
    side = flat(w_ref)
    group_row = lax.broadcasted_iota(jnp.int32, (LANES, LANES), 0)
    group_lane = lax.broadcasted_iota(jnp.int32, (LANES, LANES), 1)
    group = (group_row // HEAD_DIM == group_lane // HEAD_DIM).astype(F32).astype(BF16)
    group = jnp.concatenate([group, group], axis=0)

    lane = lax.broadcasted_iota(jnp.int32, (step, LANES), 1) % HEAD_DIM

    def body(place, carry):
        here = pl.ds(place * step, step)
        grad = dot(first_ref[here, :], side)
        for pair in range(part // LANES):
            lanes = slice(pair * LANES, (pair + 1) * LANES)
            signed = rden_ref[here, lanes].astype(F32)
            inverse = jnp.abs(signed)
            scaled = grad[:, lanes] * inverse
            product = scaled * mixed_ref[here, lanes].astype(F32)
            high = product.astype(BF16)
            rest = (product - high.astype(F32)).astype(BF16)
            inner = dot(jnp.concatenate([high, rest], axis=1), group)
            slope = jnp.where(signed > 0.0, -inner, 0.0)
            high = slope.astype(BF16).astype(F32)
            gn_ref[here, lanes] = scaled.astype(BF16)
            gd_ref[here, lanes] = jnp.where(
                lane == 0, high, jnp.where(lane == 1, slope - high, 0.0)
            ).astype(BF16)
        return carry

    lax.fori_loop(0, rows // step, body, 0)
    product_ref[:, :part] = dot_tn(first_ref[...], mixed_ref[...]).astype(BF16)
    row = lax.broadcasted_iota(jnp.int32, (8, width), 0)
    packed = jnp.where(row < 3, sum1_ref[...], pltpu.roll(sum2_ref[...], 3, 0))
    packed = jnp.where(row < 6, packed, 0.0)
    columns = jnp.concatenate([packed, jnp.zeros((LANES - 8, width), F32)], axis=0).T
    units = bias.shape[1]
    each = units // width
    if shard % 16 == 0:
        at = lax.broadcasted_iota(jnp.int32, (8, units), 0)
        both = jnp.where(at >= 6, bias, 0.0)
        turned = jnp.concatenate([both, jnp.zeros((LANES - 8, units), F32)], axis=0).T
        lane_at = lax.broadcasted_iota(jnp.int32, (shard, LANES), 1)
        for place in range(width // shard):
            piece = columns[place * shard : (place + 1) * shard]
            for turn in range(each):
                begin = (place * each + turn) * shard
                piece = jnp.where(lane_at == 6 + turn, turned[begin : begin + shard], piece)
            product_ref[place * shard : (place + 1) * shard, part:] = piece.astype(BF16)
    else:
        side_row = lax.broadcasted_iota(jnp.int32, (8, LANES), 0)
        turned = dot_tn(bias.astype(BF16), (side_row == 0).astype(F32).astype(BF16)).astype(BF16)
        lane_at = lax.broadcasted_iota(jnp.int32, (width, LANES), 1)
        for turn in range(each):
            columns = jnp.where(lane_at == 6 + turn, dot(turn_ref[turn], turned), columns)
        product_ref[:, part:] = columns.astype(BF16)
    emit(product_ref, pl.program_id(0), outs, coords)
    keep = same_head(2 * LANES, 2 * LANES)
    for pair in range(part // LANES):
        lanes = slice(pair * LANES, (pair + 1) * LANES)
        total = jnp.zeros((2 * LANES, 2 * LANES), F32)
        for place in range(rows // block):
            here = slice(place * block, (place + 1) * block)
            features = turned_features(sq_ref[here, lanes], cos_ref[here, :], sin_ref[here, :])
            state = dot_tn(
                features, jnp.concatenate([gn_ref[here, lanes], gd_ref[here, lanes]], axis=1)
            )
            state = jnp.where(keep, state, 0.0)
            st_ref[place, pair] = state.astype(BF16)
            total = total + state
        compact(total, packed_ref, tot_ref, pair, pl.program_id(0), False)


def unmix(
    coords, first, mixed, rden, sq, cosines, sines, w, sums1, sums2, turns, gbias, layout, block
):
    rows, width = first.shape
    groups, halves, shard, _ = w.shape
    part = width // halves
    pairs = width // LANES
    half = pairs // halves
    blocks = rows // block
    row_spec = pl.BlockSpec((rows, part), lambda t: (0, t))
    tile = part + LANES
    out_specs, out_shapes = piece_outputs(layout, tile, lambda t: layout[3] // tile - 1)
    units = gbias.shape[1] // halves
    full = jax.ShapeDtypeStruct((rows, width), BF16)
    return call(
        functools.partial(
            unmix_kernel, block=block, step=512, shard=layout[2]
        ),
        grid=(halves,),
        in_specs=[
            scalars(), whole((rows, width)), row_spec, row_spec, row_spec,
            whole((rows, LANES)), whole((rows, LANES)),
            pl.BlockSpec((groups, 1, shard, part), lambda t: (0, t, 0, 3)),
            whole((8, width)), whole((8, width)), whole(turns.shape),
        ]
        + [pl.BlockSpec((8, units), lambda t: (0, t))],
        out_specs=out_specs
        + [
            row_spec, row_spec,
            pl.BlockSpec((blocks, half, 2 * LANES, 2 * LANES), lambda t: (0, t, 0, 0)),
            whole((half + 1, 2 * LANES, LANES)),
        ],
        out_shape=out_shapes
        + [
            full, full,
            jax.ShapeDtypeStruct((blocks, pairs, 2 * LANES, 2 * LANES), BF16),
            jax.ShapeDtypeStruct((half + 1, 2 * LANES, LANES), BF16),
        ],
        scratch_shapes=[
            pltpu.VMEM((width, tile), BF16), pltpu.VMEM((half + 1, 2 * LANES, LANES), F32)
        ],
        compiler_params=params(),
        cost_estimate=cost(4 * rows * width * width, 16e6),
        name="unmix",
        near_in=(1, 4),
        near_out=(len(out_shapes), len(out_shapes) + 1),
    )(coords, first, mixed, rden, sq, cosines, sines, w, sums1, sums2, turns, gbias)


def unattend_kernel(
    sq_ref, sk_ref, v_ref, gn_ref, gd_ref, cm_ref, cos_ref, sin_ref, st_ref, in_ref, lt_ref, gq_ref,
    gk_ref, later_ref, *refs, start_pair
):
    query_ref, dk_ref, dv_ref = refs[-3:]
    blocks, block, _ = cm_ref.shape
    piece = min(PIECE, block)
    masks = [lane_mask(block, head) for head in range(2)]
    ones = jnp.ones((block, LANES), BF16)
    pair = start_pair + pl.program_id(0)
    each = in_ref.shape[0] - 1
    incoming = expand(in_ref, pair % each, pair // each, True)
    outgoing = expand(later_ref, pair % each, pair // each, False)
    for place in range(blocks):
        start = place * block
        all_here = slice(start, start + block)
        keys, values = sk_ref[all_here, :], v_ref[all_here, :]
        sides = jnp.concatenate([values, ones], axis=1)
        key_sides = [keys * mask for mask in masks]
        state = incoming
        for earlier in range(place):
            state = state + st_ref[earlier, 0].astype(F32)
        state = state.astype(BF16)
        grad_keys = [None] * (block // piece)
        grad_values = [None] * (block // piece)
        for low in range(0, block, piece):
            here = slice(start + low, start + low + piece)
            span = low + piece
            queries, grads, slopes = sq_ref[here, :], gn_ref[here, :], gd_ref[here, :]
            grad_queries = None
            for head in range(2):
                mask = masks[head][:piece]
                cm = cm_ref[place, low : low + piece, :span]
                masked_queries, masked_grads = queries * mask, grads * mask
                scores = dot_nt(masked_queries, keys[:span])
                weights = (scores * cm).astype(BF16)
                back = dot_nt(
                    jnp.concatenate([masked_grads, slopes * mask], axis=1), sides[:span]
                )
                back = (back * cm).astype(BF16)
                term = dot(back, key_sides[head][:span])
                grad_queries = term if grad_queries is None else grad_queries + term
                key_term = dot_tn(back, masked_queries)
                value_term = dot_tn(weights, masked_grads)
                for piece_at in range(span // piece):
                    at = slice(piece_at * piece, (piece_at + 1) * piece)
                    old = grad_keys[piece_at]
                    grad_keys[piece_at] = key_term[at] if old is None else old + key_term[at]
                    old = grad_values[piece_at]
                    grad_values[piece_at] = value_term[at] if old is None else old + value_term[at]
            far = dot_nt(jnp.concatenate([grads, slopes], axis=1), state)
            grad_queries = (
                grad_queries
                + far[:, :LANES] * cos_ref[here, :]
                + far[:, LANES:] * sin_ref[here, :]
            ) * gq_ref[here, :].astype(F32)
            query_ref[here, :] = grad_queries.astype(BF16)
        grad_keys = jnp.concatenate(grad_keys, axis=0)
        grad_values = jnp.concatenate(grad_values, axis=0)
        state = outgoing
        for later in range(place + 1, blocks):
            state = state + lt_ref[later, 0].astype(F32)
        state = state.astype(BF16)
        far = dot_nt(sides, state)
        grad_keys = (
            grad_keys
            + far[:, :LANES] * cos_ref[all_here, :]
            + far[:, LANES:] * sin_ref[all_here, :]
        ) * gk_ref[all_here, :].astype(F32)
        features = turned_features(keys, cos_ref[all_here, :], sin_ref[all_here, :])
        grad_values = grad_values + dot(features, state[:, :LANES])
        dk_ref[all_here, :] = grad_keys.astype(BF16)
        dv_ref[all_here, :] = grad_values.astype(BF16)


def unattend(
    sq, sk, v, gn, gd, cm, cosines, sines, states, incoming, later, slope_q, slope_k,
    later_in, start, count, partial
):
    rows, width = sq.shape
    blocks = cm.shape[0]
    spec = pl.BlockSpec((rows, LANES), lambda p: (0, start + p))
    state_spec = pl.BlockSpec((blocks, 1, 2 * LANES, 2 * LANES), lambda p: (0, start + p, 0, 0))
    full = jax.ShapeDtypeStruct((rows, width), BF16)
    return call(
        functools.partial(unattend_kernel, start_pair=start),
        grid=(count,),
        in_specs=[
            spec, spec, spec, spec, spec,
            whole(cm.shape), whole((rows, LANES)), whole((rows, LANES)),
            state_spec,
            whole(incoming.shape),
            state_spec, spec, spec, whole(later_in.shape),
        ]
        + [pl.BlockSpec(memory_space=pl.ANY)] * len(partial),
        out_specs=[spec, spec, spec],
        out_shape=[jax.ShapeDtypeStruct((rows, width), BF16), full, full],
        input_output_aliases={14 + at: at for at in range(len(partial))},
        compiler_params=params(),
        cost_estimate=cost(20e9, 20e6),
        name="unattend",
        near_in=(0, 1, 2, 3, 4, 14, 15, 16),
        near_out=(0, 1, 2),
    )(sq, sk, v, gn, gd, cm, cosines, sines, states, incoming, later, slope_q, slope_k, later_in, *partial)


def weights_kernel(coords_ref, x_ref, q_ref, k_ref, v_ref, edge_ref, *refs, shard):
    outs, product_ref = refs[:-1], refs[-1]
    coords = [coords_ref[place] for place in range(4)]
    rows, part = q_ref.shape
    width = x_ref.shape[1]
    ones = jnp.ones((rows, LANES), BF16)
    lane = lax.broadcasted_iota(jnp.int32, (part, LANES), 1)
    sums = jnp.zeros((part, LANES), F32)
    for place, ref in enumerate((q_ref, k_ref, v_ref)):
        at = slice(place * part, (place + 1) * part)
        product_ref[:, at] = dot_tn(x_ref[...], ref[...]).astype(BF16)
        sums = jnp.where(lane == place, dot_tn(ref[...], ones), sums)
    if shard % 16 == 0:
        edge = shard * part // width
        for place in range(width // shard):
            piece = jnp.concatenate(
                [sums[place * edge : (place + 1) * edge], jnp.zeros((shard - edge, LANES), F32)], axis=0
            )
            product_ref[place * shard : (place + 1) * shard, 3 * part :] = piece.astype(BF16)
    else:
        product_ref[:, 3 * part :] = dot(edge_ref[...], sums.astype(BF16)).astype(BF16)
    emit(product_ref, pl.program_id(0), outs, coords)


def weight_gradients(coords, x, q, k, v, edges, layout):
    rows, width = x.shape
    halves = layout[1]
    spec = pl.BlockSpec((rows, width // halves), lambda t: (0, t))
    out_specs, out_shapes = piece_outputs(layout, layout[3], lambda t: 0)
    return call(
        functools.partial(weights_kernel, shard=layout[2]),
        grid=(halves,),
        in_specs=[scalars(), whole((rows, width)), spec, spec, spec, whole(edges.shape)],
        out_specs=out_specs,
        out_shape=out_shapes,
        scratch_shapes=[pltpu.VMEM((width, layout[3]), BF16)],
        compiler_params=params(),
        cost_estimate=cost(2 * rows * width * 3 * width, 10e6),
        name="weight_gradients",
        near_in=(2, 3, 4),
    )(coords, x, q, k, v, edges)


def inputs_kernel(first_ref, q_ref, k_ref, v_ref, w_ref, out_ref):
    halves = w_ref.shape[1]
    width = first_ref.shape[1]
    part = width // halves
    total = first_ref[...].astype(F32)
    for half in range(halves):
        side = w_ref[:, half].reshape(width, 3 * part)
        at = slice(half * part, (half + 1) * part)
        joined = jnp.concatenate([q_ref[:, at], k_ref[:, at], v_ref[:, at]], axis=1)
        total = total + dot_nt(joined, side)
    out_ref[...] = total.astype(BF16)


def input_gradient(first, q, k, v, w, step):
    rows, width = first.shape
    groups, halves, shard, _ = w.shape
    part = width // halves
    spec = pl.BlockSpec((step, width), lambda i: (i, 0))
    return call(
        inputs_kernel,
        grid=(rows // step,),
        in_specs=[
            spec, spec, spec, spec,
            pl.BlockSpec((groups, halves, shard, 3 * part), lambda i: (0, 0, 0, 0)),
        ],
        out_specs=spec,
        out_shape=jax.ShapeDtypeStruct((rows, width), BF16),
        compiler_params=params(),
        cost_estimate=cost(2 * rows * width * 3 * width, 14e6),
        name="input_gradient",
        near_in=(0, 1, 2, 3),
    )(first, q, k, v, w)


def moves():
    def table(change):
        pairs = []
        for source in range(32):
            z, y, c, x = source // 8, source // 4 % 2, source // 2 % 2, source % 2
            z, y, c, x = change(z, y, c, x)
            pairs.append((source, ((z * 2 + y) * 2 + c) * 2 + x))
        return pairs

    along = [table(lambda z, y, c, x, k=k: (z ^ k, y, c, x)) for k in range(4)]
    beside = table(lambda z, y, c, x: (z, y ^ c, c, x ^ 1 ^ c))
    across = table(lambda z, y, c, x: (z, y ^ 1 ^ c, c, x ^ c))
    core = table(lambda z, y, c, x: (z, y, c ^ 1, x))
    return along, beside, across, core


def add(left, right):
    return (left.astype(F32) + right.astype(F32)).astype(BF16)


def send(value, table, begin, end, axes=BOTH):
    value = after(value, *begin) if begin else value
    value = lax.ppermute(value, axes, table)
    return after(value, *end) if end else value


class Gather:
    def __init__(self, piece):
        self.tables = moves()
        self.held = piece

    def line(self, begin=(), end=()):
        parts = [send(self.held, self.tables[0][k], begin, end) for k in (1, 2, 3)]
        self.held = join([self.held] + parts)

    def line_parts(self, begin):
        self.held = self.held, [send(self.held, self.tables[0][k], begin, ()) for k in (1, 2, 3)]

    def beside(self, begin=(), end=()):
        self.held = jnp.concatenate([self.held, send(self.held, self.tables[1], begin, end)], axis=0)

    def across(self, begin=(), end=()):
        self.held = jnp.concatenate([self.held, send(self.held, self.tables[2], begin, end)], axis=0)

    def core(self, begin=(), end=()):
        return [self.held, send(self.held, self.tables[3], begin, end)]


class Sum:
    def __init__(self, own, other):
        self.tables = moves()
        self.kept, self.sent = own, other

    def fold(self, table, begin, end):
        arrived = send(self.sent, table, begin, end)
        size = self.kept.shape[0] // 2
        kept = add(self.kept[:size], arrived[:size])
        self.kept, self.sent = kept, add(self.kept[size:], arrived[size:])

    def both(self):
        return [self.kept, self.sent]

    def core(self, begin=(), end=()):
        self.fold(self.tables[3], begin, end)

    def across(self, begin=(), end=()):
        self.fold(self.tables[2], begin, end)

    def beside(self, begin=(), end=()):
        arrived = send(self.sent, self.tables[1], begin, end)
        self.parts = [add(self.kept[k], arrived[k]) for k in range(4)]

    def line(self, begin=(), end=()):
        parts = [send(self.parts[k], self.tables[0][k], begin, end) for k in (1, 2, 3)]
        total = self.parts[0].astype(F32)
        for part in parts:
            total = total + part.astype(F32)
        return total


def local(
    inputs, w_query, w_key, w_value, b_query, b_key, b_value, w_out, b_out, norm_gain, norm_shift,
    w_up, b_up, w_down, b_down, final_gain, final_shift, piece_starts, grad_output,
):
    rows, width = inputs.shape
    halves = lax.axis_size("tp")
    replicas = lax.axis_size("fsdp")
    length = rows * halves
    block = min(512, length)
    blocks = rows // block
    shard = width // replicas
    part = width // halves
    units = w_up.shape[1]
    me = lax.axis_index("tp")
    pieces = replicas == 16 and halves == 2 and shard % 16 == 0
    place = lax.axis_index("fsdp")
    coords = jnp.stack([place // 4, place // 2 % 2, place % 2, me]).astype(jnp.int32)

    def layout(columns):
        return replicas, halves, shard, columns, pieces

    places = me * rows + jnp.arange(rows, dtype=jnp.int32)
    flags = jnp.any(piece_starts[0][:, None] == (places // PIECE * PIECE)[None, :], axis=0)
    angle = 0.5 * jnp.pi / length * places.astype(F32)
    cosines, sines = jnp.cos(angle), jnp.sin(angle)
    at = jnp.arange(block, dtype=jnp.int32)
    allowed = (at[None, None, :] <= at[None, :, None]) | (
        (at[None, None, :] // PIECE == at[None, :, None] // PIECE)
        & flags.reshape(blocks, block)[:, :, None]
    )
    c, s = cosines.reshape(blocks, block), sines.reshape(blocks, block)
    cm = jnp.where(allowed, c[:, :, None] * c[:, None, :] + s[:, :, None] * s[:, None, :], 0.0)
    cosines = jnp.broadcast_to(cosines[:, None], (rows, LANES))
    sines = jnp.broadcast_to(sines[:, None], (rows, LANES))

    each, edge = units // width, shard // halves
    if pieces:
        edges, turns = jnp.zeros((8, LANES), BF16), jnp.zeros((1, 8, LANES), BF16)
    else:
        edges, turns = selectors(width, part, shard, edge, each)
    thins = (
        b_query, b_key, b_value, b_up, b_out, norm_gain, norm_shift, b_down, final_gain, final_shift
    )
    if pieces:
        attention_shard = pack(w_query, w_key, w_value, w_out.T, thins)
    else:
        columns = []
        for thin in thins:
            thin = jnp.pad(thin, (0, -thin.shape[0] % shard))
            columns.append(thin.reshape(-1, shard).T)
        columns = jnp.concatenate(columns, axis=1)
        columns = jnp.pad(columns, ((0, 0), (0, LANES - columns.shape[1])))
        attention_shard = jnp.concatenate([w_query, w_key, w_value, w_out.T, columns], axis=1)
    down_shard = w_down.T

    def gather_all(piece):
        everything = lax.all_gather(piece, BOTH, axis=0, tiled=False)
        everything = everything.reshape(replicas, halves, shard, piece.shape[1])
        return jnp.moveaxis(everything, 1, 0).reshape(1, halves, width, piece.shape[1])

    if pieces:
        first_chunk, up_chunk, down_chunk = Gather(attention_shard), Gather(w_up), Gather(down_shard)
        first_chunk.line([], [cm, cosines, sines, coords])
        four = first_chunk.held
        first_chunk.beside()
        up_chunk.line([four])
        first_chunk.across()
        sixteen = first_chunk.held
        four = up_chunk.held
        w_attention = first_chunk.core([four])
        up_chunk.beside([sixteen, four], w_attention)
        eight = up_chunk.held
        down_chunk.line_parts([sixteen, four])
        w_attention = [after(w_attention[0], eight), w_attention[1]]
    else:
        w_attention, w_lift, w_drop = [
            [gather_all(piece)] for piece in (attention_shard, w_up, down_shard)
        ]


    columns = 4 * part + LANES
    sq, sk, v, slope_q, slope_k, states, total, w_attention = project(
        coords, inputs, w_attention, columns, edges, cosines, sines, block, shard, halves
    )
    queries, there = sq, []
    if pieces:
        up_chunk.across([], [sq])
        down_chunk.held = join(
            [down_chunk.held[0]] + [after(part, sq) for part in down_chunk.held[1]]
        )
        there = [up_chunk.held, down_chunk.held]
        queries = after(sq, *there)
    num, den = attend(queries, sk, v, cm, cosines, sines, states)
    bias_up, vectors = unpack(after(w_attention, num), turns, shard, each)
    towards = [(i, i + 1) for i in range(halves - 1)]
    incoming = send(total, towards, there, [num, vectors], "tp")
    if pieces:
        w_lift = up_chunk.core(there, [num, vectors])
        down_chunk.beside(there, [num, vectors])
        there = [down_chunk.held, incoming, w_lift[1]]
        num = after(num, *there)
    mixed, rden, normal, scale, low = mix(
        num, den, sq, incoming, cosines, sines, w_attention, inputs, vectors, 512
    )
    if pieces:
        down_chunk.across(there, [low])
        there = [down_chunk.held]
        low = after(low, *there)
    act, slope, w_lift = lift(
        coords, low, w_lift, bias_up, units, 768, 3 if pieces else 0
    )
    if pieces:
        w_drop = down_chunk.core(there, [act])
    output, branch, sums_second, w_drop = drop(
        coords, act, w_drop, normal, vectors, grad_output, units, 256
    )

    gdown = wide_gradient(coords, branch, act, layout(units), units, 512, "down_gradient")
    gl, gbias_up = bend(branch, w_drop, after(slope, *gdown), units, 768)
    if pieces:
        down_sum = Sum(*gdown)
        down_sum.core([], [gl])
        branch = after(branch, *down_sum.both())
    first_low, sums_first = lower(gl, w_lift, branch, normal, scale, vectors, units, 256)
    wide = units + part + LANES
    *gup, gn, gd, later, later_total = unmix(
        coords, first_low, mixed, rden, sq, cosines, sines, w_attention,
        sums_first, sums_second, turns, gbias_up, layout(wide), block,
    )
    there = []
    if pieces:
        down_sum.across([], [gn])
        there = down_sum.both()
    gup = wide_gradient(
        coords, after(low, *there, *gup), gl, layout(wide), units, 512, "up_gradient", gup
    )
    towards = [(i + 1, i) for i in range(halves - 1)]
    later_in = send(later_total, towards, there, gup, "tp")
    there = [later_in, *gup]
    gn = after(gn, *there)
    pairs = width // LANES
    partial = ()
    for turn, (begin, count) in enumerate(((0, pairs // 3), (pairs // 3, pairs - pairs // 3))):
        partial = unattend(
            sq, sk, v, gn, gd, cm, cosines, sines, states, incoming, later, slope_q, slope_k,
            later_in, begin, count, partial,
        )
        if pieces and turn == 0:
            up_sum = Sum(*gup)
            up_sum.core(there, partial)
            down_sum.beside(there, partial)
            there = [*up_sum.both(), *down_sum.parts]
            partial = after(tuple(partial), *there)
    query_low, key_low, value_low = partial
    if pieces:
        up_sum.across(there, [key_low])
        gdown = down_sum.line(there, [key_low])
        query_low = after(query_low, *up_sum.both(), gdown)
    gqkv = weight_gradients(
        coords, inputs, query_low, key_low, value_low, edges, layout(3 * part + LANES)
    )
    if pieces:
        up_sum.beside([], gqkv)
        rest_sum = Sum(*gqkv)
        rest_sum.core(up_sum.parts)
        rest_sum.across()
        first_low = after(first_low, *rest_sum.both())
        grad_inputs = input_gradient(first_low, query_low, key_low, value_low, w_attention, 256)
        gup = up_sum.line([], [*rest_sum.both(), grad_inputs])
        rest_sum.beside()
        rest = rest_sum.line()
    else:

        def scatter(grad):
            grad = jnp.moveaxis(grad.reshape(halves, replicas, shard, grad.shape[2]), 0, 1)
            grad = grad.reshape(replicas * halves, shard, grad.shape[3])
            return lax.psum_scatter(grad, BOTH, scatter_dimension=0, tiled=False).astype(F32)

        gdown, gup, rest = [scatter(grad[0]) for grad in (gdown, gup, gqkv)]
        grad_inputs = input_gradient(first_low, query_low, key_low, value_low, w_attention, 256)

    scaling = 1.0 / replicas
    gdown, gup, rest = gdown * scaling, gup * scaling, rest * scaling
    sums = gup[:, units + part :].T
    small = rest[:edge, 3 * part :].T
    return (
        output,
        grad_inputs,
        rest[:, :part],
        rest[:, part : 2 * part],
        rest[:, 2 * part : 3 * part],
        small[0],
        small[1],
        small[2],
        gup[:, units : units + part].T,
        sums[2],
        sums[0],
        sums[1],
        gup[:, :units],
        sums[6 : 6 + units // width].reshape(-1),
        gdown.T,
        sums[5],
        sums[3],
        sums[4],
    )


def solution(mesh):
    row = P(("fsdp", "tp"), None)
    split, turned = P("fsdp", "tp"), P("tp", "fsdp")
    thin, wide = P(("tp", "fsdp")), P("fsdp")
    return jax.shard_map(
        local,
        mesh=mesh,
        in_specs=(
            row, split, split, split, thin, thin, thin, turned, wide, wide, wide,
            split, thin, turned, wide, wide, wide, P("fsdp", None), row,
        ),
        out_specs=(
            row, row, split, split, split, thin, thin, thin, turned, wide, wide, wide,
            split, thin, turned, wide, wide, wide,
        ),
        check_vma=False,
    )
```

```python
import functools
import math

import jax
import jax.numpy as jnp
from jax import lax
from jax.experimental import pallas as pl
from jax.experimental.pallas import tpu as pltpu
from jax.sharding import PartitionSpec as P

HEAD_DIM = 64
PIECE = 256
LANES = 128
EPSILON = 1e-05
F32 = jnp.float32
BF16 = jnp.bfloat16
BOTH = ("fsdp", "tp")


def dot(left, right):
    return lax.dot_general(left, right, (((1,), (0,)), ((), ())), preferred_element_type=F32)


def dot_nt(left, right):
    return lax.dot_general(left, right, (((1,), (1,)), ((), ())), preferred_element_type=F32)


def dot_tn(left, right):
    return lax.dot_general(left, right, (((0,), (0,)), ((), ())), preferred_element_type=F32)


def flat(ref):
    value = ref[...]
    return value.reshape(value.shape[0] * value.shape[1] * value.shape[2], value.shape[3])


def lane_mask(rows, head, dtype=BF16):
    lane = lax.broadcasted_iota(jnp.int32, (rows, LANES), 1)
    return (lane // HEAD_DIM == head).astype(F32).astype(dtype)


def same_head(rows, columns):
    row = lax.broadcasted_iota(jnp.int32, (rows, columns), 0)
    lane = lax.broadcasted_iota(jnp.int32, (rows, columns), 1)
    return (row // HEAD_DIM) % 2 == (lane // HEAD_DIM) % 2


def same_rows(shape):
    row = lax.broadcasted_iota(jnp.int32, shape, 0)
    lane = lax.broadcasted_iota(jnp.int32, shape, 1)
    return (row // HEAD_DIM) % 2 == 0, lane


def compact(state, held_ref, packet_ref, place, half, spread):
    left, right = state[:, :LANES], state[:, LANES:]
    first, lane = same_rows(left.shape)
    low = lane < HEAD_DIM
    narrow = jnp.where(first, left, pltpu.roll(left, HEAD_DIM, 1))
    column = jnp.where(first, right, pltpu.roll(right, HEAD_DIM, 1))
    if not spread:
        column = column + pltpu.roll(column, LANES - 1, 1)
        column = jnp.where(lane == 0, column, 0.0)
        column = jnp.broadcast_to(jnp.sum(column, axis=1, keepdims=True), column.shape)
    count = packet_ref.shape[0] - 1
    column = jnp.where(lane == half * count + place, column, 0.0)

    @pl.when(half == 0)
    def _():
        held_ref[place] = narrow
        held_ref[count] = column if place == 0 else held_ref[count] + column

    @pl.when(half == 1)
    def _():
        turned = pltpu.roll(narrow, HEAD_DIM, 1)
        packet_ref[place] = jnp.where(low, held_ref[place], turned).astype(BF16)
        held_ref[count] = held_ref[count] + column
        if place == count - 1:
            packet_ref[count] = held_ref[count].astype(BF16)


def expand(packet_ref, place, half, spread):
    narrow = packet_ref[place].astype(F32)
    first, lane = same_rows(narrow.shape)
    low = lane < HEAD_DIM
    turned = pltpu.roll(narrow, HEAD_DIM, 1)
    here = jnp.where(half == 0, narrow, turned)
    there = jnp.where(half == 0, turned, narrow)
    own = first == low
    left = jnp.where(own, jnp.where(first, here, there), 0.0)
    count = packet_ref.shape[0] - 1
    column = packet_ref[count].astype(F32)
    column = jnp.sum(jnp.where(lane == half * count + place, column, 0.0), axis=1, keepdims=True)
    if not spread:
        own = jnp.logical_and(own, lane % HEAD_DIM == 0)
    right = jnp.where(own, jnp.broadcast_to(column, own.shape), 0.0)
    return jnp.concatenate([left, right], axis=1)


def turned_features(values, cosines, sines):
    wide = values.astype(F32)
    return jnp.concatenate([(wide * cosines).astype(BF16), (wide * sines).astype(BF16)], axis=1)


def slot(coords, z, y, c, x):
    across = jnp.where(c == 0, y ^ coords[1], x ^ coords[3])
    beside = jnp.where(c == 0, x ^ coords[1 + 2], y ^ coords[1])
    return across * 8 + beside * 4 + (z ^ coords[0])


def emit(product, half, outs, coords):
    if len(outs) == 1:
        outs[0][half] = product[...]
        return
    core = coords[2]
    shard = outs[0].shape[1]
    for group in range(product.shape[0] // (2 * shard)):
        z, y = group // 2, group % 2
        for out, c in zip(outs, (core, 1 - core)):
            begin = pl.multiple_of((2 * group + c) * shard, 16)
            out[slot(coords, z, y, c, half)] = product[pl.ds(begin, shard), :]


class Weights:
    def __init__(self, coords_ref, sources, held, out, sems, out_sems, halves):
        self.coords = [coords_ref[place] for place in range(4)]
        self.sources, self.held, self.out = sources, held, out
        self.sems, self.out_sems, self.halves = sems, out_sems, halves

    def copies(self, place):
        half = self.halves[place]
        if len(self.sources) == 1:
            return [
                pltpu.make_async_copy(
                    self.sources[0].at[0, half], self.held.at[place], self.sems.at[place, 0]
                )
            ]
        copies = []
        shard = self.sources[0].shape[1]
        for side, ref in enumerate(self.sources):
            c = self.coords[2] if side == 0 else 1 - self.coords[2]
            for group in range(8):
                z, y = group // 2, group % 2
                begin = pl.multiple_of((2 * group + c) * shard, 16)
                copies.append(
                    pltpu.make_async_copy(
                        ref.at[slot(self.coords, z, y, c, half)],
                        self.held.at[place, pl.ds(begin, shard), :],
                        self.sems.at[place, side * 8 + group],
                    )
                )
        return copies

    def start(self, place):
        for copy in self.copies(place):
            copy.start()

    def ready(self, place):
        for copy in self.copies(place):
            copy.wait()
        self.leaving(place).start()

    def leaving(self, place):
        return pltpu.make_async_copy(
            self.held.at[place], self.out.at[0, place], self.out_sems.at[place]
        )

    def left(self, place):
        self.leaving(place).wait()

    @staticmethod
    def scratch(halves, width, columns):
        return [
            pltpu.VMEM((halves, width, columns), BF16),
            pltpu.SemaphoreType.DMA((halves, 16)),
            pltpu.SemaphoreType.DMA((halves,)),
        ]


def anywhere(count):
    return [pl.BlockSpec(memory_space=pl.ANY)] * count


def scalars():
    return pl.BlockSpec(memory_space=pltpu.SMEM)


def params(megabytes=32):
    return pltpu.CompilerParams(vmem_limit_bytes=megabytes * 1024 * 1024)


def call(kernel, *, out_shape, near_in=(), near_out=(), least=65536, **options):
    shapes = list(out_shape) if isinstance(out_shape, (list, tuple)) else [out_shape]

    def large(value):
        return math.prod(value.shape) * value.dtype.itemsize > least

    placed = [
        pltpu.HBM(shape.shape, shape.dtype) if large(shape) and at not in near_out else shape
        for at, shape in enumerate(shapes)
    ]
    function = pl.pallas_call(
        kernel, out_shape=placed if isinstance(out_shape, (list, tuple)) else placed[0], **options
    )

    def run(*operands):
        count = len(operands)
        near = {at % count for at in near_in}
        return function(
            *[
                pltpu.with_memory_space_constraint(value, pltpu.HBM)
                if large(value) and at not in near
                else value
                for at, value in enumerate(operands)
            ]
        )

    return run


def whole(shape):
    zeros = (0,) * len(shape)
    return pl.BlockSpec(shape, lambda *_: zeros)


def cost(flops, moved):
    return pl.CostEstimate(flops=int(flops), bytes_accessed=int(moved), transcendentals=0)


def after(value, *others):
    return lax.optimization_barrier((value, others))[0]


def pack_kernel(*refs):
    q_ref, k_ref, v_ref, out_ref = refs[:4]
    thins = refs[4:-1]
    first_ref = refs[-1]
    shard, part = q_ref.shape

    def chosen(columns, start):
        row = lax.broadcasted_iota(jnp.int32, (shard, columns), 0)
        column = lax.broadcasted_iota(jnp.int32, (shard, columns), 1)
        return (row + start == column).astype(F32).astype(BF16)

    for place, ref in enumerate((q_ref, k_ref, v_ref, out_ref)):
        first_ref[:, place * part : (place + 1) * part] = ref[...]
    columns = jnp.zeros((shard, LANES), F32)
    lane = 0
    for ref in thins:
        size = ref.shape[1]
        for start in range(0, size, shard):
            row = lax.broadcasted_iota(jnp.int32, (LANES, size), 0)
            spread = jnp.where(row == lane, ref[...].astype(F32), 0.0).astype(BF16)
            columns = columns + dot_nt(chosen(size, start), spread)
            lane += 1
    first_ref[:, 4 * part :] = columns.astype(BF16)


def pack(q, k, v, out, thins):
    shard, part = q.shape
    return call(
        pack_kernel,
        out_shape=jax.ShapeDtypeStruct((shard, 4 * part + LANES), BF16),
        compiler_params=params(),
        cost_estimate=cost(1e8, 1e6),
        name="pack",
        least=0,
    )(q, k, v, out, *[thin.reshape(1, -1) for thin in thins])


def deal(columns, shard, size, turns):
    count = columns.shape[0] // shard
    runs = []
    for place in range(count):
        piece = columns[place * shard : place * shard + size]
        for turn in range(turns):
            runs.append(pltpu.roll(piece, LANES - turn, 1) if turn else piece)
    return jnp.concatenate(runs, axis=0)


def selectors_kernel(edge_ref, turn_ref, *, shard, edge, each):
    width, part = edge_ref.shape
    row = lax.broadcasted_iota(jnp.int32, (width, part), 0)
    column = lax.broadcasted_iota(jnp.int32, (width, part), 1)
    chosen = (row % shard < edge) & (row // shard * edge + row % shard == column)
    edge_ref[...] = chosen.astype(F32).astype(BF16)
    row = lax.broadcasted_iota(jnp.int32, (width, LANES), 0)
    source = row // shard * (each * shard) + row % shard
    lane = lax.broadcasted_iota(jnp.int32, (width, LANES), 1)
    for turn in range(each):
        for begin in range(0, each * width, LANES):
            chosen = source + (turn * shard - begin) == lane
            turn_ref[turn, :, begin : begin + LANES] = chosen.astype(F32).astype(BF16)


def selectors(width, part, shard, edge, each):
    return call(
        functools.partial(selectors_kernel, shard=shard, edge=edge, each=each),
        out_shape=[
            jax.ShapeDtypeStruct((width, part), BF16),
            jax.ShapeDtypeStruct((each, width, each * width), BF16),
        ],
        compiler_params=params(),
        cost_estimate=cost(1e8, 1e6),
        name="selectors",
    )()


def unpack_kernel(thin_ref, turn_ref, up_ref, vec_ref, *, shard, each):
    halves = thin_ref.shape[1]
    for half in range(halves):
        thin = thin_ref[0, half]
        if shard % 16 == 0:
            turned = deal(thin.astype(F32), shard, shard, each).T
            up_ref[half] = turned[0:8]
            continue
        rows = jnp.zeros((8, turn_ref.shape[2]), F32)
        for turn in range(each):
            picked = dot_tn(thin, turn_ref[turn])
            rows = rows + picked[3 + turn : 4 + turn]
        up_ref[half] = rows
    turned = thin_ref[0, 0].astype(F32).T
    vec_ref[...] = turned[3 + each : 11 + each]


def unpack(w, turns, shard, each):
    _, halves, width, columns = w.shape
    return call(
        functools.partial(unpack_kernel, shard=shard, each=each),
        grid=(1,),
        in_specs=[
            pl.BlockSpec((1, halves, width, LANES), lambda i: (0, 0, 0, columns // LANES - 1)),
            whole(turns.shape),
        ],
        out_specs=[whole((halves, 8, each * width)), whole((8, width))],
        out_shape=[
            jax.ShapeDtypeStruct((halves, 8, each * width), F32),
            jax.ShapeDtypeStruct((8, width), F32),
        ],
        compiler_params=params(),
        cost_estimate=cost(1e8, 1e6),
        name="unpack",
    )(w, turns)


def join_kernel(*refs):
    for place, ref in enumerate(refs[:-1]):
        refs[-1][place] = ref[...]


def join(parts):
    return call(
        join_kernel,
        out_shape=jax.ShapeDtypeStruct((len(parts),) + parts[0].shape, parts[0].dtype),
        compiler_params=params(),
        cost_estimate=cost(0, 1e6),
        name="join",
        least=0,
    )(*parts)


def project_kernel(
    coords_ref, *refs, block, step, shard, halves
):
    sources, refs = refs[: len(refs) - 15], refs[len(refs) - 15 :]
    x_ref, edge_ref, cos_ref, sin_ref, sq_ref, sk_ref, v_ref, gq_ref, gk_ref, st_ref, tot_ref = refs[:11]
    sources, out_ref = sources[:-1], sources[-1]
    packed_ref, held_ref, sems, out_sems = refs[11:]
    rows = x_ref.shape[0]
    part = sq_ref.shape[1]
    now = pl.program_id(0)
    weights = Weights(coords_ref, sources, held_ref, out_ref, sems, out_sems, range(halves))

    @pl.when(now == 0)
    def _():
        for half in range(halves):
            weights.start(half)

    for half in range(halves):

        @pl.when(now == half)
        def _():
            weights.ready(half)

    columns = held_ref.shape[2]
    thin = held_ref[now, :, columns - LANES :]
    if shard % 16 == 0:
        biases = deal(thin.astype(F32), shard, shard * part // x_ref.shape[1], 1).T
    else:
        biases = dot_tn(thin, edge_ref[...])

    def body(index, carry):
        here = pl.ds(index * step, step)
        sums = dot(x_ref[here, :], held_ref[now, :, : 3 * part])
        for place, (feature_ref, slope_ref) in enumerate(((sq_ref, gq_ref), (sk_ref, gk_ref))):
            value = sums[:, place * part : (place + 1) * part] + biases[place : place + 1]
            positive = jnp.maximum(value, 0.0) + jnp.log1p(jnp.exp(-jnp.abs(value)))
            feature_ref[here, :] = positive.astype(BF16)
            slope_ref[here, :] = jax.nn.sigmoid(value).astype(BF16)
        v_ref[here, :] = (sums[:, 2 * part :] + biases[2:3]).astype(BF16)
        return carry

    lax.fori_loop(0, rows // step, body, 0)
    keep = same_head(2 * LANES, 2 * LANES)
    ones = jnp.ones((block, LANES), BF16)
    for pair in range(part // LANES):
        lanes = slice(pair * LANES, (pair + 1) * LANES)
        total = jnp.zeros((2 * LANES, 2 * LANES), F32)
        for place in range(rows // block):
            here = slice(place * block, (place + 1) * block)
            features = turned_features(sk_ref[here, lanes], cos_ref[here, :], sin_ref[here, :])
            state = dot_tn(features, jnp.concatenate([v_ref[here, lanes], ones], axis=1))
            state = jnp.where(keep, state, 0.0)
            st_ref[place, pair] = state.astype(BF16)
            total = total + state
        compact(total, packed_ref, tot_ref, pair, pl.program_id(0), True)

    @pl.when(now == halves - 1)
    def _():
        for half in range(halves):
            weights.left(half)


def project(coords, x, sources, columns, edges, cosines, sines, block, shard, halves):
    rows, width = x.shape
    part = width // halves
    pairs = width // LANES
    half = pairs // halves
    blocks = rows // block
    row_spec = pl.BlockSpec((rows, part), lambda t: (0, t))
    full = jax.ShapeDtypeStruct((rows, width), BF16)

    def kernel(coords_ref, *refs):
        count = len(sources)
        others, outs, scratch = refs[count : count + 4], refs[count + 4 : -4], refs[-4:]
        project_kernel(
            coords_ref, *refs[:count], outs[-1], *others, *outs[:-1], *scratch,
            block=block, step=rows, shard=shard, halves=halves,
        )

    return call(
        kernel,
        grid=(halves,),
        in_specs=[scalars()]
        + anywhere(len(sources))
        + [
            whole((rows, width)), whole(edges.shape), whole((rows, LANES)), whole((rows, LANES)),
        ],
        out_specs=[
            row_spec, row_spec, row_spec, row_spec, row_spec,
            pl.BlockSpec((blocks, half, 2 * LANES, 2 * LANES), lambda t: (0, t, 0, 0)),
            whole((half + 1, 2 * LANES, LANES)),
        ]
        + anywhere(1),
        out_shape=[
            full, full, full, full, full,
            jax.ShapeDtypeStruct((blocks, pairs, 2 * LANES, 2 * LANES), BF16),
            jax.ShapeDtypeStruct((half + 1, 2 * LANES, LANES), BF16),
            jax.ShapeDtypeStruct((1, halves, width, columns), BF16),
        ],
        scratch_shapes=[pltpu.VMEM((half + 1, 2 * LANES, LANES), F32)]
        + Weights.scratch(halves, width, columns),
        compiler_params=params(),
        cost_estimate=cost(2 * rows * width * 3 * width, 16e6),
        name="project",
        near_out=(0, 1, 2),
    )(coords, *sources, x, edges, cosines, sines)


def attend_kernel(sq_ref, sk_ref, v_ref, cm_ref, cos_ref, sin_ref, st_ref, num_ref, den_ref):
    blocks, block, _ = cm_ref.shape
    piece = min(PIECE, block)
    masks = [lane_mask(block, head) for head in range(2)]
    for place in range(blocks):
        start = place * block
        keys = sk_ref[start : start + block, :]
        values = v_ref[start : start + block, :]
        sides = [jnp.concatenate([values * mask, mask], axis=1) for mask in masks]
        for low in range(0, block, piece):
            here = slice(start + low, start + low + piece)
            span = low + piece
            queries = sq_ref[here, :]
            sums = None
            for mask, side in zip(masks, sides):
                scores = dot_nt(queries * mask[:piece], keys[:span])
                weights = (scores * cm_ref[place, low : low + piece, :span]).astype(BF16)
                term = dot(weights, side[:span])
                sums = term if sums is None else sums + term
            for earlier in range(place):
                sums = sums + dot(
                    turned_features(queries, cos_ref[here, :], sin_ref[here, :]), st_ref[earlier, 0]
                )
            num_ref[here, :] = sums[:, :LANES]
            den_ref[here, :] = sums[:, LANES:]


def attend(sq, sk, v, cm, cosines, sines, states):
    rows, width = sq.shape
    pairs = width // LANES
    blocks = cm.shape[0]
    spec = pl.BlockSpec((rows, LANES), lambda p: (0, p))
    full = jax.ShapeDtypeStruct((rows, width), F32)
    return call(
        attend_kernel,
        grid=(pairs,),
        in_specs=[
            spec, spec, spec,
            whole(cm.shape), whole((rows, LANES)), whole((rows, LANES)),
            pl.BlockSpec((blocks, 1, 2 * LANES, 2 * LANES), lambda p: (0, p, 0, 0)),
        ],
        out_specs=[spec, spec],
        out_shape=[full, full],
        compiler_params=params(),
        cost_estimate=cost(8e9, 14e6),
        name="attend",
        near_in=(0, 1, 2),
        near_out=(0, 1),
    )(sq, sk, v, cm, cosines, sines, states)


def norm_rows(values):
    average = jnp.mean(values, axis=1, keepdims=True)
    centred = values - average
    scale = lax.rsqrt(jnp.mean(centred * centred, axis=1, keepdims=True) + EPSILON)
    return centred * scale, scale


def mix_kernel(
    num_ref, den_ref, sq_ref, in_ref, cos_ref, sin_ref, w_ref, x_ref, vec_ref,
    mixed_ref, rden_ref, normal_ref, scale_ref, low_ref, wide_ref,
):
    pairs = wide_ref.shape[0]
    halves = w_ref.shape[1]
    rows, width = x_ref.shape
    part = width // halves

    @pl.when(pl.program_id(0) == 0)
    def _():
        for pair in range(pairs):
            place, half = pair % (pairs // halves), pair // (pairs // halves)
            wide_ref[pair] = expand(in_ref, place, half, True).astype(BF16)

    for pair in range(pairs):
        lanes = slice(pair * LANES, (pair + 1) * LANES)
        sums = dot(turned_features(sq_ref[:, lanes], cos_ref[...], sin_ref[...]), wide_ref[pair])
        denominator = den_ref[:, lanes] + sums[:, LANES:]
        inverse = 1.0 / jnp.maximum(denominator, 1.0)
        rden_ref[:, lanes] = jnp.where(denominator > 1.0, inverse, -1.0).astype(BF16)
        mixed_ref[:, lanes] = ((num_ref[:, lanes] + sums[:, :LANES]) * inverse).astype(BF16)
    total = x_ref[...].astype(F32) + vec_ref[0:1, :]
    for half in range(halves):
        side = w_ref[:, half]
        side = side.reshape(width, part)
        total = total + dot_nt(mixed_ref[:, half * part : (half + 1) * part], side)
    normal, scale = norm_rows(total)
    normal_ref[...] = normal
    scale_ref[...] = jnp.broadcast_to(scale, scale_ref.shape)
    low_ref[...] = (normal * vec_ref[1:2, :] + vec_ref[2:3, :]).astype(BF16)


def mix(num, den, sq, incoming, cosines, sines, w, x, vectors, step):
    rows, width = x.shape
    groups, halves, shard, _ = w.shape
    part = width // halves
    pairs = width // LANES
    wide = pl.BlockSpec((step, width), lambda i: (i, 0))
    thin = pl.BlockSpec((step, LANES), lambda i: (i, 0))
    return call(
        mix_kernel,
        grid=(rows // step,),
        in_specs=[
            wide, wide, wide, whole(incoming.shape), thin, thin,
            pl.BlockSpec((groups, halves, shard, part), lambda i: (0, 0, 0, 3)),
            wide, whole(vectors.shape),
        ],
        out_specs=[wide, wide, wide, thin, wide],
        out_shape=[
            jax.ShapeDtypeStruct((rows, width), BF16),
            jax.ShapeDtypeStruct((rows, width), BF16),
            jax.ShapeDtypeStruct((rows, width), F32),
            jax.ShapeDtypeStruct((rows, LANES), F32),
            jax.ShapeDtypeStruct((rows, width), BF16),
        ],
        scratch_shapes=[pltpu.VMEM((pairs, 2 * LANES, 2 * LANES), BF16)],
        compiler_params=params(),
        cost_estimate=cost(2 * rows * width * width * 2, 20e6),
        name="mix",
        near_in=(0, 1, 2),
        near_out=(2, 4),
    )(num, den, sq, incoming, cosines, sines, w, x, vectors)


def norm_back(upstream, normal, scale, gain):
    scaled = upstream * gain
    inner = (
        scaled
        - jnp.mean(scaled, axis=1, keepdims=True)
        - normal * jnp.mean(scaled * normal, axis=1, keepdims=True)
    )
    return inner * scale


def lift_kernel(coords_ref, *refs, step, row, halves):
    sources, refs = refs[:-8], refs[-8:]
    low_ref, bias_ref, act_ref, slope_ref, out_ref, held_ref, sems, out_sems = refs
    tile = act_ref.shape[1]
    now = pl.program_id(0)
    tiles = pl.num_programs(0) // halves
    weights = Weights(coords_ref, sources, held_ref, out_ref, sems, out_sems, range(halves))

    @pl.when(now == 0)
    def _():
        for half in range(halves):
            weights.start(half)

    for half in range(halves):

        @pl.when(now == half * tiles)
        def _():
            weights.ready(half)

    begin = pl.multiple_of(now % tiles * tile, tile)
    up = held_ref[now // tiles, :, pl.ds(begin, tile)]

    def body(place, carry):
        here = pl.ds(place * step, step)
        lifted = dot(low_ref[here, :], up) + bias_ref[0, row : row + 1, :]
        share = 0.5 + 0.5 * lax.erf(lifted * math.sqrt(0.5))
        bell = jnp.exp(-0.5 * lifted * lifted) * (1.0 / math.sqrt(2.0 * math.pi))
        act_ref[here, :] = (lifted * share).astype(BF16)
        slope_ref[here, :] = (share + lifted * bell).astype(BF16)
        return carry

    lax.fori_loop(0, low_ref.shape[0] // step, body, 0, unroll=True)

    @pl.when(now == pl.num_programs(0) - 1)
    def _():
        for half in range(halves):
            weights.left(half)


def lift(coords, low, sources, bias, units, tile, row):
    rows, width = low.shape
    halves = bias.shape[0]
    tiles = units // tile
    unit_spec = pl.BlockSpec((rows, tile), lambda i: (0, i))
    shape = jax.ShapeDtypeStruct((rows, halves * units), BF16)
    return call(
        functools.partial(lift_kernel, step=512, row=row, halves=halves),
        grid=(halves * tiles,),
        in_specs=[scalars()]
        + anywhere(len(sources))
        + [whole((rows, width)), pl.BlockSpec((1, 8, tile), lambda i: (i // tiles, 0, i % tiles))],
        out_specs=[unit_spec, unit_spec] + anywhere(1),
        out_shape=[shape, shape, jax.ShapeDtypeStruct((1, halves, width, units), BF16)],
        scratch_shapes=Weights.scratch(halves, width, units),
        compiler_params=params(),
        cost_estimate=cost(2 * rows * width * halves * units, 20e6),
        name="lift",
        near_in=(-2,),
        near_out=(0, 1),
    )(coords, *sources, low, bias)


def in_turn(product, finish, total_ref):
    now = pl.program_id(0)
    last = pl.num_programs(0) - 1

    @pl.when(now == 0)
    def _():
        total_ref[0] = product(True)

    @pl.when((now > 0) & (now < last))
    def _():
        finish(total_ref[(now - 1) % 2])
        total_ref[now % 2] = product()

    @pl.when(now == last)
    def _():
        finish(total_ref[(now - 1) % 2])


def drop_kernel(coords_ref, *refs, halves):
    sources, act_ref, refs = refs[:-12], refs[-12], refs[-11:]
    normal_ref, vec_ref, grad_ref, out_ref, branch_ref, sum_ref = refs[:6]
    whole_ref, held_ref, sems, out_sems, total_ref = refs[6:]
    weights = Weights(coords_ref, sources, held_ref, whole_ref, sems, out_sems, range(halves))
    units = held_ref.shape[2]

    @pl.when(pl.program_id(0) == 0)
    def _():
        sum_ref[...] = jnp.zeros_like(sum_ref)
        for half in range(halves):
            weights.start(half)

    def product(fresh=False):
        total = None
        for half in range(halves):
            if fresh:
                weights.ready(half)
            term = dot_nt(act_ref[:, half * units : (half + 1) * units], held_ref[half])
            total = term if total is None else total + term
        return total

    def finish(total):
        total = total + normal_ref[...] * vec_ref[1:2, :] + vec_ref[2:3, :] + vec_ref[3:4, :]
        normal, scale = norm_rows(total)
        gain = vec_ref[4:5, :]
        out_ref[...] = (normal * gain + vec_ref[5:6, :]).astype(BF16)
        upstream = grad_ref[...].astype(F32)
        second = norm_back(upstream, normal, scale, gain)
        branch_ref[...] = second.astype(BF16)
        sum_ref[0:1, :] += jnp.sum(upstream * normal, axis=0, keepdims=True)
        sum_ref[1:2, :] += jnp.sum(upstream, axis=0, keepdims=True)
        sum_ref[2:3, :] += jnp.sum(second, axis=0, keepdims=True)

    in_turn(product, finish, total_ref)

    @pl.when(pl.program_id(0) == pl.num_programs(0) - 1)
    def _():
        for half in range(halves):
            weights.left(half)


def drop(coords, act, sources, normal, vectors, grad, units, step):
    rows, width = normal.shape
    halves = act.shape[1] // units
    steps = rows // step
    wide = pl.BlockSpec((step, width), lambda i: (jnp.maximum(i - 1, 0), 0))
    return call(
        functools.partial(drop_kernel, halves=halves),
        grid=(steps + 1,),
        in_specs=[scalars()]
        + anywhere(len(sources))
        + [
            pl.BlockSpec((step, halves * units), lambda i: (jnp.minimum(i, steps - 1), 0)),
            wide, whole(vectors.shape), wide,
        ],
        out_specs=[wide, wide, whole((8, width))] + anywhere(1),
        out_shape=[
            jax.ShapeDtypeStruct((rows, width), BF16),
            jax.ShapeDtypeStruct((rows, width), BF16),
            jax.ShapeDtypeStruct((8, width), F32),
            jax.ShapeDtypeStruct((1, halves, width, units), BF16),
        ],
        scratch_shapes=Weights.scratch(halves, width, units) + [pltpu.VMEM((2, step, width), F32)],
        compiler_params=params(),
        cost_estimate=cost(2 * rows * width * halves * units, 20e6),
        name="drop",
        near_in=(-4, -3),
        near_out=(1,),
    )(coords, *sources, act, normal, vectors, grad)


def piece_outputs(layout, tile, index_map):
    replicas, halves, shard, columns, pieces = layout[:5]
    if pieces:
        count = replicas * halves // 2
        spec = pl.BlockSpec((count, shard, tile), lambda *at: (0, 0, index_map(*at)))
        shape = jax.ShapeDtypeStruct((count, shard, columns), BF16)
        return [spec, spec], [shape, shape]
    width = replicas * shard
    spec = pl.BlockSpec((halves, width, tile), lambda *at: (0, 0, index_map(*at)))
    return [spec], [jax.ShapeDtypeStruct((halves, width, columns), BF16)]


def wide_gradient_kernel(coords_ref, left_ref, *refs, halves, partial):
    rights, product_ref = refs[:halves], refs[-1]
    outs = refs[(len(refs) - 1 + halves) // 2 : -1] if partial else refs[halves:-1]
    coords = [coords_ref[place] for place in range(4)]
    for half, right_ref in enumerate(rights):
        product_ref[...] = dot_tn(left_ref[...], right_ref[...]).astype(BF16)
        emit(product_ref, half, outs, coords)


def wide_gradient(coords, left, right, layout, units, tile, name, partial=()):
    rows, width = left.shape
    halves = layout[1]
    tiles = units // tile
    out_specs, out_shapes = piece_outputs(layout, tile, lambda j: j)
    return call(
        functools.partial(wide_gradient_kernel, halves=halves, partial=bool(partial)),
        grid=(tiles,),
        in_specs=[scalars(), whole((rows, width))]
        + [
            pl.BlockSpec((rows, tile), lambda j, half=half: (0, half * tiles + j))
            for half in range(halves)
        ]
        + anywhere(len(partial)),
        out_specs=out_specs,
        out_shape=out_shapes,
        input_output_aliases={2 + halves + at: at for at in range(len(partial))},
        scratch_shapes=[pltpu.VMEM((width, tile), BF16)],
        compiler_params=params(),
        cost_estimate=cost(2 * rows * width * halves * units, 18e6),
        name=name,
        near_in=(1, 2, 3),
    )(coords, left, *([right] * halves), *partial)


def bend_kernel(branch_ref, down_ref, slope_ref, gl_ref, gbias_ref, *, step):
    down = down_ref[0, 0]
    gbias_ref[...] = jnp.zeros_like(gbias_ref)

    def body(place, carry):
        here = pl.ds(place * step, step)
        slope = dot(branch_ref[here, :], down) * slope_ref[here, :].astype(F32)
        gbias_ref[0:1, :] += jnp.sum(slope, axis=0, keepdims=True)
        gl_ref[here, :] = slope.astype(BF16)
        return carry

    lax.fori_loop(0, branch_ref.shape[0] // step, body, 0, unroll=True)


def bend(branch, w, slope, units, tile):
    rows, width = branch.shape
    halves = w.shape[1]
    tiles = units // tile
    unit_spec = pl.BlockSpec((rows, tile), lambda i: (0, i))
    return call(
        functools.partial(bend_kernel, step=512),
        grid=(halves * tiles,),
        in_specs=[
            whole((rows, width)),
            pl.BlockSpec((1, 1, width, tile), lambda i: (0, i // tiles, 0, i % tiles)),
            unit_spec,
        ],
        out_specs=[unit_spec, pl.BlockSpec((8, tile), lambda i: (0, i))],
        out_shape=[
            jax.ShapeDtypeStruct(slope.shape, BF16),
            jax.ShapeDtypeStruct((8, halves * units), F32),
        ],
        compiler_params=params(),
        cost_estimate=cost(2 * rows * width * halves * units, 20e6),
        name="bend",
        near_in=(0, 2),
        near_out=(0,),
    )(branch, w, slope)


def lower_kernel(
    gl_ref, up_ref, branch_ref, normal_ref, scale_ref, vec_ref, firstlow_ref, sum_ref,
    total_ref,
):
    halves, units = up_ref.shape[1], up_ref.shape[3]

    @pl.when(pl.program_id(0) == 0)
    def _():
        sum_ref[...] = jnp.zeros_like(sum_ref)

    def product(fresh=False):
        total = None
        for half in range(halves):
            term = dot_nt(gl_ref[:, half * units : (half + 1) * units], up_ref[0, half])
            total = term if total is None else total + term
        return total

    def finish(total):
        upstream = branch_ref[...].astype(F32) + total
        normal = normal_ref[...]
        first = norm_back(upstream, normal, scale_ref[:, 0:1], vec_ref[1:2, :])
        firstlow_ref[...] = first.astype(BF16)
        sum_ref[0:1, :] += jnp.sum(upstream * normal, axis=0, keepdims=True)
        sum_ref[1:2, :] += jnp.sum(upstream, axis=0, keepdims=True)
        sum_ref[2:3, :] += jnp.sum(first, axis=0, keepdims=True)

    in_turn(product, finish, total_ref)


def lower(gl, w, branch, normal, scale, vectors, units, step):
    rows, width = branch.shape
    steps = rows // step
    wide = pl.BlockSpec((step, width), lambda i: (jnp.maximum(i - 1, 0), 0))
    return call(
        lower_kernel,
        grid=(steps + 1,),
        in_specs=[
            pl.BlockSpec((step, gl.shape[1]), lambda i: (jnp.minimum(i, steps - 1), 0)),
            whole(w.shape), wide, wide,
            pl.BlockSpec((step, LANES), lambda i: (jnp.maximum(i - 1, 0), 0)),
            whole(vectors.shape),
        ],
        out_specs=[wide, whole((8, width))],
        out_shape=[
            jax.ShapeDtypeStruct((rows, width), BF16),
            jax.ShapeDtypeStruct((8, width), F32),
        ],
        scratch_shapes=[pltpu.VMEM((2, step, width), F32)],
        compiler_params=params(),
        cost_estimate=cost(2 * rows * width * gl.shape[1], 20e6),
        name="lower",
        near_in=(0, 2, 3),
        near_out=(0,),
    )(gl, w, branch, normal, scale, vectors)


def unmix_kernel(
    coords_ref, first_ref, mixed_ref, rden_ref, sq_ref, cos_ref, sin_ref, w_ref,
    sum1_ref, sum2_ref, turn_ref, *refs, block, step, shard
):
    bias = jnp.broadcast_to(refs[0][0:1, :], refs[0].shape)
    refs = refs[1:]
    outs = refs[:-6]
    gn_ref, gd_ref, st_ref, tot_ref, product_ref, packed_ref = refs[-6:]
    coords = [coords_ref[place] for place in range(4)]
    rows, width = first_ref.shape
    part = mixed_ref.shape[1]
    side = flat(w_ref)
    group_row = lax.broadcasted_iota(jnp.int32, (LANES, LANES), 0)
    group_lane = lax.broadcasted_iota(jnp.int32, (LANES, LANES), 1)
    group = (group_row // HEAD_DIM == group_lane // HEAD_DIM).astype(F32).astype(BF16)
    group = jnp.concatenate([group, group], axis=0)

    lane = lax.broadcasted_iota(jnp.int32, (step, LANES), 1) % HEAD_DIM

    def body(place, carry):
        here = pl.ds(place * step, step)
        grad = dot(first_ref[here, :], side)
        for pair in range(part // LANES):
            lanes = slice(pair * LANES, (pair + 1) * LANES)
            signed = rden_ref[here, lanes].astype(F32)
            inverse = jnp.abs(signed)
            scaled = grad[:, lanes] * inverse
            product = scaled * mixed_ref[here, lanes].astype(F32)
            high = product.astype(BF16)
            rest = (product - high.astype(F32)).astype(BF16)
            inner = dot(jnp.concatenate([high, rest], axis=1), group)
            slope = jnp.where(signed > 0.0, -inner, 0.0)
            high = slope.astype(BF16).astype(F32)
            gn_ref[here, lanes] = scaled.astype(BF16)
            gd_ref[here, lanes] = jnp.where(
                lane == 0, high, jnp.where(lane == 1, slope - high, 0.0)
            ).astype(BF16)
        return carry

    lax.fori_loop(0, rows // step, body, 0)
    product_ref[:, :part] = dot_tn(first_ref[...], mixed_ref[...]).astype(BF16)
    row = lax.broadcasted_iota(jnp.int32, (8, width), 0)
    packed = jnp.where(row < 3, sum1_ref[...], pltpu.roll(sum2_ref[...], 3, 0))
    packed = jnp.where(row < 6, packed, 0.0)
    columns = jnp.concatenate([packed, jnp.zeros((LANES - 8, width), F32)], axis=0).T
    units = bias.shape[1]
    each = units // width
    if shard % 16 == 0:
        at = lax.broadcasted_iota(jnp.int32, (8, units), 0)
        both = jnp.where(at >= 6, bias, 0.0)
        turned = jnp.concatenate([both, jnp.zeros((LANES - 8, units), F32)], axis=0).T
        lane_at = lax.broadcasted_iota(jnp.int32, (shard, LANES), 1)
        for place in range(width // shard):
            piece = columns[place * shard : (place + 1) * shard]
            for turn in range(each):
                begin = (place * each + turn) * shard
                piece = jnp.where(lane_at == 6 + turn, turned[begin : begin + shard], piece)
            product_ref[place * shard : (place + 1) * shard, part:] = piece.astype(BF16)
    else:
        side_row = lax.broadcasted_iota(jnp.int32, (8, LANES), 0)
        turned = dot_tn(bias.astype(BF16), (side_row == 0).astype(F32).astype(BF16)).astype(BF16)
        lane_at = lax.broadcasted_iota(jnp.int32, (width, LANES), 1)
        for turn in range(each):
            columns = jnp.where(lane_at == 6 + turn, dot(turn_ref[turn], turned), columns)
        product_ref[:, part:] = columns.astype(BF16)
    emit(product_ref, pl.program_id(0), outs, coords)
    keep = same_head(2 * LANES, 2 * LANES)
    for pair in range(part // LANES):
        lanes = slice(pair * LANES, (pair + 1) * LANES)
        total = jnp.zeros((2 * LANES, 2 * LANES), F32)
        for place in range(rows // block):
            here = slice(place * block, (place + 1) * block)
            features = turned_features(sq_ref[here, lanes], cos_ref[here, :], sin_ref[here, :])
            state = dot_tn(
                features, jnp.concatenate([gn_ref[here, lanes], gd_ref[here, lanes]], axis=1)
            )
            state = jnp.where(keep, state, 0.0)
            st_ref[place, pair] = state.astype(BF16)
            total = total + state
        compact(total, packed_ref, tot_ref, pair, pl.program_id(0), False)


def unmix(
    coords, first, mixed, rden, sq, cosines, sines, w, sums1, sums2, turns, gbias, layout, block
):
    rows, width = first.shape
    groups, halves, shard, _ = w.shape
    part = width // halves
    pairs = width // LANES
    half = pairs // halves
    blocks = rows // block
    row_spec = pl.BlockSpec((rows, part), lambda t: (0, t))
    tile = part + LANES
    out_specs, out_shapes = piece_outputs(layout, tile, lambda t: layout[3] // tile - 1)
    units = gbias.shape[1] // halves
    full = jax.ShapeDtypeStruct((rows, width), BF16)
    return call(
        functools.partial(
            unmix_kernel, block=block, step=512, shard=layout[2]
        ),
        grid=(halves,),
        in_specs=[
            scalars(), whole((rows, width)), row_spec, row_spec, row_spec,
            whole((rows, LANES)), whole((rows, LANES)),
            pl.BlockSpec((groups, 1, shard, part), lambda t: (0, t, 0, 3)),
            whole((8, width)), whole((8, width)), whole(turns.shape),
        ]
        + [pl.BlockSpec((8, units), lambda t: (0, t))],
        out_specs=out_specs
        + [
            row_spec, row_spec,
            pl.BlockSpec((blocks, half, 2 * LANES, 2 * LANES), lambda t: (0, t, 0, 0)),
            whole((half + 1, 2 * LANES, LANES)),
        ],
        out_shape=out_shapes
        + [
            full, full,
            jax.ShapeDtypeStruct((blocks, pairs, 2 * LANES, 2 * LANES), BF16),
            jax.ShapeDtypeStruct((half + 1, 2 * LANES, LANES), BF16),
        ],
        scratch_shapes=[
            pltpu.VMEM((width, tile), BF16), pltpu.VMEM((half + 1, 2 * LANES, LANES), F32)
        ],
        compiler_params=params(),
        cost_estimate=cost(4 * rows * width * width, 16e6),
        name="unmix",
        near_in=(1, 4),
        near_out=(len(out_shapes), len(out_shapes) + 1),
    )(coords, first, mixed, rden, sq, cosines, sines, w, sums1, sums2, turns, gbias)


def unattend_kernel(
    sq_ref, sk_ref, v_ref, gn_ref, gd_ref, cm_ref, cos_ref, sin_ref, st_ref, in_ref, lt_ref, gq_ref,
    gk_ref, later_ref, *refs, start_pair
):
    query_ref, dk_ref, dv_ref = refs[-3:]
    blocks, block, _ = cm_ref.shape
    piece = min(PIECE, block)
    masks = [lane_mask(block, head) for head in range(2)]
    ones = jnp.ones((block, LANES), BF16)
    pair = start_pair + pl.program_id(0)
    each = in_ref.shape[0] - 1
    incoming = expand(in_ref, pair % each, pair // each, True)
    outgoing = expand(later_ref, pair % each, pair // each, False)
    for place in range(blocks):
        start = place * block
        all_here = slice(start, start + block)
        keys, values = sk_ref[all_here, :], v_ref[all_here, :]
        sides = jnp.concatenate([values, ones], axis=1)
        key_sides = [keys * mask for mask in masks]
        state = incoming
        for earlier in range(place):
            state = state + st_ref[earlier, 0].astype(F32)
        state = state.astype(BF16)
        grad_keys = [None] * (block // piece)
        grad_values = [None] * (block // piece)
        for low in range(0, block, piece):
            here = slice(start + low, start + low + piece)
            span = low + piece
            queries, grads, slopes = sq_ref[here, :], gn_ref[here, :], gd_ref[here, :]
            grad_queries = None
            for head in range(2):
                mask = masks[head][:piece]
                cm = cm_ref[place, low : low + piece, :span]
                masked_queries, masked_grads = queries * mask, grads * mask
                scores = dot_nt(masked_queries, keys[:span])
                weights = (scores * cm).astype(BF16)
                back = dot_nt(
                    jnp.concatenate([masked_grads, slopes * mask], axis=1), sides[:span]
                )
                back = (back * cm).astype(BF16)
                term = dot(back, key_sides[head][:span])
                grad_queries = term if grad_queries is None else grad_queries + term
                key_term = dot_tn(back, masked_queries)
                value_term = dot_tn(weights, masked_grads)
                for piece_at in range(span // piece):
                    at = slice(piece_at * piece, (piece_at + 1) * piece)
                    old = grad_keys[piece_at]
                    grad_keys[piece_at] = key_term[at] if old is None else old + key_term[at]
                    old = grad_values[piece_at]
                    grad_values[piece_at] = value_term[at] if old is None else old + value_term[at]
            far = dot_nt(jnp.concatenate([grads, slopes], axis=1), state)
            grad_queries = (
                grad_queries
                + far[:, :LANES] * cos_ref[here, :]
                + far[:, LANES:] * sin_ref[here, :]
            ) * gq_ref[here, :].astype(F32)
            query_ref[here, :] = grad_queries.astype(BF16)
        grad_keys = jnp.concatenate(grad_keys, axis=0)
        grad_values = jnp.concatenate(grad_values, axis=0)
        state = outgoing
        for later in range(place + 1, blocks):
            state = state + lt_ref[later, 0].astype(F32)
        state = state.astype(BF16)
        far = dot_nt(sides, state)
        grad_keys = (
            grad_keys
            + far[:, :LANES] * cos_ref[all_here, :]
            + far[:, LANES:] * sin_ref[all_here, :]
        ) * gk_ref[all_here, :].astype(F32)
        features = turned_features(keys, cos_ref[all_here, :], sin_ref[all_here, :])
        grad_values = grad_values + dot(features, state[:, :LANES])
        dk_ref[all_here, :] = grad_keys.astype(BF16)
        dv_ref[all_here, :] = grad_values.astype(BF16)


def unattend(
    sq, sk, v, gn, gd, cm, cosines, sines, states, incoming, later, slope_q, slope_k,
    later_in, start, count, partial
):
    rows, width = sq.shape
    blocks = cm.shape[0]
    spec = pl.BlockSpec((rows, LANES), lambda p: (0, start + p))
    state_spec = pl.BlockSpec((blocks, 1, 2 * LANES, 2 * LANES), lambda p: (0, start + p, 0, 0))
    full = jax.ShapeDtypeStruct((rows, width), BF16)
    return call(
        functools.partial(unattend_kernel, start_pair=start),
        grid=(count,),
        in_specs=[
            spec, spec, spec, spec, spec,
            whole(cm.shape), whole((rows, LANES)), whole((rows, LANES)),
            state_spec,
            whole(incoming.shape),
            state_spec, spec, spec, whole(later_in.shape),
        ]
        + [pl.BlockSpec(memory_space=pl.ANY)] * len(partial),
        out_specs=[spec, spec, spec],
        out_shape=[jax.ShapeDtypeStruct((rows, width), BF16), full, full],
        input_output_aliases={14 + at: at for at in range(len(partial))},
        compiler_params=params(),
        cost_estimate=cost(20e9, 20e6),
        name="unattend",
        near_in=(0, 1, 2, 3, 4, 14, 15, 16),
        near_out=(0, 1, 2),
    )(sq, sk, v, gn, gd, cm, cosines, sines, states, incoming, later, slope_q, slope_k, later_in, *partial)


def weights_kernel(coords_ref, x_ref, q_ref, k_ref, v_ref, edge_ref, *refs, shard):
    outs, product_ref = refs[:-1], refs[-1]
    coords = [coords_ref[place] for place in range(4)]
    rows, part = q_ref.shape
    width = x_ref.shape[1]
    ones = jnp.ones((rows, LANES), BF16)
    lane = lax.broadcasted_iota(jnp.int32, (part, LANES), 1)
    sums = jnp.zeros((part, LANES), F32)
    for place, ref in enumerate((q_ref, k_ref, v_ref)):
        at = slice(place * part, (place + 1) * part)
        product_ref[:, at] = dot_tn(x_ref[...], ref[...]).astype(BF16)
        sums = jnp.where(lane == place, dot_tn(ref[...], ones), sums)
    if shard % 16 == 0:
        edge = shard * part // width
        for place in range(width // shard):
            piece = jnp.concatenate(
                [sums[place * edge : (place + 1) * edge], jnp.zeros((shard - edge, LANES), F32)], axis=0
            )
            product_ref[place * shard : (place + 1) * shard, 3 * part :] = piece.astype(BF16)
    else:
        product_ref[:, 3 * part :] = dot(edge_ref[...], sums.astype(BF16)).astype(BF16)
    emit(product_ref, pl.program_id(0), outs, coords)


def weight_gradients(coords, x, q, k, v, edges, layout):
    rows, width = x.shape
    halves = layout[1]
    spec = pl.BlockSpec((rows, width // halves), lambda t: (0, t))
    out_specs, out_shapes = piece_outputs(layout, layout[3], lambda t: 0)
    return call(
        functools.partial(weights_kernel, shard=layout[2]),
        grid=(halves,),
        in_specs=[scalars(), whole((rows, width)), spec, spec, spec, whole(edges.shape)],
        out_specs=out_specs,
        out_shape=out_shapes,
        scratch_shapes=[pltpu.VMEM((width, layout[3]), BF16)],
        compiler_params=params(),
        cost_estimate=cost(2 * rows * width * 3 * width, 10e6),
        name="weight_gradients",
        near_in=(2, 3, 4),
    )(coords, x, q, k, v, edges)


def inputs_kernel(first_ref, q_ref, k_ref, v_ref, w_ref, out_ref):
    halves = w_ref.shape[1]
    width = first_ref.shape[1]
    part = width // halves
    total = first_ref[...].astype(F32)
    for half in range(halves):
        side = w_ref[:, half].reshape(width, 3 * part)
        at = slice(half * part, (half + 1) * part)
        joined = jnp.concatenate([q_ref[:, at], k_ref[:, at], v_ref[:, at]], axis=1)
        total = total + dot_nt(joined, side)
    out_ref[...] = total.astype(BF16)


def input_gradient(first, q, k, v, w, step):
    rows, width = first.shape
    groups, halves, shard, _ = w.shape
    part = width // halves
    spec = pl.BlockSpec((step, width), lambda i: (i, 0))
    return call(
        inputs_kernel,
        grid=(rows // step,),
        in_specs=[
            spec, spec, spec, spec,
            pl.BlockSpec((groups, halves, shard, 3 * part), lambda i: (0, 0, 0, 0)),
        ],
        out_specs=spec,
        out_shape=jax.ShapeDtypeStruct((rows, width), BF16),
        compiler_params=params(),
        cost_estimate=cost(2 * rows * width * 3 * width, 14e6),
        name="input_gradient",
        near_in=(0, 1, 2, 3),
    )(first, q, k, v, w)


def moves():
    def table(change):
        pairs = []
        for source in range(32):
            z, y, c, x = source // 8, source // 4 % 2, source // 2 % 2, source % 2
            z, y, c, x = change(z, y, c, x)
            pairs.append((source, ((z * 2 + y) * 2 + c) * 2 + x))
        return pairs

    along = [table(lambda z, y, c, x, k=k: (z ^ k, y, c, x)) for k in range(4)]
    beside = table(lambda z, y, c, x: (z, y ^ c, c, x ^ 1 ^ c))
    across = table(lambda z, y, c, x: (z, y ^ 1 ^ c, c, x ^ c))
    core = table(lambda z, y, c, x: (z, y, c ^ 1, x))
    return along, beside, across, core


def add(left, right):
    return (left.astype(F32) + right.astype(F32)).astype(BF16)


def send(value, table, begin, end, axes=BOTH):
    value = after(value, *begin) if begin else value
    value = lax.ppermute(value, axes, table)
    return after(value, *end) if end else value


class Gather:
    def __init__(self, piece):
        self.tables = moves()
        self.held = piece

    def line(self, begin=(), end=()):
        parts = [send(self.held, self.tables[0][k], begin, end) for k in (1, 2, 3)]
        self.held = join([self.held] + parts)

    def line_parts(self, begin):
        self.held = self.held, [send(self.held, self.tables[0][k], begin, ()) for k in (1, 2, 3)]

    def beside(self, begin=(), end=()):
        self.held = jnp.concatenate([self.held, send(self.held, self.tables[1], begin, end)], axis=0)

    def across(self, begin=(), end=()):
        self.held = jnp.concatenate([self.held, send(self.held, self.tables[2], begin, end)], axis=0)

    def core(self, begin=(), end=()):
        return [self.held, send(self.held, self.tables[3], begin, end)]


class Sum:
    def __init__(self, own, other):
        self.tables = moves()
        self.kept, self.sent = own, other

    def fold(self, table, begin, end):
        arrived = send(self.sent, table, begin, end)
        size = self.kept.shape[0] // 2
        kept = add(self.kept[:size], arrived[:size])
        self.kept, self.sent = kept, add(self.kept[size:], arrived[size:])

    def both(self):
        return [self.kept, self.sent]

    def core(self, begin=(), end=()):
        self.fold(self.tables[3], begin, end)

    def across(self, begin=(), end=()):
        self.fold(self.tables[2], begin, end)

    def beside(self, begin=(), end=()):
        arrived = send(self.sent, self.tables[1], begin, end)
        self.parts = [add(self.kept[k], arrived[k]) for k in range(4)]

    def line(self, begin=(), end=()):
        parts = [send(self.parts[k], self.tables[0][k], begin, end) for k in (1, 2, 3)]
        total = self.parts[0].astype(F32)
        for part in parts:
            total = total + part.astype(F32)
        return total


def local(
    inputs, w_query, w_key, w_value, b_query, b_key, b_value, w_out, b_out, norm_gain, norm_shift,
    w_up, b_up, w_down, b_down, final_gain, final_shift, piece_starts, grad_output,
):
    rows, width = inputs.shape
    halves = lax.axis_size("tp")
    replicas = lax.axis_size("fsdp")
    length = rows * halves
    block = min(512, length)
    blocks = rows // block
    shard = width // replicas
    part = width // halves
    units = w_up.shape[1]
    me = lax.axis_index("tp")
    pieces = replicas == 16 and halves == 2 and shard % 16 == 0
    place = lax.axis_index("fsdp")
    coords = jnp.stack([place // 4, place // 2 % 2, place % 2, me]).astype(jnp.int32)

    def layout(columns):
        return replicas, halves, shard, columns, pieces

    places = me * rows + jnp.arange(rows, dtype=jnp.int32)
    flags = jnp.any(piece_starts[0][:, None] == (places // PIECE * PIECE)[None, :], axis=0)
    angle = 0.5 * jnp.pi / length * places.astype(F32)
    cosines, sines = jnp.cos(angle), jnp.sin(angle)
    at = jnp.arange(block, dtype=jnp.int32)
    allowed = (at[None, None, :] <= at[None, :, None]) | (
        (at[None, None, :] // PIECE == at[None, :, None] // PIECE)
        & flags.reshape(blocks, block)[:, :, None]
    )
    c, s = cosines.reshape(blocks, block), sines.reshape(blocks, block)
    cm = jnp.where(allowed, c[:, :, None] * c[:, None, :] + s[:, :, None] * s[:, None, :], 0.0)
    cosines = jnp.broadcast_to(cosines[:, None], (rows, LANES))
    sines = jnp.broadcast_to(sines[:, None], (rows, LANES))

    each, edge = units // width, shard // halves
    if pieces:
        edges, turns = jnp.zeros((8, LANES), BF16), jnp.zeros((1, 8, LANES), BF16)
    else:
        edges, turns = selectors(width, part, shard, edge, each)
    thins = (
        b_query, b_key, b_value, b_up, b_out, norm_gain, norm_shift, b_down, final_gain, final_shift
    )
    if pieces:
        attention_shard = pack(w_query, w_key, w_value, w_out.T, thins)
    else:
        columns = []
        for thin in thins:
            thin = jnp.pad(thin, (0, -thin.shape[0] % shard))
            columns.append(thin.reshape(-1, shard).T)
        columns = jnp.concatenate(columns, axis=1)
        columns = jnp.pad(columns, ((0, 0), (0, LANES - columns.shape[1])))
        attention_shard = jnp.concatenate([w_query, w_key, w_value, w_out.T, columns], axis=1)
    down_shard = w_down.T

    def gather_all(piece):
        everything = lax.all_gather(piece, BOTH, axis=0, tiled=False)
        everything = everything.reshape(replicas, halves, shard, piece.shape[1])
        return jnp.moveaxis(everything, 1, 0).reshape(1, halves, width, piece.shape[1])

    if pieces:
        first_chunk, up_chunk, down_chunk = Gather(attention_shard), Gather(w_up), Gather(down_shard)
        first_chunk.line([], [cm, cosines, sines, coords])
        four = first_chunk.held
        first_chunk.beside()
        up_chunk.line([four])
        first_chunk.across()
        sixteen = first_chunk.held
        four = up_chunk.held
        w_attention = first_chunk.core([four])
        up_chunk.beside([sixteen, four], w_attention)
        eight = up_chunk.held
        down_chunk.line_parts([sixteen, four])
        w_attention = [after(w_attention[0], eight), w_attention[1]]
    else:
        w_attention, w_lift, w_drop = [
            [gather_all(piece)] for piece in (attention_shard, w_up, down_shard)
        ]


    columns = 4 * part + LANES
    sq, sk, v, slope_q, slope_k, states, total, w_attention = project(
        coords, inputs, w_attention, columns, edges, cosines, sines, block, shard, halves
    )
    queries, there = sq, []
    if pieces:
        up_chunk.across([], [sq])
        down_chunk.held = join(
            [down_chunk.held[0]] + [after(part, sq) for part in down_chunk.held[1]]
        )
        there = [up_chunk.held, down_chunk.held]
        queries = after(sq, *there)
    num, den = attend(queries, sk, v, cm, cosines, sines, states)
    bias_up, vectors = unpack(after(w_attention, num), turns, shard, each)
    towards = [(i, i + 1) for i in range(halves - 1)]
    incoming = send(total, towards, there, [num, vectors], "tp")
    if pieces:
        w_lift = up_chunk.core(there, [num, vectors])
        down_chunk.beside(there, [num, vectors])
        there = [down_chunk.held, incoming, w_lift[1]]
        num = after(num, *there)
    mixed, rden, normal, scale, low = mix(
        num, den, sq, incoming, cosines, sines, w_attention, inputs, vectors, 512
    )
    if pieces:
        down_chunk.across(there, [low])
        there = [down_chunk.held]
        low = after(low, *there)
    act, slope, w_lift = lift(
        coords, low, w_lift, bias_up, units, 768, 3 if pieces else 0
    )
    if pieces:
        w_drop = down_chunk.core(there, [act])
    output, branch, sums_second, w_drop = drop(
        coords, act, w_drop, normal, vectors, grad_output, units, 256
    )

    gdown = wide_gradient(coords, branch, act, layout(units), units, 512, "down_gradient")
    gl, gbias_up = bend(branch, w_drop, after(slope, *gdown), units, 768)
    if pieces:
        down_sum = Sum(*gdown)
        down_sum.core([], [gl])
        branch = after(branch, *down_sum.both())
    first_low, sums_first = lower(gl, w_lift, branch, normal, scale, vectors, units, 256)
    wide = units + part + LANES
    *gup, gn, gd, later, later_total = unmix(
        coords, first_low, mixed, rden, sq, cosines, sines, w_attention,
        sums_first, sums_second, turns, gbias_up, layout(wide), block,
    )
    there = []
    if pieces:
        down_sum.across([], [gn])
        there = down_sum.both()
    gup = wide_gradient(
        coords, after(low, *there, *gup), gl, layout(wide), units, 512, "up_gradient", gup
    )
    towards = [(i + 1, i) for i in range(halves - 1)]
    later_in = send(later_total, towards, there, gup, "tp")
    there = [later_in, *gup]
    gn = after(gn, *there)
    pairs = width // LANES
    partial = ()
    for turn, (begin, count) in enumerate(((0, pairs // 3), (pairs // 3, pairs - pairs // 3))):
        partial = unattend(
            sq, sk, v, gn, gd, cm, cosines, sines, states, incoming, later, slope_q, slope_k,
            later_in, begin, count, partial,
        )
        if pieces and turn == 0:
            up_sum = Sum(*gup)
            up_sum.core(there, partial)
            down_sum.beside(there, partial)
            there = [*up_sum.both(), *down_sum.parts]
            partial = after(tuple(partial), *there)
    query_low, key_low, value_low = partial
    if pieces:
        up_sum.across(there, [key_low])
        gdown = down_sum.line(there, [key_low])
        query_low = after(query_low, *up_sum.both(), gdown)
    gqkv = weight_gradients(
        coords, inputs, query_low, key_low, value_low, edges, layout(3 * part + LANES)
    )
    if pieces:
        up_sum.beside([], gqkv)
        rest_sum = Sum(*gqkv)
        rest_sum.core(up_sum.parts)
        rest_sum.across()
        first_low = after(first_low, *rest_sum.both())
        grad_inputs = input_gradient(first_low, query_low, key_low, value_low, w_attention, 256)
        gup = up_sum.line([], [*rest_sum.both(), grad_inputs])
        rest_sum.beside()
        rest = rest_sum.line()
    else:

        def scatter(grad):
            grad = jnp.moveaxis(grad.reshape(halves, replicas, shard, grad.shape[2]), 0, 1)
            grad = grad.reshape(replicas * halves, shard, grad.shape[3])
            return lax.psum_scatter(grad, BOTH, scatter_dimension=0, tiled=False).astype(F32)

        gdown, gup, rest = [scatter(grad[0]) for grad in (gdown, gup, gqkv)]
        grad_inputs = input_gradient(first_low, query_low, key_low, value_low, w_attention, 256)

    scaling = 1.0 / replicas
    gdown, gup, rest = gdown * scaling, gup * scaling, rest * scaling
    sums = gup[:, units + part :].T
    small = rest[:edge, 3 * part :].T
    return (
        output,
        grad_inputs,
        rest[:, :part],
        rest[:, part : 2 * part],
        rest[:, 2 * part : 3 * part],
        small[0],
        small[1],
        small[2],
        gup[:, units : units + part].T,
        sums[2],
        sums[0],
        sums[1],
        gup[:, :units],
        sums[6 : 6 + units // width].reshape(-1),
        gdown.T,
        sums[5],
        sums[3],
        sums[4],
    )


def solution(mesh):
    row = P(("fsdp", "tp"), None)
    split, turned = P("fsdp", "tp"), P("tp", "fsdp")
    thin, wide = P(("tp", "fsdp")), P("fsdp")
    return jax.shard_map(
        local,
        mesh=mesh,
        in_specs=(
            row, split, split, split, thin, thin, thin, turned, wide, wide, wide,
            split, thin, turned, wide, wide, wide, P("fsdp", None), row,
        ),
        out_specs=(
            row, row, split, split, split, thin, thin, thin, turned, wide, wide, wide,
            split, thin, turned, wide, wide, wide,
        ),
        check_vma=False,
    )
```
